32 devices in a mesh: groups: 2 (over x), space: 16 (over z, y, core).
Axes of the slice: x: 2, y: 2, z: 4, core: 2. Of those that a mesh axis runs over, the one named last changes fastest.
Arguments:
- mol_feats: bfloat16 [8192, 512], P(('groups', 'space')), parts along dimension 0, may hold values from -6 to 6
- w_src: bfloat16 [512, 512], replicated, may hold values from -0.25 to 0.25
- w_dst: bfloat16 [512, 512], replicated, may hold values from -0.25 to 0.25
- w_out: bfloat16 [512, 529], replicated, may hold values from -0.25 to 0.25
- grad_blocks: bfloat16 [16, 32, 128, 529], P('space', 'groups'), parts along dimension 1, may hold values from -6 to 6
- edge_src: int32 [65536], P(('groups', 'space')), parts along dimension 0, may hold values from 0 to 255
- edge_dst: int32 [65536], P(('groups', 'space')), parts along dimension 0, may hold values from 0 to 383
- edge_live: int32 [65536], P(('groups', 'space')), parts along dimension 0, may hold values from 0 to 1, as said below
Outputs:
- feature_grad: float32 [8192, 512], P(('groups', 'space')), parts along dimension 0
- src_weight_grad: float32 [1024, 512], P(('groups', 'space')), parts along dimension 0
- dst_weight_grad: float32 [1024, 512], P(('groups', 'space')), parts along dimension 0
- out_weight_grad: float32 [1024, 529], P(('groups', 'space')), parts along dimension 0
The draws below stay inside these ranges and needn't reach their ends.
There are 2 independent parts, one for each index of `groups`. The reference program is written for one: setup_inputs(seed, part) draws one part's arguments, and reference() takes and returns one part's arrays. A program takes and returns all parts, laid end to end along the dimension named above; an argument that names none is the same for every part. Nothing has to cross between parts.
Inputs may be any that keep to these rules, and one draw needn't show every extreme that they name: `edge_live`: on every slab the live slots of each owner come first among its 128 slots, and the slab's own blocks fill all 128 of theirs. Any other owner has at most 64 live slots for a slab, and on every slab some other owner has exactly 64. `edge_dst`: index into the slab's molecules extended by 64 molecules of the slab below (first) and 64 of the slab above (last), periodic.
All inputs are finite; a program needn't handle non-finite values.
Results may differ from the reference program's by a relative error of at most 0.0029.
Values may be sent and summed in bfloat16 or wider, within the bound.
No kernel may reach another device: no remote copies, remote signals or barrier semaphores. Data moves between devices by JAX's collectives and lax.ppermute only.
A program may use at most 64 MiB of HBM per device.

```python
import jax
import jax.numpy as jnp
from jax import lax

WIDTH = 512
BLOCK = 23
MOL_DEV = 256
EDGE_DEV = 2048
REACH = 64
CAP = 128
MOLS = 4096
EDGES = 32768
N_SPACE = 16


def draw_edge_live(key, part):
    half = CAP // 2
    counts = jax.random.randint(jax.random.fold_in(key, 7), (N_SPACE, N_SPACE), 3 * CAP // 8, half + 1)
    rows = jnp.arange(N_SPACE)[:, None]
    cols = jnp.arange(N_SPACE)[None, :]
    counts = jnp.where(cols == (rows + 1) % N_SPACE, half, counts)
    counts = jnp.where(rows == cols, CAP, counts)
    slots = jnp.arange(CAP)[None, None, :]
    live = (slots < counts[:, :, None]).astype(jnp.int32)
    return live.reshape(N_SPACE * N_SPACE * CAP)


def set_ends(values, stream_key, low, top_value):
    extent = values.shape
    spot = [jax.random.randint(jax.random.fold_in(stream_key, axis), (), 0, extent[axis]) for axis in range(len(extent))]
    values = values.at[tuple(spot)].set(low)
    longest = extent.index(max(extent))
    spot[longest] = (spot[longest] + 1) % extent[longest]
    return values.at[tuple(spot)].set(top_value)


def raised(result, key, source, target, parts, factor):
    owner, partner = [(jnp.arange(result.shape[position]) // (result.shape[position] // parts)).reshape([-1 if axis == position else 1 for axis in range(result.ndim)]) for position in (source, target)]
    chosen = jax.random.permutation(key, parts)[partner]
    strong = (owner == chosen) | (owner == (partner + parts // 2) % parts)
    return jnp.where(strong, factor * result, result)


def block_scale(own_key, dims, shards, smallest, largest):
    level = 1.0
    for dim, blocks in shards:
        draws = jax.random.uniform(jax.random.fold_in(jax.random.fold_in(own_key, 6), dim), (blocks,), jnp.float32, smallest / len(shards), largest / len(shards))
        level = level * jnp.repeat(jnp.exp(draws), dims[dim] // blocks).reshape((-1,) + (1,) * (len(dims) - 1 - dim))
    return level


def centred(key, dims, scale, reach, split=(), held_as=jnp.bfloat16):
    factor_of = block_scale(key, dims, split, -0.22, 0.18) if split else 1.0
    result = jax.random.normal(key, dims, jnp.float32) * scale * factor_of
    return jnp.minimum(jnp.maximum(result, -reach), reach).astype(held_as)


def bell_draw_with(key, extent, scale, limit, shards, heavy, held_as=jnp.bfloat16):
    drawn = scale * jax.random.normal(key, extent, jnp.float32)
    if shards:
        drawn = drawn * block_scale(key, extent, shards, -0.22, 0.18)
    return jnp.clip(raised(drawn, jax.random.fold_in(key, 3), *heavy), -limit, limit).astype(held_as)


def setup_inputs(seed: int = 0, part: int = 0) -> dict:
    key_list = jax.random.split(jax.random.key(seed), 9)
    own_keys = jax.random.split(jax.random.fold_in(key_list[8], part), 9)
    return {
        "mol_feats": bell_draw_with(own_keys[0], (MOLS, WIDTH), 1.0, 6.0, ((0, 16),), (0, 1, 16, 2.0)),
        "w_src": centred(key_list[1], (WIDTH, WIDTH), WIDTH ** -0.5, 0.25),
        "w_dst": centred(key_list[2], (WIDTH, WIDTH), WIDTH ** -0.5, 0.25),
        "w_out": centred(key_list[3], (WIDTH, BLOCK * BLOCK), WIDTH ** -0.5, 0.25),
        "grad_blocks": centred(own_keys[4], (N_SPACE, N_SPACE, CAP, BLOCK * BLOCK), 1.0, 6.0, ((0, 16),)),
        "edge_src": set_ends(jax.random.randint(own_keys[5], (EDGES,), 0, MOL_DEV), jax.random.fold_in(own_keys[5], 1), 0, MOL_DEV - 1).astype(jnp.int32),
        "edge_dst": set_ends(jax.random.randint(own_keys[6], (EDGES,), 0, MOL_DEV + 2 * REACH), jax.random.fold_in(own_keys[6], 1), 0, (MOL_DEV + 2 * REACH) - 1).astype(jnp.int32),
        "edge_live": draw_edge_live(jax.random.fold_in(jax.random.fold_in(key_list[8], part), 71), part),
    }


def reference(mol_feats, w_src, w_dst, w_out, grad_blocks, edge_src, edge_dst, edge_live):
    highest = lax.Precision.HIGHEST
    proj_src = jnp.dot(mol_feats, w_src, preferred_element_type=jnp.float32)
    proj_dst = jnp.dot(mol_feats, w_dst, preferred_element_type=jnp.float32)
    width = mol_feats.shape[1]
    entries = w_out.shape[1]

    def step(carry, inputs):
        src_sum, dst_sum, out_sum = carry
        index, local_src, local_dst, live = inputs
        src_rows = (index * MOL_DEV + local_src).astype(jnp.int32)
        dst_rows = ((index * MOL_DEV + local_dst - REACH) % MOLS).astype(jnp.int32)
        blocks = lax.dynamic_index_in_dim(grad_blocks, index, 1, keepdims=False).reshape(EDGE_DEV, entries)
        blocks = jnp.where(live[:, None] > 0, blocks, jnp.zeros_like(blocks))
        pre = proj_src[src_rows] + proj_dst[dst_rows]
        sigma = jax.nn.sigmoid(pre)
        hidden = (pre * sigma).astype(jnp.bfloat16)
        grad_hidden = jnp.dot(blocks, w_out.T, preferred_element_type=jnp.float32)
        grad_pre = (grad_hidden * sigma * (1.0 + pre * (1.0 - sigma))).astype(jnp.bfloat16)
        grad_wide = lax.optimization_barrier(grad_pre).astype(jnp.float32)
        src_sum = src_sum + jax.ops.segment_sum(grad_wide, src_rows, num_segments=MOLS)
        dst_sum = dst_sum + jax.ops.segment_sum(grad_wide, dst_rows, num_segments=MOLS)
        out_sum = out_sum + jnp.dot(hidden.T, blocks, preferred_element_type=jnp.float32)
        return (src_sum, dst_sum, out_sum), None

    start = (jnp.zeros((MOLS, width), jnp.float32), jnp.zeros((MOLS, width), jnp.float32), jnp.zeros((width, entries), jnp.float32))
    inputs = (jnp.arange(N_SPACE, dtype=jnp.int32), edge_src.reshape(N_SPACE, EDGE_DEV), edge_dst.reshape(N_SPACE, EDGE_DEV), edge_live.reshape(N_SPACE, EDGE_DEV))
    (src_sum, dst_sum, out_sum), unused = lax.scan(step, start, inputs)
    factor = float(EDGES) ** -0.5
    feats_wide = mol_feats.astype(jnp.float32)
    feature_grad = jnp.dot(src_sum, w_src.astype(jnp.float32).T, precision=highest) + jnp.dot(dst_sum, w_dst.astype(jnp.float32).T, precision=highest)
    src_weight_grad = factor * jnp.dot(feats_wide.T, src_sum, precision=highest)
    dst_weight_grad = factor * jnp.dot(feats_wide.T, dst_sum, precision=highest)
    out_weight_grad = factor * out_sum
    return (feature_grad, src_weight_grad, dst_weight_grad, out_weight_grad)
```

```python
import functools

import jax
import jax.numpy as jnp
from jax import lax
from jax.experimental import pallas as pl
from jax.experimental.pallas import tpu as pltpu
from jax.sharding import PartitionSpec as P

F32 = jnp.float32
BF16 = jnp.bfloat16
LANES = 128
PACK = 16
NN = (((1,), (0,)), ((), ()))
NT = (((1,), (1,)), ((), ()))


def mm(left, right, dims=NN):
    return lax.dot_general(left, right, dims, preferred_element_type=F32)


def halves(x):
    high = x.astype(BF16)
    return high, (x - high.astype(F32)).astype(BF16)


def round_up(x, to):
    return -(-x // to) * to


def vmem(count):
    return [pl.BlockSpec(memory_space=pltpu.VMEM)] * count


def pack_kernel(rows, half, me_ref, g_ref, out_ref, own_ref, late_ref):
    entries, slabs, cap = g_ref.shape
    groups = LANES // half
    size = PACK * slabs
    to = lax.broadcasted_iota(jnp.int32, (size, size), 0)
    source = lax.broadcasted_iota(jnp.int32, (size, size), 1)
    perm = jnp.where((to % PACK) * slabs + to // PACK == source, 1.0, 0.0).astype(BF16)
    for block in range(rows // PACK):
        early, late = [], []
        for group in range(groups):
            first = group * rows + block * PACK
            valid = max(0, min(PACK, entries - first))
            parts = []
            if valid:
                parts.append(g_ref[first : first + valid])
            if valid < PACK:
                parts.append(jnp.zeros((PACK - valid, slabs, cap), BF16))
            tile = parts[0] if len(parts) == 1 else jnp.concatenate(parts, axis=0)
            tile = tile.reshape(size, cap)
            early.append(tile[:, :half])
            late.append(tile[:, half:])
        both = jnp.concatenate(early + late, axis=1)
        moved = mm(perm, both).astype(BF16).reshape(slabs, PACK, 2 * LANES)
        here = pl.ds(block * PACK, PACK)
        out_ref[:, here, :] = moved[:, :, :LANES]
        late_ref[:, here, :] = moved[:, :, LANES:]
    own_ref[...] = late_ref[me_ref[0]]


def slot_rows(ref, me, half):
    slabs, cap = ref.shape
    per = LANES // half
    rows = []
    for tile in range(slabs // per):
        rows.append(jnp.concatenate([ref[tile * per + k : tile * per + k + 1, :half] for k in range(per)], axis=1))
    own = ref[pl.ds(me, 1), :][:, half:]
    rows.append(jnp.concatenate([own, jnp.full((1, LANES - half), -1, jnp.int32)], axis=1))
    return rows


def edge_kernel(
    half, me_ref, feats_ref, below_ref, above_ref, w_src_ref, w_dst_ref, src_ref, dst_ref, live_ref,
    onehot_ref, hidden_ref, slope_ref,
):
    me = me_ref[0]
    mols = feats_ref.shape[0]
    reach = below_ref.shape[0]
    wide = mols + 2 * reach
    feats = feats_ref[...]
    ext = jnp.concatenate([feats, below_ref[...], above_ref[...]], axis=0)
    proj_src = mm(feats, w_src_ref[...])
    proj_dst = mm(ext, w_dst_ref[...])
    proj = jnp.concatenate([proj_src, proj_dst], axis=0).T
    high, low = halves(proj)
    mol_src = lax.broadcasted_iota(jnp.int32, (mols, LANES), 0)
    mol_dst = lax.broadcasted_iota(jnp.int32, (wide, LANES), 0)
    lists = [slot_rows(ref, me, half) for ref in (src_ref, dst_ref, live_ref)]
    for tile, (src, dst, live) in enumerate(zip(*lists)):
        src = jnp.where(live > 0, src, -1)
        moved = jnp.where(dst < reach, dst + mols, jnp.where(dst < reach + mols, dst - reach, dst))
        dst = jnp.where(live > 0, moved, -1)
        one_src = jnp.where(mol_src == src, 1.0, 0.0).astype(BF16)
        one_dst = jnp.where(mol_dst == dst, 1.0, 0.0).astype(BF16)
        onehot = jnp.concatenate([one_src, one_dst], axis=0)
        here = pl.ds(tile * LANES, LANES)
        onehot_ref[:, here] = onehot
        pre = mm(high, onehot) + mm(low, onehot)
        sigma = 1.0 / (1.0 + jnp.exp(-pre))
        hidden_ref[:, here] = (pre * sigma).astype(BF16)
        slope_ref[:, here] = sigma * (1.0 + pre * (1.0 - sigma))


def grad_kernel(
    half, factor, came_ref, own_ref, onehot_ref, hidden_ref, slope_ref, w_out_ref, ext_ref, w_src_ref, w_dst_ref,
    terms_ref, feature_ref, rims_ref, g_ref,
):
    slabs, rows, _ = came_ref.shape
    groups = LANES // half
    mols = feature_ref.shape[0]
    width = w_src_ref.shape[0]
    for tile in range(slabs // groups + 1):
        if tile < slabs // groups:
            chunks = [came_ref[tile * groups + k] for k in range(groups)]
        else:
            chunks = [own_ref[...]] + [jnp.zeros((rows, LANES), BF16)] * (groups - 1)
        for group in range(groups):
            lanes = slice(group * half, (group + 1) * half)
            g_ref[group * rows : (group + 1) * rows, tile * LANES : (tile + 1) * LANES] = jnp.concatenate(
                [chunk[:, lanes] for chunk in chunks], axis=1
            )
    g = g_ref[...]
    dpre = (mm(w_out_ref[...], g) * slope_ref[...]).astype(BF16)
    sums = mm(onehot_ref[...], dpre, NT)
    rims_ref[...] = sums[2 * mols :]
    high, low = halves(sums)
    feats = ext_ref[:, :mols]
    terms_ref[:, :width] = (factor * (mm(feats, high[:mols]) + mm(feats, low[:mols]))).astype(BF16)
    ext = ext_ref[...]
    terms_ref[:, width : 2 * width] = (factor * (mm(ext, high[mols:]) + mm(ext, low[mols:]))).astype(BF16)
    out_term = factor * mm(hidden_ref[...], g, NT)
    padding = terms_ref.shape[1] - 2 * width - out_term.shape[1]
    if padding:
        out_term = jnp.concatenate([out_term, jnp.zeros((out_term.shape[0], padding), F32)], axis=1)
    terms_ref[:, 2 * width :] = out_term.astype(BF16)
    w_src = w_src_ref[...]
    w_dst = w_dst_ref[...]
    feature_ref[...] = (
        mm(high[:mols], w_src, NT)
        + mm(low[:mols], w_src, NT)
        + mm(high[mols : 2 * mols], w_dst, NT)
        + mm(low[mols : 2 * mols], w_dst, NT)
    )


def rim_kernel(part_ref, from_below_ref, from_above_ref, w_dst_ref, out_ref):
    mols = part_ref.shape[0]
    reach = from_below_ref.shape[0]
    rims = jnp.concatenate([from_below_ref[...], from_above_ref[...]], axis=0)
    high, low = halves(rims)
    w_dst = w_dst_ref[...]
    grad = mm(high, w_dst, NT) + mm(low, w_dst, NT)
    out_ref[:reach] = part_ref[:reach] + grad[:reach]
    out_ref[reach : mols - reach] = part_ref[reach : mols - reach]
    out_ref[mols - reach :] = part_ref[mols - reach :] + grad[reach:]


def total_kernel(terms_ref, src_ref, dst_ref, out_ref):
    width = src_ref.shape[1]
    total = terms_ref[0].astype(F32)
    for slab in range(1, terms_ref.shape[0]):
        total = total + terms_ref[slab].astype(F32)
    src_ref[...] = total[:, :width]
    dst_ref[...] = total[:, width : 2 * width]
    out_ref[...] = total[:, 2 * width : 2 * width + out_ref.shape[1]]


def on_device(mol_feats, w_src, w_dst, w_out, grad_blocks, edge_src, edge_dst, edge_live):
    slabs = lax.axis_size("space")
    mols, width = mol_feats.shape
    entries = w_out.shape[1]
    cap = grad_blocks.shape[2]
    half = cap // 2
    reach = mols // 4
    groups = LANES // half
    rows = round_up(pl.cdiv(entries, groups), PACK)
    slots = (slabs // groups + 1) * LANES
    factor = float(edge_src.shape[0] * slabs) ** (-0.5)
    me = lax.axis_index("space").astype(jnp.int32).reshape(1)
    smem = pl.BlockSpec(memory_space=pltpu.SMEM)
    big = pltpu.CompilerParams(vmem_limit_bytes=48 * 1024 * 1024)
    up = [(i, (i + 1) % slabs) for i in range(slabs)]
    down = [((i + 1) % slabs, i) for i in range(slabs)]

    below = lax.ppermute(mol_feats[mols - reach :], "space", up)
    above = lax.ppermute(mol_feats[:reach], "space", down)

    packed, own = pl.pallas_call(
        functools.partial(pack_kernel, rows, half),
        out_shape=(
            jax.ShapeDtypeStruct((slabs, rows, LANES), BF16),
            jax.ShapeDtypeStruct((rows, LANES), BF16),
        ),
        in_specs=[smem] + vmem(1),
        out_specs=tuple(vmem(2)),
        scratch_shapes=[pltpu.VMEM((slabs, rows, LANES), BF16)],
        compiler_params=big,
        name="pack",
    )(me, jnp.transpose(grad_blocks[0], (2, 0, 1)))
    came = lax.all_to_all(packed, "space", split_axis=0, concat_axis=0, tiled=True)

    onehot, hidden, slope = pl.pallas_call(
        functools.partial(edge_kernel, half),
        out_shape=(
            jax.ShapeDtypeStruct((2 * mols + 2 * reach, slots), BF16),
            jax.ShapeDtypeStruct((width, slots), BF16),
            jax.ShapeDtypeStruct((width, slots), F32),
        ),
        in_specs=[smem] + vmem(8),
        out_specs=tuple(vmem(3)),
        compiler_params=big,
        name="edges",
        cost_estimate=pl.CostEstimate(
            flops=2 * width * slots * 2 * (2 * mols + 2 * reach), bytes_accessed=8 * 1024 * 1024,
            transcendentals=width * slots,
        ),
    )(
        me, mol_feats, below, above, w_src, w_dst,
        edge_src.reshape(slabs, cap), edge_dst.reshape(slabs, cap), edge_live.reshape(slabs, cap),
    )

    ext = jnp.concatenate([mol_feats, below, above], axis=0).T
    w_out_wide = jnp.pad(w_out, ((0, 0), (0, groups * rows - entries)))
    terms, feature_part, rims = pl.pallas_call(
        functools.partial(grad_kernel, half, factor),
        out_shape=(
            jax.ShapeDtypeStruct((width, 2 * width + round_up(groups * rows, LANES)), BF16),
            jax.ShapeDtypeStruct((mols, width), F32),
            jax.ShapeDtypeStruct((2 * reach, width), F32),
        ),
        in_specs=vmem(9),
        out_specs=tuple(vmem(3)),
        scratch_shapes=[pltpu.VMEM((groups * rows, slots), BF16)],
        compiler_params=big,
        name="grads",
    )(came, own, onehot, hidden, slope, w_out_wide, ext, w_src, w_dst)

    from_above = lax.ppermute(rims[:reach], "space", down)
    from_below = lax.ppermute(rims[reach:], "space", up)
    spread = lax.all_to_all(
        terms.reshape(slabs, width // slabs, -1), "space", split_axis=0, concat_axis=0, tiled=True
    )
    feature_grad = pl.pallas_call(
        rim_kernel,
        out_shape=jax.ShapeDtypeStruct((mols, width), F32),
        in_specs=vmem(4),
        out_specs=vmem(1)[0],
        compiler_params=big,
        name="rims",
    )(feature_part, from_below, from_above, w_dst)
    part = width // slabs
    src_grad, dst_grad, out_grad = pl.pallas_call(
        total_kernel,
        out_shape=(
            jax.ShapeDtypeStruct((part, width), F32),
            jax.ShapeDtypeStruct((part, width), F32),
            jax.ShapeDtypeStruct((part, entries), F32),
        ),
        in_specs=vmem(1),
        out_specs=tuple(vmem(3)),
        compiler_params=big,
        name="totals",
    )(spread)
    return (feature_grad, src_grad, dst_grad, out_grad)


def solution(mesh):
    placed = (
        P(("groups", "space"), None),
        P(),
        P(),
        P(),
        P("space", "groups", None, None),
        P(("groups", "space")),
        P(("groups", "space")),
        P(("groups", "space")),
    )
    return jax.shard_map(
        on_device,
        mesh=mesh,
        in_specs=placed,
        out_specs=(
            P(("groups", "space"), None),
            P(("groups", "space"), None),
            P(("groups", "space"), None),
            P(("groups", "space"), None),
        ),
        check_vma=False,
    )
```

```python
import functools

import jax
import jax.numpy as jnp
from jax import lax
from jax.experimental import pallas as pl
from jax.experimental.pallas import tpu as pltpu
from jax.sharding import PartitionSpec as P

F32 = jnp.float32
BF16 = jnp.bfloat16
LANES = 128
PACK = 16
NN = (((1,), (0,)), ((), ()))
NT = (((1,), (1,)), ((), ()))


def mm(left, right, dims=NN):
    return lax.dot_general(left, right, dims, preferred_element_type=F32)


def halves(x):
    high = x.astype(BF16)
    return high, (x - high.astype(F32)).astype(BF16)


def round_up(x, to):
    return -(-x // to) * to


def vmem(count):
    return [pl.BlockSpec(memory_space=pltpu.VMEM)] * count


def pack_kernel(rows, half, me_ref, g_ref, out_ref, own_ref, late_ref):
    entries, slabs, cap = g_ref.shape
    groups = LANES // half
    size = PACK * slabs
    to = lax.broadcasted_iota(jnp.int32, (size, size), 0)
    source = lax.broadcasted_iota(jnp.int32, (size, size), 1)
    perm = jnp.where((to % PACK) * slabs + to // PACK == source, 1.0, 0.0).astype(BF16)
    for block in range(rows // PACK):
        early, late = [], []
        for group in range(groups):
            first = group * rows + block * PACK
            valid = max(0, min(PACK, entries - first))
            parts = []
            if valid:
                parts.append(g_ref[first : first + valid])
            if valid < PACK:
                parts.append(jnp.zeros((PACK - valid, slabs, cap), BF16))
            tile = parts[0] if len(parts) == 1 else jnp.concatenate(parts, axis=0)
            tile = tile.reshape(size, cap)
            early.append(tile[:, :half])
            late.append(tile[:, half:])
        both = jnp.concatenate(early + late, axis=1)
        moved = mm(perm, both).astype(BF16).reshape(slabs, PACK, 2 * LANES)
        here = pl.ds(block * PACK, PACK)
        out_ref[:, here, :] = moved[:, :, :LANES]
        late_ref[:, here, :] = moved[:, :, LANES:]
    own_ref[...] = late_ref[me_ref[0]]


def slot_rows(ref, me, half):
    slabs, cap = ref.shape
    per = LANES // half
    rows = []
    for tile in range(slabs // per):
        rows.append(jnp.concatenate([ref[tile * per + k : tile * per + k + 1, :half] for k in range(per)], axis=1))
    own = ref[pl.ds(me, 1), :][:, half:]
    rows.append(jnp.concatenate([own, jnp.full((1, LANES - half), -1, jnp.int32)], axis=1))
    return rows


def edge_kernel(
    half, me_ref, feats_ref, below_ref, above_ref, w_src_ref, w_dst_ref, src_ref, dst_ref, live_ref,
    onehot_ref, hidden_ref, slope_ref, ext_ref,
):
    me = me_ref[0]
    mols = feats_ref.shape[0]
    reach = below_ref.shape[0]
    wide = mols + 2 * reach
    feats = feats_ref[...]
    ext = jnp.concatenate([feats, below_ref[...], above_ref[...]], axis=0)
    ext_ref[...] = ext.T
    proj_src = mm(feats, w_src_ref[...])
    proj_dst = mm(ext, w_dst_ref[...])
    proj = jnp.concatenate([proj_src, proj_dst], axis=0).T
    high, low = halves(proj)
    mol_src = lax.broadcasted_iota(jnp.int32, (mols, LANES), 0)
    mol_dst = lax.broadcasted_iota(jnp.int32, (wide, LANES), 0)
    lists = [slot_rows(ref, me, half) for ref in (src_ref, dst_ref, live_ref)]
    for tile, (src, dst, live) in enumerate(zip(*lists)):
        src = jnp.where(live > 0, src, -1)
        moved = jnp.where(dst < reach, dst + mols, jnp.where(dst < reach + mols, dst - reach, dst))
        dst = jnp.where(live > 0, moved, -1)
        one_src = jnp.where(mol_src == src, 1.0, 0.0).astype(BF16)
        one_dst = jnp.where(mol_dst == dst, 1.0, 0.0).astype(BF16)
        onehot = jnp.concatenate([one_src, one_dst], axis=0)
        here = pl.ds(tile * LANES, LANES)
        onehot_ref[:, here] = onehot
        pre = mm(high, onehot) + mm(low, onehot)
        sigma = 1.0 / (1.0 + jnp.exp(-pre))
        hidden_ref[:, here] = (pre * sigma).astype(BF16)
        slope_ref[:, here] = sigma * (1.0 + pre * (1.0 - sigma))


def halve(terms, odd, keep_ref, send_ref, first):
    count, rows, _ = keep_ref.shape
    lanes = slice(first, first + terms.shape[-1])
    pairs = terms.reshape(count, 2, rows, terms.shape[-1])
    even_part, odd_part = pairs[:, 0], pairs[:, 1]
    keep_ref[:, :, lanes] = jnp.where(odd > 0, odd_part, even_part)
    send_ref[:, :, lanes] = jnp.where(odd > 0, even_part, odd_part).astype(BF16)


def fold_kernel(bit, me_ref, keep_ref, came_ref, next_ref, send_ref):
    odd = (me_ref[0] >> bit) % 2
    halve(keep_ref[...] + came_ref[...].astype(F32), odd, next_ref, send_ref, 0)


def direct_kernel(bit, me_ref, keep_ref, came_ref, own_ref, *rest):
    *send_refs, total_ref = rest
    mine = me_ref[0] >> bit
    total_ref[...] = keep_ref[...] + came_ref[...].astype(F32)
    own_ref[...] = total_ref[mine]
    for step, send_ref in enumerate(send_refs):
        send_ref[...] = total_ref[mine ^ (step + 1)].astype(BF16)


def grad_kernel(
    half, factor, me_ref, came_ref, own_ref, onehot_ref, hidden_ref, slope_ref, w_out_ref, ext_ref, w_src_ref, w_dst_ref,
    keep_ref, send_ref, feature_ref, rims_ref, g_ref,
):
    odd = me_ref[0] % 2
    slabs, rows, _ = came_ref.shape
    groups = LANES // half
    mols = feature_ref.shape[0]
    width = w_src_ref.shape[0]
    for tile in range(slabs // groups + 1):
        if tile < slabs // groups:
            chunks = [came_ref[tile * groups + k] for k in range(groups)]
        else:
            chunks = [own_ref[...]] + [jnp.zeros((rows, LANES), BF16)] * (groups - 1)
        for group in range(groups):
            lanes = slice(group * half, (group + 1) * half)
            g_ref[group * rows : (group + 1) * rows, tile * LANES : (tile + 1) * LANES] = jnp.concatenate(
                [chunk[:, lanes] for chunk in chunks], axis=1
            )
    g = g_ref[...]
    dpre = (mm(w_out_ref[...], g) * slope_ref[...]).astype(BF16)
    sums = mm(onehot_ref[...], dpre, NT)
    rims_ref[...] = sums[2 * mols :]
    high, low = halves(sums)
    feats = ext_ref[:, :mols]
    ext = ext_ref[...]
    halve(factor * (mm(feats, high[:mols]) + mm(feats, low[:mols])), odd, keep_ref, send_ref, 0)
    halve(factor * (mm(ext, high[mols:]) + mm(ext, low[mols:])), odd, keep_ref, send_ref, width)
    out_term = factor * mm(hidden_ref[...], g, NT)
    padding = keep_ref.shape[2] - 2 * width - out_term.shape[1]
    if padding:
        out_term = jnp.concatenate([out_term, jnp.zeros((out_term.shape[0], padding), F32)], axis=1)
    halve(out_term, odd, keep_ref, send_ref, 2 * width)
    w_src = w_src_ref[...]
    w_dst = w_dst_ref[...]
    feature_ref[...] = (
        mm(high[:mols], w_src, NT)
        + mm(low[:mols], w_src, NT)
        + mm(high[mols : 2 * mols], w_dst, NT)
        + mm(low[mols : 2 * mols], w_dst, NT)
    )


def rim_kernel(part_ref, from_below_ref, from_above_ref, w_dst_ref, out_ref):
    mols = part_ref.shape[0]
    reach = from_below_ref.shape[0]
    rims = jnp.concatenate([from_below_ref[...], from_above_ref[...]], axis=0)
    high, low = halves(rims)
    w_dst = w_dst_ref[...]
    grad = mm(high, w_dst, NT) + mm(low, w_dst, NT)
    out_ref[:reach] = part_ref[:reach] + grad[:reach]
    out_ref[reach : mols - reach] = part_ref[reach : mols - reach]
    out_ref[mols - reach :] = part_ref[mols - reach :] + grad[reach:]


def total_kernel(own_ref, *rest):
    *came_refs, src_ref, dst_ref, out_ref = rest
    width = src_ref.shape[1]
    total = own_ref[...]
    for came_ref in came_refs:
        total = total + came_ref[...].astype(F32)
    src_ref[...] = total[:, :width]
    dst_ref[...] = total[:, width : 2 * width]
    out_ref[...] = total[:, 2 * width : 2 * width + out_ref.shape[1]]


def swap(block, bit, slabs):
    return lax.ppermute(block, "space", [(i, i ^ (1 << bit)) for i in range(slabs)])


def on_device(mol_feats, w_src, w_dst, w_out, grad_blocks, edge_src, edge_dst, edge_live):
    slabs = lax.axis_size("space")
    mols, width = mol_feats.shape
    entries = w_out.shape[1]
    cap = grad_blocks.shape[2]
    half = cap // 2
    reach = mols // 4
    groups = LANES // half
    rows = round_up(pl.cdiv(entries, groups), PACK)
    slots = (slabs // groups + 1) * LANES
    factor = float(edge_src.shape[0] * slabs) ** (-0.5)
    me = lax.axis_index("space").astype(jnp.int32).reshape(1)
    smem = pl.BlockSpec(memory_space=pltpu.SMEM)
    big = pltpu.CompilerParams(vmem_limit_bytes=24 * 1024 * 1024)
    up = [(i, (i + 1) % slabs) for i in range(slabs)]
    down = [((i + 1) % slabs, i) for i in range(slabs)]

    below = lax.ppermute(mol_feats[mols - reach :], "space", up)
    above = lax.ppermute(mol_feats[:reach], "space", down)

    packed, own = pl.pallas_call(
        functools.partial(pack_kernel, rows, half),
        out_shape=(
            jax.ShapeDtypeStruct((slabs, rows, LANES), BF16),
            jax.ShapeDtypeStruct((rows, LANES), BF16),
        ),
        in_specs=[smem] + vmem(1),
        out_specs=tuple(vmem(2)),
        scratch_shapes=[pltpu.VMEM((slabs, rows, LANES), BF16)],
        compiler_params=big,
        name="pack",
    )(me, jnp.transpose(grad_blocks[0], (2, 0, 1)))
    packed, below, above = lax.optimization_barrier((packed, below, above))
    came = lax.all_to_all(packed, "space", split_axis=0, concat_axis=0, tiled=True)

    onehot, hidden, slope, ext = pl.pallas_call(
        functools.partial(edge_kernel, half),
        out_shape=(
            jax.ShapeDtypeStruct((2 * mols + 2 * reach, slots), BF16),
            jax.ShapeDtypeStruct((width, slots), BF16),
            jax.ShapeDtypeStruct((width, slots), F32),
            jax.ShapeDtypeStruct((width, mols + 2 * reach), BF16),
        ),
        in_specs=[smem] + vmem(8),
        out_specs=tuple(vmem(4)),
        compiler_params=big,
        name="edges",
        cost_estimate=pl.CostEstimate(
            flops=2 * width * slots * 2 * (2 * mols + 2 * reach), bytes_accessed=8 * 1024 * 1024,
            transcendentals=width * slots,
        ),
    )(
        me, mol_feats, below, above, w_src, w_dst,
        edge_src.reshape(slabs, cap), edge_dst.reshape(slabs, cap), edge_live.reshape(slabs, cap),
    )

    w_out_wide = jnp.pad(w_out, ((0, 0), (0, groups * rows - entries)))
    part = width // slabs
    lanes = 2 * width + round_up(groups * rows, LANES)
    bits = 2
    rest = slabs >> bits

    def chunks(count, dtype):
        return jax.ShapeDtypeStruct((count, part, lanes), dtype)

    keep, send, feature_part, rims = pl.pallas_call(
        functools.partial(grad_kernel, half, factor),
        out_shape=(
            chunks(slabs // 2, F32),
            chunks(slabs // 2, BF16),
            jax.ShapeDtypeStruct((mols, width), F32),
            jax.ShapeDtypeStruct((2 * reach, width), F32),
        ),
        in_specs=[smem] + vmem(9),
        out_specs=tuple(vmem(4)),
        scratch_shapes=[pltpu.VMEM((groups * rows, slots), BF16)],
        compiler_params=big,
        name="grads",
    )(me, came, own, onehot, hidden, slope, w_out_wide, ext, w_src, w_dst)

    crossed = swap(send, 0, slabs)
    from_above = lax.ppermute(rims[:reach], "space", down)
    from_below = lax.ppermute(rims[reach:], "space", up)
    for bit in range(1, bits):
        keep, send = pl.pallas_call(
            functools.partial(fold_kernel, bit),
            out_shape=(chunks(keep.shape[0] // 2, F32), chunks(keep.shape[0] // 2, BF16)),
            in_specs=[smem] + vmem(2),
            out_specs=tuple(vmem(2)),
            compiler_params=big,
            name="fold",
        )(me, keep, crossed)
        crossed = swap(send, bit, slabs)
    one = jax.ShapeDtypeStruct((part, lanes), BF16)
    own_term, *sends = pl.pallas_call(
        functools.partial(direct_kernel, bits),
        out_shape=(jax.ShapeDtypeStruct((part, lanes), F32),) + (one,) * (rest - 1),
        in_specs=[smem] + vmem(2),
        out_specs=tuple(vmem(rest)),
        scratch_shapes=[pltpu.VMEM((rest, part, lanes), F32)],
        compiler_params=big,
        name="direct",
    )(me, keep, crossed)
    cames = [
        lax.ppermute(block, "space", [(i, i ^ ((step + 1) << bits)) for i in range(slabs)])
        for step, block in enumerate(sends)
    ]
    feature_grad = pl.pallas_call(
        rim_kernel,
        out_shape=jax.ShapeDtypeStruct((mols, width), F32),
        in_specs=vmem(4),
        out_specs=vmem(1)[0],
        compiler_params=big,
        name="rims",
    )(feature_part, from_below, from_above, w_dst)
    src_grad, dst_grad, out_grad = pl.pallas_call(
        total_kernel,
        out_shape=(
            jax.ShapeDtypeStruct((part, width), F32),
            jax.ShapeDtypeStruct((part, width), F32),
            jax.ShapeDtypeStruct((part, entries), F32),
        ),
        in_specs=vmem(rest),
        out_specs=tuple(vmem(3)),
        compiler_params=big,
        name="totals",
    )(own_term, *cames)
    return (feature_grad, src_grad, dst_grad, out_grad)


def solution(mesh):
    placed = (
        P(("groups", "space"), None),
        P(),
        P(),
        P(),
        P("space", "groups", None, None),
        P(("groups", "space")),
        P(("groups", "space")),
        P(("groups", "space")),
    )
    return jax.shard_map(
        on_device,
        mesh=mesh,
        in_specs=placed,
        out_specs=(
            P(("groups", "space"), None),
            P(("groups", "space"), None),
            P(("groups", "space"), None),
            P(("groups", "space"), None),
        ),
        check_vma=False,
    )
```

```python
import functools

import jax
import jax.numpy as jnp
from jax import lax
from jax.experimental import pallas as pl
from jax.experimental.pallas import tpu as pltpu
from jax.sharding import PartitionSpec as P

F32 = jnp.float32
BF16 = jnp.bfloat16
LANES = 128
PACK = 16
NN = (((1,), (0,)), ((), ()))
NT = (((1,), (1,)), ((), ()))


def mm(left, right, dims=NN):
    return lax.dot_general(left, right, dims, preferred_element_type=F32)


def halves(x):
    high = x.astype(BF16)
    return high, (x - high.astype(F32)).astype(BF16)


def round_up(x, to):
    return -(-x // to) * to


def vmem(count):
    return [pl.BlockSpec(memory_space=pltpu.VMEM)] * count


def pack_kernel(rows, half, me_ref, feats_ref, g_ref, out_ref, own_ref, low_ref, top_ref, late_ref, here_ref, sems, rim_sems):
    entries, slabs, cap = g_ref.shape
    mols = feats_ref.shape[0]
    reach = low_ref.shape[0]
    groups = LANES // half
    blocks = rows // PACK
    count = sems.shape[0]
    stages = []
    for stage in range(count):
        begin, end = stage * blocks // count, (stage + 1) * blocks // count
        copies = []
        for group in range(groups):
            first = min(entries, group * rows + begin * PACK)
            last = min(entries, group * rows + end * PACK)
            if first < last:
                copies.append(
                    pltpu.make_async_copy(g_ref.at[first:last], here_ref.at[first:last], sems.at[stage, group])
                )
        stages.append((begin, end, copies))
        for copy in copies:
            copy.start()
    rims = [
        pltpu.make_async_copy(feats_ref.at[:reach], low_ref, rim_sems.at[0]),
        pltpu.make_async_copy(feats_ref.at[mols - reach :], top_ref, rim_sems.at[1]),
    ]
    for copy in rims:
        copy.start()
    size = PACK * slabs
    to = lax.broadcasted_iota(jnp.int32, (size, size), 0)
    source = lax.broadcasted_iota(jnp.int32, (size, size), 1)
    perm = jnp.where((to % PACK) * slabs + to // PACK == source, 1.0, 0.0).astype(BF16)
    for begin, end, copies in stages:
        for copy in copies:
            copy.wait()
        for block in range(begin, end):
            early, late = [], []
            for group in range(groups):
                first = group * rows + block * PACK
                valid = max(0, min(PACK, entries - first))
                tiles = []
                if valid:
                    tiles.append(here_ref[first : first + valid])
                if valid < PACK:
                    tiles.append(jnp.zeros((PACK - valid, slabs, cap), BF16))
                tile = tiles[0] if len(tiles) == 1 else jnp.concatenate(tiles, axis=0)
                tile = tile.reshape(size, cap)
                early.append(tile[:, :half])
                late.append(tile[:, half:])
            both = jnp.concatenate(early + late, axis=1)
            moved = mm(perm, both).astype(BF16).reshape(slabs, PACK, 2 * LANES)
            here = pl.ds(block * PACK, PACK)
            out_ref[:, here, :] = moved[:, :, :LANES]
            late_ref[:, here, :] = moved[:, :, LANES:]
    own_ref[...] = late_ref[me_ref[0]]
    for copy in rims:
        copy.wait()


def unpack(half, came_ref, own_ref, g_ref):
    slabs, rows, _ = came_ref.shape
    groups = LANES // half
    for tile in range(slabs // groups + 1):
        if tile < slabs // groups:
            chunks = [came_ref[tile * groups + k] for k in range(groups)]
        else:
            chunks = [own_ref[...]] + [jnp.zeros((rows, LANES), BF16)] * (groups - 1)
        for group in range(groups):
            lanes = slice(group * half, (group + 1) * half)
            g_ref[group * rows : (group + 1) * rows, tile * LANES : (tile + 1) * LANES] = jnp.concatenate(
                [chunk[:, lanes] for chunk in chunks], axis=1
            )


def slot_rows(ref, me, half):
    slabs, cap = ref.shape
    per = LANES // half
    rows = []
    for tile in range(slabs // per):
        rows.append(jnp.concatenate([ref[tile * per + k : tile * per + k + 1, :half] for k in range(per)], axis=1))
    own = ref[pl.ds(me, 1), :][:, half:]
    rows.append(jnp.concatenate([own, jnp.full((1, LANES - half), -1, jnp.int32)], axis=1))
    return rows


def edge_kernel(
    half, me_ref, feats_ref, below_ref, above_ref, w_src_ref, w_dst_ref, src_ref, dst_ref, live_ref,
    onehot_ref, hidden_ref, slope_ref, ext_ref,
):
    me = me_ref[0]
    mols = feats_ref.shape[0]
    reach = below_ref.shape[0]
    wide = mols + 2 * reach
    feats = feats_ref[...]
    ext = jnp.concatenate([feats, below_ref[...], above_ref[...]], axis=0)
    ext_ref[...] = ext.T
    proj_src = mm(feats, w_src_ref[...])
    proj_dst = mm(ext, w_dst_ref[...])
    proj = jnp.concatenate([proj_src, proj_dst], axis=0).T
    high, low = halves(proj)
    mol_src = lax.broadcasted_iota(jnp.int32, (mols, LANES), 0)
    mol_dst = lax.broadcasted_iota(jnp.int32, (wide, LANES), 0)
    lists = [slot_rows(ref, me, half) for ref in (src_ref, dst_ref, live_ref)]
    for tile, (src, dst, live) in enumerate(zip(*lists)):
        src = jnp.where(live > 0, src, -1)
        moved = jnp.where(dst < reach, dst + mols, jnp.where(dst < reach + mols, dst - reach, dst))
        dst = jnp.where(live > 0, moved, -1)
        one_src = jnp.where(mol_src == src, 1.0, 0.0).astype(BF16)
        one_dst = jnp.where(mol_dst == dst, 1.0, 0.0).astype(BF16)
        onehot = jnp.concatenate([one_src, one_dst], axis=0)
        here = pl.ds(tile * LANES, LANES)
        onehot_ref[:, here] = onehot
        pre = mm(high, onehot) + mm(low, onehot)
        sigma = 1.0 / (1.0 + jnp.exp(-pre))
        hidden_ref[:, here] = (pre * sigma).astype(BF16)
        slope_ref[:, here] = sigma * (1.0 + pre * (1.0 - sigma))


def halve(terms, odd, place, keep_ref, send_ref, first):
    count, rows, _ = keep_ref.shape
    width = terms.shape[-1]
    lanes = slice(first, first + width)
    inner = 1 << place
    pairs = terms.reshape(count // inner, 2, inner, rows, width)
    even_part = pairs[:, 0].reshape(count, rows, width)
    odd_part = pairs[:, 1].reshape(count, rows, width)
    keep_ref[:, :, lanes] = jnp.where(odd > 0, odd_part, even_part)
    send_ref[:, :, lanes] = jnp.where(odd > 0, even_part, odd_part).astype(BF16)


def fold_kernel(bit, place, me_ref, keep_ref, came_ref, next_ref, send_ref):
    odd = (me_ref[0] >> bit) % 2
    halve(keep_ref[...] + came_ref[...].astype(F32), odd, place, next_ref, send_ref, 0)


def close_kernel(keep_ref, came_ref, send_ref):
    send_ref[...] = (keep_ref[...] + came_ref[...].astype(F32)).astype(BF16)


def grad_kernel(
    half, factor, me_ref, came_ref, own_ref, w_out_ref, slope_hbm, onehot_hbm, ext_hbm,
    keep_ref, send_ref, sums_ref, lower_ref, upper_ref, g_ref, slope_ref, onehot_ref, ext_ref, sems,
):
    odd = me_ref[0] % 2
    width = w_out_ref.shape[0]
    slots = g_ref.shape[1]
    inside = sums_ref.shape[0]
    mols = inside // 2
    step = slots // 3
    tiles = []
    for tile in range(3):
        lanes = pl.ds(tile * step, step)
        copies = [
            pltpu.make_async_copy(slope_hbm.at[:, lanes], slope_ref.at[:, lanes], sems.at[tile, 0]),
            pltpu.make_async_copy(onehot_hbm.at[:, lanes], onehot_ref.at[:, lanes], sems.at[tile, 1]),
        ]
        for copy in copies:
            copy.start()
        tiles.append(copies)
    ext_copy = pltpu.make_async_copy(ext_hbm, ext_ref, sems.at[3, 0])
    ext_copy.start()
    unpack(half, came_ref, own_ref, g_ref)
    sums = None
    for tile, copies in enumerate(tiles):
        lanes = slice(tile * step, (tile + 1) * step)
        dh = mm(w_out_ref[...], g_ref[:, lanes])
        for copy in copies:
            copy.wait()
        dpre = (dh * slope_ref[:, lanes]).astype(BF16)
        term = mm(onehot_ref[:, lanes], dpre, NT)
        sums = term if sums is None else sums + term
    reach = lower_ref.shape[0]
    lower_ref[...] = sums[inside : inside + reach]
    upper_ref[...] = sums[inside + reach :]
    sums_ref[...] = sums[:inside]
    high, low = halves(sums)
    ext_copy.wait()
    feats = ext_ref[:, :mols]
    ext = ext_ref[...]
    halve(factor * (mm(feats, high[:mols]) + mm(feats, low[:mols])), odd, 0, keep_ref, send_ref, 0)
    halve(factor * (mm(ext, high[mols:]) + mm(ext, low[mols:])), odd, 0, keep_ref, send_ref, width)


def outer_kernel(factor, me_ref, hidden_ref, g_ref, keep_ref, send_ref):
    term = factor * mm(hidden_ref[...], g_ref[...], NT)
    padding = keep_ref.shape[2] - term.shape[1]
    if padding > 0:
        term = jnp.concatenate([term, jnp.zeros((term.shape[0], padding), F32)], axis=1)
    halve(term, me_ref[0] % 2, 0, keep_ref, send_ref, 0)


def rim_kernel(sums_ref, from_below_ref, from_above_ref, w_src_ref, w_dst_ref, out_ref):
    mols = out_ref.shape[0]
    reach = from_below_ref.shape[0]
    src = sums_ref[:mols]
    dst = sums_ref[mols:]
    dst = jnp.concatenate(
        [dst[:reach] + from_below_ref[...], dst[reach : mols - reach], dst[mols - reach :] + from_above_ref[...]], axis=0
    )
    w_src = w_src_ref[...]
    w_dst = w_dst_ref[...]
    src_high, src_low = halves(src)
    dst_high, dst_low = halves(dst)
    out_ref[...] = mm(src_high, w_src, NT) + mm(src_low, w_src, NT) + mm(dst_high, w_dst, NT) + mm(dst_low, w_dst, NT)


def total_kernel(*refs):
    *refs, src_ref, dst_ref, out_ref = refs
    count = len(refs) // 2
    width = src_ref.shape[1]
    totals = []
    for piece in (refs[:count], refs[count:]):
        terms = [ref[slab].astype(F32) for ref in piece for slab in range(ref.shape[0])]
        totals.append(functools.reduce(jnp.add, terms))
    sides, outer = totals
    src_ref[...] = sides[:, :width]
    dst_ref[...] = sides[:, width:]
    out_ref[...] = outer[:, : out_ref.shape[1]]


def in_hbm(x):
    return pltpu.with_memory_space_constraint(x, pltpu.HBM)


def swap(block, bit, slabs):
    return lax.ppermute(block, "space", [(i, i ^ (1 << bit)) for i in range(slabs)])


def on_device(mol_feats, w_src, w_dst, w_out, grad_blocks, edge_src, edge_dst, edge_live):
    slabs = lax.axis_size("space")
    mols, width = mol_feats.shape
    entries = w_out.shape[1]
    cap = grad_blocks.shape[2]
    half = cap // 2
    reach = mols // 4
    groups = LANES // half
    slots = (slabs // groups + 1) * LANES
    bits = slabs.bit_length() - 1
    if 3 <= bits <= 4:
        late_bits = tuple((bit, 0) for bit in range(3, bits))
        paths = (((0, 0), (1, 0), (2, 0)) + late_bits, ((0, 0), (2, 1), (1, 0)) + late_bits)
    else:
        paths = (tuple((bit, 0) for bit in range(min(bits, 2))),) * 2
    rest = slabs >> len(paths[0])
    part = width // slabs
    factor = float(edge_src.shape[0] * slabs) ** (-0.5)
    me = lax.axis_index("space").astype(jnp.int32).reshape(1)
    smem = pl.BlockSpec(memory_space=pltpu.SMEM)
    hbm = pl.BlockSpec(memory_space=pltpu.HBM)
    big = pltpu.CompilerParams(vmem_limit_bytes=24 * 1024 * 1024)
    up = [(i, (i + 1) % slabs) for i in range(slabs)]
    down = [((i + 1) % slabs, i) for i in range(slabs)]

    rows = round_up(pl.cdiv(entries, groups), PACK)
    stages = 4
    packed, own, low, top = pl.pallas_call(
        functools.partial(pack_kernel, rows, half),
        out_shape=(
            jax.ShapeDtypeStruct((slabs, rows, LANES), BF16),
            jax.ShapeDtypeStruct((rows, LANES), BF16),
            jax.ShapeDtypeStruct((reach, width), BF16),
            jax.ShapeDtypeStruct((reach, width), BF16),
        ),
        in_specs=[smem, hbm, hbm],
        out_specs=tuple(vmem(4)),
        scratch_shapes=[
            pltpu.VMEM((slabs, rows, LANES), BF16),
            pltpu.VMEM((entries, slabs, cap), BF16),
            pltpu.SemaphoreType.DMA((stages, groups)),
            pltpu.SemaphoreType.DMA((2,)),
        ],
        compiler_params=big,
        name="pack",
    )(me, in_hbm(mol_feats), in_hbm(jnp.transpose(grad_blocks[0], (2, 0, 1))))
    below = lax.ppermute(top, "space", up)
    above = lax.ppermute(low, "space", down)
    came = lax.all_to_all(packed, "space", split_axis=0, concat_axis=0, tiled=True)

    onehot, hidden, slope, ext = pl.pallas_call(
        functools.partial(edge_kernel, half),
        out_shape=(
            jax.ShapeDtypeStruct((2 * mols + 2 * reach, slots), BF16),
            jax.ShapeDtypeStruct((width, slots), BF16),
            jax.ShapeDtypeStruct((width, slots), F32),
            jax.ShapeDtypeStruct((width, mols + 2 * reach), BF16),
        ),
        in_specs=[smem] + vmem(8),
        out_specs=tuple(vmem(4)),
        compiler_params=big,
        name="edges",
        cost_estimate=pl.CostEstimate(
            flops=40 * width * slots * 2 * (2 * mols + 2 * reach), bytes_accessed=8 * 1024 * 1024,
            transcendentals=width * slots,
        ),
    )(
        me, mol_feats, below, above, w_src, w_dst,
        edge_src.reshape(slabs, cap), edge_dst.reshape(slabs, cap), edge_live.reshape(slabs, cap),
    )

    def chunks(count, lanes, dtype):
        return jax.ShapeDtypeStruct((count, part, lanes), dtype)

    entries_wide = groups * rows
    w_out_wide = jnp.pad(w_out, ((0, 0), (0, entries_wide - entries)))
    wide = mols + 2 * reach
    keep, send, sums, lower, upper, g = pl.pallas_call(
        functools.partial(grad_kernel, half, factor),
        out_shape=(
            chunks(slabs // 2, 2 * width, F32),
            chunks(slabs // 2, 2 * width, BF16),
            jax.ShapeDtypeStruct((2 * mols, width), F32),
            jax.ShapeDtypeStruct((reach, width), F32),
            jax.ShapeDtypeStruct((reach, width), F32),
            jax.ShapeDtypeStruct((entries_wide, slots), BF16),
        ),
        in_specs=[smem] + vmem(3) + [hbm] * 3,
        out_specs=tuple(vmem(6)),
        scratch_shapes=[
            pltpu.VMEM((width, slots), F32),
            pltpu.VMEM((mols + wide, slots), BF16),
            pltpu.VMEM((width, wide), BF16),
            pltpu.SemaphoreType.DMA((4, 2)),
        ],
        compiler_params=big,
        name="grads",
    )(me, came, own, w_out_wide, in_hbm(slope), in_hbm(onehot), in_hbm(ext))
    lanes = round_up(entries_wide, LANES)
    keep_o, send_o = pl.pallas_call(
        functools.partial(outer_kernel, factor),
        out_shape=(chunks(slabs // 2, lanes, F32), chunks(slabs // 2, lanes, BF16)),
        in_specs=[smem] + vmem(2),
        out_specs=tuple(vmem(2)),
        compiler_params=big,
        name="outer",
        cost_estimate=pl.CostEstimate(
            flops=40 * width * slots * entries_wide, bytes_accessed=4 * 1024 * 1024, transcendentals=0
        ),
    )(me, hidden, g)

    def fold(bit, place, keep, crossed):
        shape = (keep.shape[0] // 2, keep.shape[2])
        return pl.pallas_call(
            functools.partial(fold_kernel, bit, place),
            out_shape=(chunks(*shape, F32), chunks(*shape, BF16)),
            in_specs=[smem] + vmem(2),
            out_specs=tuple(vmem(2)),
            compiler_params=big,
            name="fold",
        )(me, keep, crossed)

    def close(keep, crossed):
        if rest == 1:
            return [keep, crossed]
        sends = pl.pallas_call(
            close_kernel,
            out_shape=chunks(rest, keep.shape[2], BF16),
            in_specs=vmem(2),
            out_specs=vmem(1)[0],
            compiler_params=big,
            name="close",
        )(keep, crossed)
        same = [[low + rank * (slabs // rest) for rank in range(rest)] for low in range(slabs // rest)]
        return [
            lax.all_to_all(sends, "space", split_axis=0, concat_axis=0, tiled=True, axis_index_groups=same)
        ]

    from_above = lax.ppermute(lower, "space", down)
    from_below = lax.ppermute(upper, "space", up)
    crossed = swap(send, 0, slabs)
    crossed_o = swap(send_o, 0, slabs)
    keep, crossed, from_above, from_below = lax.optimization_barrier((keep, crossed, from_above, from_below))
    for (bit, place), (bit_o, place_o) in zip(paths[0][1:], paths[1][1:]):
        keep, send = fold(bit, place, keep, crossed)
        crossed = swap(send, bit, slabs)
        keep_o, crossed_o, _ = lax.optimization_barrier((keep_o, crossed_o, send))
        keep_o, send_o = fold(bit_o, place_o, keep_o, crossed_o)
        crossed_o = swap(send_o, bit_o, slabs)
    terms = close(keep, crossed)
    terms_o = close(keep_o, crossed_o)
    feature_grad = pl.pallas_call(
        rim_kernel,
        out_shape=jax.ShapeDtypeStruct((mols, width), F32),
        in_specs=vmem(5),
        out_specs=vmem(1)[0],
        compiler_params=big,
        name="rims",
        cost_estimate=pl.CostEstimate(flops=2 * width * slots * width * 40, bytes_accessed=4 * 1024 * 1024, transcendentals=0),
    )(sums, from_below, from_above, w_src, w_dst)
    src_grad, dst_grad, out_grad = pl.pallas_call(
        total_kernel,
        out_shape=(
            jax.ShapeDtypeStruct((part, width), F32),
            jax.ShapeDtypeStruct((part, width), F32),
            jax.ShapeDtypeStruct((part, entries), F32),
        ),
        in_specs=vmem(len(terms) + len(terms_o)),
        out_specs=tuple(vmem(3)),
        compiler_params=big,
        name="totals",
    )(*terms, *terms_o)
    return (feature_grad, src_grad, dst_grad, out_grad)


def solution(mesh):
    placed = (
        P(("groups", "space"), None),
        P(),
        P(),
        P(),
        P("space", "groups", None, None),
        P(("groups", "space")),
        P(("groups", "space")),
        P(("groups", "space")),
    )
    return jax.shard_map(
        on_device,
        mesh=mesh,
        in_specs=placed,
        out_specs=(
            P(("groups", "space"), None),
            P(("groups", "space"), None),
            P(("groups", "space"), None),
            P(("groups", "space"), None),
        ),
        check_vma=False,
    )
```

```python
import functools

import jax
import jax.numpy as jnp
from jax import lax
from jax.experimental import pallas as pl
from jax.experimental.pallas import tpu as pltpu
from jax.sharding import PartitionSpec as P

F32 = jnp.float32
BF16 = jnp.bfloat16
LANES = 128
PACK = 16
NN = (((1,), (0,)), ((), ()))
NT = (((1,), (1,)), ((), ()))


def mm(left, right, dims=NN):
    return lax.dot_general(left, right, dims, preferred_element_type=F32)


def halves(x):
    high = x.astype(BF16)
    return high, (x - high.astype(F32)).astype(BF16)


def round_up(x, to):
    return -(-x // to) * to


def vmem(count):
    return [pl.BlockSpec(memory_space=pltpu.VMEM)] * count


def pack_kernel(rows, half, linked, me_ref, feats_ref, g_ref, even_ref, odd_ref, low_ref, top_ref, here_ref, sems, rim_sems):
    entries, slabs, cap = g_ref.shape
    mols = feats_ref.shape[0]
    reach = low_ref.shape[0]
    groups = LANES // half
    blocks = rows // PACK
    count = sems.shape[0]
    stages = []
    for stage in range(count):
        begin, end = stage * blocks // count, (stage + 1) * blocks // count
        copies = []
        for group in range(groups):
            first = min(entries, group * rows + begin * PACK)
            last = min(entries, group * rows + end * PACK)
            if first < last:
                copies.append(
                    pltpu.make_async_copy(g_ref.at[first:last], here_ref.at[first:last], sems.at[stage, group])
                )
        stages.append((begin, end, copies))
        for copy in copies:
            copy.start()
    rims = [
        pltpu.make_async_copy(feats_ref.at[:reach], low_ref, rim_sems.at[0]),
        pltpu.make_async_copy(feats_ref.at[mols - reach :], top_ref, rim_sems.at[1]),
    ]
    for copy in rims:
        copy.start()
    size = PACK * slabs
    to = lax.broadcasted_iota(jnp.int32, (size, size), 0)
    source = lax.broadcasted_iota(jnp.int32, (size, size), 1)
    slab = to // PACK
    if linked:
        slab = slab ^ me_ref[0]
    perm = jnp.where((to % PACK) * slabs + slab == source, 1.0, 0.0).astype(BF16)

    def lanes_of(block):
        early = []
        for group in range(groups):
            first = group * rows + block * PACK
            valid = max(0, min(PACK, entries - first))
            tiles = []
            if valid:
                tiles.append(here_ref[first : first + valid])
            if valid < PACK:
                tiles.append(jnp.zeros((PACK - valid, slabs, cap), BF16))
            tile = tiles[0] if len(tiles) == 1 else jnp.concatenate(tiles, axis=0)
            early.append(tile.reshape(size, cap)[:, :half])
        return early

    for begin, end, copies in stages:
        for copy in copies:
            copy.wait()
        for block in range(begin, end, 2):
            together = range(block, min(block + 2, end))
            lanes = [piece for one in together for piece in lanes_of(one)]
            moved = mm(perm, jnp.concatenate(lanes, axis=1)).astype(BF16)
            for index, one in enumerate(together):
                chunk = moved[:, index * LANES : (index + 1) * LANES].reshape(slabs // 2, 2, PACK, LANES)
                here = pl.ds(one * PACK, PACK)
                even_ref[:, here, :] = chunk[:, 0]
                odd_ref[:, here, :] = chunk[:, 1]
    for copy in rims:
        copy.wait()


def unpack(half, chunks, own_ref, g_ref):
    groups = LANES // half
    rows = g_ref.shape[0] // groups
    tiles = len(chunks) // groups
    for tile in range(tiles):
        here = [chunk() for chunk in chunks[tile * groups : (tile + 1) * groups]]
        for group in range(groups):
            lanes = slice(group * half, (group + 1) * half)
            g_ref[group * rows : (group + 1) * rows, tile * LANES : (tile + 1) * LANES] = jnp.concatenate(
                [chunk[:, lanes] for chunk in here], axis=1
            )
    g_ref[:, tiles * LANES :] = own_ref[...]


def slot_rows(ref, me, half, linked):
    slabs, cap = ref.shape
    per = LANES // half
    rows = []
    for tile in range(slabs // per):
        ids = [tile * per + k for k in range(per)]
        pieces = [ref[pl.ds(me ^ i if linked else i, 1), :] for i in ids]
        rows.append(jnp.concatenate([piece[:, :half] for piece in pieces], axis=1))
    own = ref[pl.ds(me, 1), :][:, half:]
    rows.append(jnp.concatenate([own, jnp.full((1, LANES - half), -1, jnp.int32)], axis=1))
    return rows


def edge_kernel(
    half, linked, me_ref, feats_ref, below_ref, above_ref, w_src_ref, w_dst_ref, src_ref, dst_ref, live_ref,
    onehot_ref, hidden_ref, slope_ref, ext_ref,
):
    me = me_ref[0]
    mols = feats_ref.shape[0]
    reach = below_ref.shape[0]
    wide = mols + 2 * reach
    feats = feats_ref[...]
    ext = jnp.concatenate([feats, below_ref[...], above_ref[...]], axis=0)
    ext_ref[...] = ext.T
    proj_src = mm(feats, w_src_ref[...])
    proj_dst = mm(ext, w_dst_ref[...])
    proj = jnp.concatenate([proj_src, proj_dst], axis=0).T
    high, low = halves(proj)
    mol_src = lax.broadcasted_iota(jnp.int32, (mols, LANES), 0)
    mol_dst = lax.broadcasted_iota(jnp.int32, (wide, LANES), 0)
    lists = [slot_rows(ref, me, half, linked) for ref in (src_ref, dst_ref, live_ref)]
    for tile, (src, dst, live) in enumerate(zip(*lists)):
        src = jnp.where(live > 0, src, -1)
        moved = jnp.where(dst < reach, dst + mols, jnp.where(dst < reach + mols, dst - reach, dst))
        dst = jnp.where(live > 0, moved, -1)
        one_src = jnp.where(mol_src == src, 1.0, 0.0).astype(BF16)
        one_dst = jnp.where(mol_dst == dst, 1.0, 0.0).astype(BF16)
        onehot = jnp.concatenate([one_src, one_dst], axis=0)
        here = pl.ds(tile * LANES, LANES)
        onehot_ref[:, here] = onehot
        pre = mm(high, onehot) + mm(low, onehot)
        sigma = 1.0 / (1.0 + jnp.exp(-pre))
        hidden_ref[:, here] = (pre * sigma).astype(BF16)
        slope_ref[:, here] = sigma * (1.0 + pre * (1.0 - sigma))


def halve(terms, odd, place, keep_ref, send_ref, first):
    count, rows, _ = keep_ref.shape
    width = terms.shape[-1]
    lanes = slice(first, first + width)
    inner = 1 << place
    pairs = terms.reshape(count // inner, 2, inner, rows, width)
    even_part = pairs[:, 0].reshape(count, rows, width)
    odd_part = pairs[:, 1].reshape(count, rows, width)
    keep_ref[:, :, lanes] = jnp.where(odd > 0, odd_part, even_part)
    send_ref[:, :, lanes] = jnp.where(odd > 0, even_part, odd_part).astype(BF16)


def fold_kernel(bit, place, me_ref, keep_ref, came_ref, next_ref, send_ref):
    odd = (me_ref[0] >> bit) % 2
    halve(keep_ref[...] + came_ref[...].astype(F32), odd, place, next_ref, send_ref, 0)


def close_kernel(keep_ref, came_ref, send_ref):
    send_ref[...] = (keep_ref[...] + came_ref[...].astype(F32)).astype(BF16)


def grad_kernel(
    half, factor, me_ref, own_ref, w_out_ref, slope_hbm, onehot_hbm, ext_hbm, *rest,
):
    (
        *came_refs, keep_ref, send_ref, sums_ref, lower_ref, upper_ref, g_ref, slope_ref, onehot_ref, ext_ref, sems,
    ) = rest
    odd = me_ref[0] % 2
    width = w_out_ref.shape[0]
    slots = g_ref.shape[1]
    inside = sums_ref.shape[0]
    mols = inside // 2
    step = slots // 3
    tiles = []
    for tile in range(3):
        lanes = pl.ds(tile * step, step)
        copies = [
            pltpu.make_async_copy(slope_hbm.at[:, lanes], slope_ref.at[:, lanes], sems.at[tile, 0]),
            pltpu.make_async_copy(onehot_hbm.at[:, lanes], onehot_ref.at[:, lanes], sems.at[tile, 1]),
        ]
        for copy in copies:
            copy.start()
        tiles.append(copies)
    ext_copy = pltpu.make_async_copy(ext_hbm, ext_ref, sems.at[3, 0])
    ext_copy.start()
    chunks = [functools.partial(lambda ref, i: ref[i], ref, i) for ref in came_refs for i in range(ref.shape[0])]
    unpack(half, chunks, own_ref, g_ref)
    sums = None
    for tile, copies in enumerate(tiles):
        lanes = slice(tile * step, (tile + 1) * step)
        dh = mm(w_out_ref[...], g_ref[:, lanes])
        for copy in copies:
            copy.wait()
        dpre = (dh * slope_ref[:, lanes]).astype(BF16)
        term = mm(onehot_ref[:, lanes], dpre, NT)
        sums = term if sums is None else sums + term
    reach = lower_ref.shape[0]
    lower_ref[...] = sums[inside : inside + reach]
    upper_ref[...] = sums[inside + reach :]
    sums_ref[...] = sums[:inside]
    high, low = halves(sums)
    ext_copy.wait()
    feats = ext_ref[:, :mols]
    ext = ext_ref[...]
    halve(factor * (mm(feats, high[:mols]) + mm(feats, low[:mols])), odd, 0, keep_ref, send_ref, 0)
    halve(factor * (mm(ext, high[mols:]) + mm(ext, low[mols:])), odd, 0, keep_ref, send_ref, width)


def outer_kernel(factor, me_ref, hidden_ref, g_ref, keep_ref, send_ref):
    term = factor * mm(hidden_ref[...], g_ref[...], NT)
    padding = keep_ref.shape[2] - term.shape[1]
    if padding > 0:
        term = jnp.concatenate([term, jnp.zeros((term.shape[0], padding), F32)], axis=1)
    halve(term, me_ref[0] % 2, 0, keep_ref, send_ref, 0)


def rim_kernel(sums_ref, from_below_ref, from_above_ref, w_src_ref, w_dst_ref, out_ref):
    mols = out_ref.shape[0]
    reach = from_below_ref.shape[0]
    src = sums_ref[:mols]
    dst = sums_ref[mols:]
    dst = jnp.concatenate(
        [dst[:reach] + from_below_ref[...], dst[reach : mols - reach], dst[mols - reach :] + from_above_ref[...]], axis=0
    )
    w_src = w_src_ref[...]
    w_dst = w_dst_ref[...]
    src_high, src_low = halves(src)
    dst_high, dst_low = halves(dst)
    out_ref[...] = mm(src_high, w_src, NT) + mm(src_low, w_src, NT) + mm(dst_high, w_dst, NT) + mm(dst_low, w_dst, NT)


def total_kernel(*refs):
    *refs, src_ref, dst_ref, out_ref = refs
    count = len(refs) // 2
    width = src_ref.shape[1]
    totals = []
    for piece in (refs[:count], refs[count:]):
        terms = [ref[slab].astype(F32) for ref in piece for slab in range(ref.shape[0])]
        totals.append(functools.reduce(jnp.add, terms))
    sides, outer = totals
    src_ref[...] = sides[:, :width]
    dst_ref[...] = sides[:, width:]
    out_ref[...] = outer[:, : out_ref.shape[1]]


def in_hbm(x):
    return pltpu.with_memory_space_constraint(x, pltpu.HBM)


def swap(block, bit, slabs):
    return lax.ppermute(block, "space", [(i, i ^ (1 << bit)) for i in range(slabs)])


def on_device(mol_feats, w_src, w_dst, w_out, grad_blocks, edge_src, edge_dst, edge_live):
    slabs = lax.axis_size("space")
    mols, width = mol_feats.shape
    entries = w_out.shape[1]
    cap = grad_blocks.shape[2]
    half = cap // 2
    reach = mols // 4
    groups = LANES // half
    slots = (slabs // groups + 1) * LANES
    bits = slabs.bit_length() - 1
    if 3 <= bits <= 4:
        late_bits = tuple((bit, 0) for bit in range(3, bits))
        paths = (((0, 0), (1, 0), (2, 0)) + late_bits, ((0, 0), (2, 1), (1, 0)) + late_bits)
    else:
        paths = (tuple((bit, 0) for bit in range(min(bits, 2))),) * 2
    rest = slabs >> len(paths[0])
    part = width // slabs
    factor = float(edge_src.shape[0] * slabs) ** (-0.5)
    me = lax.axis_index("space").astype(jnp.int32).reshape(1)
    smem = pl.BlockSpec(memory_space=pltpu.SMEM)
    hbm = pl.BlockSpec(memory_space=pltpu.HBM)
    big = pltpu.CompilerParams(vmem_limit_bytes=24 * 1024 * 1024)
    up = [(i, (i + 1) % slabs) for i in range(slabs)]
    down = [((i + 1) % slabs, i) for i in range(slabs)]

    rows = round_up(pl.cdiv(entries, groups), PACK)
    stages = 4
    linked = slabs <= 16
    even, odd, low, top = pl.pallas_call(
        functools.partial(pack_kernel, rows, half, linked),
        out_shape=(
            jax.ShapeDtypeStruct((slabs // 2, rows, LANES), BF16),
            jax.ShapeDtypeStruct((slabs // 2, rows, LANES), BF16),
            jax.ShapeDtypeStruct((reach, width), BF16),
            jax.ShapeDtypeStruct((reach, width), BF16),
        ),
        in_specs=[smem, hbm, hbm],
        out_specs=tuple(vmem(4)),
        scratch_shapes=[
            pltpu.VMEM((entries, slabs, cap), BF16),
            pltpu.SemaphoreType.DMA((stages, groups)),
            pltpu.SemaphoreType.DMA((2,)),
        ],
        compiler_params=big,
        name="pack",
    )(me, in_hbm(mol_feats), in_hbm(jnp.transpose(grad_blocks[0], (2, 0, 1))))
    below = lax.ppermute(top, "space", up)
    above = lax.ppermute(low, "space", down)
    if linked:
        other = swap(odd, 0, slabs)
        messages = [jnp.stack([even[k], other[k]]) for k in range(slabs // 2)]
        messages = list(lax.optimization_barrier(tuple(messages)))
        came = messages[:1] + [None] * (slabs // 2 - 1)
        for k in sorted(range(1, slabs // 2), key=lambda k: (k < slabs // 4, k)):
            came[k] = lax.ppermute(messages[k], "space", [(i, i ^ (2 * k)) for i in range(slabs)])
    else:
        packed = jnp.stack([even, odd], axis=1).reshape(slabs, rows, LANES)
        came = [lax.all_to_all(packed, "space", split_axis=0, concat_axis=0, tiled=True)]
    late = lax.dynamic_index_in_dim(grad_blocks[0], me[0], 0, keepdims=False)[half:]
    own = jnp.pad(late.T, ((0, groups * rows - entries), (0, LANES - half)))

    onehot, hidden, slope, ext = pl.pallas_call(
        functools.partial(edge_kernel, half, linked),
        out_shape=(
            jax.ShapeDtypeStruct((2 * mols + 2 * reach, slots), BF16),
            jax.ShapeDtypeStruct((width, slots), BF16),
            jax.ShapeDtypeStruct((width, slots), F32),
            jax.ShapeDtypeStruct((width, mols + 2 * reach), BF16),
        ),
        in_specs=[smem] + vmem(8),
        out_specs=tuple(vmem(4)),
        compiler_params=big,
        name="edges",
        cost_estimate=pl.CostEstimate(
            flops=40 * width * slots * 2 * (2 * mols + 2 * reach), bytes_accessed=8 * 1024 * 1024,
            transcendentals=width * slots,
        ),
    )(
        me, mol_feats, below, above, w_src, w_dst,
        edge_src.reshape(slabs, cap), edge_dst.reshape(slabs, cap), edge_live.reshape(slabs, cap),
    )

    def chunks(count, lanes, dtype):
        return jax.ShapeDtypeStruct((count, part, lanes), dtype)

    entries_wide = groups * rows
    w_out_wide = jnp.pad(w_out, ((0, 0), (0, entries_wide - entries)))
    wide = mols + 2 * reach
    keep, send, sums, lower, upper, g = pl.pallas_call(
        functools.partial(grad_kernel, half, factor),
        out_shape=(
            chunks(slabs // 2, 2 * width, F32),
            chunks(slabs // 2, 2 * width, BF16),
            jax.ShapeDtypeStruct((2 * mols, width), F32),
            jax.ShapeDtypeStruct((reach, width), F32),
            jax.ShapeDtypeStruct((reach, width), F32),
            jax.ShapeDtypeStruct((entries_wide, slots), BF16),
        ),
        in_specs=[smem] + vmem(2) + [hbm] * 3 + vmem(len(came)),
        out_specs=tuple(vmem(6)),
        scratch_shapes=[
            pltpu.VMEM((width, slots), F32),
            pltpu.VMEM((mols + wide, slots), BF16),
            pltpu.VMEM((width, wide), BF16),
            pltpu.SemaphoreType.DMA((4, 2)),
        ],
        compiler_params=big,
        name="grads",
    )(me, own, w_out_wide, in_hbm(slope), in_hbm(onehot), in_hbm(ext), *came)
    lanes = round_up(entries_wide, LANES)
    keep_o, send_o = pl.pallas_call(
        functools.partial(outer_kernel, factor),
        out_shape=(chunks(slabs // 2, lanes, F32), chunks(slabs // 2, lanes, BF16)),
        in_specs=[smem] + vmem(2),
        out_specs=tuple(vmem(2)),
        compiler_params=big,
        name="outer",
        cost_estimate=pl.CostEstimate(
            flops=40 * width * slots * entries_wide, bytes_accessed=4 * 1024 * 1024, transcendentals=0
        ),
    )(me, hidden, g)

    def fold(bit, place, keep, crossed):
        shape = (keep.shape[0] // 2, keep.shape[2])
        return pl.pallas_call(
            functools.partial(fold_kernel, bit, place),
            out_shape=(chunks(*shape, F32), chunks(*shape, BF16)),
            in_specs=[smem] + vmem(2),
            out_specs=tuple(vmem(2)),
            compiler_params=big,
            name="fold",
        )(me, keep, crossed)

    def close(keep, crossed):
        if rest == 1:
            return [keep, crossed]
        sends = pl.pallas_call(
            close_kernel,
            out_shape=chunks(rest, keep.shape[2], BF16),
            in_specs=vmem(2),
            out_specs=vmem(1)[0],
            compiler_params=big,
            name="close",
        )(keep, crossed)
        same = [[low + rank * (slabs // rest) for rank in range(rest)] for low in range(slabs // rest)]
        return [
            lax.all_to_all(sends, "space", split_axis=0, concat_axis=0, tiled=True, axis_index_groups=same)
        ]

    from_above = lax.ppermute(lower, "space", down)
    from_below = lax.ppermute(upper, "space", up)
    crossed = swap(send, 0, slabs)
    crossed_o = swap(send_o, 0, slabs)
    for (bit, place), (bit_o, place_o) in zip(paths[0][1:], paths[1][1:]):
        keep, send = fold(bit, place, keep, crossed)
        crossed = swap(send, bit, slabs)
        keep_o, crossed_o, _ = lax.optimization_barrier((keep_o, crossed_o, send))
        keep_o, send_o = fold(bit_o, place_o, keep_o, crossed_o)
        crossed_o = swap(send_o, bit_o, slabs)
    terms = close(keep, crossed)
    terms_o = close(keep_o, crossed_o)
    feature_grad = pl.pallas_call(
        rim_kernel,
        out_shape=jax.ShapeDtypeStruct((mols, width), F32),
        in_specs=vmem(5),
        out_specs=vmem(1)[0],
        compiler_params=big,
        name="rims",
        cost_estimate=pl.CostEstimate(flops=2 * width * slots * width * 40, bytes_accessed=4 * 1024 * 1024, transcendentals=0),
    )(sums, from_below, from_above, w_src, w_dst)
    src_grad, dst_grad, out_grad = pl.pallas_call(
        total_kernel,
        out_shape=(
            jax.ShapeDtypeStruct((part, width), F32),
            jax.ShapeDtypeStruct((part, width), F32),
            jax.ShapeDtypeStruct((part, entries), F32),
        ),
        in_specs=vmem(len(terms) + len(terms_o)),
        out_specs=tuple(vmem(3)),
        compiler_params=big,
        name="totals",
    )(*terms, *terms_o)
    return (feature_grad, src_grad, dst_grad, out_grad)


def solution(mesh):
    placed = (
        P(("groups", "space"), None),
        P(),
        P(),
        P(),
        P("space", "groups", None, None),
        P(("groups", "space")),
        P(("groups", "space")),
        P(("groups", "space")),
    )
    return jax.shard_map(
        on_device,
        mesh=mesh,
        in_specs=placed,
        out_specs=(
            P(("groups", "space"), None),
            P(("groups", "space"), None),
            P(("groups", "space"), None),
            P(("groups", "space"), None),
        ),
        check_vma=False,
    )
```

```python
import functools

import jax
import jax.numpy as jnp
from jax import lax
from jax.experimental import pallas as pl
from jax.experimental.pallas import tpu as pltpu
from jax.sharding import PartitionSpec as P

F32 = jnp.float32
BF16 = jnp.bfloat16
LANES = 128
PACK = 16
NN = (((1,), (0,)), ((), ()))
NT = (((1,), (1,)), ((), ()))


def mm(left, right, dims=NN):
    return lax.dot_general(left, right, dims, preferred_element_type=F32)


def halves(x):
    high = x.astype(BF16)
    return high, (x - high.astype(F32)).astype(BF16)


def round_up(x, to):
    return -(-x // to) * to


def vmem(count):
    return [pl.BlockSpec(memory_space=pltpu.VMEM)] * count


def pack_kernel(rows, half, linked, me_ref, feats_ref, g_ref, even_ref, odd_ref, low_ref, top_ref, here_ref, sems, rim_sems):
    entries, slabs, cap = g_ref.shape
    mols = feats_ref.shape[0]
    reach = low_ref.shape[0]
    groups = LANES // half
    blocks = rows // PACK
    count = sems.shape[0]
    stages = []
    for stage in range(count):
        begin, end = stage * blocks // count, (stage + 1) * blocks // count
        copies = []
        for group in range(groups):
            first = min(entries, group * rows + begin * PACK)
            last = min(entries, group * rows + end * PACK)
            if first < last:
                copies.append(
                    pltpu.make_async_copy(g_ref.at[first:last], here_ref.at[first:last], sems.at[stage, group])
                )
        stages.append((begin, end, copies))
        for copy in copies:
            copy.start()
    rims = [
        pltpu.make_async_copy(feats_ref.at[:reach], low_ref, rim_sems.at[0]),
        pltpu.make_async_copy(feats_ref.at[mols - reach :], top_ref, rim_sems.at[1]),
    ]
    for copy in rims:
        copy.start()
    size = PACK * slabs
    to = lax.broadcasted_iota(jnp.int32, (size, size), 0)
    source = lax.broadcasted_iota(jnp.int32, (size, size), 1)
    slab = to // PACK
    if linked:
        slab = slab ^ me_ref[0]
    perm = jnp.where((to % PACK) * slabs + slab == source, 1.0, 0.0).astype(BF16)

    def lanes_of(block):
        early = []
        for group in range(groups):
            first = group * rows + block * PACK
            valid = max(0, min(PACK, entries - first))
            tiles = []
            if valid:
                tiles.append(here_ref[first : first + valid])
            if valid < PACK:
                tiles.append(jnp.zeros((PACK - valid, slabs, cap), BF16))
            tile = tiles[0] if len(tiles) == 1 else jnp.concatenate(tiles, axis=0)
            early.append(tile.reshape(size, cap)[:, :half])
        return early

    for begin, end, copies in stages:
        for copy in copies:
            copy.wait()
        for block in range(begin, end, 2):
            together = range(block, min(block + 2, end))
            lanes = [piece for one in together for piece in lanes_of(one)]
            moved = mm(perm, jnp.concatenate(lanes, axis=1)).astype(BF16)
            for index, one in enumerate(together):
                chunk = moved[:, index * LANES : (index + 1) * LANES].reshape(slabs // 2, 2, PACK, LANES)
                here = pl.ds(one * PACK, PACK)
                even_ref[:, here, :] = chunk[:, 0]
                odd_ref[:, here, :] = chunk[:, 1]
    for copy in rims:
        copy.wait()


def join_kernel(even_ref, other_ref, *message_refs):
    for k, message_ref in enumerate(message_refs):
        message_ref[0] = even_ref[k]
        message_ref[1] = other_ref[k]


def unpack(half, chunks, own_ref, g_ref):
    groups = LANES // half
    rows = g_ref.shape[0] // groups
    tiles = len(chunks) // groups
    for tile in range(tiles):
        here = [chunk() for chunk in chunks[tile * groups : (tile + 1) * groups]]
        for group in range(groups):
            lanes = slice(group * half, (group + 1) * half)
            g_ref[group * rows : (group + 1) * rows, tile * LANES : (tile + 1) * LANES] = jnp.concatenate(
                [chunk[:, lanes] for chunk in here], axis=1
            )
    g_ref[:, tiles * LANES :] = own_ref[...]


def slot_rows(ref, me, half, order):
    slabs, cap = ref.shape
    per = LANES // half
    rows = []
    for tile in range(slabs // per):
        ids = range(tile * per, tile * per + per)
        pieces = [ref[pl.ds(me ^ order[i] if order else i, 1), :] for i in ids]
        rows.append(jnp.concatenate([piece[:, :half] for piece in pieces], axis=1))
    own = ref[pl.ds(me, 1), :][:, half:]
    rows.append(jnp.concatenate([own, jnp.full((1, LANES - half), -1, jnp.int32)], axis=1))
    return rows


def edge_kernel(
    half, order, me_ref, feats_ref, below_ref, above_ref, w_src_ref, w_dst_ref, src_ref, dst_ref, live_ref,
    onehot_ref, hidden_ref, slope_ref, ext_ref,
):
    me = me_ref[0]
    mols = feats_ref.shape[0]
    reach = below_ref.shape[0]
    wide = mols + 2 * reach
    feats = feats_ref[...]
    ext = jnp.concatenate([feats, below_ref[...], above_ref[...]], axis=0)
    ext_ref[...] = ext.T
    proj_src = mm(feats, w_src_ref[...])
    proj_dst = mm(ext, w_dst_ref[...])
    proj = jnp.concatenate([proj_src, proj_dst], axis=0).T
    high, low = halves(proj)
    mol_src = lax.broadcasted_iota(jnp.int32, (mols, LANES), 0)
    mol_dst = lax.broadcasted_iota(jnp.int32, (wide, LANES), 0)
    lists = [slot_rows(ref, me, half, order) for ref in (src_ref, dst_ref, live_ref)]
    for tile, (src, dst, live) in enumerate(zip(*lists)):
        src = jnp.where(live > 0, src, -1)
        moved = jnp.where(dst < reach, dst + mols, jnp.where(dst < reach + mols, dst - reach, dst))
        dst = jnp.where(live > 0, moved, -1)
        one_src = jnp.where(mol_src == src, 1.0, 0.0).astype(BF16)
        one_dst = jnp.where(mol_dst == dst, 1.0, 0.0).astype(BF16)
        onehot = jnp.concatenate([one_src, one_dst], axis=0)
        here = pl.ds(tile * LANES, LANES)
        onehot_ref[:, here] = onehot
        pre = mm(high, onehot) + mm(low, onehot)
        sigma = 1.0 / (1.0 + jnp.exp(-pre))
        hidden_ref[:, here] = (pre * sigma).astype(BF16)
        slope_ref[:, here] = sigma * (1.0 + pre * (1.0 - sigma))


def halve(terms, odd, place, keep_ref, send_ref, first):
    count, rows, _ = keep_ref.shape
    width = terms.shape[-1]
    lanes = slice(first, first + width)
    inner = 1 << place
    pairs = terms.reshape(count // inner, 2, inner, rows, width)
    even_part = pairs[:, 0].reshape(count, rows, width)
    odd_part = pairs[:, 1].reshape(count, rows, width)
    keep_ref[:, :, lanes] = jnp.where(odd > 0, odd_part, even_part)
    send_ref[:, :, lanes] = jnp.where(odd > 0, even_part, odd_part).astype(BF16)


def fold_kernel(bit, place, me_ref, keep_ref, came_ref, next_ref, send_ref):
    odd = (me_ref[0] >> bit) % 2
    halve(keep_ref[...] + came_ref[...].astype(F32), odd, place, next_ref, send_ref, 0)


def close_kernel(keep_ref, came_ref, send_ref):
    send_ref[...] = (keep_ref[...] + came_ref[...].astype(F32)).astype(BF16)


def grad_kernel(
    half, factor, me_ref, own_ref, w_out_ref, slope_hbm, onehot_hbm, ext_hbm, *rest,
):
    (
        *came_refs, keep_ref, send_ref, sums_ref, lower_ref, upper_ref, g_ref, slope_ref, onehot_ref, ext_ref, sems,
    ) = rest
    odd = me_ref[0] % 2
    width = w_out_ref.shape[0]
    slots = g_ref.shape[1]
    inside = sums_ref.shape[0]
    mols = inside // 2
    step = slots // 3
    tiles = []
    for tile in range(3):
        lanes = pl.ds(tile * step, step)
        copies = [
            pltpu.make_async_copy(slope_hbm.at[:, lanes], slope_ref.at[:, lanes], sems.at[tile, 0]),
            pltpu.make_async_copy(onehot_hbm.at[:, lanes], onehot_ref.at[:, lanes], sems.at[tile, 1]),
        ]
        for copy in copies:
            copy.start()
        tiles.append(copies)
    ext_copy = pltpu.make_async_copy(ext_hbm, ext_ref, sems.at[3, 0])
    ext_copy.start()
    chunks = [functools.partial(lambda ref, i: ref[i], ref, i) for ref in came_refs for i in range(ref.shape[0])]
    unpack(half, chunks, own_ref, g_ref)
    sums = None
    for tile, copies in enumerate(tiles):
        lanes = slice(tile * step, (tile + 1) * step)
        dh = mm(w_out_ref[...], g_ref[:, lanes])
        for copy in copies:
            copy.wait()
        dpre = (dh * slope_ref[:, lanes]).astype(BF16)
        term = mm(onehot_ref[:, lanes], dpre, NT)
        sums = term if sums is None else sums + term
    reach = lower_ref.shape[0]
    lower_ref[...] = sums[inside : inside + reach].astype(BF16)
    upper_ref[...] = sums[inside + reach :].astype(BF16)
    sums_ref[...] = sums[:inside]
    high, low = halves(sums)
    ext_copy.wait()
    feats = ext_ref[:, :mols]
    ext = ext_ref[...]
    halve(factor * (mm(feats, high[:mols]) + mm(feats, low[:mols])), odd, 0, keep_ref, send_ref, 0)
    halve(factor * (mm(ext, high[mols:]) + mm(ext, low[mols:])), odd, 0, keep_ref, send_ref, width)


def outer_kernel(factor, me_ref, hidden_ref, g_ref, keep_ref, send_ref):
    term = factor * mm(hidden_ref[...], g_ref[...], NT)
    padding = keep_ref.shape[2] - term.shape[1]
    if padding > 0:
        term = jnp.concatenate([term, jnp.zeros((term.shape[0], padding), F32)], axis=1)
    halve(term, me_ref[0] % 2, 0, keep_ref, send_ref, 0)


def rim_kernel(sums_ref, from_below_ref, from_above_ref, w_src_ref, w_dst_ref, out_ref):
    mols = out_ref.shape[0]
    reach = from_below_ref.shape[0]
    src = sums_ref[:mols]
    dst = sums_ref[mols:]
    dst = jnp.concatenate(
        [
            dst[:reach] + from_below_ref[...].astype(F32),
            dst[reach : mols - reach],
            dst[mols - reach :] + from_above_ref[...].astype(F32),
        ],
        axis=0,
    )
    w_src = w_src_ref[...]
    w_dst = w_dst_ref[...]
    src_high, src_low = halves(src)
    dst_high, dst_low = halves(dst)
    out_ref[...] = mm(src_high, w_src, NT) + mm(src_low, w_src, NT) + mm(dst_high, w_dst, NT) + mm(dst_low, w_dst, NT)


def total_kernel(*refs):
    *refs, src_ref, dst_ref, out_ref = refs
    count = len(refs) // 2
    width = src_ref.shape[1]
    totals = []
    for piece in (refs[:count], refs[count:]):
        terms = [ref[slab].astype(F32) for ref in piece for slab in range(ref.shape[0])]
        totals.append(functools.reduce(jnp.add, terms))
    sides, outer = totals
    src_ref[...] = sides[:, :width]
    dst_ref[...] = sides[:, width:]
    out_ref[...] = outer[:, : out_ref.shape[1]]


def in_hbm(x):
    return pltpu.with_memory_space_constraint(x, pltpu.HBM)


def swap(block, bit, slabs):
    return lax.ppermute(block, "space", [(i, i ^ (1 << bit)) for i in range(slabs)])


def on_device(mol_feats, w_src, w_dst, w_out, grad_blocks, edge_src, edge_dst, edge_live):
    slabs = lax.axis_size("space")
    mols, width = mol_feats.shape
    entries = w_out.shape[1]
    cap = grad_blocks.shape[2]
    half = cap // 2
    reach = mols // 4
    groups = LANES // half
    slots = (slabs // groups + 1) * LANES
    bits = slabs.bit_length() - 1
    if 3 <= bits <= 4:
        late_bits = tuple((bit, 0) for bit in range(3, bits))
        paths = (((0, 0), (1, 0), (2, 0)) + late_bits, ((0, 0), (2, 1), (1, 0)) + late_bits)
    else:
        paths = (tuple((bit, 0) for bit in range(min(bits, 2))),) * 2
    rest = slabs >> len(paths[0])
    part = width // slabs
    factor = float(edge_src.shape[0] * slabs) ** (-0.5)
    me = lax.axis_index("space").astype(jnp.int32).reshape(1)
    smem = pl.BlockSpec(memory_space=pltpu.SMEM)
    hbm = pl.BlockSpec(memory_space=pltpu.HBM)
    big = pltpu.CompilerParams(vmem_limit_bytes=24 * 1024 * 1024)
    up = [(i, (i + 1) % slabs) for i in range(slabs)]
    down = [((i + 1) % slabs, i) for i in range(slabs)]

    rows = round_up(pl.cdiv(entries, groups), PACK)
    stages = 4
    linked = slabs <= 16
    even, odd, low, top = pl.pallas_call(
        functools.partial(pack_kernel, rows, half, linked),
        out_shape=(
            jax.ShapeDtypeStruct((slabs // 2, rows, LANES), BF16),
            jax.ShapeDtypeStruct((slabs // 2, rows, LANES), BF16),
            jax.ShapeDtypeStruct((reach, width), BF16),
            jax.ShapeDtypeStruct((reach, width), BF16),
        ),
        in_specs=[smem, hbm, hbm],
        out_specs=tuple(vmem(4)),
        scratch_shapes=[
            pltpu.VMEM((entries, slabs, cap), BF16),
            pltpu.SemaphoreType.DMA((stages, groups)),
            pltpu.SemaphoreType.DMA((2,)),
        ],
        compiler_params=big,
        name="pack",
    )(me, in_hbm(mol_feats), in_hbm(jnp.transpose(grad_blocks[0], (2, 0, 1))))
    below = lax.ppermute(top, "space", up)
    above = lax.ppermute(low, "space", down)
    order = ()
    if linked:
        other = swap(odd, 0, slabs)
        other, below, above = lax.optimization_barrier((other, below, above))
        messages = pl.pallas_call(
            join_kernel,
            out_shape=(jax.ShapeDtypeStruct((2, rows, LANES), BF16),) * (slabs // 2),
            in_specs=vmem(2),
            out_specs=tuple(vmem(slabs // 2)),
            compiler_params=big,
            name="join",
        )(even, other)
        turns = sorted(range(slabs // 2), key=lambda k: (k < slabs // 4, k))
        order = tuple(2 * k + j for k in turns for j in range(2))
        came = [
            lax.ppermute(messages[k], "space", [(i, i ^ (2 * k)) for i in range(slabs)]) if k else messages[0]
            for k in turns
        ]
    else:
        packed = jnp.stack([even, odd], axis=1).reshape(slabs, rows, LANES)
        came = [lax.all_to_all(packed, "space", split_axis=0, concat_axis=0, tiled=True)]

    onehot, hidden, slope, ext = pl.pallas_call(
        functools.partial(edge_kernel, half, order),
        out_shape=(
            jax.ShapeDtypeStruct((2 * mols + 2 * reach, slots), BF16),
            jax.ShapeDtypeStruct((width, slots), BF16),
            jax.ShapeDtypeStruct((width, slots), F32),
            jax.ShapeDtypeStruct((width, mols + 2 * reach), BF16),
        ),
        in_specs=[smem] + vmem(8),
        out_specs=tuple(vmem(4)),
        compiler_params=big,
        name="edges",
        cost_estimate=pl.CostEstimate(
            flops=40 * width * slots * 2 * (2 * mols + 2 * reach), bytes_accessed=8 * 1024 * 1024,
            transcendentals=width * slots,
        ),
    )(
        me, mol_feats, below, above, w_src, w_dst,
        edge_src.reshape(slabs, cap), edge_dst.reshape(slabs, cap), edge_live.reshape(slabs, cap),
    )

    here, w_out, slope = lax.optimization_barrier((me, w_out, slope))
    late = lax.dynamic_index_in_dim(grad_blocks[0], here[0], 0, keepdims=False)[half:]
    own = jnp.pad(late.T, ((0, groups * rows - entries), (0, LANES - half)))

    def chunks(count, lanes, dtype):
        return jax.ShapeDtypeStruct((count, part, lanes), dtype)

    entries_wide = groups * rows
    w_out_wide = jnp.pad(w_out, ((0, 0), (0, entries_wide - entries)))
    wide = mols + 2 * reach
    keep, send, sums, lower, upper, g = pl.pallas_call(
        functools.partial(grad_kernel, half, factor),
        out_shape=(
            chunks(slabs // 2, 2 * width, F32),
            chunks(slabs // 2, 2 * width, BF16),
            jax.ShapeDtypeStruct((2 * mols, width), F32),
            jax.ShapeDtypeStruct((reach, width), BF16),
            jax.ShapeDtypeStruct((reach, width), BF16),
            jax.ShapeDtypeStruct((entries_wide, slots), BF16),
        ),
        in_specs=[smem] + vmem(2) + [hbm] * 3 + vmem(len(came)),
        out_specs=tuple(vmem(6)),
        scratch_shapes=[
            pltpu.VMEM((width, slots), F32),
            pltpu.VMEM((mols + wide, slots), BF16),
            pltpu.VMEM((width, wide), BF16),
            pltpu.SemaphoreType.DMA((4, 2)),
        ],
        compiler_params=big,
        name="grads",
    )(me, own, w_out_wide, in_hbm(slope), in_hbm(onehot), in_hbm(ext), *came)
    lanes = round_up(entries_wide, LANES)
    keep_o, send_o = pl.pallas_call(
        functools.partial(outer_kernel, factor),
        out_shape=(chunks(slabs // 2, lanes, F32), chunks(slabs // 2, lanes, BF16)),
        in_specs=[smem] + vmem(2),
        out_specs=tuple(vmem(2)),
        compiler_params=big,
        name="outer",
        cost_estimate=pl.CostEstimate(
            flops=40 * width * slots * entries_wide, bytes_accessed=4 * 1024 * 1024, transcendentals=0
        ),
    )(me, hidden, g)

    def fold(bit, place, keep, crossed):
        shape = (keep.shape[0] // 2, keep.shape[2])
        return pl.pallas_call(
            functools.partial(fold_kernel, bit, place),
            out_shape=(chunks(*shape, F32), chunks(*shape, BF16)),
            in_specs=[smem] + vmem(2),
            out_specs=tuple(vmem(2)),
            compiler_params=big,
            name="fold",
        )(me, keep, crossed)

    def close(keep, crossed):
        if rest == 1:
            return [keep, crossed]
        sends = pl.pallas_call(
            close_kernel,
            out_shape=chunks(rest, keep.shape[2], BF16),
            in_specs=vmem(2),
            out_specs=vmem(1)[0],
            compiler_params=big,
            name="close",
        )(keep, crossed)
        same = [[low + rank * (slabs // rest) for rank in range(rest)] for low in range(slabs // rest)]
        return [
            lax.all_to_all(sends, "space", split_axis=0, concat_axis=0, tiled=True, axis_index_groups=same)
        ]

    from_above = lax.ppermute(lower, "space", down)
    from_below = lax.ppermute(upper, "space", up)
    crossed = swap(send, 0, slabs)
    crossed_o = swap(send_o, 0, slabs)
    crossed_o, from_above, from_below = lax.optimization_barrier((crossed_o, from_above, from_below))
    for (bit, place), (bit_o, place_o) in zip(paths[0][1:], paths[1][1:]):
        keep, send = fold(bit, place, keep, crossed)
        crossed = swap(send, bit, slabs)
        keep_o, crossed_o, _ = lax.optimization_barrier((keep_o, crossed_o, send))
        keep_o, send_o = fold(bit_o, place_o, keep_o, crossed_o)
        crossed_o = swap(send_o, bit_o, slabs)
    terms = close(keep, crossed)
    terms_o = close(keep_o, crossed_o)
    feature_grad = pl.pallas_call(
        rim_kernel,
        out_shape=jax.ShapeDtypeStruct((mols, width), F32),
        in_specs=vmem(5),
        out_specs=vmem(1)[0],
        compiler_params=big,
        name="rims",
        cost_estimate=pl.CostEstimate(flops=2 * width * slots * width * 40, bytes_accessed=4 * 1024 * 1024, transcendentals=0),
    )(sums, from_below, from_above, w_src, w_dst)
    src_grad, dst_grad, out_grad = pl.pallas_call(
        total_kernel,
        out_shape=(
            jax.ShapeDtypeStruct((part, width), F32),
            jax.ShapeDtypeStruct((part, width), F32),
            jax.ShapeDtypeStruct((part, entries), F32),
        ),
        in_specs=vmem(len(terms) + len(terms_o)),
        out_specs=tuple(vmem(3)),
        compiler_params=big,
        name="totals",
    )(*terms, *terms_o)
    return (feature_grad, src_grad, dst_grad, out_grad)


def solution(mesh):
    placed = (
        P(("groups", "space"), None),
        P(),
        P(),
        P(),
        P("space", "groups", None, None),
        P(("groups", "space")),
        P(("groups", "space")),
        P(("groups", "space")),
    )
    return jax.shard_map(
        on_device,
        mesh=mesh,
        in_specs=placed,
        out_specs=(
            P(("groups", "space"), None),
            P(("groups", "space"), None),
            P(("groups", "space"), None),
            P(("groups", "space"), None),
        ),
        check_vma=False,
    )
```

```python
import functools

import jax
import jax.numpy as jnp
from jax import lax
from jax.experimental import pallas as pl
from jax.experimental.pallas import tpu as pltpu
from jax.sharding import PartitionSpec as P

F32 = jnp.float32
BF16 = jnp.bfloat16
LANES = 128
PACK = 16
NN = (((1,), (0,)), ((), ()))
NT = (((1,), (1,)), ((), ()))


def mm(left, right, dims=NN):
    return lax.dot_general(left, right, dims, preferred_element_type=F32)


def halves(x):
    high = x.astype(BF16)
    return high, (x - high.astype(F32)).astype(BF16)


def round_up(x, to):
    return -(-x // to) * to


def vmem(count):
    return [pl.BlockSpec(memory_space=pltpu.VMEM)] * count


def pack_kernel(rows, half, linked, me_ref, feats_ref, g_ref, even_ref, odd_ref, low_ref, top_ref, here_ref, sems, rim_sems):
    entries, slabs, cap = g_ref.shape
    mols = feats_ref.shape[0]
    reach = low_ref.shape[0]
    groups = LANES // half
    blocks = rows // PACK
    count = sems.shape[0]
    stages = []
    for stage in range(count):
        begin, end = stage * blocks // count, (stage + 1) * blocks // count
        copies = []
        for group in range(groups):
            first = min(entries, group * rows + begin * PACK)
            last = min(entries, group * rows + end * PACK)
            if first < last:
                copies.append(
                    pltpu.make_async_copy(g_ref.at[first:last], here_ref.at[first:last], sems.at[stage, group])
                )
        stages.append((begin, end, copies))
        for copy in copies:
            copy.start()
    rims = [
        pltpu.make_async_copy(feats_ref.at[:reach], low_ref, rim_sems.at[0]),
        pltpu.make_async_copy(feats_ref.at[mols - reach :], top_ref, rim_sems.at[1]),
    ]
    for copy in rims:
        copy.start()
    size = PACK * slabs
    to = lax.broadcasted_iota(jnp.int32, (size, size), 0)
    source = lax.broadcasted_iota(jnp.int32, (size, size), 1)
    slab = to // PACK
    if linked:
        slab = slab ^ me_ref[0]
    perm = jnp.where((to % PACK) * slabs + slab == source, 1.0, 0.0).astype(BF16)

    def lanes_of(block):
        early = []
        for group in range(groups):
            first = group * rows + block * PACK
            valid = max(0, min(PACK, entries - first))
            tiles = []
            if valid:
                tiles.append(here_ref[first : first + valid])
            if valid < PACK:
                tiles.append(jnp.zeros((PACK - valid, slabs, cap), BF16))
            tile = tiles[0] if len(tiles) == 1 else jnp.concatenate(tiles, axis=0)
            early.append(tile.reshape(size, cap)[:, :half])
        return early

    for begin, end, copies in stages:
        for copy in copies:
            copy.wait()
        for block in range(begin, end, 2):
            together = range(block, min(block + 2, end))
            lanes = [piece for one in together for piece in lanes_of(one)]
            moved = mm(perm, jnp.concatenate(lanes, axis=1)).astype(BF16)
            for index, one in enumerate(together):
                chunk = moved[:, index * LANES : (index + 1) * LANES].reshape(slabs // 2, 2, PACK, LANES)
                here = pl.ds(one * PACK, PACK)
                even_ref[:, here, :] = chunk[:, 0]
                odd_ref[:, here, :] = chunk[:, 1]
    for copy in rims:
        copy.wait()


def join_kernel(even_ref, other_ref, *message_refs):
    for k, message_ref in enumerate(message_refs):
        message_ref[0] = even_ref[k]
        message_ref[1] = other_ref[k]


def unpack(half, chunks, own_ref, g_ref):
    groups = LANES // half
    rows = g_ref.shape[0] // groups
    tiles = len(chunks) // groups
    for tile in range(tiles):
        here = [chunk() for chunk in chunks[tile * groups : (tile + 1) * groups]]
        for group in range(groups):
            lanes = slice(group * half, (group + 1) * half)
            g_ref[group * rows : (group + 1) * rows, tile * LANES : (tile + 1) * LANES] = jnp.concatenate(
                [chunk[:, lanes] for chunk in here], axis=1
            )
    g_ref[:, tiles * LANES :] = own_ref[...]


def slot_rows(ref, me, half, order):
    slabs, cap = ref.shape
    per = LANES // half
    rows = []
    for tile in range(slabs // per):
        ids = range(tile * per, tile * per + per)
        pieces = [ref[pl.ds(me ^ order[i] if order else i, 1), :] for i in ids]
        rows.append(jnp.concatenate([piece[:, :half] for piece in pieces], axis=1))
    own = ref[pl.ds(me, 1), :][:, half:]
    rows.append(jnp.concatenate([own, jnp.full((1, LANES - half), -1, jnp.int32)], axis=1))
    return rows


def edge_kernel(
    half, order, me_ref, feats_ref, below_ref, above_ref, w_src_ref, w_dst_ref, src_ref, dst_ref, live_ref,
    onehot_ref, hidden_ref, slope_ref, ext_ref,
):
    me = me_ref[0]
    mols = feats_ref.shape[0]
    reach = below_ref.shape[0]
    wide = mols + 2 * reach
    feats = feats_ref[...]
    ext = jnp.concatenate([feats, below_ref[...], above_ref[...]], axis=0)
    ext_ref[...] = ext.T
    proj_src = mm(feats, w_src_ref[...])
    proj_dst = mm(ext, w_dst_ref[...])
    proj = jnp.concatenate([proj_src, proj_dst], axis=0).T
    high, low = halves(proj)
    mol_src = lax.broadcasted_iota(jnp.int32, (mols, LANES), 0)
    mol_dst = lax.broadcasted_iota(jnp.int32, (wide, LANES), 0)
    lists = [slot_rows(ref, me, half, order) for ref in (src_ref, dst_ref, live_ref)]
    for tile, (src, dst, live) in enumerate(zip(*lists)):
        src = jnp.where(live > 0, src, -1)
        moved = jnp.where(dst < reach, dst + mols, jnp.where(dst < reach + mols, dst - reach, dst))
        dst = jnp.where(live > 0, moved, -1)
        one_src = jnp.where(mol_src == src, 1.0, 0.0).astype(BF16)
        one_dst = jnp.where(mol_dst == dst, 1.0, 0.0).astype(BF16)
        onehot = jnp.concatenate([one_src, one_dst], axis=0)
        here = pl.ds(tile * LANES, LANES)
        onehot_ref[:, here] = onehot
        pre = mm(high, onehot) + mm(low, onehot)
        sigma = 1.0 / (1.0 + jnp.exp(-pre))
        hidden_ref[:, here] = (pre * sigma).astype(BF16)
        slope_ref[:, here] = sigma * (1.0 + pre * (1.0 - sigma))


def halve(terms, odd, place, keep_ref, send_ref, first):
    count, rows, _ = keep_ref.shape
    width = terms.shape[-1]
    lanes = slice(first, first + width)
    inner = 1 << place
    pairs = terms.reshape(count // inner, 2, inner, rows, width)
    even_part = pairs[:, 0].reshape(count, rows, width)
    odd_part = pairs[:, 1].reshape(count, rows, width)
    keep_ref[:, :, lanes] = jnp.where(odd > 0, odd_part, even_part)
    send_ref[:, :, lanes] = jnp.where(odd > 0, even_part, odd_part).astype(BF16)


def fold_kernel(bit, place, me_ref, keep_ref, came_ref, next_ref, send_ref):
    odd = (me_ref[0] >> bit) % 2
    halve(keep_ref[...] + came_ref[...].astype(F32), odd, place, next_ref, send_ref, 0)


def close_kernel(keep_ref, came_ref, send_ref):
    send_ref[...] = (keep_ref[...] + came_ref[...].astype(F32)).astype(BF16)


def grad_kernel(
    half, factor, me_ref, own_ref, w_out_ref, slope_hbm, onehot_hbm, ext_hbm, *rest,
):
    (
        *came_refs, keep_ref, send_ref, sums_ref, lower_ref, upper_ref, g_ref, slope_ref, onehot_ref, ext_ref, sems,
    ) = rest
    odd = me_ref[0] % 2
    width = w_out_ref.shape[0]
    slots = g_ref.shape[1]
    inside = sums_ref.shape[0]
    mols = inside // 2
    step = slots // 3
    tiles = []
    for tile in range(3):
        lanes = pl.ds(tile * step, step)
        copies = [
            pltpu.make_async_copy(slope_hbm.at[:, lanes], slope_ref.at[:, lanes], sems.at[tile, 0]),
            pltpu.make_async_copy(onehot_hbm.at[:, lanes], onehot_ref.at[:, lanes], sems.at[tile, 1]),
        ]
        for copy in copies:
            copy.start()
        tiles.append(copies)
    ext_copy = pltpu.make_async_copy(ext_hbm, ext_ref, sems.at[3, 0])
    ext_copy.start()
    chunks = [functools.partial(lambda ref, i: ref[i], ref, i) for ref in came_refs for i in range(ref.shape[0])]
    unpack(half, chunks, own_ref, g_ref)
    sums = None
    for tile, copies in enumerate(tiles):
        lanes = slice(tile * step, (tile + 1) * step)
        dh = mm(w_out_ref[...], g_ref[:, lanes])
        for copy in copies:
            copy.wait()
        dpre = (dh * slope_ref[:, lanes]).astype(BF16)
        term = mm(onehot_ref[:, lanes], dpre, NT)
        sums = term if sums is None else sums + term
    reach = lower_ref.shape[0]
    lower_ref[...] = sums[inside : inside + reach].astype(BF16)
    upper_ref[...] = sums[inside + reach :].astype(BF16)
    sums_ref[...] = sums[:inside]
    high, low = halves(sums)
    ext_copy.wait()
    feats = ext_ref[:, :mols]
    ext = ext_ref[...]
    halve(factor * (mm(feats, high[:mols]) + mm(feats, low[:mols])), odd, 0, keep_ref, send_ref, 0)
    halve(factor * (mm(ext, high[mols:]) + mm(ext, low[mols:])), odd, 0, keep_ref, send_ref, width)


def outer_kernel(factor, me_ref, hidden_ref, g_ref, keep_ref, send_ref):
    term = factor * mm(hidden_ref[...], g_ref[...], NT)
    padding = keep_ref.shape[2] - term.shape[1]
    if padding > 0:
        term = jnp.concatenate([term, jnp.zeros((term.shape[0], padding), F32)], axis=1)
    halve(term, me_ref[0] % 2, 0, keep_ref, send_ref, 0)


def rim_kernel(sums_ref, from_below_ref, from_above_ref, w_src_ref, w_dst_ref, out_ref):
    mols = out_ref.shape[0]
    reach = from_below_ref.shape[0]
    src = sums_ref[:mols]
    dst = sums_ref[mols:]
    dst = jnp.concatenate(
        [
            dst[:reach] + from_below_ref[...].astype(F32),
            dst[reach : mols - reach],
            dst[mols - reach :] + from_above_ref[...].astype(F32),
        ],
        axis=0,
    )
    w_src = w_src_ref[...]
    w_dst = w_dst_ref[...]
    src_high, src_low = halves(src)
    dst_high, dst_low = halves(dst)
    out_ref[...] = mm(src_high, w_src, NT) + mm(src_low, w_src, NT) + mm(dst_high, w_dst, NT) + mm(dst_low, w_dst, NT)


def total_kernel(*refs):
    *refs, src_ref, dst_ref, out_ref = refs
    count = len(refs) // 2
    width = src_ref.shape[1]
    totals = []
    for piece in (refs[:count], refs[count:]):
        terms = [ref[slab].astype(F32) for ref in piece for slab in range(ref.shape[0])]
        totals.append(functools.reduce(jnp.add, terms))
    sides, outer = totals
    src_ref[...] = sides[:, :width]
    dst_ref[...] = sides[:, width:]
    out_ref[...] = outer[:, : out_ref.shape[1]]


def in_hbm(x):
    return pltpu.with_memory_space_constraint(x, pltpu.HBM)


def swap(block, bit, slabs):
    return lax.ppermute(block, "space", [(i, i ^ (1 << bit)) for i in range(slabs)])


def on_device(mol_feats, w_src, w_dst, w_out, grad_blocks, edge_src, edge_dst, edge_live):
    slabs = lax.axis_size("space")
    mols, width = mol_feats.shape
    entries = w_out.shape[1]
    cap = grad_blocks.shape[2]
    half = cap // 2
    reach = mols // 4
    groups = LANES // half
    slots = (slabs // groups + 1) * LANES
    bits = slabs.bit_length() - 1
    if 3 <= bits <= 4:
        late_bits = tuple((bit, 0) for bit in range(3, bits))
        paths = (((0, 0), (1, 0), (2, 0)) + late_bits, ((0, 0), (2, 1), (1, 0)) + late_bits)
    else:
        paths = (tuple((bit, 0) for bit in range(min(bits, 2))),) * 2
    rest = slabs >> len(paths[0])
    part = width // slabs
    factor = float(edge_src.shape[0] * slabs) ** (-0.5)
    me = lax.axis_index("space").astype(jnp.int32).reshape(1)
    smem = pl.BlockSpec(memory_space=pltpu.SMEM)
    hbm = pl.BlockSpec(memory_space=pltpu.HBM)
    big = pltpu.CompilerParams(vmem_limit_bytes=24 * 1024 * 1024)
    up = [(i, (i + 1) % slabs) for i in range(slabs)]
    down = [((i + 1) % slabs, i) for i in range(slabs)]

    rows = round_up(pl.cdiv(entries, groups), PACK)
    stages = 4
    linked = slabs <= 16
    even, odd, low, top = pl.pallas_call(
        functools.partial(pack_kernel, rows, half, linked),
        out_shape=(
            jax.ShapeDtypeStruct((slabs // 2, rows, LANES), BF16),
            jax.ShapeDtypeStruct((slabs // 2, rows, LANES), BF16),
            jax.ShapeDtypeStruct((reach, width), BF16),
            jax.ShapeDtypeStruct((reach, width), BF16),
        ),
        in_specs=[smem, hbm, hbm],
        out_specs=tuple(vmem(4)),
        scratch_shapes=[
            pltpu.VMEM((entries, slabs, cap), BF16),
            pltpu.SemaphoreType.DMA((stages, groups)),
            pltpu.SemaphoreType.DMA((2,)),
        ],
        compiler_params=big,
        name="pack",
    )(me, in_hbm(mol_feats), in_hbm(jnp.transpose(grad_blocks[0], (2, 0, 1))))
    below = lax.ppermute(top, "space", up)
    above = lax.ppermute(low, "space", down)
    order = ()
    if linked:
        other = swap(odd, 0, slabs)
        other, below, above = lax.optimization_barrier((other, below, above))
        messages = pl.pallas_call(
            join_kernel,
            out_shape=(jax.ShapeDtypeStruct((2, rows, LANES), BF16),) * (slabs // 2),
            in_specs=vmem(2),
            out_specs=tuple(vmem(slabs // 2)),
            compiler_params=big,
            name="join",
        )(even, other)
        far = slabs // 4
        turns = [0, *range(1, far - 1), *range(far, slabs // 2), *range(max(far - 1, 1), far)]
        order = tuple(2 * k + j for k in turns for j in range(2))
        came = [
            lax.ppermute(messages[k], "space", [(i, i ^ (2 * k)) for i in range(slabs)]) if k else messages[0]
            for k in turns
        ]
    else:
        packed = jnp.stack([even, odd], axis=1).reshape(slabs, rows, LANES)
        came = [lax.all_to_all(packed, "space", split_axis=0, concat_axis=0, tiled=True)]

    onehot, hidden, slope, ext = pl.pallas_call(
        functools.partial(edge_kernel, half, order),
        out_shape=(
            jax.ShapeDtypeStruct((2 * mols + 2 * reach, slots), BF16),
            jax.ShapeDtypeStruct((width, slots), BF16),
            jax.ShapeDtypeStruct((width, slots), F32),
            jax.ShapeDtypeStruct((width, mols + 2 * reach), BF16),
        ),
        in_specs=[smem] + vmem(8),
        out_specs=tuple(vmem(4)),
        compiler_params=big,
        name="edges",
        cost_estimate=pl.CostEstimate(
            flops=40 * width * slots * 2 * (2 * mols + 2 * reach), bytes_accessed=8 * 1024 * 1024,
            transcendentals=width * slots,
        ),
    )(
        me, mol_feats, below, above, w_src, w_dst,
        edge_src.reshape(slabs, cap), edge_dst.reshape(slabs, cap), edge_live.reshape(slabs, cap),
    )

    here, w_out, slope = lax.optimization_barrier((me, w_out, slope))
    late = lax.dynamic_index_in_dim(grad_blocks[0], here[0], 0, keepdims=False)[half:]
    own = jnp.pad(late.T, ((0, groups * rows - entries), (0, LANES - half)))

    def chunks(count, lanes, dtype):
        return jax.ShapeDtypeStruct((count, part, lanes), dtype)

    entries_wide = groups * rows
    w_out_wide = jnp.pad(w_out, ((0, 0), (0, entries_wide - entries)))
    wide = mols + 2 * reach
    keep, send, sums, lower, upper, g = pl.pallas_call(
        functools.partial(grad_kernel, half, factor),
        out_shape=(
            chunks(slabs // 2, 2 * width, F32),
            chunks(slabs // 2, 2 * width, BF16),
            jax.ShapeDtypeStruct((2 * mols, width), F32),
            jax.ShapeDtypeStruct((reach, width), BF16),
            jax.ShapeDtypeStruct((reach, width), BF16),
            jax.ShapeDtypeStruct((entries_wide, slots), BF16),
        ),
        in_specs=[smem] + vmem(2) + [hbm] * 3 + vmem(len(came)),
        out_specs=tuple(vmem(6)),
        scratch_shapes=[
            pltpu.VMEM((width, slots), F32),
            pltpu.VMEM((mols + wide, slots), BF16),
            pltpu.VMEM((width, wide), BF16),
            pltpu.SemaphoreType.DMA((4, 2)),
        ],
        compiler_params=big,
        name="grads",
    )(me, own, w_out_wide, in_hbm(slope), in_hbm(onehot), in_hbm(ext), *came)
    lanes = round_up(entries_wide, LANES)
    keep_o, send_o = pl.pallas_call(
        functools.partial(outer_kernel, factor),
        out_shape=(chunks(slabs // 2, lanes, F32), chunks(slabs // 2, lanes, BF16)),
        in_specs=[smem] + vmem(2),
        out_specs=tuple(vmem(2)),
        compiler_params=big,
        name="outer",
        cost_estimate=pl.CostEstimate(
            flops=40 * width * slots * entries_wide, bytes_accessed=4 * 1024 * 1024, transcendentals=0
        ),
    )(me, hidden, g)

    def fold(bit, place, keep, crossed):
        shape = (keep.shape[0] // 2, keep.shape[2])
        return pl.pallas_call(
            functools.partial(fold_kernel, bit, place),
            out_shape=(chunks(*shape, F32), chunks(*shape, BF16)),
            in_specs=[smem] + vmem(2),
            out_specs=tuple(vmem(2)),
            compiler_params=big,
            name="fold",
        )(me, keep, crossed)

    def close(keep, crossed):
        if rest == 1:
            return [keep, crossed]
        sends = pl.pallas_call(
            close_kernel,
            out_shape=chunks(rest, keep.shape[2], BF16),
            in_specs=vmem(2),
            out_specs=vmem(1)[0],
            compiler_params=big,
            name="close",
        )(keep, crossed)
        same = [[low + rank * (slabs // rest) for rank in range(rest)] for low in range(slabs // rest)]
        return [
            lax.all_to_all(sends, "space", split_axis=0, concat_axis=0, tiled=True, axis_index_groups=same)
        ]

    from_above = lax.ppermute(lower, "space", down)
    from_below = lax.ppermute(upper, "space", up)
    crossed = swap(send, 0, slabs)
    crossed_o = swap(send_o, 0, slabs)
    for (bit, place), (bit_o, place_o) in zip(paths[0][1:], paths[1][1:]):
        if bit == 2:
            keep, crossed, from_above, from_below = lax.optimization_barrier((keep, crossed, from_above, from_below))
        keep, send = fold(bit, place, keep, crossed)
        crossed = swap(send, bit, slabs)
        keep_o, crossed_o, _ = lax.optimization_barrier((keep_o, crossed_o, send))
        keep_o, send_o = fold(bit_o, place_o, keep_o, crossed_o)
        crossed_o = swap(send_o, bit_o, slabs)
    terms = close(keep, crossed)
    terms_o = close(keep_o, crossed_o)
    feature_grad = pl.pallas_call(
        rim_kernel,
        out_shape=jax.ShapeDtypeStruct((mols, width), F32),
        in_specs=vmem(5),
        out_specs=vmem(1)[0],
        compiler_params=big,
        name="rims",
        cost_estimate=pl.CostEstimate(flops=2 * width * slots * width * 40, bytes_accessed=4 * 1024 * 1024, transcendentals=0),
    )(sums, from_below, from_above, w_src, w_dst)
    src_grad, dst_grad, out_grad = pl.pallas_call(
        total_kernel,
        out_shape=(
            jax.ShapeDtypeStruct((part, width), F32),
            jax.ShapeDtypeStruct((part, width), F32),
            jax.ShapeDtypeStruct((part, entries), F32),
        ),
        in_specs=vmem(len(terms) + len(terms_o)),
        out_specs=tuple(vmem(3)),
        compiler_params=big,
        name="totals",
    )(*terms, *terms_o)
    return (feature_grad, src_grad, dst_grad, out_grad)


def solution(mesh):
    placed = (
        P(("groups", "space"), None),
        P(),
        P(),
        P(),
        P("space", "groups", None, None),
        P(("groups", "space")),
        P(("groups", "space")),
        P(("groups", "space")),
    )
    return jax.shard_map(
        on_device,
        mesh=mesh,
        in_specs=placed,
        out_specs=(
            P(("groups", "space"), None),
            P(("groups", "space"), None),
            P(("groups", "space"), None),
            P(("groups", "space"), None),
        ),
        check_vma=False,
    )
```

```python
import functools

import jax
import jax.numpy as jnp
from jax import lax
from jax.experimental import pallas as pl
from jax.experimental.pallas import tpu as pltpu
from jax.sharding import PartitionSpec as P

F32 = jnp.float32
BF16 = jnp.bfloat16
LANES = 128
PACK = 16
NN = (((1,), (0,)), ((), ()))
NT = (((1,), (1,)), ((), ()))


def mm(left, right, dims=NN):
    return lax.dot_general(left, right, dims, preferred_element_type=F32)


def halves(x):
    high = x.astype(BF16)
    return high, (x - high.astype(F32)).astype(BF16)


def round_up(x, to):
    return -(-x // to) * to


def vmem(count):
    return [pl.BlockSpec(memory_space=pltpu.VMEM)] * count


def pack_kernel(rows, half, linked, me_ref, feats_ref, g_ref, even_ref, odd_ref, low_ref, top_ref, here_ref, sems, rim_sems):
    entries, slabs, cap = g_ref.shape
    mols = feats_ref.shape[0]
    reach = low_ref.shape[0]
    groups = LANES // half
    blocks = rows // PACK
    count = sems.shape[0]
    stages = []
    for stage in range(count):
        begin, end = stage * blocks // count, (stage + 1) * blocks // count
        copies = []
        for group in range(groups):
            first = min(entries, group * rows + begin * PACK)
            last = min(entries, group * rows + end * PACK)
            if first < last:
                copies.append(
                    pltpu.make_async_copy(g_ref.at[first:last], here_ref.at[first:last], sems.at[stage, group])
                )
        stages.append((begin, end, copies))
        for copy in copies:
            copy.start()
    rims = [
        pltpu.make_async_copy(feats_ref.at[:reach], low_ref, rim_sems.at[0]),
        pltpu.make_async_copy(feats_ref.at[mols - reach :], top_ref, rim_sems.at[1]),
    ]
    for copy in rims:
        copy.start()
    size = PACK * slabs
    to = lax.broadcasted_iota(jnp.int32, (size, size), 0)
    source = lax.broadcasted_iota(jnp.int32, (size, size), 1)
    slab = to // PACK
    if linked:
        slab = slab ^ me_ref[0]
    perm = jnp.where((to % PACK) * slabs + slab == source, 1.0, 0.0).astype(BF16)

    def lanes_of(block):
        early = []
        for group in range(groups):
            first = group * rows + block * PACK
            valid = max(0, min(PACK, entries - first))
            tiles = []
            if valid:
                tiles.append(here_ref[first : first + valid])
            if valid < PACK:
                tiles.append(jnp.zeros((PACK - valid, slabs, cap), BF16))
            tile = tiles[0] if len(tiles) == 1 else jnp.concatenate(tiles, axis=0)
            early.append(tile.reshape(size, cap)[:, :half])
        return early

    for begin, end, copies in stages:
        for copy in copies:
            copy.wait()
        for block in range(begin, end, 2):
            together = range(block, min(block + 2, end))
            lanes = [piece for one in together for piece in lanes_of(one)]
            moved = mm(perm, jnp.concatenate(lanes, axis=1)).astype(BF16)
            for index, one in enumerate(together):
                chunk = moved[:, index * LANES : (index + 1) * LANES].reshape(slabs // 2, 2, PACK, LANES)
                here = pl.ds(one * PACK, PACK)
                even_ref[:, here, :] = chunk[:, 0]
                odd_ref[:, here, :] = chunk[:, 1]
    for copy in rims:
        copy.wait()


def join_kernel(even_ref, other_ref, *message_refs):
    for k, message_ref in enumerate(message_refs):
        message_ref[0] = even_ref[k]
        message_ref[1] = other_ref[k]


def unpack(half, refs, g_ref):
    groups = LANES // half
    rows = g_ref.shape[0] // groups
    chunks = [(ref, index) for ref in refs for index in range(ref.shape[0])]
    tiles = len(chunks) // groups
    for tile in range(tiles):
        here = [ref[index] for ref, index in chunks[tile * groups : (tile + 1) * groups]]
        for group in range(groups):
            lanes = slice(group * half, (group + 1) * half)
            g_ref[group * rows : (group + 1) * rows, tile * LANES : (tile + 1) * LANES] = jnp.concatenate(
                [chunk[:, lanes] for chunk in here], axis=1
            )
    return tiles * LANES


def slot_rows(ref, me, half, linked, near, far):
    per = LANES // half

    def rows_of(ids):
        rows = []
        for tile in range(len(ids) // per):
            pieces = [ref[pl.ds(me ^ i if linked else i, 1), :] for i in ids[tile * per : (tile + 1) * per]]
            rows.append(jnp.concatenate([piece[:, :half] for piece in pieces], axis=1))
        return rows

    own = ref[pl.ds(me, 1), :][:, half:]
    own = jnp.concatenate([own, jnp.full((1, LANES - half), -1, jnp.int32)], axis=1)
    return rows_of(near) + [own] + rows_of(far)


def edge_kernel(
    half, linked, near, far, me_ref, feats_ref, below_ref, above_ref, w_src_ref, w_dst_ref, src_ref, dst_ref, live_ref,
    onehot_ref, hidden_ref, slope_ref, ext_ref,
):
    me = me_ref[0]
    mols = feats_ref.shape[0]
    reach = below_ref.shape[0]
    wide = mols + 2 * reach
    feats = feats_ref[...]
    ext = jnp.concatenate([feats, below_ref[...], above_ref[...]], axis=0)
    ext_ref[...] = ext.T
    proj_src = mm(feats, w_src_ref[...])
    proj_dst = mm(ext, w_dst_ref[...])
    proj = jnp.concatenate([proj_src, proj_dst], axis=0).T
    high, low = halves(proj)
    mol_src = lax.broadcasted_iota(jnp.int32, (mols, LANES), 0)
    mol_dst = lax.broadcasted_iota(jnp.int32, (wide, LANES), 0)
    lists = [slot_rows(ref, me, half, linked, near, far) for ref in (src_ref, dst_ref, live_ref)]
    for tile, (src, dst, live) in enumerate(zip(*lists)):
        src = jnp.where(live > 0, src, -1)
        moved = jnp.where(dst < reach, dst + mols, jnp.where(dst < reach + mols, dst - reach, dst))
        dst = jnp.where(live > 0, moved, -1)
        one_src = jnp.where(mol_src == src, 1.0, 0.0).astype(BF16)
        one_dst = jnp.where(mol_dst == dst, 1.0, 0.0).astype(BF16)
        onehot = jnp.concatenate([one_src, one_dst], axis=0)
        here = pl.ds(tile * LANES, LANES)
        onehot_ref[:, here] = onehot
        pre = mm(high, onehot) + mm(low, onehot)
        sigma = 1.0 / (1.0 + jnp.exp(-pre))
        hidden_ref[:, here] = (pre * sigma).astype(BF16)
        slope_ref[:, here] = sigma * (1.0 + pre * (1.0 - sigma))


def halve(terms, odd, place, keep_ref, send_ref, first):
    count, rows, _ = keep_ref.shape
    width = terms.shape[-1]
    lanes = slice(first, first + width)
    inner = 1 << place
    pairs = terms.reshape(count // inner, 2, inner, rows, width)
    even_part = pairs[:, 0].reshape(count, rows, width)
    odd_part = pairs[:, 1].reshape(count, rows, width)
    keep_ref[:, :, lanes] = jnp.where(odd > 0, odd_part, even_part)
    send_ref[:, :, lanes] = jnp.where(odd > 0, even_part, odd_part).astype(BF16)


def fold_kernel(bit, place, me_ref, keep_ref, came_ref, next_ref, send_ref):
    odd = (me_ref[0] >> bit) % 2
    halve(keep_ref[...] + came_ref[...].astype(F32), odd, place, next_ref, send_ref, 0)


def close_kernel(keep_ref, came_ref, send_ref):
    send_ref[...] = (keep_ref[...] + came_ref[...].astype(F32)).astype(BF16)


def slot_tiles(slots):
    step = 2 * LANES
    return [(first, min(first + step, slots)) for first in range(0, slots, step)]


def start_tiles(slots, offset, slope_hbm, onehot_hbm, slope_ref, onehot_ref, sems):
    tiles = []
    for tile, (first, last) in enumerate(slot_tiles(slots)):
        there, here = pl.ds(offset + first, last - first), pl.ds(first, last - first)
        copies = [
            pltpu.make_async_copy(slope_hbm.at[:, there], slope_ref.at[:, here], sems.at[tile, 0]),
            pltpu.make_async_copy(onehot_hbm.at[:, there], onehot_ref.at[:, here], sems.at[tile, 1]),
        ]
        for copy in copies:
            copy.start()
        tiles.append((slice(first, last), copies))
    return tiles


def sum_edges(tiles, w_out_ref, g_ref, slope_ref, onehot_ref):
    sums = None
    for lanes, copies in tiles:
        dh = mm(w_out_ref[...], g_ref[:, lanes])
        for copy in copies:
            copy.wait()
        dpre = (dh * slope_ref[:, lanes]).astype(BF16)
        term = mm(onehot_ref[:, lanes], dpre, NT)
        sums = term if sums is None else sums + term
    return sums


def near_kernel(half, own_ref, w_out_ref, hidden_ref, slope_hbm, onehot_hbm, *rest):
    *came_refs, sums_ref, outer_ref, g_ref, slope_ref, onehot_ref, sems = rest
    slots = g_ref.shape[1]
    tiles = start_tiles(slots, 0, slope_hbm, onehot_hbm, slope_ref, onehot_ref, sems)
    filled = unpack(half, came_refs, g_ref)
    g_ref[:, filled:] = own_ref[...]
    sums_ref[...] = sum_edges(tiles, w_out_ref, g_ref, slope_ref, onehot_ref)
    outer_ref[...] = mm(hidden_ref[:, :slots], g_ref[...], NT)


def grad_kernel(half, factor, me_ref, w_out_ref, slope_hbm, onehot_hbm, ext_hbm, near_hbm, *rest):
    (
        *came_refs, keep_ref, send_ref, sums_ref, lower_ref, upper_ref, g_ref,
        slope_ref, onehot_ref, ext_ref, near_ref, tile_sems, sems,
    ) = rest
    odd = me_ref[0] % 2
    width = w_out_ref.shape[0]
    slots = g_ref.shape[1]
    inside = sums_ref.shape[0]
    mols = inside // 2
    reach = lower_ref.shape[0]
    tiles = start_tiles(slots, slope_hbm.shape[1] - slots, slope_hbm, onehot_hbm, slope_ref, onehot_ref, tile_sems)
    whole = [
        pltpu.make_async_copy(near_hbm, near_ref, sems.at[0]),
        pltpu.make_async_copy(ext_hbm, ext_ref, sems.at[1]),
    ]
    for copy in whole:
        copy.start()
    unpack(half, came_refs, g_ref)
    sums = sum_edges(tiles, w_out_ref, g_ref, slope_ref, onehot_ref)
    for copy in whole:
        copy.wait()
    sums = sums + near_ref[...]
    lower_ref[...] = sums[inside : inside + reach].astype(BF16)
    upper_ref[...] = sums[inside + reach :].astype(BF16)
    sums_ref[...] = sums[:inside]
    high, low = halves(sums)
    feats = ext_ref[:, :mols]
    rim = ext_ref[:, mols:]
    halve(factor * (mm(feats, high[:mols]) + mm(feats, low[:mols])), odd, 0, keep_ref, send_ref, 0)
    rim_term = mm(jnp.concatenate([rim, rim], axis=1), jnp.concatenate([high[inside:], low[inside:]], axis=0))
    dst_term = mm(feats, high[mols:inside]) + mm(feats, low[mols:inside]) + rim_term
    halve(factor * dst_term, odd, 0, keep_ref, send_ref, width)


def outer_kernel(factor, me_ref, hidden_ref, g_ref, near_hbm, keep_ref, send_ref, near_ref, sem):
    copy = pltpu.make_async_copy(near_hbm, near_ref, sem)
    copy.start()
    slots = g_ref.shape[1]
    term = mm(hidden_ref[:, hidden_ref.shape[1] - slots :], g_ref[...], NT)
    copy.wait()
    term = factor * (term + near_ref[...])
    padding = keep_ref.shape[2] - term.shape[1]
    if padding > 0:
        term = jnp.concatenate([term, jnp.zeros((term.shape[0], padding), F32)], axis=1)
    halve(term, me_ref[0] % 2, 0, keep_ref, send_ref, 0)


def rim_kernel(sums_ref, from_below_ref, from_above_ref, w_src_ref, w_dst_ref, out_ref):
    mols = out_ref.shape[0]
    reach = from_below_ref.shape[0]
    src = sums_ref[:mols]
    dst = sums_ref[mols:]
    dst = jnp.concatenate(
        [
            dst[:reach] + from_below_ref[...].astype(F32),
            dst[reach : mols - reach],
            dst[mols - reach :] + from_above_ref[...].astype(F32),
        ],
        axis=0,
    )
    w_src = w_src_ref[...]
    w_dst = w_dst_ref[...]
    src_high, src_low = halves(src)
    dst_high, dst_low = halves(dst)
    out_ref[...] = mm(src_high, w_src, NT) + mm(src_low, w_src, NT) + mm(dst_high, w_dst, NT) + mm(dst_low, w_dst, NT)


def total_kernel(*refs):
    *refs, src_ref, dst_ref, out_ref = refs
    count = len(refs) // 2
    width = src_ref.shape[1]
    totals = []
    for piece in (refs[:count], refs[count:]):
        terms = [ref[slab].astype(F32) for ref in piece for slab in range(ref.shape[0])]
        totals.append(functools.reduce(jnp.add, terms))
    sides, outer = totals
    src_ref[...] = sides[:, :width]
    dst_ref[...] = sides[:, width:]
    out_ref[...] = outer[:, : out_ref.shape[1]]


def in_hbm(x):
    return pltpu.with_memory_space_constraint(x, pltpu.HBM)


def swap(block, bit, slabs):
    return lax.ppermute(block, "space", [(i, i ^ (1 << bit)) for i in range(slabs)])


def on_device(mol_feats, w_src, w_dst, w_out, grad_blocks, edge_src, edge_dst, edge_live):
    slabs = lax.axis_size("space")
    mols, width = mol_feats.shape
    entries = w_out.shape[1]
    cap = grad_blocks.shape[2]
    half = cap // 2
    reach = mols // 4
    groups = LANES // half
    slots = (slabs // groups + 1) * LANES
    bits = slabs.bit_length() - 1
    if 3 <= bits <= 4:
        late_bits = tuple((bit, 0) for bit in range(3, bits))
        paths = (((0, 0), (1, 0), (2, 0)) + late_bits, ((0, 0), (2, 1), (1, 0)) + late_bits)
    else:
        paths = (tuple((bit, 0) for bit in range(min(bits, 2))),) * 2
    rest = slabs >> len(paths[0])
    part = width // slabs
    factor = float(edge_src.shape[0] * slabs) ** (-0.5)
    me = lax.axis_index("space").astype(jnp.int32).reshape(1)
    smem = pl.BlockSpec(memory_space=pltpu.SMEM)
    hbm = pl.BlockSpec(memory_space=pltpu.HBM)
    big = pltpu.CompilerParams(vmem_limit_bytes=24 * 1024 * 1024)
    up = [(i, (i + 1) % slabs) for i in range(slabs)]
    down = [((i + 1) % slabs, i) for i in range(slabs)]

    rows = round_up(pl.cdiv(entries, groups), PACK)
    stages = 4
    linked = slabs <= 16
    even, odd, low, top = pl.pallas_call(
        functools.partial(pack_kernel, rows, half, linked),
        out_shape=(
            jax.ShapeDtypeStruct((slabs // 2, rows, LANES), BF16),
            jax.ShapeDtypeStruct((slabs // 2, rows, LANES), BF16),
            jax.ShapeDtypeStruct((reach, width), BF16),
            jax.ShapeDtypeStruct((reach, width), BF16),
        ),
        in_specs=[smem, hbm, hbm],
        out_specs=tuple(vmem(4)),
        scratch_shapes=[
            pltpu.VMEM((entries, slabs, cap), BF16),
            pltpu.SemaphoreType.DMA((stages, groups)),
            pltpu.SemaphoreType.DMA((2,)),
        ],
        compiler_params=big,
        name="pack",
    )(me, in_hbm(mol_feats), in_hbm(jnp.transpose(grad_blocks[0], (2, 0, 1))))
    below = lax.ppermute(top, "space", up)
    above = lax.ppermute(low, "space", down)
    if linked:
        other = swap(odd, 0, slabs)
        other, below, above = lax.optimization_barrier((other, below, above))
        messages = pl.pallas_call(
            join_kernel,
            out_shape=(jax.ShapeDtypeStruct((2, rows, LANES), BF16),) * (slabs // 2),
            in_specs=vmem(2),
            out_specs=tuple(vmem(slabs // 2)),
            compiler_params=big,
            name="join",
        )(even, other)
        quarter = slabs // 4
        came = {0: messages[0]}
        for k in (*range(1, quarter - 1), *range(quarter, 2 * quarter), *range(max(quarter - 1, 1), quarter)):
            came[k] = lax.ppermute(messages[k], "space", [(i, i ^ (2 * k)) for i in range(slabs)])
        for k in range(1, quarter - 1):
            came[k], below, above, me = lax.optimization_barrier((came[k], below, above, me))
        near = tuple(range(2 * quarter))
        far = tuple(range(2 * quarter, slabs))
        came_near = [came[k] for k in range(quarter)]
        came_far = [came[k] for k in range(quarter, 2 * quarter)]
    else:
        packed = jnp.stack([even, odd], axis=1).reshape(slabs, rows, LANES)
        near, far = (), tuple(range(slabs))
        came_near = []
        came_far = [lax.all_to_all(packed, "space", split_axis=0, concat_axis=0, tiled=True)]
    far_slots = len(far) * half
    near_slots = slots - far_slots

    onehot, hidden, slope, ext = pl.pallas_call(
        functools.partial(edge_kernel, half, linked, near, far),
        out_shape=(
            jax.ShapeDtypeStruct((2 * mols + 2 * reach, slots), BF16),
            jax.ShapeDtypeStruct((width, slots), BF16),
            jax.ShapeDtypeStruct((width, slots), F32),
            jax.ShapeDtypeStruct((width, mols + 2 * reach), BF16),
        ),
        in_specs=[smem] + vmem(8),
        out_specs=tuple(vmem(4)),
        compiler_params=big,
        name="edges",
        cost_estimate=pl.CostEstimate(
            flops=40 * width * slots * 2 * (2 * mols + 2 * reach), bytes_accessed=8 * 1024 * 1024,
            transcendentals=width * slots,
        ),
    )(
        me, mol_feats, below, above, w_src, w_dst,
        edge_src.reshape(slabs, cap), edge_dst.reshape(slabs, cap), edge_live.reshape(slabs, cap),
    )

    w_out = lax.optimization_barrier((w_out, me))[0]
    late = lax.dynamic_index_in_dim(grad_blocks[0], me[0], 0, keepdims=False)[half:]
    own = jnp.pad(late.T, ((0, groups * rows - entries), (0, LANES - half)))

    def chunks(count, lanes, dtype):
        return jax.ShapeDtypeStruct((count, part, lanes), dtype)

    entries_wide = groups * rows
    w_out_wide = jnp.pad(w_out, ((0, 0), (0, entries_wide - entries)))
    wide = mols + 2 * reach
    near_sums, near_outer = pl.pallas_call(
        functools.partial(near_kernel, half),
        out_shape=(
            jax.ShapeDtypeStruct((mols + wide, width), F32),
            jax.ShapeDtypeStruct((width, entries_wide), F32),
        ),
        in_specs=vmem(3) + [hbm] * 2 + vmem(len(came_near)),
        out_specs=tuple(vmem(2)),
        scratch_shapes=[
            pltpu.VMEM((entries_wide, near_slots), BF16),
            pltpu.VMEM((width, near_slots), F32),
            pltpu.VMEM((mols + wide, near_slots), BF16),
            pltpu.SemaphoreType.DMA((len(slot_tiles(near_slots)), 2)),
        ],
        compiler_params=big,
        name="near",
        cost_estimate=pl.CostEstimate(
            flops=40 * width * near_slots * entries_wide, bytes_accessed=6 * 1024 * 1024, transcendentals=0
        ),
    )(own, w_out_wide, hidden, in_hbm(slope), in_hbm(onehot), *came_near)
    keep, send, sums, lower, upper, g = pl.pallas_call(
        functools.partial(grad_kernel, half, factor),
        out_shape=(
            chunks(slabs // 2, 2 * width, F32),
            chunks(slabs // 2, 2 * width, BF16),
            jax.ShapeDtypeStruct((2 * mols, width), F32),
            jax.ShapeDtypeStruct((reach, width), BF16),
            jax.ShapeDtypeStruct((reach, width), BF16),
            jax.ShapeDtypeStruct((entries_wide, far_slots), BF16),
        ),
        in_specs=[smem] + vmem(1) + [hbm] * 4 + vmem(len(came_far)),
        out_specs=tuple(vmem(6)),
        scratch_shapes=[
            pltpu.VMEM((width, far_slots), F32),
            pltpu.VMEM((mols + wide, far_slots), BF16),
            pltpu.VMEM((width, wide), BF16),
            pltpu.VMEM((mols + wide, width), F32),
            pltpu.SemaphoreType.DMA((len(slot_tiles(far_slots)), 2)),
            pltpu.SemaphoreType.DMA((2,)),
        ],
        compiler_params=big,
        name="grads",
    )(me, w_out_wide, in_hbm(slope), in_hbm(onehot), in_hbm(ext), in_hbm(near_sums), *came_far)
    lanes = round_up(entries_wide, LANES)
    keep_o, send_o = pl.pallas_call(
        functools.partial(outer_kernel, factor),
        out_shape=(chunks(slabs // 2, lanes, F32), chunks(slabs // 2, lanes, BF16)),
        in_specs=[smem] + vmem(2) + [hbm],
        out_specs=tuple(vmem(2)),
        scratch_shapes=[pltpu.VMEM((width, entries_wide), F32), pltpu.SemaphoreType.DMA(())],
        compiler_params=big,
        name="outer",
        cost_estimate=pl.CostEstimate(
            flops=40 * width * slots * entries_wide, bytes_accessed=4 * 1024 * 1024, transcendentals=0
        ),
    )(me, hidden, g, in_hbm(near_outer))

    def fold(bit, place, keep, crossed):
        shape = (keep.shape[0] // 2, keep.shape[2])
        return pl.pallas_call(
            functools.partial(fold_kernel, bit, place),
            out_shape=(chunks(*shape, F32), chunks(*shape, BF16)),
            in_specs=[smem] + vmem(2),
            out_specs=tuple(vmem(2)),
            compiler_params=big,
            name="fold",
        )(me, keep, crossed)

    def close(keep, crossed):
        if rest == 1:
            return [keep, crossed]
        sends = pl.pallas_call(
            close_kernel,
            out_shape=chunks(rest, keep.shape[2], BF16),
            in_specs=vmem(2),
            out_specs=vmem(1)[0],
            compiler_params=big,
            name="close",
        )(keep, crossed)
        same = [[low + rank * (slabs // rest) for rank in range(rest)] for low in range(slabs // rest)]
        return [
            lax.all_to_all(sends, "space", split_axis=0, concat_axis=0, tiled=True, axis_index_groups=same)
        ]

    from_above = lax.ppermute(lower, "space", down)
    from_below = lax.ppermute(upper, "space", up)
    crossed = swap(send, 0, slabs)
    crossed_o = swap(send_o, 0, slabs)
    for (bit, place), (bit_o, place_o) in zip(paths[0][1:], paths[1][1:]):
        if bit == 2:
            keep, crossed, from_above, from_below = lax.optimization_barrier((keep, crossed, from_above, from_below))
        keep, send = fold(bit, place, keep, crossed)
        crossed = swap(send, bit, slabs)
        keep_o, crossed_o, _ = lax.optimization_barrier((keep_o, crossed_o, send))
        keep_o, send_o = fold(bit_o, place_o, keep_o, crossed_o)
        crossed_o = swap(send_o, bit_o, slabs)
    terms = close(keep, crossed)
    terms_o = close(keep_o, crossed_o)
    feature_grad = pl.pallas_call(
        rim_kernel,
        out_shape=jax.ShapeDtypeStruct((mols, width), F32),
        in_specs=vmem(5),
        out_specs=vmem(1)[0],
        compiler_params=big,
        name="rims",
        cost_estimate=pl.CostEstimate(flops=2 * width * slots * width * 40, bytes_accessed=4 * 1024 * 1024, transcendentals=0),
    )(sums, from_below, from_above, w_src, w_dst)
    src_grad, dst_grad, out_grad = pl.pallas_call(
        total_kernel,
        out_shape=(
            jax.ShapeDtypeStruct((part, width), F32),
            jax.ShapeDtypeStruct((part, width), F32),
            jax.ShapeDtypeStruct((part, entries), F32),
        ),
        in_specs=vmem(len(terms) + len(terms_o)),
        out_specs=tuple(vmem(3)),
        compiler_params=big,
        name="totals",
    )(*terms, *terms_o)
    return (feature_grad, src_grad, dst_grad, out_grad)


def solution(mesh):
    placed = (
        P(("groups", "space"), None),
        P(),
        P(),
        P(),
        P("space", "groups", None, None),
        P(("groups", "space")),
        P(("groups", "space")),
        P(("groups", "space")),
    )
    return jax.shard_map(
        on_device,
        mesh=mesh,
        in_specs=placed,
        out_specs=(
            P(("groups", "space"), None),
            P(("groups", "space"), None),
            P(("groups", "space"), None),
            P(("groups", "space"), None),
        ),
        check_vma=False,
    )
```

```python
import functools

import jax
import jax.numpy as jnp
from jax import lax
from jax.experimental import pallas as pl
from jax.experimental.pallas import tpu as pltpu
from jax.sharding import PartitionSpec as P

F32 = jnp.float32
BF16 = jnp.bfloat16
LANES = 128
PACK = 16
NN = (((1,), (0,)), ((), ()))
NT = (((1,), (1,)), ((), ()))


def mm(left, right, dims=NN):
    return lax.dot_general(left, right, dims, preferred_element_type=F32)


def halves(x):
    high = x.astype(BF16)
    return high, (x - high.astype(F32)).astype(BF16)


def round_up(x, to):
    return -(-x // to) * to


def vmem(count):
    return [pl.BlockSpec(memory_space=pltpu.VMEM)] * count


def pack_kernel(rows, half, linked, me_ref, feats_ref, g_ref, even_ref, odd_ref, low_ref, top_ref, here_ref, sems, rim_sems):
    entries, slabs, cap = g_ref.shape
    mols = feats_ref.shape[0]
    reach = low_ref.shape[0]
    groups = LANES // half
    blocks = rows // PACK
    count = sems.shape[0]
    stages = []
    for stage in range(count):
        begin, end = stage * blocks // count, (stage + 1) * blocks // count
        copies = []
        for group in range(groups):
            first = min(entries, group * rows + begin * PACK)
            last = min(entries, group * rows + end * PACK)
            if first < last:
                copies.append(
                    pltpu.make_async_copy(g_ref.at[first:last], here_ref.at[first:last], sems.at[stage, group])
                )
        stages.append((begin, end, copies))
        for copy in copies:
            copy.start()
    rims = [
        pltpu.make_async_copy(feats_ref.at[:reach], low_ref, rim_sems.at[0]),
        pltpu.make_async_copy(feats_ref.at[mols - reach :], top_ref, rim_sems.at[1]),
    ]
    for copy in rims:
        copy.start()
    size = PACK * slabs
    to = lax.broadcasted_iota(jnp.int32, (size, size), 0)
    source = lax.broadcasted_iota(jnp.int32, (size, size), 1)
    slab = to // PACK
    if linked:
        slab = slab ^ me_ref[0]
    perm = jnp.where((to % PACK) * slabs + slab == source, 1.0, 0.0).astype(BF16)

    def lanes_of(block):
        early = []
        for group in range(groups):
            first = group * rows + block * PACK
            valid = max(0, min(PACK, entries - first))
            tiles = []
            if valid:
                tiles.append(here_ref[first : first + valid])
            if valid < PACK:
                tiles.append(jnp.zeros((PACK - valid, slabs, cap), BF16))
            tile = tiles[0] if len(tiles) == 1 else jnp.concatenate(tiles, axis=0)
            early.append(tile.reshape(size, cap)[:, :half])
        return early

    for begin, end, copies in stages:
        for copy in copies:
            copy.wait()
        for block in range(begin, end, 2):
            together = range(block, min(block + 2, end))
            lanes = [piece for one in together for piece in lanes_of(one)]
            moved = mm(perm, jnp.concatenate(lanes, axis=1)).astype(BF16)
            for index, one in enumerate(together):
                chunk = moved[:, index * LANES : (index + 1) * LANES].reshape(slabs // 2, 2, PACK, LANES)
                here = pl.ds(one * PACK, PACK)
                even_ref[:, here, :] = chunk[:, 0]
                odd_ref[:, here, :] = chunk[:, 1]
    for copy in rims:
        copy.wait()


def join_kernel(even_ref, other_ref, *message_refs):
    for k, message_ref in enumerate(message_refs):
        message_ref[0] = even_ref[k]
        message_ref[1] = other_ref[k]


def unpack(half, refs, g_ref):
    groups = LANES // half
    rows = g_ref.shape[0] // groups
    chunks = [(ref, index) for ref in refs for index in range(ref.shape[0])]
    tiles = len(chunks) // groups
    for tile in range(tiles):
        here = [ref[index] for ref, index in chunks[tile * groups : (tile + 1) * groups]]
        for group in range(groups):
            lanes = slice(group * half, (group + 1) * half)
            g_ref[group * rows : (group + 1) * rows, tile * LANES : (tile + 1) * LANES] = jnp.concatenate(
                [chunk[:, lanes] for chunk in here], axis=1
            )
    return tiles * LANES


def slot_rows(ref, me, half, linked, near, far):
    per = LANES // half

    def rows_of(ids):
        rows = []
        for tile in range(len(ids) // per):
            pieces = [ref[pl.ds(me ^ i if linked else i, 1), :] for i in ids[tile * per : (tile + 1) * per]]
            rows.append(jnp.concatenate([piece[:, :half] for piece in pieces], axis=1))
        return rows

    own = ref[pl.ds(me, 1), :][:, half:]
    own = jnp.concatenate([own, jnp.full((1, LANES - half), -1, jnp.int32)], axis=1)
    return rows_of(near) + [own] + rows_of(far)


def edge_kernel(
    half, linked, near, far, me_ref, feats_ref, below_ref, above_ref, w_src_ref, w_dst_ref, w_out_ref, src_ref, dst_ref,
    live_ref, onehot_hbm, slope_hbm, ext_hbm, near_hidden_ref, far_hidden_ref, w_wide_ref,
    onehot_ref, slope_ref, ext_ref, w_rows_ref, sems,
):
    me = me_ref[0]
    mols = feats_ref.shape[0]
    reach = below_ref.shape[0]
    wide = mols + 2 * reach
    slots = slope_ref.shape[1]
    entries = w_out_ref.shape[0]
    near_slots = near_hidden_ref.shape[1]
    copies = []

    def send(source, target):
        copy = pltpu.make_async_copy(source, target, sems.at[len(copies)])
        copy.start()
        copies.append(copy)

    feats = feats_ref[...]
    ext = jnp.concatenate([feats, below_ref[...], above_ref[...]], axis=0)
    ext_ref[...] = ext.T
    send(ext_ref, ext_hbm)
    proj_src = mm(feats, w_src_ref[...])
    proj_dst = mm(ext, w_dst_ref[...])
    proj = jnp.concatenate([proj_src, proj_dst], axis=0).T
    high, low = halves(proj)
    mol_src = lax.broadcasted_iota(jnp.int32, (mols, LANES), 0)
    mol_dst = lax.broadcasted_iota(jnp.int32, (wide, LANES), 0)
    lists = [slot_rows(ref, me, half, linked, near, far) for ref in (src_ref, dst_ref, live_ref)]
    for tile, (src, dst, live) in enumerate(zip(*lists)):
        src = jnp.where(live > 0, src, -1)
        moved = jnp.where(dst < reach, dst + mols, jnp.where(dst < reach + mols, dst - reach, dst))
        dst = jnp.where(live > 0, moved, -1)
        one_src = jnp.where(mol_src == src, 1.0, 0.0).astype(BF16)
        one_dst = jnp.where(mol_dst == dst, 1.0, 0.0).astype(BF16)
        here = pl.ds(tile * LANES, LANES)
        onehot_ref[:, here] = jnp.concatenate([one_src, one_dst], axis=0)
    for first, last in slot_tiles(near_slots) + [(near_slots + f, near_slots + l) for f, l in slot_tiles(slots - near_slots)]:
        here = pl.ds(first, last - first)
        send(onehot_ref.at[:, here], onehot_hbm.at[:, here])
        onehot = onehot_ref[:, here]
        pre = mm(high, onehot) + mm(low, onehot)
        sigma = 1.0 / (1.0 + jnp.exp(-pre))
        hidden = (pre * sigma).astype(BF16)
        if first < near_slots:
            near_hidden_ref[:, here] = hidden
        else:
            far_hidden_ref[:, pl.ds(first - near_slots, last - first)] = hidden
        slope_ref[:, here] = sigma * (1.0 + pre * (1.0 - sigma))
        send(slope_ref.at[:, here], slope_hbm.at[:, here])
    whole = entries // LANES * LANES
    w_rows_ref[whole:] = jnp.zeros((w_rows_ref.shape[0] - whole, w_rows_ref.shape[1]), BF16)
    w_rows_ref[:whole] = w_out_ref[:whole]
    w_rows_ref[whole:entries] = w_out_ref[whole:]
    w_wide_ref[...] = w_rows_ref[...].T
    for copy in copies:
        copy.wait()


def halve(terms, odd, place, keep_ref, send_ref, first):
    count, rows, _ = keep_ref.shape
    width = terms.shape[-1]
    lanes = slice(first, first + width)
    inner = 1 << place
    pairs = terms.reshape(count // inner, 2, inner, rows, width)
    even_part = pairs[:, 0].reshape(count, rows, width)
    odd_part = pairs[:, 1].reshape(count, rows, width)
    keep_ref[:, :, lanes] = jnp.where(odd > 0, odd_part, even_part)
    send_ref[:, :, lanes] = jnp.where(odd > 0, even_part, odd_part).astype(BF16)


def fold_kernel(bit, place, me_ref, keep_ref, came_ref, next_ref, send_ref):
    odd = (me_ref[0] >> bit) % 2
    halve(keep_ref[...] + came_ref[...].astype(F32), odd, place, next_ref, send_ref, 0)


def close_kernel(keep_ref, came_ref, send_ref):
    send_ref[...] = (keep_ref[...] + came_ref[...].astype(F32)).astype(BF16)


def slot_tiles(slots):
    step = 2 * LANES
    return [(first, min(first + step, slots)) for first in range(0, slots, step)]


def start_tiles(slots, offset, slope_hbm, onehot_hbm, slope_ref, onehot_ref, sems):
    tiles = []
    for tile, (first, last) in enumerate(slot_tiles(slots)):
        there, here = pl.ds(offset + first, last - first), pl.ds(first, last - first)
        copies = [
            pltpu.make_async_copy(slope_hbm.at[:, there], slope_ref.at[:, here], sems.at[tile, 0]),
            pltpu.make_async_copy(onehot_hbm.at[:, there], onehot_ref.at[:, here], sems.at[tile, 1]),
        ]
        for copy in copies:
            copy.start()
        tiles.append((slice(first, last), copies))
    return tiles


def sum_edges(tiles, w_out_ref, g_ref, slope_ref, onehot_ref):
    sums = None
    for lanes, copies in tiles:
        dh = mm(w_out_ref[...], g_ref[:, lanes])
        for copy in copies:
            copy.wait()
        dpre = (dh * slope_ref[:, lanes]).astype(BF16)
        term = mm(onehot_ref[:, lanes], dpre, NT)
        sums = term if sums is None else sums + term
    return sums


def near_kernel(half, own_ref, w_out_ref, hidden_ref, slope_hbm, onehot_hbm, *rest):
    *came_refs, sums_hbm, outer_hbm, g_ref, slope_ref, onehot_ref, sums_ref, outer_ref, sems, out_sems = rest
    slots = g_ref.shape[1]
    tiles = start_tiles(slots, 0, slope_hbm, onehot_hbm, slope_ref, onehot_ref, sems)
    filled = unpack(half, came_refs, g_ref)
    g_ref[:, filled:] = own_ref[...]
    outer_ref[...] = mm(hidden_ref[...], g_ref[...], NT)
    outer_copy = pltpu.make_async_copy(outer_ref, outer_hbm, out_sems.at[0])
    outer_copy.start()
    sums_ref[...] = sum_edges(tiles, w_out_ref, g_ref, slope_ref, onehot_ref)
    sums_copy = pltpu.make_async_copy(sums_ref, sums_hbm, out_sems.at[1])
    sums_copy.start()
    outer_copy.wait()
    sums_copy.wait()


def grad_kernel(half, factor, me_ref, w_out_ref, slope_hbm, onehot_hbm, ext_hbm, near_hbm, *rest):
    (
        *came_refs, keep_ref, send_ref, sums_ref, lower_ref, upper_ref, g_ref,
        slope_ref, onehot_ref, ext_ref, near_ref, tile_sems, sems,
    ) = rest
    odd = me_ref[0] % 2
    width = w_out_ref.shape[0]
    slots = g_ref.shape[1]
    inside = sums_ref.shape[0]
    mols = inside // 2
    reach = lower_ref.shape[0]
    tiles = start_tiles(slots, slope_hbm.shape[1] - slots, slope_hbm, onehot_hbm, slope_ref, onehot_ref, tile_sems)
    whole = [
        pltpu.make_async_copy(near_hbm, near_ref, sems.at[0]),
        pltpu.make_async_copy(ext_hbm, ext_ref, sems.at[1]),
    ]
    for copy in whole:
        copy.start()
    unpack(half, came_refs, g_ref)
    sums = sum_edges(tiles, w_out_ref, g_ref, slope_ref, onehot_ref)
    for copy in whole:
        copy.wait()
    sums = sums + near_ref[...]
    lower_ref[...] = sums[inside : inside + reach].astype(BF16)
    upper_ref[...] = sums[inside + reach :].astype(BF16)
    sums_ref[...] = sums[:inside]
    high, low = halves(sums)
    feats = ext_ref[:, :mols]
    rim = ext_ref[:, mols:]
    halve(factor * (mm(feats, high[:mols]) + mm(feats, low[:mols])), odd, 0, keep_ref, send_ref, 0)
    rim_term = mm(jnp.concatenate([rim, rim], axis=1), jnp.concatenate([high[inside:], low[inside:]], axis=0))
    dst_term = mm(feats, high[mols:inside]) + mm(feats, low[mols:inside]) + rim_term
    halve(factor * dst_term, odd, 0, keep_ref, send_ref, width)


def outer_kernel(factor, me_ref, hidden_ref, g_ref, near_hbm, keep_ref, send_ref, near_ref, sem):
    copy = pltpu.make_async_copy(near_hbm, near_ref, sem)
    copy.start()
    term = mm(hidden_ref[...], g_ref[...], NT)
    copy.wait()
    term = factor * (term + near_ref[...])
    padding = keep_ref.shape[2] - term.shape[1]
    if padding > 0:
        term = jnp.concatenate([term, jnp.zeros((term.shape[0], padding), F32)], axis=1)
    halve(term, me_ref[0] % 2, 0, keep_ref, send_ref, 0)


def rim_kernel(sums_ref, from_below_ref, from_above_ref, w_src_ref, w_dst_ref, out_ref):
    mols = out_ref.shape[0]
    reach = from_below_ref.shape[0]
    src = sums_ref[:mols]
    dst = sums_ref[mols:]
    dst = jnp.concatenate(
        [
            dst[:reach] + from_below_ref[...].astype(F32),
            dst[reach : mols - reach],
            dst[mols - reach :] + from_above_ref[...].astype(F32),
        ],
        axis=0,
    )
    w_src = w_src_ref[...]
    w_dst = w_dst_ref[...]
    src_high, src_low = halves(src)
    dst_high, dst_low = halves(dst)
    out_ref[...] = mm(src_high, w_src, NT) + mm(src_low, w_src, NT) + mm(dst_high, w_dst, NT) + mm(dst_low, w_dst, NT)


def total_kernel(*refs):
    *refs, src_ref, dst_ref, out_ref = refs
    count = len(refs) // 2
    width = src_ref.shape[1]
    totals = []
    for piece in (refs[:count], refs[count:]):
        terms = [ref[slab].astype(F32) for ref in piece for slab in range(ref.shape[0])]
        totals.append(functools.reduce(jnp.add, terms))
    sides, outer = totals
    src_ref[...] = sides[:, :width]
    dst_ref[...] = sides[:, width:]
    out_ref[...] = outer[:, : out_ref.shape[1]]


def in_hbm(x):
    return pltpu.with_memory_space_constraint(x, pltpu.HBM)


def swap(block, bit, slabs):
    return lax.ppermute(block, "space", [(i, i ^ (1 << bit)) for i in range(slabs)])


def on_device(mol_feats, w_src, w_dst, w_out, grad_blocks, edge_src, edge_dst, edge_live):
    slabs = lax.axis_size("space")
    mols, width = mol_feats.shape
    entries = w_out.shape[1]
    cap = grad_blocks.shape[2]
    half = cap // 2
    reach = mols // 4
    groups = LANES // half
    slots = (slabs // groups + 1) * LANES
    bits = slabs.bit_length() - 1
    if 3 <= bits <= 4:
        late_bits = tuple((bit, 0) for bit in range(3, bits))
        paths = (((0, 0), (1, 0), (2, 0)) + late_bits, ((0, 0), (2, 1), (1, 0)) + late_bits)
    else:
        paths = (tuple((bit, 0) for bit in range(min(bits, 2))),) * 2
    rest = slabs >> len(paths[0])
    part = width // slabs
    factor = float(edge_src.shape[0] * slabs) ** (-0.5)
    me = lax.axis_index("space").astype(jnp.int32).reshape(1)
    smem = pl.BlockSpec(memory_space=pltpu.SMEM)
    hbm = pl.BlockSpec(memory_space=pltpu.HBM)
    big = pltpu.CompilerParams(vmem_limit_bytes=24 * 1024 * 1024)
    up = [(i, (i + 1) % slabs) for i in range(slabs)]
    down = [((i + 1) % slabs, i) for i in range(slabs)]

    rows = round_up(pl.cdiv(entries, groups), PACK)
    stages = 4
    linked = slabs <= 16
    even, odd, low, top = pl.pallas_call(
        functools.partial(pack_kernel, rows, half, linked),
        out_shape=(
            jax.ShapeDtypeStruct((slabs // 2, rows, LANES), BF16),
            jax.ShapeDtypeStruct((slabs // 2, rows, LANES), BF16),
            jax.ShapeDtypeStruct((reach, width), BF16),
            jax.ShapeDtypeStruct((reach, width), BF16),
        ),
        in_specs=[smem, hbm, hbm],
        out_specs=tuple(vmem(4)),
        scratch_shapes=[
            pltpu.VMEM((entries, slabs, cap), BF16),
            pltpu.SemaphoreType.DMA((stages, groups)),
            pltpu.SemaphoreType.DMA((2,)),
        ],
        compiler_params=big,
        name="pack",
    )(me, in_hbm(mol_feats), in_hbm(jnp.transpose(grad_blocks[0], (2, 0, 1))))
    below = lax.ppermute(top, "space", up)
    above = lax.ppermute(low, "space", down)
    late = lax.dynamic_index_in_dim(grad_blocks[0], me[0], 0, keepdims=False)[half:]
    own = jnp.pad(late.T, ((0, groups * rows - entries), (0, LANES - half)))
    if linked:
        other = swap(odd, 0, slabs)
        other, below, above, own = lax.optimization_barrier((other, below, above, own))
        messages = pl.pallas_call(
            join_kernel,
            out_shape=(jax.ShapeDtypeStruct((2, rows, LANES), BF16),) * (slabs // 2),
            in_specs=vmem(2),
            out_specs=tuple(vmem(slabs // 2)),
            compiler_params=big,
            name="join",
        )(even, other)
        quarter = slabs // 4
        came = {0: messages[0]}
        for k in (*range(1, quarter - 1), *range(quarter, 2 * quarter), *range(max(quarter - 1, 1), quarter)):
            came[k] = lax.ppermute(messages[k], "space", [(i, i ^ (2 * k)) for i in range(slabs)])
        for k in range(1, quarter - 1):
            came[k], below, above, me = lax.optimization_barrier((came[k], below, above, me))
        near = tuple(range(2 * quarter))
        far = tuple(range(2 * quarter, slabs))
        came_near = [came[k] for k in range(quarter)]
        came_far = [came[k] for k in range(quarter, 2 * quarter)]
    else:
        packed = jnp.stack([even, odd], axis=1).reshape(slabs, rows, LANES)
        near, far = (), tuple(range(slabs))
        came_near = []
        came_far = [lax.all_to_all(packed, "space", split_axis=0, concat_axis=0, tiled=True)]
    far_slots = len(far) * half
    near_slots = slots - far_slots

    wide = mols + 2 * reach
    entries_wide = groups * rows
    pieces = len(slot_tiles(near_slots)) + len(slot_tiles(far_slots))
    onehot, slope, ext, near_hidden, far_hidden, w_out_wide = pl.pallas_call(
        functools.partial(edge_kernel, half, linked, near, far),
        out_shape=(
            pltpu.HBM((mols + wide, slots), BF16),
            pltpu.HBM((width, slots), F32),
            pltpu.HBM((width, wide), BF16),
            jax.ShapeDtypeStruct((width, near_slots), BF16),
            jax.ShapeDtypeStruct((width, far_slots), BF16),
            jax.ShapeDtypeStruct((width, entries_wide), BF16),
        ),
        in_specs=[smem] + vmem(9),
        out_specs=(hbm,) * 3 + tuple(vmem(3)),
        scratch_shapes=[
            pltpu.VMEM((mols + wide, slots), BF16),
            pltpu.VMEM((width, slots), F32),
            pltpu.VMEM((width, wide), BF16),
            pltpu.VMEM((entries_wide, width), BF16),
            pltpu.SemaphoreType.DMA((2 * pieces + 1,)),
        ],
        compiler_params=big,
        name="edges",
        cost_estimate=pl.CostEstimate(
            flops=40 * width * slots * 2 * (2 * mols + 2 * reach), bytes_accessed=8 * 1024 * 1024,
            transcendentals=width * slots,
        ),
    )(
        me, mol_feats, below, above, w_src, w_dst, w_out.T,
        edge_src.reshape(slabs, cap), edge_dst.reshape(slabs, cap), edge_live.reshape(slabs, cap),
    )
    onehot, slope, ext = in_hbm(onehot), in_hbm(slope), in_hbm(ext)

    def chunks(count, lanes, dtype):
        return jax.ShapeDtypeStruct((count, part, lanes), dtype)

    near_sums, near_outer = pl.pallas_call(
        functools.partial(near_kernel, half),
        out_shape=(
            pltpu.HBM((mols + wide, width), F32),
            pltpu.HBM((width, entries_wide), F32),
        ),
        in_specs=vmem(3) + [hbm] * 2 + vmem(len(came_near)),
        out_specs=(hbm, hbm),
        scratch_shapes=[
            pltpu.VMEM((entries_wide, near_slots), BF16),
            pltpu.VMEM((width, near_slots), F32),
            pltpu.VMEM((mols + wide, near_slots), BF16),
            pltpu.VMEM((mols + wide, width), F32),
            pltpu.VMEM((width, entries_wide), F32),
            pltpu.SemaphoreType.DMA((len(slot_tiles(near_slots)), 2)),
            pltpu.SemaphoreType.DMA((2,)),
        ],
        compiler_params=big,
        name="near",
        cost_estimate=pl.CostEstimate(
            flops=40 * width * near_slots * entries_wide, bytes_accessed=6 * 1024 * 1024, transcendentals=0
        ),
    )(own, w_out_wide, near_hidden, slope, onehot, *came_near)
    near_sums, near_outer = in_hbm(near_sums), in_hbm(near_outer)
    keep, send, sums, lower, upper, g = pl.pallas_call(
        functools.partial(grad_kernel, half, factor),
        out_shape=(
            chunks(slabs // 2, 2 * width, F32),
            chunks(slabs // 2, 2 * width, BF16),
            jax.ShapeDtypeStruct((2 * mols, width), F32),
            jax.ShapeDtypeStruct((reach, width), BF16),
            jax.ShapeDtypeStruct((reach, width), BF16),
            jax.ShapeDtypeStruct((entries_wide, far_slots), BF16),
        ),
        in_specs=[smem] + vmem(1) + [hbm] * 4 + vmem(len(came_far)),
        out_specs=tuple(vmem(6)),
        scratch_shapes=[
            pltpu.VMEM((width, far_slots), F32),
            pltpu.VMEM((mols + wide, far_slots), BF16),
            pltpu.VMEM((width, wide), BF16),
            pltpu.VMEM((mols + wide, width), F32),
            pltpu.SemaphoreType.DMA((len(slot_tiles(far_slots)), 2)),
            pltpu.SemaphoreType.DMA((2,)),
        ],
        compiler_params=big,
        name="grads",
    )(me, w_out_wide, slope, onehot, ext, near_sums, *came_far)
    lanes = round_up(entries_wide, LANES)
    keep_o, send_o = pl.pallas_call(
        functools.partial(outer_kernel, factor),
        out_shape=(chunks(slabs // 2, lanes, F32), chunks(slabs // 2, lanes, BF16)),
        in_specs=[smem] + vmem(2) + [hbm],
        out_specs=tuple(vmem(2)),
        scratch_shapes=[pltpu.VMEM((width, entries_wide), F32), pltpu.SemaphoreType.DMA(())],
        compiler_params=big,
        name="outer",
        cost_estimate=pl.CostEstimate(
            flops=40 * width * slots * entries_wide, bytes_accessed=4 * 1024 * 1024, transcendentals=0
        ),
    )(me, far_hidden, g, near_outer)

    def fold(bit, place, keep, crossed):
        shape = (keep.shape[0] // 2, keep.shape[2])
        return pl.pallas_call(
            functools.partial(fold_kernel, bit, place),
            out_shape=(chunks(*shape, F32), chunks(*shape, BF16)),
            in_specs=[smem] + vmem(2),
            out_specs=tuple(vmem(2)),
            compiler_params=big,
            name="fold",
        )(me, keep, crossed)

    def close(keep, crossed):
        if rest == 1:
            return [keep, crossed]
        sends = pl.pallas_call(
            close_kernel,
            out_shape=chunks(rest, keep.shape[2], BF16),
            in_specs=vmem(2),
            out_specs=vmem(1)[0],
            compiler_params=big,
            name="close",
        )(keep, crossed)
        same = [[low + rank * (slabs // rest) for rank in range(rest)] for low in range(slabs // rest)]
        return [
            lax.all_to_all(sends, "space", split_axis=0, concat_axis=0, tiled=True, axis_index_groups=same)
        ]

    from_above = lax.ppermute(lower, "space", down)
    from_below = lax.ppermute(upper, "space", up)
    crossed = swap(send, 0, slabs)
    crossed_o = swap(send_o, 0, slabs)
    for (bit, place), (bit_o, place_o) in zip(paths[0][1:], paths[1][1:]):
        if bit == 2:
            keep, crossed, from_above, from_below = lax.optimization_barrier((keep, crossed, from_above, from_below))
        keep, send = fold(bit, place, keep, crossed)
        crossed = swap(send, bit, slabs)
        keep_o, crossed_o, _ = lax.optimization_barrier((keep_o, crossed_o, send))
        keep_o, send_o = fold(bit_o, place_o, keep_o, crossed_o)
        crossed_o = swap(send_o, bit_o, slabs)
    terms = close(keep, crossed)
    terms_o = close(keep_o, crossed_o)
    feature_grad = pl.pallas_call(
        rim_kernel,
        out_shape=jax.ShapeDtypeStruct((mols, width), F32),
        in_specs=vmem(5),
        out_specs=vmem(1)[0],
        compiler_params=big,
        name="rims",
        cost_estimate=pl.CostEstimate(flops=2 * width * slots * width * 40, bytes_accessed=4 * 1024 * 1024, transcendentals=0),
    )(sums, from_below, from_above, w_src, w_dst)
    src_grad, dst_grad, out_grad = pl.pallas_call(
        total_kernel,
        out_shape=(
            jax.ShapeDtypeStruct((part, width), F32),
            jax.ShapeDtypeStruct((part, width), F32),
            jax.ShapeDtypeStruct((part, entries), F32),
        ),
        in_specs=vmem(len(terms) + len(terms_o)),
        out_specs=tuple(vmem(3)),
        compiler_params=big,
        name="totals",
    )(*terms, *terms_o)
    return (feature_grad, src_grad, dst_grad, out_grad)


def solution(mesh):
    placed = (
        P(("groups", "space"), None),
        P(),
        P(),
        P(),
        P("space", "groups", None, None),
        P(("groups", "space")),
        P(("groups", "space")),
        P(("groups", "space")),
    )
    return jax.shard_map(
        on_device,
        mesh=mesh,
        in_specs=placed,
        out_specs=(
            P(("groups", "space"), None),
            P(("groups", "space"), None),
            P(("groups", "space"), None),
            P(("groups", "space"), None),
        ),
        check_vma=False,
    )
```

```python
import functools

import jax
import jax.numpy as jnp
from jax import lax
from jax.experimental import pallas as pl
from jax.experimental.pallas import tpu as pltpu
from jax.sharding import PartitionSpec as P

F32 = jnp.float32
BF16 = jnp.bfloat16
LANES = 128
PACK = 16
NN = (((1,), (0,)), ((), ()))
NT = (((1,), (1,)), ((), ()))


def mm(left, right, dims=NN):
    return lax.dot_general(left, right, dims, preferred_element_type=F32)


def halves(x):
    high = x.astype(BF16)
    return high, (x - high.astype(F32)).astype(BF16)


def round_up(x, to):
    return -(-x // to) * to


def vmem(count):
    return [pl.BlockSpec(memory_space=pltpu.VMEM)] * count


def pack_kernel(rows, half, linked, me_ref, feats_ref, g_ref, even_ref, odd_ref, low_ref, top_ref, here_ref, sems, rim_sems):
    entries, slabs, cap = g_ref.shape
    mols = feats_ref.shape[0]
    reach = low_ref.shape[0]
    groups = LANES // half
    blocks = rows // PACK
    count = sems.shape[0]
    stages = []
    for stage in range(count):
        begin, end = stage * blocks // count, (stage + 1) * blocks // count
        copies = []
        for group in range(groups):
            first = min(entries, group * rows + begin * PACK)
            last = min(entries, group * rows + end * PACK)
            if first < last:
                copies.append(
                    pltpu.make_async_copy(g_ref.at[first:last], here_ref.at[first:last], sems.at[stage, group])
                )
        stages.append((begin, end, copies))
        for copy in copies:
            copy.start()
    rims = [
        pltpu.make_async_copy(feats_ref.at[:reach], low_ref, rim_sems.at[0]),
        pltpu.make_async_copy(feats_ref.at[mols - reach :], top_ref, rim_sems.at[1]),
    ]
    for copy in rims:
        copy.start()
    size = PACK * slabs
    to = lax.broadcasted_iota(jnp.int32, (size, size), 0)
    source = lax.broadcasted_iota(jnp.int32, (size, size), 1)
    slab = to // PACK
    if linked:
        slab = slab ^ me_ref[0]
    perm = jnp.where((to % PACK) * slabs + slab == source, 1.0, 0.0).astype(BF16)

    def lanes_of(block):
        early = []
        for group in range(groups):
            first = group * rows + block * PACK
            valid = max(0, min(PACK, entries - first))
            tiles = []
            if valid:
                tiles.append(here_ref[first : first + valid])
            if valid < PACK:
                tiles.append(jnp.zeros((PACK - valid, slabs, cap), BF16))
            tile = tiles[0] if len(tiles) == 1 else jnp.concatenate(tiles, axis=0)
            early.append(tile.reshape(size, cap)[:, :half])
        return early

    for begin, end, copies in stages:
        for copy in copies:
            copy.wait()
        for block in range(begin, end, 2):
            together = range(block, min(block + 2, end))
            lanes = [piece for one in together for piece in lanes_of(one)]
            moved = mm(perm, jnp.concatenate(lanes, axis=1)).astype(BF16)
            for index, one in enumerate(together):
                chunk = moved[:, index * LANES : (index + 1) * LANES].reshape(slabs // 2, 2, PACK, LANES)
                here = pl.ds(one * PACK, PACK)
                even_ref[:, here, :] = chunk[:, 0]
                odd_ref[:, here, :] = chunk[:, 1]
    for copy in rims:
        copy.wait()


def join_kernel(even_ref, other_ref, *message_refs):
    for k, message_ref in enumerate(message_refs):
        message_ref[0] = even_ref[k]
        message_ref[1] = other_ref[k]


def unpack(half, refs, g_ref):
    groups = LANES // half
    rows = g_ref.shape[0] // groups
    chunks = [(ref, index) for ref in refs for index in range(ref.shape[0])]
    tiles = len(chunks) // groups
    for tile in range(tiles):
        here = [ref[index] for ref, index in chunks[tile * groups : (tile + 1) * groups]]
        for group in range(groups):
            lanes = slice(group * half, (group + 1) * half)
            g_ref[group * rows : (group + 1) * rows, tile * LANES : (tile + 1) * LANES] = jnp.concatenate(
                [chunk[:, lanes] for chunk in here], axis=1
            )
    return tiles * LANES


def slot_rows(ref, me, half, linked, near, far):
    per = LANES // half

    def rows_of(ids):
        rows = []
        for tile in range(len(ids) // per):
            pieces = [ref[pl.ds(me ^ i if linked else i, 1), :] for i in ids[tile * per : (tile + 1) * per]]
            rows.append(jnp.concatenate([piece[:, :half] for piece in pieces], axis=1))
        return rows

    own = ref[pl.ds(me, 1), :][:, half:]
    own = jnp.concatenate([own, jnp.full((1, LANES - half), -1, jnp.int32)], axis=1)
    return rows_of(near) + [own] + rows_of(far)


def edge_kernel(
    half, linked, near, far, me_ref, feats_hbm, w_src_hbm, w_dst_hbm, w_out_hbm, below_ref, above_ref, src_ref, dst_ref,
    live_ref, onehot_hbm, slope_hbm, ext_hbm, near_hidden_ref, far_hidden_ref, w_wide_ref,
    onehot_ref, slope_ref, ext_ref, w_rows_ref, feats_ref, w_src_ref, w_dst_ref, w_out_ref, sems, in_sems,
):
    inputs = [
        pltpu.make_async_copy(hbm, ref, in_sems.at[index])
        for index, (hbm, ref) in enumerate(
            ((feats_hbm, feats_ref), (w_src_hbm, w_src_ref), (w_dst_hbm, w_dst_ref), (w_out_hbm, w_out_ref))
        )
    ]
    for copy in inputs:
        copy.start()
    me = me_ref[0]
    mols = feats_ref.shape[0]
    reach = below_ref.shape[0]
    wide = mols + 2 * reach
    slots = slope_ref.shape[1]
    entries = w_out_ref.shape[0]
    near_slots = near_hidden_ref.shape[1]
    copies = []

    def send(source, target):
        copy = pltpu.make_async_copy(source, target, sems.at[len(copies)])
        copy.start()
        copies.append(copy)

    mol_src = lax.broadcasted_iota(jnp.int32, (mols, LANES), 0)
    mol_dst = lax.broadcasted_iota(jnp.int32, (wide, LANES), 0)
    lists = [slot_rows(ref, me, half, linked, near, far) for ref in (src_ref, dst_ref, live_ref)]
    for tile, (src, dst, live) in enumerate(zip(*lists)):
        src = jnp.where(live > 0, src, -1)
        moved = jnp.where(dst < reach, dst + mols, jnp.where(dst < reach + mols, dst - reach, dst))
        dst = jnp.where(live > 0, moved, -1)
        one_src = jnp.where(mol_src == src, 1.0, 0.0).astype(BF16)
        one_dst = jnp.where(mol_dst == dst, 1.0, 0.0).astype(BF16)
        here = pl.ds(tile * LANES, LANES)
        onehot_ref[:, here] = jnp.concatenate([one_src, one_dst], axis=0)
    for copy in inputs[:3]:
        copy.wait()
    feats = feats_ref[...]
    ext = jnp.concatenate([feats, below_ref[...], above_ref[...]], axis=0)
    ext_ref[...] = ext.T
    send(ext_ref, ext_hbm)
    proj_src = mm(feats, w_src_ref[...])
    proj_dst = mm(ext, w_dst_ref[...])
    proj = jnp.concatenate([proj_src, proj_dst], axis=0).T
    high, low = halves(proj)
    for first, last in slot_tiles(near_slots) + [(near_slots + f, near_slots + l) for f, l in slot_tiles(slots - near_slots)]:
        here = pl.ds(first, last - first)
        send(onehot_ref.at[:, here], onehot_hbm.at[:, here])
        onehot = onehot_ref[:, here]
        pre = mm(high, onehot) + mm(low, onehot)
        sigma = 1.0 / (1.0 + jnp.exp(-pre))
        hidden = (pre * sigma).astype(BF16)
        if first < near_slots:
            near_hidden_ref[:, here] = hidden
        else:
            far_hidden_ref[:, pl.ds(first - near_slots, last - first)] = hidden
        slope_ref[:, here] = sigma * (1.0 + pre * (1.0 - sigma))
        send(slope_ref.at[:, here], slope_hbm.at[:, here])
    inputs[3].wait()
    whole = entries // LANES * LANES
    w_rows_ref[whole:] = jnp.zeros((w_rows_ref.shape[0] - whole, w_rows_ref.shape[1]), BF16)
    w_rows_ref[:whole] = w_out_ref[:whole]
    w_rows_ref[whole:entries] = w_out_ref[whole:]
    w_wide_ref[...] = w_rows_ref[...].T
    for copy in copies:
        copy.wait()


def halve(terms, odd, place, keep_ref, send_ref, first):
    count, rows, _ = keep_ref.shape
    width = terms.shape[-1]
    lanes = slice(first, first + width)
    inner = 1 << place
    pairs = terms.reshape(count // inner, 2, inner, rows, width)
    even_part = pairs[:, 0].reshape(count, rows, width)
    odd_part = pairs[:, 1].reshape(count, rows, width)
    keep_ref[:, :, lanes] = jnp.where(odd > 0, odd_part, even_part)
    send_ref[:, :, lanes] = jnp.where(odd > 0, even_part, odd_part).astype(BF16)


def fold_kernel(bit, place, me_ref, keep_ref, came_ref, next_ref, send_ref):
    odd = (me_ref[0] >> bit) % 2
    halve(keep_ref[...] + came_ref[...].astype(F32), odd, place, next_ref, send_ref, 0)


def close_kernel(keep_ref, came_ref, send_ref):
    send_ref[...] = (keep_ref[...] + came_ref[...].astype(F32)).astype(BF16)


def slot_tiles(slots):
    step = 2 * LANES
    return [(first, min(first + step, slots)) for first in range(0, slots, step)]


def start_tiles(slots, offset, slope_hbm, onehot_hbm, slope_ref, onehot_ref, sems):
    tiles = []
    for tile, (first, last) in enumerate(slot_tiles(slots)):
        there, here = pl.ds(offset + first, last - first), pl.ds(first, last - first)
        copies = [
            pltpu.make_async_copy(slope_hbm.at[:, there], slope_ref.at[:, here], sems.at[tile, 0]),
            pltpu.make_async_copy(onehot_hbm.at[:, there], onehot_ref.at[:, here], sems.at[tile, 1]),
        ]
        for copy in copies:
            copy.start()
        tiles.append((slice(first, last), copies))
    return tiles


def sum_edges(tiles, w_out_ref, g_ref, slope_ref, onehot_ref):
    sums = None
    for lanes, copies in tiles:
        dh = mm(w_out_ref[...], g_ref[:, lanes])
        for copy in copies:
            copy.wait()
        dpre = (dh * slope_ref[:, lanes]).astype(BF16)
        term = mm(onehot_ref[:, lanes], dpre, NT)
        sums = term if sums is None else sums + term
    return sums


def near_kernel(half, own_ref, w_out_ref, hidden_ref, slope_hbm, onehot_hbm, *rest):
    *came_refs, sums_hbm, outer_hbm, g_ref, slope_ref, onehot_ref, sums_ref, outer_ref, sems, out_sems = rest
    slots = g_ref.shape[1]
    tiles = start_tiles(slots, 0, slope_hbm, onehot_hbm, slope_ref, onehot_ref, sems)
    filled = unpack(half, came_refs, g_ref)
    g_ref[:, filled:] = own_ref[...]
    outer_ref[...] = mm(hidden_ref[...], g_ref[...], NT)
    outer_copy = pltpu.make_async_copy(outer_ref, outer_hbm, out_sems.at[0])
    outer_copy.start()
    sums_ref[...] = sum_edges(tiles, w_out_ref, g_ref, slope_ref, onehot_ref)
    sums_copy = pltpu.make_async_copy(sums_ref, sums_hbm, out_sems.at[1])
    sums_copy.start()
    outer_copy.wait()
    sums_copy.wait()


def grad_kernel(half, factor, me_ref, w_out_ref, slope_hbm, onehot_hbm, ext_hbm, near_hbm, *rest):
    (
        *came_refs, keep_ref, send_ref, sums_ref, lower_ref, upper_ref, g_ref,
        slope_ref, onehot_ref, ext_ref, near_ref, tile_sems, sems,
    ) = rest
    odd = me_ref[0] % 2
    width = w_out_ref.shape[0]
    slots = g_ref.shape[1]
    inside = sums_ref.shape[0]
    mols = inside // 2
    reach = lower_ref.shape[0]
    tiles = start_tiles(slots, slope_hbm.shape[1] - slots, slope_hbm, onehot_hbm, slope_ref, onehot_ref, tile_sems)
    whole = [
        pltpu.make_async_copy(near_hbm, near_ref, sems.at[0]),
        pltpu.make_async_copy(ext_hbm, ext_ref, sems.at[1]),
    ]
    for copy in whole:
        copy.start()
    unpack(half, came_refs, g_ref)
    sums = sum_edges(tiles, w_out_ref, g_ref, slope_ref, onehot_ref)
    for copy in whole:
        copy.wait()
    sums = sums + near_ref[...]
    lower_ref[...] = sums[inside : inside + reach].astype(BF16)
    upper_ref[...] = sums[inside + reach :].astype(BF16)
    sums_ref[...] = sums[:inside]
    high, low = halves(sums)
    feats = ext_ref[:, :mols]
    rim = ext_ref[:, mols:]
    halve(factor * (mm(feats, high[:mols]) + mm(feats, low[:mols])), odd, 0, keep_ref, send_ref, 0)
    rim_term = mm(jnp.concatenate([rim, rim], axis=1), jnp.concatenate([high[inside:], low[inside:]], axis=0))
    dst_term = mm(feats, high[mols:inside]) + mm(feats, low[mols:inside]) + rim_term
    halve(factor * dst_term, odd, 0, keep_ref, send_ref, width)


def outer_kernel(factor, me_ref, hidden_ref, g_ref, near_hbm, keep_ref, send_ref, near_ref, sem):
    copy = pltpu.make_async_copy(near_hbm, near_ref, sem)
    copy.start()
    term = mm(hidden_ref[...], g_ref[...], NT)
    copy.wait()
    term = factor * (term + near_ref[...])
    padding = keep_ref.shape[2] - term.shape[1]
    if padding > 0:
        term = jnp.concatenate([term, jnp.zeros((term.shape[0], padding), F32)], axis=1)
    halve(term, me_ref[0] % 2, 0, keep_ref, send_ref, 0)


def rim_kernel(sums_ref, from_below_ref, from_above_ref, w_src_ref, w_dst_ref, out_ref):
    mols = out_ref.shape[0]
    reach = from_below_ref.shape[0]
    src = sums_ref[:mols]
    dst = sums_ref[mols:]
    dst = jnp.concatenate(
        [
            dst[:reach] + from_below_ref[...].astype(F32),
            dst[reach : mols - reach],
            dst[mols - reach :] + from_above_ref[...].astype(F32),
        ],
        axis=0,
    )
    w_src = w_src_ref[...]
    w_dst = w_dst_ref[...]
    src_high, src_low = halves(src)
    dst_high, dst_low = halves(dst)
    out_ref[...] = mm(src_high, w_src, NT) + mm(src_low, w_src, NT) + mm(dst_high, w_dst, NT) + mm(dst_low, w_dst, NT)


def total_kernel(*refs):
    *refs, src_ref, dst_ref, out_ref = refs
    count = len(refs) // 2
    width = src_ref.shape[1]
    totals = []
    for piece in (refs[:count], refs[count:]):
        terms = [ref[slab].astype(F32) for ref in piece for slab in range(ref.shape[0])]
        totals.append(functools.reduce(jnp.add, terms))
    sides, outer = totals
    src_ref[...] = sides[:, :width]
    dst_ref[...] = sides[:, width:]
    out_ref[...] = outer[:, : out_ref.shape[1]]


def in_hbm(x):
    return pltpu.with_memory_space_constraint(x, pltpu.HBM)


def swap(block, bit, slabs):
    return lax.ppermute(block, "space", [(i, i ^ (1 << bit)) for i in range(slabs)])


def on_device(mol_feats, w_src, w_dst, w_out, grad_blocks, edge_src, edge_dst, edge_live):
    slabs = lax.axis_size("space")
    mols, width = mol_feats.shape
    entries = w_out.shape[1]
    cap = grad_blocks.shape[2]
    half = cap // 2
    reach = mols // 4
    groups = LANES // half
    slots = (slabs // groups + 1) * LANES
    bits = slabs.bit_length() - 1
    if 3 <= bits <= 4:
        late_bits = tuple((bit, 0) for bit in range(3, bits))
        paths = (((0, 0), (1, 0), (2, 0)) + late_bits, ((0, 0), (2, 1), (1, 0)) + late_bits)
    else:
        paths = (tuple((bit, 0) for bit in range(min(bits, 2))),) * 2
    rest = slabs >> len(paths[0])
    part = width // slabs
    factor = float(edge_src.shape[0] * slabs) ** (-0.5)
    me = lax.axis_index("space").astype(jnp.int32).reshape(1)
    smem = pl.BlockSpec(memory_space=pltpu.SMEM)
    hbm = pl.BlockSpec(memory_space=pltpu.HBM)
    big = pltpu.CompilerParams(vmem_limit_bytes=24 * 1024 * 1024)
    up = [(i, (i + 1) % slabs) for i in range(slabs)]
    down = [((i + 1) % slabs, i) for i in range(slabs)]

    rows = round_up(pl.cdiv(entries, groups), PACK)
    stages = 4
    linked = slabs <= 16
    even, odd, low, top = pl.pallas_call(
        functools.partial(pack_kernel, rows, half, linked),
        out_shape=(
            jax.ShapeDtypeStruct((slabs // 2, rows, LANES), BF16),
            jax.ShapeDtypeStruct((slabs // 2, rows, LANES), BF16),
            jax.ShapeDtypeStruct((reach, width), BF16),
            jax.ShapeDtypeStruct((reach, width), BF16),
        ),
        in_specs=[smem, hbm, hbm],
        out_specs=tuple(vmem(4)),
        scratch_shapes=[
            pltpu.VMEM((entries, slabs, cap), BF16),
            pltpu.SemaphoreType.DMA((stages, groups)),
            pltpu.SemaphoreType.DMA((2,)),
        ],
        compiler_params=big,
        name="pack",
    )(me, in_hbm(mol_feats), in_hbm(jnp.transpose(grad_blocks[0], (2, 0, 1))))
    below = lax.ppermute(top, "space", up)
    above = lax.ppermute(low, "space", down)
    late = lax.dynamic_index_in_dim(grad_blocks[0], me[0], 0, keepdims=False)[half:]
    own = jnp.pad(late.T, ((0, groups * rows - entries), (0, LANES - half)))
    if linked:
        other = swap(odd, 0, slabs)
        other, below, above, own = lax.optimization_barrier((other, below, above, own))
        messages = pl.pallas_call(
            join_kernel,
            out_shape=(jax.ShapeDtypeStruct((2, rows, LANES), BF16),) * (slabs // 2),
            in_specs=vmem(2),
            out_specs=tuple(vmem(slabs // 2)),
            compiler_params=big,
            name="join",
        )(even, other)
        quarter = slabs // 4
        came = {0: messages[0]}
        for k in range(1, 2 * quarter):
            message = messages[k]
            if k == quarter - 1:
                message = lax.optimization_barrier((message, came[1], came[2]))[0]
            came[k] = lax.ppermute(message, "space", [(i, i ^ (2 * k)) for i in range(slabs)])
        near = tuple(range(2 * quarter))
        far = tuple(range(2 * quarter, slabs))
        came_near = [came[k] for k in range(quarter)]
        came_far = [came[k] for k in range(quarter, 2 * quarter)]
    else:
        packed = jnp.stack([even, odd], axis=1).reshape(slabs, rows, LANES)
        near, far = (), tuple(range(slabs))
        came_near = []
        came_far = [lax.all_to_all(packed, "space", split_axis=0, concat_axis=0, tiled=True)]
    far_slots = len(far) * half
    near_slots = slots - far_slots

    wide = mols + 2 * reach
    entries_wide = groups * rows
    pieces = len(slot_tiles(near_slots)) + len(slot_tiles(far_slots))
    onehot, slope, ext, near_hidden, far_hidden, w_out_wide = pl.pallas_call(
        functools.partial(edge_kernel, half, linked, near, far),
        out_shape=(
            pltpu.HBM((mols + wide, slots), BF16),
            pltpu.HBM((width, slots), F32),
            pltpu.HBM((width, wide), BF16),
            jax.ShapeDtypeStruct((width, near_slots), BF16),
            jax.ShapeDtypeStruct((width, far_slots), BF16),
            jax.ShapeDtypeStruct((width, entries_wide), BF16),
        ),
        in_specs=[smem] + [hbm] * 4 + vmem(5),
        out_specs=(hbm,) * 3 + tuple(vmem(3)),
        scratch_shapes=[
            pltpu.VMEM((mols + wide, slots), BF16),
            pltpu.VMEM((width, slots), F32),
            pltpu.VMEM((width, wide), BF16),
            pltpu.VMEM((entries_wide, width), BF16),
            pltpu.VMEM((mols, width), BF16),
            pltpu.VMEM((width, width), BF16),
            pltpu.VMEM((width, width), BF16),
            pltpu.VMEM((entries, width), BF16),
            pltpu.SemaphoreType.DMA((2 * pieces + 1,)),
            pltpu.SemaphoreType.DMA((4,)),
        ],
        compiler_params=big,
        name="edges",
        cost_estimate=pl.CostEstimate(
            flops=40 * width * slots * 2 * (2 * mols + 2 * reach), bytes_accessed=8 * 1024 * 1024,
            transcendentals=width * slots,
        ),
    )(
        me, in_hbm(mol_feats), in_hbm(w_src), in_hbm(w_dst), in_hbm(w_out.T), below, above,
        edge_src.reshape(slabs, cap), edge_dst.reshape(slabs, cap), edge_live.reshape(slabs, cap),
    )
    onehot, slope, ext = in_hbm(onehot), in_hbm(slope), in_hbm(ext)

    def chunks(count, lanes, dtype):
        return jax.ShapeDtypeStruct((count, part, lanes), dtype)

    near_sums, near_outer = pl.pallas_call(
        functools.partial(near_kernel, half),
        out_shape=(
            pltpu.HBM((mols + wide, width), F32),
            pltpu.HBM((width, entries_wide), F32),
        ),
        in_specs=vmem(3) + [hbm] * 2 + vmem(len(came_near)),
        out_specs=(hbm, hbm),
        scratch_shapes=[
            pltpu.VMEM((entries_wide, near_slots), BF16),
            pltpu.VMEM((width, near_slots), F32),
            pltpu.VMEM((mols + wide, near_slots), BF16),
            pltpu.VMEM((mols + wide, width), F32),
            pltpu.VMEM((width, entries_wide), F32),
            pltpu.SemaphoreType.DMA((len(slot_tiles(near_slots)), 2)),
            pltpu.SemaphoreType.DMA((2,)),
        ],
        compiler_params=big,
        name="near",
        cost_estimate=pl.CostEstimate(
            flops=40 * width * near_slots * entries_wide, bytes_accessed=6 * 1024 * 1024, transcendentals=0
        ),
    )(own, w_out_wide, near_hidden, slope, onehot, *came_near)
    near_sums, near_outer = in_hbm(near_sums), in_hbm(near_outer)
    keep, send, sums, lower, upper, g = pl.pallas_call(
        functools.partial(grad_kernel, half, factor),
        out_shape=(
            chunks(slabs // 2, 2 * width, F32),
            chunks(slabs // 2, 2 * width, BF16),
            jax.ShapeDtypeStruct((2 * mols, width), F32),
            jax.ShapeDtypeStruct((reach, width), BF16),
            jax.ShapeDtypeStruct((reach, width), BF16),
            jax.ShapeDtypeStruct((entries_wide, far_slots), BF16),
        ),
        in_specs=[smem] + vmem(1) + [hbm] * 4 + vmem(len(came_far)),
        out_specs=tuple(vmem(6)),
        scratch_shapes=[
            pltpu.VMEM((width, far_slots), F32),
            pltpu.VMEM((mols + wide, far_slots), BF16),
            pltpu.VMEM((width, wide), BF16),
            pltpu.VMEM((mols + wide, width), F32),
            pltpu.SemaphoreType.DMA((len(slot_tiles(far_slots)), 2)),
            pltpu.SemaphoreType.DMA((2,)),
        ],
        compiler_params=big,
        name="grads",
    )(me, w_out_wide, slope, onehot, ext, near_sums, *came_far)
    lanes = round_up(entries_wide, LANES)
    keep_o, send_o = pl.pallas_call(
        functools.partial(outer_kernel, factor),
        out_shape=(chunks(slabs // 2, lanes, F32), chunks(slabs // 2, lanes, BF16)),
        in_specs=[smem] + vmem(2) + [hbm],
        out_specs=tuple(vmem(2)),
        scratch_shapes=[pltpu.VMEM((width, entries_wide), F32), pltpu.SemaphoreType.DMA(())],
        compiler_params=big,
        name="outer",
        cost_estimate=pl.CostEstimate(
            flops=40 * width * slots * entries_wide, bytes_accessed=4 * 1024 * 1024, transcendentals=0
        ),
    )(me, far_hidden, g, near_outer)

    def fold(bit, place, keep, crossed):
        shape = (keep.shape[0] // 2, keep.shape[2])
        return pl.pallas_call(
            functools.partial(fold_kernel, bit, place),
            out_shape=(chunks(*shape, F32), chunks(*shape, BF16)),
            in_specs=[smem] + vmem(2),
            out_specs=tuple(vmem(2)),
            compiler_params=big,
            name="fold",
        )(me, keep, crossed)

    def close(keep, crossed):
        if rest == 1:
            return [keep, crossed]
        sends = pl.pallas_call(
            close_kernel,
            out_shape=chunks(rest, keep.shape[2], BF16),
            in_specs=vmem(2),
            out_specs=vmem(1)[0],
            compiler_params=big,
            name="close",
        )(keep, crossed)
        same = [[low + rank * (slabs // rest) for rank in range(rest)] for low in range(slabs // rest)]
        return [
            lax.all_to_all(sends, "space", split_axis=0, concat_axis=0, tiled=True, axis_index_groups=same)
        ]

    from_above = lax.ppermute(lower, "space", down)
    from_below = lax.ppermute(upper, "space", up)
    crossed = swap(send, 0, slabs)
    crossed_o = swap(send_o, 0, slabs)
    for (bit, place), (bit_o, place_o) in zip(paths[0][1:], paths[1][1:]):
        if bit == 2:
            keep, crossed, from_above, from_below = lax.optimization_barrier((keep, crossed, from_above, from_below))
        keep, send = fold(bit, place, keep, crossed)
        crossed = swap(send, bit, slabs)
        keep_o, crossed_o, _ = lax.optimization_barrier((keep_o, crossed_o, send))
        keep_o, send_o = fold(bit_o, place_o, keep_o, crossed_o)
        crossed_o = swap(send_o, bit_o, slabs)
    terms = close(keep, crossed)
    terms_o = close(keep_o, crossed_o)
    feature_grad = pl.pallas_call(
        rim_kernel,
        out_shape=jax.ShapeDtypeStruct((mols, width), F32),
        in_specs=vmem(5),
        out_specs=vmem(1)[0],
        compiler_params=big,
        name="rims",
        cost_estimate=pl.CostEstimate(flops=2 * width * slots * width * 40, bytes_accessed=4 * 1024 * 1024, transcendentals=0),
    )(sums, from_below, from_above, w_src, w_dst)
    src_grad, dst_grad, out_grad = pl.pallas_call(
        total_kernel,
        out_shape=(
            jax.ShapeDtypeStruct((part, width), F32),
            jax.ShapeDtypeStruct((part, width), F32),
            jax.ShapeDtypeStruct((part, entries), F32),
        ),
        in_specs=vmem(len(terms) + len(terms_o)),
        out_specs=tuple(vmem(3)),
        compiler_params=big,
        name="totals",
    )(*terms, *terms_o)
    return (feature_grad, src_grad, dst_grad, out_grad)


def solution(mesh):
    placed = (
        P(("groups", "space"), None),
        P(),
        P(),
        P(),
        P("space", "groups", None, None),
        P(("groups", "space")),
        P(("groups", "space")),
        P(("groups", "space")),
    )
    return jax.shard_map(
        on_device,
        mesh=mesh,
        in_specs=placed,
        out_specs=(
            P(("groups", "space"), None),
            P(("groups", "space"), None),
            P(("groups", "space"), None),
            P(("groups", "space"), None),
        ),
        check_vma=False,
    )
```

```python
import functools

import jax
import jax.numpy as jnp
from jax import lax
from jax.experimental import pallas as pl
from jax.experimental.pallas import tpu as pltpu
from jax.sharding import PartitionSpec as P

F32 = jnp.float32
BF16 = jnp.bfloat16
LANES = 128
PACK = 16
NN = (((1,), (0,)), ((), ()))
NT = (((1,), (1,)), ((), ()))


def mm(left, right, dims=NN):
    return lax.dot_general(left, right, dims, preferred_element_type=F32)


def halves(x):
    high = x.astype(BF16)
    return high, (x - high.astype(F32)).astype(BF16)


def round_up(x, to):
    return -(-x // to) * to


def vmem(count):
    return [pl.BlockSpec(memory_space=pltpu.VMEM)] * count


def pack_kernel(rows, half, linked, me_ref, feats_ref, g_ref, even_ref, odd_ref, low_ref, top_ref, here_ref, sems, rim_sems):
    entries, slabs, cap = g_ref.shape
    mols = feats_ref.shape[0]
    reach = low_ref.shape[0]
    groups = LANES // half
    blocks = rows // PACK
    count = sems.shape[0]
    stages = []
    for stage in range(count):
        begin, end = stage * blocks // count, (stage + 1) * blocks // count
        copies = []
        for group in range(groups):
            first = min(entries, group * rows + begin * PACK)
            last = min(entries, group * rows + end * PACK)
            if first < last:
                copies.append(
                    pltpu.make_async_copy(g_ref.at[first:last], here_ref.at[first:last], sems.at[stage, group])
                )
        stages.append((begin, end, copies))
        for copy in copies:
            copy.start()
    rims = [
        pltpu.make_async_copy(feats_ref.at[:reach], low_ref, rim_sems.at[0]),
        pltpu.make_async_copy(feats_ref.at[mols - reach :], top_ref, rim_sems.at[1]),
    ]
    for copy in rims:
        copy.start()
    size = PACK * slabs
    to = lax.broadcasted_iota(jnp.int32, (size, size), 0)
    source = lax.broadcasted_iota(jnp.int32, (size, size), 1)
    slab = to // PACK
    if linked:
        slab = slab ^ me_ref[0]
    perm = jnp.where((to % PACK) * slabs + slab == source, 1.0, 0.0).astype(BF16)

    def lanes_of(block):
        early = []
        for group in range(groups):
            first = group * rows + block * PACK
            valid = max(0, min(PACK, entries - first))
            tiles = []
            if valid:
                tiles.append(here_ref[first : first + valid])
            if valid < PACK:
                tiles.append(jnp.zeros((PACK - valid, slabs, cap), BF16))
            tile = tiles[0] if len(tiles) == 1 else jnp.concatenate(tiles, axis=0)
            early.append(tile.reshape(size, cap)[:, :half])
        return early

    for begin, end, copies in stages:
        for copy in copies:
            copy.wait()
        for block in range(begin, end, 2):
            together = range(block, min(block + 2, end))
            lanes = [piece for one in together for piece in lanes_of(one)]
            moved = mm(perm, jnp.concatenate(lanes, axis=1)).astype(BF16)
            for index, one in enumerate(together):
                chunk = moved[:, index * LANES : (index + 1) * LANES].reshape(slabs // 2, 2, PACK, LANES)
                here = pl.ds(one * PACK, PACK)
                even_ref[:, here, :] = chunk[:, 0]
                odd_ref[:, here, :] = chunk[:, 1]
    for copy in rims:
        copy.wait()


def join_kernel(even_ref, other_ref, *message_refs):
    for k, message_ref in enumerate(message_refs):
        message_ref[0] = even_ref[k]
        message_ref[1] = other_ref[k]


def unpack(half, refs, g_ref):
    groups = LANES // half
    rows = g_ref.shape[0] // groups
    chunks = [(ref, index) for ref in refs for index in range(ref.shape[0])]
    tiles = len(chunks) // groups
    for tile in range(tiles):
        here = [ref[index] for ref, index in chunks[tile * groups : (tile + 1) * groups]]
        for group in range(groups):
            lanes = slice(group * half, (group + 1) * half)
            g_ref[group * rows : (group + 1) * rows, tile * LANES : (tile + 1) * LANES] = jnp.concatenate(
                [chunk[:, lanes] for chunk in here], axis=1
            )
    return tiles * LANES


def slot_rows(ref, me, half, linked, near, far):
    per = LANES // half

    def rows_of(ids):
        rows = []
        for tile in range(len(ids) // per):
            pieces = [ref[pl.ds(me ^ i if linked else i, 1), :] for i in ids[tile * per : (tile + 1) * per]]
            rows.append(jnp.concatenate([piece[:, :half] for piece in pieces], axis=1))
        return rows

    own = ref[pl.ds(me, 1), :][:, half:]
    own = jnp.concatenate([own, jnp.full((1, LANES - half), -1, jnp.int32)], axis=1)
    return rows_of(near) + [own] + rows_of(far)


def edge_kernel(
    half, linked, near, far, me_ref, feats_hbm, w_src_hbm, w_dst_hbm, w_out_hbm, below_ref, above_ref, src_ref, dst_ref,
    live_ref, onehot_hbm, slope_hbm, ext_hbm, near_hidden_ref, far_hidden_ref, w_wide_ref,
    onehot_ref, slope_ref, ext_ref, w_rows_ref, feats_ref, w_src_ref, w_dst_ref, w_out_ref, sems, in_sems,
):
    inputs = [
        pltpu.make_async_copy(hbm, ref, in_sems.at[index])
        for index, (hbm, ref) in enumerate(
            ((feats_hbm, feats_ref), (w_src_hbm, w_src_ref), (w_dst_hbm, w_dst_ref), (w_out_hbm, w_out_ref))
        )
    ]
    for copy in inputs:
        copy.start()
    me = me_ref[0]
    mols = feats_ref.shape[0]
    reach = below_ref.shape[0]
    wide = mols + 2 * reach
    slots = slope_ref.shape[1]
    entries = w_out_ref.shape[0]
    near_slots = near_hidden_ref.shape[1]
    copies = []

    def send(source, target):
        copy = pltpu.make_async_copy(source, target, sems.at[len(copies)])
        copy.start()
        copies.append(copy)

    mol_src = lax.broadcasted_iota(jnp.int32, (mols, LANES), 0)
    mol_dst = lax.broadcasted_iota(jnp.int32, (wide, LANES), 0)
    lists = [slot_rows(ref, me, half, linked, near, far) for ref in (src_ref, dst_ref, live_ref)]
    for tile, (src, dst, live) in enumerate(zip(*lists)):
        src = jnp.where(live > 0, src, -1)
        moved = jnp.where(dst < reach, dst + mols, jnp.where(dst < reach + mols, dst - reach, dst))
        dst = jnp.where(live > 0, moved, -1)
        one_src = jnp.where(mol_src == src, 1.0, 0.0).astype(BF16)
        one_dst = jnp.where(mol_dst == dst, 1.0, 0.0).astype(BF16)
        here = pl.ds(tile * LANES, LANES)
        onehot_ref[:, here] = jnp.concatenate([one_src, one_dst], axis=0)
    for copy in inputs[:3]:
        copy.wait()
    feats = feats_ref[...]
    ext = jnp.concatenate([feats, below_ref[...], above_ref[...]], axis=0)
    ext_ref[...] = ext.T
    send(ext_ref, ext_hbm)
    proj_src = mm(feats, w_src_ref[...])
    proj_dst = mm(ext, w_dst_ref[...])
    proj = jnp.concatenate([proj_src, proj_dst], axis=0).T
    high, low = halves(proj)
    for first, last in slot_tiles(near_slots) + [(near_slots + f, near_slots + l) for f, l in slot_tiles(slots - near_slots)]:
        here = pl.ds(first, last - first)
        send(onehot_ref.at[:, here], onehot_hbm.at[:, here])
        onehot = onehot_ref[:, here]
        pre = mm(high, onehot) + mm(low, onehot)
        sigma = 1.0 / (1.0 + jnp.exp(-pre))
        hidden = (pre * sigma).astype(BF16)
        if first < near_slots:
            near_hidden_ref[:, here] = hidden
        else:
            far_hidden_ref[:, pl.ds(first - near_slots, last - first)] = hidden
        slope_ref[:, here] = sigma * (1.0 + pre * (1.0 - sigma))
        send(slope_ref.at[:, here], slope_hbm.at[:, here])
    inputs[3].wait()
    whole = entries // LANES * LANES
    w_rows_ref[whole:] = jnp.zeros((w_rows_ref.shape[0] - whole, w_rows_ref.shape[1]), BF16)
    w_rows_ref[:whole] = w_out_ref[:whole]
    w_rows_ref[whole:entries] = w_out_ref[whole:]
    w_wide_ref[...] = w_rows_ref[...].T
    for copy in copies:
        copy.wait()


def halve(terms, odd, place, keep_ref, send_ref, first):
    count, rows, _ = keep_ref.shape
    width = terms.shape[-1]
    lanes = slice(first, first + width)
    inner = 1 << place
    pairs = terms.reshape(count // inner, 2, inner, rows, width)
    even_part = pairs[:, 0].reshape(count, rows, width)
    odd_part = pairs[:, 1].reshape(count, rows, width)
    keep_ref[:, :, lanes] = jnp.where(odd > 0, odd_part, even_part)
    send_ref[:, :, lanes] = jnp.where(odd > 0, even_part, odd_part).astype(BF16)


def fold_kernel(bit, place, me_ref, keep_ref, came_ref, next_ref, send_ref):
    odd = (me_ref[0] >> bit) % 2
    halve(keep_ref[...] + came_ref[...].astype(F32), odd, place, next_ref, send_ref, 0)


def close_kernel(keep_ref, came_ref, send_ref):
    send_ref[...] = (keep_ref[...] + came_ref[...].astype(F32)).astype(BF16)


def slot_tiles(slots):
    step = 2 * LANES
    return [(first, min(first + step, slots)) for first in range(0, slots, step)]


def start_tiles(slots, offset, slope_hbm, onehot_hbm, slope_ref, onehot_ref, sems):
    tiles = []
    for tile, (first, last) in enumerate(slot_tiles(slots)):
        there, here = pl.ds(offset + first, last - first), pl.ds(first, last - first)
        copies = [
            pltpu.make_async_copy(slope_hbm.at[:, there], slope_ref.at[:, here], sems.at[tile, 0]),
            pltpu.make_async_copy(onehot_hbm.at[:, there], onehot_ref.at[:, here], sems.at[tile, 1]),
        ]
        for copy in copies:
            copy.start()
        tiles.append((slice(first, last), copies))
    return tiles


def sum_edges(tiles, w_out_ref, g_ref, slope_ref, onehot_ref):
    sums = None
    for lanes, copies in tiles:
        dh = mm(w_out_ref[...], g_ref[:, lanes])
        for copy in copies:
            copy.wait()
        dpre = (dh * slope_ref[:, lanes]).astype(BF16)
        term = mm(onehot_ref[:, lanes], dpre, NT)
        sums = term if sums is None else sums + term
    return sums


def near_kernel(half, own_ref, w_out_ref, hidden_ref, slope_hbm, onehot_hbm, *rest):
    *came_refs, sums_hbm, outer_hbm, g_ref, slope_ref, onehot_ref, sums_ref, outer_ref, sems, out_sems = rest
    slots = g_ref.shape[1]
    tiles = start_tiles(slots, 0, slope_hbm, onehot_hbm, slope_ref, onehot_ref, sems)
    filled = unpack(half, came_refs, g_ref)
    g_ref[:, filled:] = own_ref[...]
    outer_ref[...] = mm(hidden_ref[...], g_ref[...], NT)
    outer_copy = pltpu.make_async_copy(outer_ref, outer_hbm, out_sems.at[0])
    outer_copy.start()
    sums_ref[...] = sum_edges(tiles, w_out_ref, g_ref, slope_ref, onehot_ref)
    sums_copy = pltpu.make_async_copy(sums_ref, sums_hbm, out_sems.at[1])
    sums_copy.start()
    outer_copy.wait()
    sums_copy.wait()


def grad_kernel(half, factor, me_ref, w_out_ref, slope_hbm, onehot_hbm, ext_hbm, near_hbm, *rest):
    (
        *came_refs, keep_ref, send_ref, sums_ref, lower_ref, upper_ref, g_ref,
        slope_ref, onehot_ref, ext_ref, near_ref, tile_sems, sems,
    ) = rest
    odd = me_ref[0] % 2
    width = w_out_ref.shape[0]
    slots = g_ref.shape[1]
    inside = sums_ref.shape[0]
    mols = inside // 2
    reach = lower_ref.shape[0]
    tiles = start_tiles(slots, slope_hbm.shape[1] - slots, slope_hbm, onehot_hbm, slope_ref, onehot_ref, tile_sems)
    whole = [
        pltpu.make_async_copy(near_hbm, near_ref, sems.at[0]),
        pltpu.make_async_copy(ext_hbm, ext_ref, sems.at[1]),
    ]
    for copy in whole:
        copy.start()
    unpack(half, came_refs, g_ref)
    sums = sum_edges(tiles, w_out_ref, g_ref, slope_ref, onehot_ref)
    for copy in whole:
        copy.wait()
    sums = sums + near_ref[...]
    lower_ref[...] = sums[inside : inside + reach].astype(BF16)
    upper_ref[...] = sums[inside + reach :].astype(BF16)
    sums_ref[...] = sums[:inside]
    high, low = halves(sums)
    feats = ext_ref[:, :mols]
    rim = ext_ref[:, mols:]
    halve(factor * (mm(feats, high[:mols]) + mm(feats, low[:mols])), odd, 0, keep_ref, send_ref, 0)
    rim_term = mm(jnp.concatenate([rim, rim], axis=1), jnp.concatenate([high[inside:], low[inside:]], axis=0))
    dst_term = mm(feats, high[mols:inside]) + mm(feats, low[mols:inside]) + rim_term
    halve(factor * dst_term, odd, 0, keep_ref, send_ref, width)


def outer_kernel(factor, me_ref, hidden_ref, g_ref, near_hbm, keep_ref, send_ref, near_ref, sem):
    copy = pltpu.make_async_copy(near_hbm, near_ref, sem)
    copy.start()
    term = mm(hidden_ref[...], g_ref[...], NT)
    copy.wait()
    term = factor * (term + near_ref[...])
    padding = keep_ref.shape[2] - term.shape[1]
    if padding > 0:
        term = jnp.concatenate([term, jnp.zeros((term.shape[0], padding), F32)], axis=1)
    halve(term, me_ref[0] % 2, 0, keep_ref, send_ref, 0)


def rim_kernel(sums_ref, from_below_ref, from_above_ref, w_src_ref, w_dst_ref, out_ref):
    mols = out_ref.shape[0]
    reach = from_below_ref.shape[0]
    src = sums_ref[:mols]
    dst = sums_ref[mols:]
    dst = jnp.concatenate(
        [
            dst[:reach] + from_below_ref[...].astype(F32),
            dst[reach : mols - reach],
            dst[mols - reach :] + from_above_ref[...].astype(F32),
        ],
        axis=0,
    )
    w_src = w_src_ref[...]
    w_dst = w_dst_ref[...]
    src_high, src_low = halves(src)
    dst_high, dst_low = halves(dst)
    out_ref[...] = mm(src_high, w_src, NT) + mm(src_low, w_src, NT) + mm(dst_high, w_dst, NT) + mm(dst_low, w_dst, NT)


def total_kernel(*refs):
    *refs, src_ref, dst_ref, out_ref = refs
    count = len(refs) // 2
    width = src_ref.shape[1]
    totals = []
    for piece in (refs[:count], refs[count:]):
        terms = [ref[slab].astype(F32) for ref in piece for slab in range(ref.shape[0])]
        totals.append(functools.reduce(jnp.add, terms))
    sides, outer = totals
    src_ref[...] = sides[:, :width]
    dst_ref[...] = sides[:, width:]
    out_ref[...] = outer[:, : out_ref.shape[1]]


def in_hbm(x):
    return pltpu.with_memory_space_constraint(x, pltpu.HBM)


def swap(block, bit, slabs):
    return lax.ppermute(block, "space", [(i, i ^ (1 << bit)) for i in range(slabs)])


def on_device(mol_feats, w_src, w_dst, w_out, grad_blocks, edge_src, edge_dst, edge_live):
    slabs = lax.axis_size("space")
    mols, width = mol_feats.shape
    entries = w_out.shape[1]
    cap = grad_blocks.shape[2]
    half = cap // 2
    reach = mols // 4
    groups = LANES // half
    slots = (slabs // groups + 1) * LANES
    bits = slabs.bit_length() - 1
    if 3 <= bits <= 4:
        late_bits = tuple((bit, 0) for bit in range(3, bits))
        paths = (((0, 0), (1, 0), (2, 0)) + late_bits, ((0, 0), (2, 1), (1, 0)) + late_bits)
    else:
        paths = (tuple((bit, 0) for bit in range(min(bits, 2))),) * 2
    rest = slabs >> len(paths[0])
    part = width // slabs
    factor = float(edge_src.shape[0] * slabs) ** (-0.5)
    me = lax.axis_index("space").astype(jnp.int32).reshape(1)
    smem = pl.BlockSpec(memory_space=pltpu.SMEM)
    hbm = pl.BlockSpec(memory_space=pltpu.HBM)
    big = pltpu.CompilerParams(vmem_limit_bytes=24 * 1024 * 1024)
    up = [(i, (i + 1) % slabs) for i in range(slabs)]
    down = [((i + 1) % slabs, i) for i in range(slabs)]

    rows = round_up(pl.cdiv(entries, groups), PACK)
    stages = 4
    linked = slabs <= 16
    even, odd, low, top = pl.pallas_call(
        functools.partial(pack_kernel, rows, half, linked),
        out_shape=(
            jax.ShapeDtypeStruct((slabs // 2, rows, LANES), BF16),
            jax.ShapeDtypeStruct((slabs // 2, rows, LANES), BF16),
            jax.ShapeDtypeStruct((reach, width), BF16),
            jax.ShapeDtypeStruct((reach, width), BF16),
        ),
        in_specs=[smem, hbm, hbm],
        out_specs=tuple(vmem(4)),
        scratch_shapes=[
            pltpu.VMEM((entries, slabs, cap), BF16),
            pltpu.SemaphoreType.DMA((stages, groups)),
            pltpu.SemaphoreType.DMA((2,)),
        ],
        compiler_params=big,
        name="pack",
    )(me, in_hbm(mol_feats), in_hbm(jnp.transpose(grad_blocks[0], (2, 0, 1))))
    below = lax.ppermute(top, "space", up)
    above = lax.ppermute(low, "space", down)
    late = lax.dynamic_index_in_dim(grad_blocks[0], me[0], 0, keepdims=False)[half:]
    own = jnp.pad(late.T, ((0, groups * rows - entries), (0, LANES - half)))
    if linked:
        other = swap(odd, 0, slabs)
        other, below, above, own = lax.optimization_barrier((other, below, above, own))
        messages = pl.pallas_call(
            join_kernel,
            out_shape=(jax.ShapeDtypeStruct((2, rows, LANES), BF16),) * (slabs // 2),
            in_specs=vmem(2),
            out_specs=tuple(vmem(slabs // 2)),
            compiler_params=big,
            name="join",
        )(even, other)
        quarter = slabs // 4
        came = {0: messages[0]}
        for k in range(1, 2 * quarter):
            came[k] = lax.ppermute(messages[k], "space", [(i, i ^ (2 * k)) for i in range(slabs)])
        for k in range(1, quarter - 1):
            came[k], below, above, me = lax.optimization_barrier((came[k], below, above, me))
        turns = [*range(quarter - 1), *range(quarter, 2 * quarter), quarter - 1]
        near = tuple(2 * k + j for k in turns[: quarter - 1] for j in range(2))
        far = tuple(2 * k + j for k in turns[quarter - 1 :] for j in range(2))
        came_near = [came[k] for k in turns[: quarter - 1]]
        came_far = [came[k] for k in turns[quarter - 1 :]]
    else:
        packed = jnp.stack([even, odd], axis=1).reshape(slabs, rows, LANES)
        near, far = (), tuple(range(slabs))
        came_near = []
        came_far = [lax.all_to_all(packed, "space", split_axis=0, concat_axis=0, tiled=True)]
    far_slots = len(far) * half
    near_slots = slots - far_slots

    wide = mols + 2 * reach
    entries_wide = groups * rows
    pieces = len(slot_tiles(near_slots)) + len(slot_tiles(far_slots))
    onehot, slope, ext, near_hidden, far_hidden, w_out_wide = pl.pallas_call(
        functools.partial(edge_kernel, half, linked, near, far),
        out_shape=(
            pltpu.HBM((mols + wide, slots), BF16),
            pltpu.HBM((width, slots), F32),
            pltpu.HBM((width, wide), BF16),
            jax.ShapeDtypeStruct((width, near_slots), BF16),
            jax.ShapeDtypeStruct((width, far_slots), BF16),
            jax.ShapeDtypeStruct((width, entries_wide), BF16),
        ),
        in_specs=[smem] + [hbm] * 4 + vmem(5),
        out_specs=(hbm,) * 3 + tuple(vmem(3)),
        scratch_shapes=[
            pltpu.VMEM((mols + wide, slots), BF16),
            pltpu.VMEM((width, slots), F32),
            pltpu.VMEM((width, wide), BF16),
            pltpu.VMEM((entries_wide, width), BF16),
            pltpu.VMEM((mols, width), BF16),
            pltpu.VMEM((width, width), BF16),
            pltpu.VMEM((width, width), BF16),
            pltpu.VMEM((entries, width), BF16),
            pltpu.SemaphoreType.DMA((2 * pieces + 1,)),
            pltpu.SemaphoreType.DMA((4,)),
        ],
        compiler_params=big,
        name="edges",
        cost_estimate=pl.CostEstimate(
            flops=40 * width * slots * 2 * (2 * mols + 2 * reach), bytes_accessed=8 * 1024 * 1024,
            transcendentals=width * slots,
        ),
    )(
        me, in_hbm(mol_feats), in_hbm(w_src), in_hbm(w_dst), in_hbm(w_out.T), below, above,
        edge_src.reshape(slabs, cap), edge_dst.reshape(slabs, cap), edge_live.reshape(slabs, cap),
    )
    onehot, slope, ext = in_hbm(onehot), in_hbm(slope), in_hbm(ext)

    def chunks(count, lanes, dtype):
        return jax.ShapeDtypeStruct((count, part, lanes), dtype)

    near_sums, near_outer = pl.pallas_call(
        functools.partial(near_kernel, half),
        out_shape=(
            pltpu.HBM((mols + wide, width), F32),
            pltpu.HBM((width, entries_wide), F32),
        ),
        in_specs=vmem(3) + [hbm] * 2 + vmem(len(came_near)),
        out_specs=(hbm, hbm),
        scratch_shapes=[
            pltpu.VMEM((entries_wide, near_slots), BF16),
            pltpu.VMEM((width, near_slots), F32),
            pltpu.VMEM((mols + wide, near_slots), BF16),
            pltpu.VMEM((mols + wide, width), F32),
            pltpu.VMEM((width, entries_wide), F32),
            pltpu.SemaphoreType.DMA((len(slot_tiles(near_slots)), 2)),
            pltpu.SemaphoreType.DMA((2,)),
        ],
        compiler_params=big,
        name="near",
        cost_estimate=pl.CostEstimate(
            flops=40 * width * near_slots * entries_wide, bytes_accessed=6 * 1024 * 1024, transcendentals=0
        ),
    )(own, w_out_wide, near_hidden, slope, onehot, *came_near)
    near_sums, near_outer = in_hbm(near_sums), in_hbm(near_outer)
    keep, send, sums, lower, upper, g = pl.pallas_call(
        functools.partial(grad_kernel, half, factor),
        out_shape=(
            chunks(slabs // 2, 2 * width, F32),
            chunks(slabs // 2, 2 * width, BF16),
            jax.ShapeDtypeStruct((2 * mols, width), F32),
            jax.ShapeDtypeStruct((reach, width), BF16),
            jax.ShapeDtypeStruct((reach, width), BF16),
            jax.ShapeDtypeStruct((entries_wide, far_slots), BF16),
        ),
        in_specs=[smem] + vmem(1) + [hbm] * 4 + vmem(len(came_far)),
        out_specs=tuple(vmem(6)),
        scratch_shapes=[
            pltpu.VMEM((width, far_slots), F32),
            pltpu.VMEM((mols + wide, far_slots), BF16),
            pltpu.VMEM((width, wide), BF16),
            pltpu.VMEM((mols + wide, width), F32),
            pltpu.SemaphoreType.DMA((len(slot_tiles(far_slots)), 2)),
            pltpu.SemaphoreType.DMA((2,)),
        ],
        compiler_params=big,
        name="grads",
    )(me, w_out_wide, slope, onehot, ext, near_sums, *came_far)
    lanes = round_up(entries_wide, LANES)
    keep_o, send_o = pl.pallas_call(
        functools.partial(outer_kernel, factor),
        out_shape=(chunks(slabs // 2, lanes, F32), chunks(slabs // 2, lanes, BF16)),
        in_specs=[smem] + vmem(2) + [hbm],
        out_specs=tuple(vmem(2)),
        scratch_shapes=[pltpu.VMEM((width, entries_wide), F32), pltpu.SemaphoreType.DMA(())],
        compiler_params=big,
        name="outer",
        cost_estimate=pl.CostEstimate(
            flops=40 * width * slots * entries_wide, bytes_accessed=4 * 1024 * 1024, transcendentals=0
        ),
    )(me, far_hidden, g, near_outer)

    def fold(bit, place, keep, crossed):
        shape = (keep.shape[0] // 2, keep.shape[2])
        return pl.pallas_call(
            functools.partial(fold_kernel, bit, place),
            out_shape=(chunks(*shape, F32), chunks(*shape, BF16)),
            in_specs=[smem] + vmem(2),
            out_specs=tuple(vmem(2)),
            compiler_params=big,
            name="fold",
        )(me, keep, crossed)

    def close(keep, crossed):
        if rest == 1:
            return [keep, crossed]
        sends = pl.pallas_call(
            close_kernel,
            out_shape=chunks(rest, keep.shape[2], BF16),
            in_specs=vmem(2),
            out_specs=vmem(1)[0],
            compiler_params=big,
            name="close",
        )(keep, crossed)
        same = [[low + rank * (slabs // rest) for rank in range(rest)] for low in range(slabs // rest)]
        return [
            lax.all_to_all(sends, "space", split_axis=0, concat_axis=0, tiled=True, axis_index_groups=same)
        ]

    from_above = lax.ppermute(lower, "space", down)
    from_below = lax.ppermute(upper, "space", up)
    crossed = swap(send, 0, slabs)
    crossed_o = swap(send_o, 0, slabs)
    for (bit, place), (bit_o, place_o) in zip(paths[0][1:], paths[1][1:]):
        if bit == 2:
            keep, crossed, from_above, from_below = lax.optimization_barrier((keep, crossed, from_above, from_below))
        keep, send = fold(bit, place, keep, crossed)
        crossed = swap(send, bit, slabs)
        keep_o, crossed_o, _ = lax.optimization_barrier((keep_o, crossed_o, send))
        keep_o, send_o = fold(bit_o, place_o, keep_o, crossed_o)
        crossed_o = swap(send_o, bit_o, slabs)
    terms = close(keep, crossed)
    terms_o = close(keep_o, crossed_o)
    feature_grad = pl.pallas_call(
        rim_kernel,
        out_shape=jax.ShapeDtypeStruct((mols, width), F32),
        in_specs=vmem(5),
        out_specs=vmem(1)[0],
        compiler_params=big,
        name="rims",
        cost_estimate=pl.CostEstimate(flops=2 * width * slots * width * 40, bytes_accessed=4 * 1024 * 1024, transcendentals=0),
    )(sums, from_below, from_above, w_src, w_dst)
    src_grad, dst_grad, out_grad = pl.pallas_call(
        total_kernel,
        out_shape=(
            jax.ShapeDtypeStruct((part, width), F32),
            jax.ShapeDtypeStruct((part, width), F32),
            jax.ShapeDtypeStruct((part, entries), F32),
        ),
        in_specs=vmem(len(terms) + len(terms_o)),
        out_specs=tuple(vmem(3)),
        compiler_params=big,
        name="totals",
    )(*terms, *terms_o)
    return (feature_grad, src_grad, dst_grad, out_grad)


def solution(mesh):
    placed = (
        P(("groups", "space"), None),
        P(),
        P(),
        P(),
        P("space", "groups", None, None),
        P(("groups", "space")),
        P(("groups", "space")),
        P(("groups", "space")),
    )
    return jax.shard_map(
        on_device,
        mesh=mesh,
        in_specs=placed,
        out_specs=(
            P(("groups", "space"), None),
            P(("groups", "space"), None),
            P(("groups", "space"), None),
            P(("groups", "space"), None),
        ),
        check_vma=False,
    )
```

```python
import functools

import jax
import jax.numpy as jnp
from jax import lax
from jax.experimental import pallas as pl
from jax.experimental.pallas import tpu as pltpu
from jax.sharding import PartitionSpec as P

F32 = jnp.float32
BF16 = jnp.bfloat16
LANES = 128
PACK = 16
NN = (((1,), (0,)), ((), ()))
NT = (((1,), (1,)), ((), ()))


def mm(left, right, dims=NN):
    return lax.dot_general(left, right, dims, preferred_element_type=F32)


def halves(x):
    high = x.astype(BF16)
    return high, (x - high.astype(F32)).astype(BF16)


def round_up(x, to):
    return -(-x // to) * to


def vmem(count):
    return [pl.BlockSpec(memory_space=pltpu.VMEM)] * count


def pack_kernel(rows, half, linked, me_ref, feats_ref, g_ref, even_ref, odd_ref, low_ref, top_ref, here_ref, sems, rim_sems):
    entries, slabs, cap = g_ref.shape
    mols = feats_ref.shape[0]
    reach = low_ref.shape[0]
    groups = LANES // half
    blocks = rows // PACK
    count = sems.shape[0]
    stages = []
    for stage in range(count):
        begin, end = stage * blocks // count, (stage + 1) * blocks // count
        copies = []
        for group in range(groups):
            first = min(entries, group * rows + begin * PACK)
            last = min(entries, group * rows + end * PACK)
            if first < last:
                copies.append(
                    pltpu.make_async_copy(g_ref.at[first:last], here_ref.at[first:last], sems.at[stage, group])
                )
        stages.append((begin, end, copies))
        for copy in copies:
            copy.start()
    rims = [
        pltpu.make_async_copy(feats_ref.at[:reach], low_ref, rim_sems.at[0]),
        pltpu.make_async_copy(feats_ref.at[mols - reach :], top_ref, rim_sems.at[1]),
    ]
    for copy in rims:
        copy.start()
    size = PACK * slabs
    to = lax.broadcasted_iota(jnp.int32, (size, size), 0)
    source = lax.broadcasted_iota(jnp.int32, (size, size), 1)
    slab = to // PACK
    if linked:
        slab = slab ^ me_ref[0]
    perm = jnp.where((to % PACK) * slabs + slab == source, 1.0, 0.0).astype(BF16)

    def lanes_of(block):
        early = []
        for group in range(groups):
            first = group * rows + block * PACK
            valid = max(0, min(PACK, entries - first))
            tiles = []
            if valid:
                tiles.append(here_ref[first : first + valid])
            if valid < PACK:
                tiles.append(jnp.zeros((PACK - valid, slabs, cap), BF16))
            tile = tiles[0] if len(tiles) == 1 else jnp.concatenate(tiles, axis=0)
            early.append(tile.reshape(size, cap)[:, :half])
        return early

    for begin, end, copies in stages:
        for copy in copies:
            copy.wait()
        for block in range(begin, end, 2):
            together = range(block, min(block + 2, end))
            lanes = [piece for one in together for piece in lanes_of(one)]
            moved = mm(perm, jnp.concatenate(lanes, axis=1)).astype(BF16)
            for index, one in enumerate(together):
                chunk = moved[:, index * LANES : (index + 1) * LANES].reshape(slabs // 2, 2, PACK, LANES)
                here = pl.ds(one * PACK, PACK)
                even_ref[:, here, :] = chunk[:, 0]
                odd_ref[:, here, :] = chunk[:, 1]
    for copy in rims:
        copy.wait()


def by_core(pair, me):
    return pair[0] + (me % 2) * (pair[1] - pair[0])


def join_kernel(turns, me_ref, even_ref, other_ref, *message_refs):
    for pair, message_ref in zip(turns, message_refs):
        k = by_core(pair, me_ref[0])
        message_ref[0] = even_ref[k]
        message_ref[1] = other_ref[k]


def unpack(half, refs, g_ref):
    groups = LANES // half
    rows = g_ref.shape[0] // groups
    chunks = [(ref, index) for ref in refs for index in range(ref.shape[0])]
    tiles = len(chunks) // groups
    for tile in range(tiles):
        here = [ref[index] for ref, index in chunks[tile * groups : (tile + 1) * groups]]
        for group in range(groups):
            lanes = slice(group * half, (group + 1) * half)
            g_ref[group * rows : (group + 1) * rows, tile * LANES : (tile + 1) * LANES] = jnp.concatenate(
                [chunk[:, lanes] for chunk in here], axis=1
            )
    return tiles * LANES


def slot_rows(ref, me, half, linked, near, far):
    per = LANES // half

    def rows_of(ids):
        rows = []
        for tile in range(len(ids) // per):
            here = ids[tile * per : (tile + 1) * per]
            pieces = [ref[pl.ds(me ^ by_core(i, me) if linked else i, 1), :] for i in here]
            rows.append(jnp.concatenate([piece[:, :half] for piece in pieces], axis=1))
        return rows

    own = ref[pl.ds(me, 1), :][:, half:]
    own = jnp.concatenate([own, jnp.full((1, LANES - half), -1, jnp.int32)], axis=1)
    return rows_of(near) + [own] + rows_of(far)


def edge_kernel(
    half, linked, near, far, me_ref, feats_hbm, w_src_hbm, w_dst_hbm, w_out_hbm, below_ref, above_ref, src_ref, dst_ref,
    live_ref, onehot_hbm, slope_hbm, ext_hbm, near_hidden_ref, far_hidden_ref, w_wide_ref,
    onehot_ref, slope_ref, ext_ref, w_rows_ref, feats_ref, w_src_ref, w_dst_ref, w_out_ref, sems, in_sems,
):
    inputs = [
        pltpu.make_async_copy(hbm, ref, in_sems.at[index])
        for index, (hbm, ref) in enumerate(
            ((feats_hbm, feats_ref), (w_src_hbm, w_src_ref), (w_dst_hbm, w_dst_ref), (w_out_hbm, w_out_ref))
        )
    ]
    for copy in inputs:
        copy.start()
    me = me_ref[0]
    mols = feats_ref.shape[0]
    reach = below_ref.shape[0]
    wide = mols + 2 * reach
    slots = slope_ref.shape[1]
    entries = w_out_ref.shape[0]
    near_slots = near_hidden_ref.shape[1]
    copies = []

    def send(source, target):
        copy = pltpu.make_async_copy(source, target, sems.at[len(copies)])
        copy.start()
        copies.append(copy)

    mol_src = lax.broadcasted_iota(jnp.int32, (mols, LANES), 0)
    mol_dst = lax.broadcasted_iota(jnp.int32, (wide, LANES), 0)
    lists = [slot_rows(ref, me, half, linked, near, far) for ref in (src_ref, dst_ref, live_ref)]
    for tile, (src, dst, live) in enumerate(zip(*lists)):
        src = jnp.where(live > 0, src, -1)
        moved = jnp.where(dst < reach, dst + mols, jnp.where(dst < reach + mols, dst - reach, dst))
        dst = jnp.where(live > 0, moved, -1)
        one_src = jnp.where(mol_src == src, 1.0, 0.0).astype(BF16)
        one_dst = jnp.where(mol_dst == dst, 1.0, 0.0).astype(BF16)
        here = pl.ds(tile * LANES, LANES)
        onehot_ref[:, here] = jnp.concatenate([one_src, one_dst], axis=0)
    for copy in inputs[:3]:
        copy.wait()
    feats = feats_ref[...]
    ext = jnp.concatenate([feats, below_ref[...], above_ref[...]], axis=0)
    ext_ref[...] = ext.T
    send(ext_ref, ext_hbm)
    proj_src = mm(feats, w_src_ref[...])
    proj_dst = mm(ext, w_dst_ref[...])
    proj = jnp.concatenate([proj_src, proj_dst], axis=0).T
    high, low = halves(proj)
    for first, last in slot_tiles(near_slots) + [(near_slots + f, near_slots + l) for f, l in slot_tiles(slots - near_slots)]:
        here = pl.ds(first, last - first)
        send(onehot_ref.at[:, here], onehot_hbm.at[:, here])
        onehot = onehot_ref[:, here]
        pre = mm(high, onehot) + mm(low, onehot)
        sigma = 1.0 / (1.0 + jnp.exp(-pre))
        hidden = (pre * sigma).astype(BF16)
        if first < near_slots:
            near_hidden_ref[:, here] = hidden
        else:
            far_hidden_ref[:, pl.ds(first - near_slots, last - first)] = hidden
        slope_ref[:, here] = sigma * (1.0 + pre * (1.0 - sigma))
        send(slope_ref.at[:, here], slope_hbm.at[:, here])
    inputs[3].wait()
    whole = entries // LANES * LANES
    w_rows_ref[whole:] = jnp.zeros((w_rows_ref.shape[0] - whole, w_rows_ref.shape[1]), BF16)
    w_rows_ref[:whole] = w_out_ref[:whole]
    w_rows_ref[whole:entries] = w_out_ref[whole:]
    w_wide_ref[...] = w_rows_ref[...].T
    for copy in copies:
        copy.wait()


def halve(terms, odd, place, keep_ref, send_ref, first):
    count, rows, _ = keep_ref.shape
    width = terms.shape[-1]
    lanes = slice(first, first + width)
    inner = 1 << place
    pairs = terms.reshape(count // inner, 2, inner, rows, width)
    even_part = pairs[:, 0].reshape(count, rows, width)
    odd_part = pairs[:, 1].reshape(count, rows, width)
    keep_ref[:, :, lanes] = jnp.where(odd > 0, odd_part, even_part)
    send_ref[:, :, lanes] = jnp.where(odd > 0, even_part, odd_part).astype(BF16)


def fold_kernel(bit, place, me_ref, keep_ref, came_ref, next_ref, send_ref):
    odd = (me_ref[0] >> bit) % 2
    halve(keep_ref[...] + came_ref[...].astype(F32), odd, place, next_ref, send_ref, 0)


def close_kernel(keep_ref, came_ref, send_ref):
    send_ref[...] = (keep_ref[...] + came_ref[...].astype(F32)).astype(BF16)


def slot_tiles(slots):
    step = 2 * LANES
    return [(first, min(first + step, slots)) for first in range(0, slots, step)]


def start_tiles(slots, offset, slope_hbm, onehot_hbm, slope_ref, onehot_ref, sems):
    tiles = []
    for tile, (first, last) in enumerate(slot_tiles(slots)):
        there, here = pl.ds(offset + first, last - first), pl.ds(first, last - first)
        copies = [
            pltpu.make_async_copy(slope_hbm.at[:, there], slope_ref.at[:, here], sems.at[tile, 0]),
            pltpu.make_async_copy(onehot_hbm.at[:, there], onehot_ref.at[:, here], sems.at[tile, 1]),
        ]
        for copy in copies:
            copy.start()
        tiles.append((slice(first, last), copies))
    return tiles


def sum_edges(tiles, w_out_ref, g_ref, slope_ref, onehot_ref):
    sums = None
    for lanes, copies in tiles:
        dh = mm(w_out_ref[...], g_ref[:, lanes])
        for copy in copies:
            copy.wait()
        dpre = (dh * slope_ref[:, lanes]).astype(BF16)
        term = mm(onehot_ref[:, lanes], dpre, NT)
        sums = term if sums is None else sums + term
    return sums


def near_kernel(half, own_ref, w_out_ref, hidden_ref, slope_hbm, onehot_hbm, *rest):
    *came_refs, sums_hbm, outer_hbm, g_ref, slope_ref, onehot_ref, sums_ref, outer_ref, sems, out_sems = rest
    slots = g_ref.shape[1]
    tiles = start_tiles(slots, 0, slope_hbm, onehot_hbm, slope_ref, onehot_ref, sems)
    filled = unpack(half, came_refs, g_ref)
    g_ref[:, filled:] = own_ref[...]
    outer_ref[...] = mm(hidden_ref[...], g_ref[...], NT)
    outer_copy = pltpu.make_async_copy(outer_ref, outer_hbm, out_sems.at[0])
    outer_copy.start()
    sums_ref[...] = sum_edges(tiles, w_out_ref, g_ref, slope_ref, onehot_ref)
    sums_copy = pltpu.make_async_copy(sums_ref, sums_hbm, out_sems.at[1])
    sums_copy.start()
    outer_copy.wait()
    sums_copy.wait()


def grad_kernel(half, factor, me_ref, w_out_ref, slope_hbm, onehot_hbm, ext_hbm, near_hbm, *rest):
    (
        *came_refs, keep_ref, send_ref, sums_ref, lower_ref, upper_ref, g_ref,
        slope_ref, onehot_ref, ext_ref, near_ref, tile_sems, sems,
    ) = rest
    odd = me_ref[0] % 2
    width = w_out_ref.shape[0]
    slots = g_ref.shape[1]
    inside = sums_ref.shape[0]
    mols = inside // 2
    reach = lower_ref.shape[0]
    tiles = start_tiles(slots, slope_hbm.shape[1] - slots, slope_hbm, onehot_hbm, slope_ref, onehot_ref, tile_sems)
    whole = [
        pltpu.make_async_copy(near_hbm, near_ref, sems.at[0]),
        pltpu.make_async_copy(ext_hbm, ext_ref, sems.at[1]),
    ]
    for copy in whole:
        copy.start()
    unpack(half, came_refs, g_ref)
    sums = sum_edges(tiles, w_out_ref, g_ref, slope_ref, onehot_ref)
    for copy in whole:
        copy.wait()
    sums = sums + near_ref[...]
    lower_ref[...] = sums[inside : inside + reach].astype(BF16)
    upper_ref[...] = sums[inside + reach :].astype(BF16)
    sums_ref[...] = sums[:inside]
    high, low = halves(sums)
    feats = ext_ref[:, :mols]
    rim = ext_ref[:, mols:]
    halve(factor * (mm(feats, high[:mols]) + mm(feats, low[:mols])), odd, 0, keep_ref, send_ref, 0)
    rim_term = mm(jnp.concatenate([rim, rim], axis=1), jnp.concatenate([high[inside:], low[inside:]], axis=0))
    dst_term = mm(feats, high[mols:inside]) + mm(feats, low[mols:inside]) + rim_term
    halve(factor * dst_term, odd, 0, keep_ref, send_ref, width)


def outer_kernel(factor, me_ref, hidden_ref, g_ref, near_hbm, keep_ref, send_ref, near_ref, sem):
    copy = pltpu.make_async_copy(near_hbm, near_ref, sem)
    copy.start()
    term = mm(hidden_ref[...], g_ref[...], NT)
    copy.wait()
    term = factor * (term + near_ref[...])
    padding = keep_ref.shape[2] - term.shape[1]
    if padding > 0:
        term = jnp.concatenate([term, jnp.zeros((term.shape[0], padding), F32)], axis=1)
    halve(term, me_ref[0] % 2, 0, keep_ref, send_ref, 0)


def rim_kernel(sums_ref, from_below_ref, from_above_ref, w_src_ref, w_dst_ref, out_ref):
    mols = out_ref.shape[0]
    reach = from_below_ref.shape[0]
    src = sums_ref[:mols]
    dst = sums_ref[mols:]
    dst = jnp.concatenate(
        [
            dst[:reach] + from_below_ref[...].astype(F32),
            dst[reach : mols - reach],
            dst[mols - reach :] + from_above_ref[...].astype(F32),
        ],
        axis=0,
    )
    w_src = w_src_ref[...]
    w_dst = w_dst_ref[...]
    src_high, src_low = halves(src)
    dst_high, dst_low = halves(dst)
    out_ref[...] = mm(src_high, w_src, NT) + mm(src_low, w_src, NT) + mm(dst_high, w_dst, NT) + mm(dst_low, w_dst, NT)


def total_kernel(*refs):
    *refs, src_ref, dst_ref, out_ref = refs
    count = len(refs) // 2
    width = src_ref.shape[1]
    totals = []
    for piece in (refs[:count], refs[count:]):
        terms = [ref[slab].astype(F32) for ref in piece for slab in range(ref.shape[0])]
        totals.append(functools.reduce(jnp.add, terms))
    sides, outer = totals
    src_ref[...] = sides[:, :width]
    dst_ref[...] = sides[:, width:]
    out_ref[...] = outer[:, : out_ref.shape[1]]


def in_hbm(x):
    return pltpu.with_memory_space_constraint(x, pltpu.HBM)


def swap(block, bit, slabs):
    return lax.ppermute(block, "space", [(i, i ^ (1 << bit)) for i in range(slabs)])


def on_device(mol_feats, w_src, w_dst, w_out, grad_blocks, edge_src, edge_dst, edge_live):
    slabs = lax.axis_size("space")
    mols, width = mol_feats.shape
    entries = w_out.shape[1]
    cap = grad_blocks.shape[2]
    half = cap // 2
    reach = mols // 4
    groups = LANES // half
    slots = (slabs // groups + 1) * LANES
    bits = slabs.bit_length() - 1
    if 3 <= bits <= 4:
        late_bits = tuple((bit, 0) for bit in range(3, bits))
        paths = (((0, 0), (1, 0), (2, 0)) + late_bits, ((0, 0), (2, 1), (1, 0)) + late_bits)
    else:
        paths = (tuple((bit, 0) for bit in range(min(bits, 2))),) * 2
    rest = slabs >> len(paths[0])
    part = width // slabs
    factor = float(edge_src.shape[0] * slabs) ** (-0.5)
    me = lax.axis_index("space").astype(jnp.int32).reshape(1)
    smem = pl.BlockSpec(memory_space=pltpu.SMEM)
    hbm = pl.BlockSpec(memory_space=pltpu.HBM)
    big = pltpu.CompilerParams(vmem_limit_bytes=24 * 1024 * 1024)
    up = [(i, (i + 1) % slabs) for i in range(slabs)]
    down = [((i + 1) % slabs, i) for i in range(slabs)]

    rows = round_up(pl.cdiv(entries, groups), PACK)
    stages = 4
    linked = slabs <= 16
    even, odd, low, top = pl.pallas_call(
        functools.partial(pack_kernel, rows, half, linked),
        out_shape=(
            jax.ShapeDtypeStruct((slabs // 2, rows, LANES), BF16),
            jax.ShapeDtypeStruct((slabs // 2, rows, LANES), BF16),
            jax.ShapeDtypeStruct((reach, width), BF16),
            jax.ShapeDtypeStruct((reach, width), BF16),
        ),
        in_specs=[smem, hbm, hbm],
        out_specs=tuple(vmem(4)),
        scratch_shapes=[
            pltpu.VMEM((entries, slabs, cap), BF16),
            pltpu.SemaphoreType.DMA((stages, groups)),
            pltpu.SemaphoreType.DMA((2,)),
        ],
        compiler_params=big,
        name="pack",
    )(me, in_hbm(mol_feats), in_hbm(jnp.transpose(grad_blocks[0], (2, 0, 1))))
    below = lax.ppermute(top, "space", up)
    above = lax.ppermute(low, "space", down)
    late = lax.dynamic_index_in_dim(grad_blocks[0], me[0], 0, keepdims=False)[half:]
    own = jnp.pad(late.T, ((0, groups * rows - entries), (0, LANES - half)))
    if linked:
        other = swap(odd, 0, slabs)
        other, below, above, own = lax.optimization_barrier((other, below, above, own))
        quarter = slabs // 4
        mixed = [pair for k in range(1, quarter) for pair in ((quarter + k - 1, k), (k, quarter + k - 1))]
        turns = [(0, 0), *mixed, (2 * quarter - 1, 2 * quarter - 1)]
        messages = pl.pallas_call(
            functools.partial(join_kernel, turns),
            out_shape=(jax.ShapeDtypeStruct((2, rows, LANES), BF16),) * (slabs // 2),
            in_specs=[smem] + vmem(2),
            out_specs=tuple(vmem(slabs // 2)),
            compiler_params=big,
            name="join",
        )(me, even, other)
        came = [messages[0]]
        for turn in range(1, 2 * quarter):
            route = [(i, i ^ (2 * turns[turn][i % 2])) for i in range(slabs)]
            came.append(lax.ppermute(messages[turn], "space", route))
        for turn in range(1, quarter - 1):
            came[turn], below, above, me = lax.optimization_barrier((came[turn], below, above, me))
        ids = [(2 * first + j, 2 * second + j) for first, second in turns for j in range(2)]
        near, far = tuple(ids[: 2 * quarter - 2]), tuple(ids[2 * quarter - 2 :])
        came_near, came_far = came[: quarter - 1], came[quarter - 1 :]
    else:
        packed = jnp.stack([even, odd], axis=1).reshape(slabs, rows, LANES)
        near, far = (), tuple(range(slabs))
        came_near = []
        came_far = [lax.all_to_all(packed, "space", split_axis=0, concat_axis=0, tiled=True)]
    far_slots = len(far) * half
    near_slots = slots - far_slots

    wide = mols + 2 * reach
    entries_wide = groups * rows
    pieces = len(slot_tiles(near_slots)) + len(slot_tiles(far_slots))
    onehot, slope, ext, near_hidden, far_hidden, w_out_wide = pl.pallas_call(
        functools.partial(edge_kernel, half, linked, near, far),
        out_shape=(
            pltpu.HBM((mols + wide, slots), BF16),
            pltpu.HBM((width, slots), F32),
            pltpu.HBM((width, wide), BF16),
            jax.ShapeDtypeStruct((width, near_slots), BF16),
            jax.ShapeDtypeStruct((width, far_slots), BF16),
            jax.ShapeDtypeStruct((width, entries_wide), BF16),
        ),
        in_specs=[smem] + [hbm] * 4 + vmem(5),
        out_specs=(hbm,) * 3 + tuple(vmem(3)),
        scratch_shapes=[
            pltpu.VMEM((mols + wide, slots), BF16),
            pltpu.VMEM((width, slots), F32),
            pltpu.VMEM((width, wide), BF16),
            pltpu.VMEM((entries_wide, width), BF16),
            pltpu.VMEM((mols, width), BF16),
            pltpu.VMEM((width, width), BF16),
            pltpu.VMEM((width, width), BF16),
            pltpu.VMEM((entries, width), BF16),
            pltpu.SemaphoreType.DMA((2 * pieces + 1,)),
            pltpu.SemaphoreType.DMA((4,)),
        ],
        compiler_params=big,
        name="edges",
        cost_estimate=pl.CostEstimate(
            flops=40 * width * slots * 2 * (2 * mols + 2 * reach), bytes_accessed=8 * 1024 * 1024,
            transcendentals=width * slots,
        ),
    )(
        me, in_hbm(mol_feats), in_hbm(w_src), in_hbm(w_dst), in_hbm(w_out.T), below, above,
        edge_src.reshape(slabs, cap), edge_dst.reshape(slabs, cap), edge_live.reshape(slabs, cap),
    )
    onehot, slope, ext = in_hbm(onehot), in_hbm(slope), in_hbm(ext)

    def chunks(count, lanes, dtype):
        return jax.ShapeDtypeStruct((count, part, lanes), dtype)

    near_sums, near_outer = pl.pallas_call(
        functools.partial(near_kernel, half),
        out_shape=(
            pltpu.HBM((mols + wide, width), F32),
            pltpu.HBM((width, entries_wide), F32),
        ),
        in_specs=vmem(3) + [hbm] * 2 + vmem(len(came_near)),
        out_specs=(hbm, hbm),
        scratch_shapes=[
            pltpu.VMEM((entries_wide, near_slots), BF16),
            pltpu.VMEM((width, near_slots), F32),
            pltpu.VMEM((mols + wide, near_slots), BF16),
            pltpu.VMEM((mols + wide, width), F32),
            pltpu.VMEM((width, entries_wide), F32),
            pltpu.SemaphoreType.DMA((len(slot_tiles(near_slots)), 2)),
            pltpu.SemaphoreType.DMA((2,)),
        ],
        compiler_params=big,
        name="near",
        cost_estimate=pl.CostEstimate(
            flops=40 * width * near_slots * entries_wide, bytes_accessed=6 * 1024 * 1024, transcendentals=0
        ),
    )(own, w_out_wide, near_hidden, slope, onehot, *came_near)
    near_sums, near_outer = in_hbm(near_sums), in_hbm(near_outer)
    keep, send, sums, lower, upper, g = pl.pallas_call(
        functools.partial(grad_kernel, half, factor),
        out_shape=(
            chunks(slabs // 2, 2 * width, F32),
            chunks(slabs // 2, 2 * width, BF16),
            jax.ShapeDtypeStruct((2 * mols, width), F32),
            jax.ShapeDtypeStruct((reach, width), BF16),
            jax.ShapeDtypeStruct((reach, width), BF16),
            jax.ShapeDtypeStruct((entries_wide, far_slots), BF16),
        ),
        in_specs=[smem] + vmem(1) + [hbm] * 4 + vmem(len(came_far)),
        out_specs=tuple(vmem(6)),
        scratch_shapes=[
            pltpu.VMEM((width, far_slots), F32),
            pltpu.VMEM((mols + wide, far_slots), BF16),
            pltpu.VMEM((width, wide), BF16),
            pltpu.VMEM((mols + wide, width), F32),
            pltpu.SemaphoreType.DMA((len(slot_tiles(far_slots)), 2)),
            pltpu.SemaphoreType.DMA((2,)),
        ],
        compiler_params=big,
        name="grads",
    )(me, w_out_wide, slope, onehot, ext, near_sums, *came_far)
    lanes = round_up(entries_wide, LANES)
    keep_o, send_o = pl.pallas_call(
        functools.partial(outer_kernel, factor),
        out_shape=(chunks(slabs // 2, lanes, F32), chunks(slabs // 2, lanes, BF16)),
        in_specs=[smem] + vmem(2) + [hbm],
        out_specs=tuple(vmem(2)),
        scratch_shapes=[pltpu.VMEM((width, entries_wide), F32), pltpu.SemaphoreType.DMA(())],
        compiler_params=big,
        name="outer",
        cost_estimate=pl.CostEstimate(
            flops=40 * width * slots * entries_wide, bytes_accessed=4 * 1024 * 1024, transcendentals=0
        ),
    )(me, far_hidden, g, near_outer)

    def fold(bit, place, keep, crossed):
        shape = (keep.shape[0] // 2, keep.shape[2])
        return pl.pallas_call(
            functools.partial(fold_kernel, bit, place),
            out_shape=(chunks(*shape, F32), chunks(*shape, BF16)),
            in_specs=[smem] + vmem(2),
            out_specs=tuple(vmem(2)),
            compiler_params=big,
            name="fold",
        )(me, keep, crossed)

    def close(keep, crossed):
        if rest == 1:
            return [keep, crossed]
        sends = pl.pallas_call(
            close_kernel,
            out_shape=chunks(rest, keep.shape[2], BF16),
            in_specs=vmem(2),
            out_specs=vmem(1)[0],
            compiler_params=big,
            name="close",
        )(keep, crossed)
        same = [[low + rank * (slabs // rest) for rank in range(rest)] for low in range(slabs // rest)]
        return [
            lax.all_to_all(sends, "space", split_axis=0, concat_axis=0, tiled=True, axis_index_groups=same)
        ]

    from_above = lax.ppermute(lower, "space", down)
    from_below = lax.ppermute(upper, "space", up)
    crossed = swap(send, 0, slabs)
    crossed_o = swap(send_o, 0, slabs)
    for (bit, place), (bit_o, place_o) in zip(paths[0][1:], paths[1][1:]):
        if bit == 2:
            keep, crossed, from_above, from_below = lax.optimization_barrier((keep, crossed, from_above, from_below))
        keep, send = fold(bit, place, keep, crossed)
        crossed = swap(send, bit, slabs)
        keep_o, crossed_o, _ = lax.optimization_barrier((keep_o, crossed_o, send))
        keep_o, send_o = fold(bit_o, place_o, keep_o, crossed_o)
        crossed_o = swap(send_o, bit_o, slabs)
    terms = close(keep, crossed)
    terms_o = close(keep_o, crossed_o)
    feature_grad = pl.pallas_call(
        rim_kernel,
        out_shape=jax.ShapeDtypeStruct((mols, width), F32),
        in_specs=vmem(5),
        out_specs=vmem(1)[0],
        compiler_params=big,
        name="rims",
        cost_estimate=pl.CostEstimate(flops=2 * width * slots * width * 40, bytes_accessed=4 * 1024 * 1024, transcendentals=0),
    )(sums, from_below, from_above, w_src, w_dst)
    src_grad, dst_grad, out_grad = pl.pallas_call(
        total_kernel,
        out_shape=(
            jax.ShapeDtypeStruct((part, width), F32),
            jax.ShapeDtypeStruct((part, width), F32),
            jax.ShapeDtypeStruct((part, entries), F32),
        ),
        in_specs=vmem(len(terms) + len(terms_o)),
        out_specs=tuple(vmem(3)),
        compiler_params=big,
        name="totals",
    )(*terms, *terms_o)
    return (feature_grad, src_grad, dst_grad, out_grad)


def solution(mesh):
    placed = (
        P(("groups", "space"), None),
        P(),
        P(),
        P(),
        P("space", "groups", None, None),
        P(("groups", "space")),
        P(("groups", "space")),
        P(("groups", "space")),
    )
    return jax.shard_map(
        on_device,
        mesh=mesh,
        in_specs=placed,
        out_specs=(
            P(("groups", "space"), None),
            P(("groups", "space"), None),
            P(("groups", "space"), None),
            P(("groups", "space"), None),
        ),
        check_vma=False,
    )
```

```python
import functools

import jax
import jax.numpy as jnp
from jax import lax
from jax.experimental import pallas as pl
from jax.experimental.pallas import tpu as pltpu
from jax.sharding import PartitionSpec as P

F32 = jnp.float32
BF16 = jnp.bfloat16
LANES = 128
PACK = 16
NN = (((1,), (0,)), ((), ()))
NT = (((1,), (1,)), ((), ()))


def mm(left, right, dims=NN):
    return lax.dot_general(left, right, dims, preferred_element_type=F32)


def halves(x):
    high = x.astype(BF16)
    return high, (x - high.astype(F32)).astype(BF16)


def round_up(x, to):
    return -(-x // to) * to


def vmem(count):
    return [pl.BlockSpec(memory_space=pltpu.VMEM)] * count


def pack_kernel(rows, half, linked, me_ref, feats_ref, g_ref, even_ref, odd_ref, low_ref, top_ref, here_ref, sems, rim_sems):
    entries, slabs, cap = g_ref.shape
    mols = feats_ref.shape[0]
    reach = low_ref.shape[0]
    groups = LANES // half
    blocks = rows // PACK
    count = sems.shape[0]
    stages = []
    for stage in range(count):
        begin, end = stage * blocks // count, (stage + 1) * blocks // count
        copies = []
        for group in range(groups):
            first = min(entries, group * rows + begin * PACK)
            last = min(entries, group * rows + end * PACK)
            if first < last:
                copies.append(
                    pltpu.make_async_copy(g_ref.at[first:last], here_ref.at[first:last], sems.at[stage, group])
                )
        stages.append((begin, end, copies))
        for copy in copies:
            copy.start()
    rims = [
        pltpu.make_async_copy(feats_ref.at[:reach], low_ref, rim_sems.at[0]),
        pltpu.make_async_copy(feats_ref.at[mols - reach :], top_ref, rim_sems.at[1]),
    ]
    for copy in rims:
        copy.start()
    size = PACK * slabs
    to = lax.broadcasted_iota(jnp.int32, (size, size), 0)
    source = lax.broadcasted_iota(jnp.int32, (size, size), 1)
    slab = to // PACK
    if linked:
        slab = slab ^ me_ref[0]
    perm = jnp.where((to % PACK) * slabs + slab == source, 1.0, 0.0).astype(BF16)

    def lanes_of(block):
        early = []
        for group in range(groups):
            first = group * rows + block * PACK
            valid = max(0, min(PACK, entries - first))
            tiles = []
            if valid:
                tiles.append(here_ref[first : first + valid])
            if valid < PACK:
                tiles.append(jnp.zeros((PACK - valid, slabs, cap), BF16))
            tile = tiles[0] if len(tiles) == 1 else jnp.concatenate(tiles, axis=0)
            early.append(tile.reshape(size, cap)[:, :half])
        return early

    for begin, end, copies in stages:
        for copy in copies:
            copy.wait()
        for block in range(begin, end, 2):
            together = range(block, min(block + 2, end))
            lanes = [piece for one in together for piece in lanes_of(one)]
            moved = mm(perm, jnp.concatenate(lanes, axis=1)).astype(BF16)
            for index, one in enumerate(together):
                chunk = moved[:, index * LANES : (index + 1) * LANES].reshape(slabs // 2, 2, PACK, LANES)
                here = pl.ds(one * PACK, PACK)
                even_ref[:, here, :] = chunk[:, 0]
                odd_ref[:, here, :] = chunk[:, 1]
    for copy in rims:
        copy.wait()


def by_core(pair, me):
    return pair[0] + (me % 2) * (pair[1] - pair[0])


def join_kernel(turns, me_ref, even_ref, other_ref, *message_refs):
    for pair, message_ref in zip(turns, message_refs):
        k = by_core(pair, me_ref[0])
        message_ref[0] = even_ref[k]
        message_ref[1] = other_ref[k]


def unpack(half, refs, g_ref):
    groups = LANES // half
    rows = g_ref.shape[0] // groups
    chunks = [(ref, index) for ref in refs for index in range(ref.shape[0])]
    tiles = len(chunks) // groups
    for tile in range(tiles):
        here = [ref[index] for ref, index in chunks[tile * groups : (tile + 1) * groups]]
        for group in range(groups):
            lanes = slice(group * half, (group + 1) * half)
            g_ref[group * rows : (group + 1) * rows, tile * LANES : (tile + 1) * LANES] = jnp.concatenate(
                [chunk[:, lanes] for chunk in here], axis=1
            )
    return tiles * LANES


def slot_rows(ref, me, half, linked, near, far):
    per = LANES // half

    def rows_of(ids):
        rows = []
        for tile in range(len(ids) // per):
            here = ids[tile * per : (tile + 1) * per]
            pieces = [ref[pl.ds(me ^ by_core(i, me) if linked else i, 1), :] for i in here]
            rows.append(jnp.concatenate([piece[:, :half] for piece in pieces], axis=1))
        return rows

    own = ref[pl.ds(me, 1), :][:, half:]
    own = jnp.concatenate([own, jnp.full((1, LANES - half), -1, jnp.int32)], axis=1)
    return rows_of(near) + [own] + rows_of(far)


def edge_kernel(
    half, linked, near, far, me_ref, feats_hbm, w_src_hbm, w_dst_hbm, w_out_hbm, below_ref, above_ref, src_ref, dst_ref,
    live_ref, onehot_hbm, slope_hbm, ext_hbm, near_hidden_ref, far_hidden_ref, w_wide_ref,
    onehot_ref, slope_ref, ext_ref, w_rows_ref, feats_ref, w_src_ref, w_dst_ref, w_out_ref, sems, in_sems,
):
    inputs = [
        pltpu.make_async_copy(hbm, ref, in_sems.at[index])
        for index, (hbm, ref) in enumerate(
            ((feats_hbm, feats_ref), (w_src_hbm, w_src_ref), (w_dst_hbm, w_dst_ref), (w_out_hbm, w_out_ref))
        )
    ]
    for copy in inputs:
        copy.start()
    me = me_ref[0]
    mols = feats_ref.shape[0]
    reach = below_ref.shape[0]
    wide = mols + 2 * reach
    slots = slope_ref.shape[1]
    entries = w_out_ref.shape[0]
    near_slots = near_hidden_ref.shape[1]
    copies = []

    def send(source, target):
        copy = pltpu.make_async_copy(source, target, sems.at[len(copies)])
        copy.start()
        copies.append(copy)

    mol_src = lax.broadcasted_iota(jnp.int32, (mols, LANES), 0)
    mol_dst = lax.broadcasted_iota(jnp.int32, (wide, LANES), 0)
    lists = [slot_rows(ref, me, half, linked, near, far) for ref in (src_ref, dst_ref, live_ref)]
    for tile, (src, dst, live) in enumerate(zip(*lists)):
        src = jnp.where(live > 0, src, -1)
        moved = jnp.where(dst < reach, dst + mols, jnp.where(dst < reach + mols, dst - reach, dst))
        dst = jnp.where(live > 0, moved, -1)
        one_src = jnp.where(mol_src == src, 1.0, 0.0).astype(BF16)
        one_dst = jnp.where(mol_dst == dst, 1.0, 0.0).astype(BF16)
        here = pl.ds(tile * LANES, LANES)
        onehot_ref[:, here] = jnp.concatenate([one_src, one_dst], axis=0)
    for copy in inputs[:3]:
        copy.wait()
    feats = feats_ref[...]
    ext = jnp.concatenate([feats, below_ref[...], above_ref[...]], axis=0)
    ext_ref[...] = ext.T
    send(ext_ref, ext_hbm)
    proj_src = mm(feats, w_src_ref[...])
    proj_dst = mm(ext, w_dst_ref[...])
    proj = jnp.concatenate([proj_src, proj_dst], axis=0).T
    high, low = halves(proj)
    for first, last in slot_tiles(near_slots) + [(near_slots + f, near_slots + l) for f, l in slot_tiles(slots - near_slots)]:
        here = pl.ds(first, last - first)
        send(onehot_ref.at[:, here], onehot_hbm.at[:, here])
        onehot = onehot_ref[:, here]
        pre = mm(high, onehot) + mm(low, onehot)
        sigma = 1.0 / (1.0 + jnp.exp(-pre))
        hidden = (pre * sigma).astype(BF16)
        if first < near_slots:
            near_hidden_ref[:, here] = hidden
        else:
            far_hidden_ref[:, pl.ds(first - near_slots, last - first)] = hidden
        slope_ref[:, here] = sigma * (1.0 + pre * (1.0 - sigma))
        send(slope_ref.at[:, here], slope_hbm.at[:, here])
    inputs[3].wait()
    whole = entries // LANES * LANES
    w_rows_ref[whole:] = jnp.zeros((w_rows_ref.shape[0] - whole, w_rows_ref.shape[1]), BF16)
    w_rows_ref[:whole] = w_out_ref[:whole]
    w_rows_ref[whole:entries] = w_out_ref[whole:]
    w_wide_ref[...] = w_rows_ref[...].T
    for copy in copies:
        copy.wait()


def halve(terms, odd, place, keep_ref, send_ref, first):
    count, rows, _ = keep_ref.shape
    width = terms.shape[-1]
    lanes = slice(first, first + width)
    inner = 1 << place
    pairs = terms.reshape(count // inner, 2, inner, rows, width)
    even_part = pairs[:, 0].reshape(count, rows, width)
    odd_part = pairs[:, 1].reshape(count, rows, width)
    keep_ref[:, :, lanes] = jnp.where(odd > 0, odd_part, even_part)
    send_ref[:, :, lanes] = jnp.where(odd > 0, even_part, odd_part).astype(BF16)


def fold_kernel(bit, place, me_ref, keep_ref, came_ref, next_ref, send_ref):
    odd = (me_ref[0] >> bit) % 2
    halve(keep_ref[...] + came_ref[...].astype(F32), odd, place, next_ref, send_ref, 0)


def close_kernel(keep_ref, came_ref, send_ref):
    send_ref[...] = (keep_ref[...] + came_ref[...].astype(F32)).astype(BF16)


def slot_tiles(slots):
    step = 2 * LANES
    return [(first, min(first + step, slots)) for first in range(0, slots, step)]


def start_tiles(slots, offset, slope_hbm, onehot_hbm, slope_ref, onehot_ref, sems):
    tiles = []
    for tile, (first, last) in enumerate(slot_tiles(slots)):
        there, here = pl.ds(offset + first, last - first), pl.ds(first, last - first)
        copies = [
            pltpu.make_async_copy(slope_hbm.at[:, there], slope_ref.at[:, here], sems.at[tile, 0]),
            pltpu.make_async_copy(onehot_hbm.at[:, there], onehot_ref.at[:, here], sems.at[tile, 1]),
        ]
        for copy in copies:
            copy.start()
        tiles.append((slice(first, last), copies))
    return tiles


def sum_edges(tiles, w_out_ref, g_ref, slope_ref, onehot_ref):
    sums = None
    for lanes, copies in tiles:
        dh = mm(w_out_ref[...], g_ref[:, lanes])
        for copy in copies:
            copy.wait()
        dpre = (dh * slope_ref[:, lanes]).astype(BF16)
        term = mm(onehot_ref[:, lanes], dpre, NT)
        sums = term if sums is None else sums + term
    return sums


def near_kernel(half, own_ref, w_out_ref, hidden_ref, slope_hbm, onehot_hbm, *rest):
    *came_refs, sums_hbm, outer_hbm, g_ref, slope_ref, onehot_ref, sums_ref, outer_ref, sems, out_sems = rest
    slots = g_ref.shape[1]
    tiles = start_tiles(slots, 0, slope_hbm, onehot_hbm, slope_ref, onehot_ref, sems)
    filled = unpack(half, came_refs, g_ref)
    g_ref[:, filled:] = own_ref[...]
    outer_ref[...] = mm(hidden_ref[...], g_ref[...], NT)
    outer_copy = pltpu.make_async_copy(outer_ref, outer_hbm, out_sems.at[0])
    outer_copy.start()
    sums_ref[...] = sum_edges(tiles, w_out_ref, g_ref, slope_ref, onehot_ref)
    sums_copy = pltpu.make_async_copy(sums_ref, sums_hbm, out_sems.at[1])
    sums_copy.start()
    outer_copy.wait()
    sums_copy.wait()


def grad_kernel(half, factor, me_ref, w_out_ref, slope_hbm, onehot_hbm, ext_hbm, near_hbm, *rest):
    (
        *came_refs, keep_ref, send_ref, sums_ref, lower_ref, upper_ref, g_ref,
        slope_ref, onehot_ref, ext_ref, near_ref, tile_sems, sems,
    ) = rest
    odd = me_ref[0] % 2
    width = w_out_ref.shape[0]
    slots = g_ref.shape[1]
    inside = sums_ref.shape[0]
    mols = inside // 2
    reach = lower_ref.shape[0]
    tiles = start_tiles(slots, slope_hbm.shape[1] - slots, slope_hbm, onehot_hbm, slope_ref, onehot_ref, tile_sems)
    whole = [
        pltpu.make_async_copy(near_hbm, near_ref, sems.at[0]),
        pltpu.make_async_copy(ext_hbm, ext_ref, sems.at[1]),
    ]
    for copy in whole:
        copy.start()
    unpack(half, came_refs, g_ref)
    sums = sum_edges(tiles, w_out_ref, g_ref, slope_ref, onehot_ref)
    for copy in whole:
        copy.wait()
    sums = sums + near_ref[...]
    lower_ref[...] = sums[inside : inside + reach].astype(BF16)
    upper_ref[...] = sums[inside + reach :].astype(BF16)
    sums_ref[...] = sums[:inside]
    high, low = halves(sums)
    feats = ext_ref[:, :mols]
    rim = ext_ref[:, mols:]
    halve(factor * (mm(feats, high[:mols]) + mm(feats, low[:mols])), odd, 0, keep_ref, send_ref, 0)
    rim_term = mm(jnp.concatenate([rim, rim], axis=1), jnp.concatenate([high[inside:], low[inside:]], axis=0))
    dst_term = mm(feats, high[mols:inside]) + mm(feats, low[mols:inside]) + rim_term
    halve(factor * dst_term, odd, 0, keep_ref, send_ref, width)


def outer_kernel(factor, me_ref, hidden_ref, g_ref, near_hbm, keep_ref, send_ref, near_ref, sem):
    copy = pltpu.make_async_copy(near_hbm, near_ref, sem)
    copy.start()
    term = mm(hidden_ref[...], g_ref[...], NT)
    copy.wait()
    term = factor * (term + near_ref[...])
    padding = keep_ref.shape[2] - term.shape[1]
    if padding > 0:
        term = jnp.concatenate([term, jnp.zeros((term.shape[0], padding), F32)], axis=1)
    halve(term, me_ref[0] % 2, 0, keep_ref, send_ref, 0)


def rim_kernel(sums_ref, from_below_ref, from_above_ref, w_src_ref, w_dst_ref, out_ref):
    mols = out_ref.shape[0]
    reach = from_below_ref.shape[0]
    src = sums_ref[:mols]
    dst = sums_ref[mols:]
    dst = jnp.concatenate(
        [
            dst[:reach] + from_below_ref[...].astype(F32),
            dst[reach : mols - reach],
            dst[mols - reach :] + from_above_ref[...].astype(F32),
        ],
        axis=0,
    )
    w_src = w_src_ref[...]
    w_dst = w_dst_ref[...]
    src_high, src_low = halves(src)
    dst_high, dst_low = halves(dst)
    out_ref[...] = mm(src_high, w_src, NT) + mm(src_low, w_src, NT) + mm(dst_high, w_dst, NT) + mm(dst_low, w_dst, NT)


def total_kernel(*refs):
    *refs, src_ref, dst_ref, out_ref = refs
    count = len(refs) // 2
    width = src_ref.shape[1]
    totals = []
    for piece in (refs[:count], refs[count:]):
        terms = [ref[slab].astype(F32) for ref in piece for slab in range(ref.shape[0])]
        totals.append(functools.reduce(jnp.add, terms))
    sides, outer = totals
    src_ref[...] = sides[:, :width]
    dst_ref[...] = sides[:, width:]
    out_ref[...] = outer[:, : out_ref.shape[1]]


def in_hbm(x):
    return pltpu.with_memory_space_constraint(x, pltpu.HBM)


def swap(block, bit, slabs):
    return lax.ppermute(block, "space", [(i, i ^ (1 << bit)) for i in range(slabs)])


def on_device(mol_feats, w_src, w_dst, w_out, grad_blocks, edge_src, edge_dst, edge_live):
    slabs = lax.axis_size("space")
    mols, width = mol_feats.shape
    entries = w_out.shape[1]
    cap = grad_blocks.shape[2]
    half = cap // 2
    reach = mols // 4
    groups = LANES // half
    slots = (slabs // groups + 1) * LANES
    bits = slabs.bit_length() - 1
    if 3 <= bits <= 4:
        late_bits = tuple((bit, 0) for bit in range(3, bits))
        paths = (((0, 0), (1, 0), (2, 0)) + late_bits, ((0, 0), (2, 1), (1, 0)) + late_bits)
    else:
        paths = (tuple((bit, 0) for bit in range(min(bits, 2))),) * 2
    rest = slabs >> len(paths[0])
    part = width // slabs
    factor = float(edge_src.shape[0] * slabs) ** (-0.5)
    me = lax.axis_index("space").astype(jnp.int32).reshape(1)
    smem = pl.BlockSpec(memory_space=pltpu.SMEM)
    hbm = pl.BlockSpec(memory_space=pltpu.HBM)
    big = pltpu.CompilerParams(vmem_limit_bytes=24 * 1024 * 1024)
    up = [(i, (i + 1) % slabs) for i in range(slabs)]
    down = [((i + 1) % slabs, i) for i in range(slabs)]

    rows = round_up(pl.cdiv(entries, groups), PACK)
    stages = 4
    linked = slabs <= 16
    even, odd, low, top = pl.pallas_call(
        functools.partial(pack_kernel, rows, half, linked),
        out_shape=(
            jax.ShapeDtypeStruct((slabs // 2, rows, LANES), BF16),
            jax.ShapeDtypeStruct((slabs // 2, rows, LANES), BF16),
            jax.ShapeDtypeStruct((reach, width), BF16),
            jax.ShapeDtypeStruct((reach, width), BF16),
        ),
        in_specs=[smem, hbm, hbm],
        out_specs=tuple(vmem(4)),
        scratch_shapes=[
            pltpu.VMEM((entries, slabs, cap), BF16),
            pltpu.SemaphoreType.DMA((stages, groups)),
            pltpu.SemaphoreType.DMA((2,)),
        ],
        compiler_params=big,
        name="pack",
    )(me, in_hbm(mol_feats), in_hbm(jnp.transpose(grad_blocks[0], (2, 0, 1))))
    below = lax.ppermute(top, "space", up)
    above = lax.ppermute(low, "space", down)
    late = lax.dynamic_index_in_dim(grad_blocks[0], me[0], 0, keepdims=False)[half:]
    own = jnp.pad(late.T, ((0, groups * rows - entries), (0, LANES - half)))
    if linked:
        other = swap(odd, 0, slabs)
        other, below, above, own = lax.optimization_barrier((other, below, above, own))
        quarter = slabs // 4
        mixed = [pair for k in range(1, quarter) for pair in ((quarter + k - 1, k), (k, quarter + k - 1))]
        turns = [(0, 0), *mixed, (2 * quarter - 1, 2 * quarter - 1)]
        messages = pl.pallas_call(
            functools.partial(join_kernel, turns),
            out_shape=(jax.ShapeDtypeStruct((2, rows, LANES), BF16),) * (slabs // 2),
            in_specs=[smem] + vmem(2),
            out_specs=tuple(vmem(slabs // 2)),
            compiler_params=big,
            name="join",
        )(me, even, other)
        came = [messages[0]]
        for turn in range(1, 2 * quarter):
            route = [(i, i ^ (2 * turns[turn][i % 2])) for i in range(slabs)]
            came.append(lax.ppermute(messages[turn], "space", route))
        for turn in range(1, quarter - 1):
            came[turn], below, above, me = lax.optimization_barrier((came[turn], below, above, me))
        ids = [(2 * first + j, 2 * second + j) for first, second in turns for j in range(2)]
        near, far = tuple(ids[: 2 * quarter]), tuple(ids[2 * quarter :])
        came_near, came_far = came[:quarter], came[quarter:]
    else:
        packed = jnp.stack([even, odd], axis=1).reshape(slabs, rows, LANES)
        near, far = (), tuple(range(slabs))
        came_near = []
        came_far = [lax.all_to_all(packed, "space", split_axis=0, concat_axis=0, tiled=True)]
    far_slots = len(far) * half
    near_slots = slots - far_slots

    wide = mols + 2 * reach
    entries_wide = groups * rows
    pieces = len(slot_tiles(near_slots)) + len(slot_tiles(far_slots))
    onehot, slope, ext, near_hidden, far_hidden, w_out_wide = pl.pallas_call(
        functools.partial(edge_kernel, half, linked, near, far),
        out_shape=(
            pltpu.HBM((mols + wide, slots), BF16),
            pltpu.HBM((width, slots), F32),
            pltpu.HBM((width, wide), BF16),
            jax.ShapeDtypeStruct((width, near_slots), BF16),
            jax.ShapeDtypeStruct((width, far_slots), BF16),
            jax.ShapeDtypeStruct((width, entries_wide), BF16),
        ),
        in_specs=[smem] + [hbm] * 4 + vmem(5),
        out_specs=(hbm,) * 3 + tuple(vmem(3)),
        scratch_shapes=[
            pltpu.VMEM((mols + wide, slots), BF16),
            pltpu.VMEM((width, slots), F32),
            pltpu.VMEM((width, wide), BF16),
            pltpu.VMEM((entries_wide, width), BF16),
            pltpu.VMEM((mols, width), BF16),
            pltpu.VMEM((width, width), BF16),
            pltpu.VMEM((width, width), BF16),
            pltpu.VMEM((entries, width), BF16),
            pltpu.SemaphoreType.DMA((2 * pieces + 1,)),
            pltpu.SemaphoreType.DMA((4,)),
        ],
        compiler_params=big,
        name="edges",
        cost_estimate=pl.CostEstimate(
            flops=40 * width * slots * 2 * (2 * mols + 2 * reach), bytes_accessed=8 * 1024 * 1024,
            transcendentals=width * slots,
        ),
    )(
        me, in_hbm(mol_feats), in_hbm(w_src), in_hbm(w_dst), in_hbm(w_out.T), below, above,
        edge_src.reshape(slabs, cap), edge_dst.reshape(slabs, cap), edge_live.reshape(slabs, cap),
    )
    onehot, slope, ext = in_hbm(onehot), in_hbm(slope), in_hbm(ext)

    def chunks(count, lanes, dtype):
        return jax.ShapeDtypeStruct((count, part, lanes), dtype)

    near_sums, near_outer = pl.pallas_call(
        functools.partial(near_kernel, half),
        out_shape=(
            pltpu.HBM((mols + wide, width), F32),
            pltpu.HBM((width, entries_wide), F32),
        ),
        in_specs=vmem(3) + [hbm] * 2 + vmem(len(came_near)),
        out_specs=(hbm, hbm),
        scratch_shapes=[
            pltpu.VMEM((entries_wide, near_slots), BF16),
            pltpu.VMEM((width, near_slots), F32),
            pltpu.VMEM((mols + wide, near_slots), BF16),
            pltpu.VMEM((mols + wide, width), F32),
            pltpu.VMEM((width, entries_wide), F32),
            pltpu.SemaphoreType.DMA((len(slot_tiles(near_slots)), 2)),
            pltpu.SemaphoreType.DMA((2,)),
        ],
        compiler_params=big,
        name="near",
        cost_estimate=pl.CostEstimate(
            flops=40 * width * near_slots * entries_wide, bytes_accessed=6 * 1024 * 1024, transcendentals=0
        ),
    )(own, w_out_wide, near_hidden, slope, onehot, *came_near)
    near_sums, near_outer = in_hbm(near_sums), in_hbm(near_outer)
    keep, send, sums, lower, upper, g = pl.pallas_call(
        functools.partial(grad_kernel, half, factor),
        out_shape=(
            chunks(slabs // 2, 2 * width, F32),
            chunks(slabs // 2, 2 * width, BF16),
            jax.ShapeDtypeStruct((2 * mols, width), F32),
            jax.ShapeDtypeStruct((reach, width), BF16),
            jax.ShapeDtypeStruct((reach, width), BF16),
            jax.ShapeDtypeStruct((entries_wide, far_slots), BF16),
        ),
        in_specs=[smem] + vmem(1) + [hbm] * 4 + vmem(len(came_far)),
        out_specs=tuple(vmem(6)),
        scratch_shapes=[
            pltpu.VMEM((width, far_slots), F32),
            pltpu.VMEM((mols + wide, far_slots), BF16),
            pltpu.VMEM((width, wide), BF16),
            pltpu.VMEM((mols + wide, width), F32),
            pltpu.SemaphoreType.DMA((len(slot_tiles(far_slots)), 2)),
            pltpu.SemaphoreType.DMA((2,)),
        ],
        compiler_params=big,
        name="grads",
    )(me, w_out_wide, slope, onehot, ext, near_sums, *came_far)
    lanes = round_up(entries_wide, LANES)
    keep_o, send_o = pl.pallas_call(
        functools.partial(outer_kernel, factor),
        out_shape=(chunks(slabs // 2, lanes, F32), chunks(slabs // 2, lanes, BF16)),
        in_specs=[smem] + vmem(2) + [hbm],
        out_specs=tuple(vmem(2)),
        scratch_shapes=[pltpu.VMEM((width, entries_wide), F32), pltpu.SemaphoreType.DMA(())],
        compiler_params=big,
        name="outer",
        cost_estimate=pl.CostEstimate(
            flops=40 * width * slots * entries_wide, bytes_accessed=4 * 1024 * 1024, transcendentals=0
        ),
    )(me, far_hidden, g, near_outer)

    def fold(bit, place, keep, crossed):
        shape = (keep.shape[0] // 2, keep.shape[2])
        return pl.pallas_call(
            functools.partial(fold_kernel, bit, place),
            out_shape=(chunks(*shape, F32), chunks(*shape, BF16)),
            in_specs=[smem] + vmem(2),
            out_specs=tuple(vmem(2)),
            compiler_params=big,
            name="fold",
        )(me, keep, crossed)

    def close(keep, crossed):
        if rest == 1:
            return [keep, crossed]
        sends = pl.pallas_call(
            close_kernel,
            out_shape=chunks(rest, keep.shape[2], BF16),
            in_specs=vmem(2),
            out_specs=vmem(1)[0],
            compiler_params=big,
            name="close",
        )(keep, crossed)
        same = [[low + rank * (slabs // rest) for rank in range(rest)] for low in range(slabs // rest)]
        return [
            lax.all_to_all(sends, "space", split_axis=0, concat_axis=0, tiled=True, axis_index_groups=same)
        ]

    from_above = lax.ppermute(lower, "space", down)
    from_below = lax.ppermute(upper, "space", up)
    crossed = swap(send, 0, slabs)
    crossed_o = swap(send_o, 0, slabs)
    for (bit, place), (bit_o, place_o) in zip(paths[0][1:], paths[1][1:]):
        if bit == 2:
            keep, crossed, from_above, from_below = lax.optimization_barrier((keep, crossed, from_above, from_below))
        keep, send = fold(bit, place, keep, crossed)
        crossed = swap(send, bit, slabs)
        keep_o, crossed_o, _ = lax.optimization_barrier((keep_o, crossed_o, send))
        keep_o, send_o = fold(bit_o, place_o, keep_o, crossed_o)
        crossed_o = swap(send_o, bit_o, slabs)
    terms = close(keep, crossed)
    terms_o = close(keep_o, crossed_o)
    feature_grad = pl.pallas_call(
        rim_kernel,
        out_shape=jax.ShapeDtypeStruct((mols, width), F32),
        in_specs=vmem(5),
        out_specs=vmem(1)[0],
        compiler_params=big,
        name="rims",
        cost_estimate=pl.CostEstimate(flops=2 * width * slots * width * 40, bytes_accessed=4 * 1024 * 1024, transcendentals=0),
    )(sums, from_below, from_above, w_src, w_dst)
    src_grad, dst_grad, out_grad = pl.pallas_call(
        total_kernel,
        out_shape=(
            jax.ShapeDtypeStruct((part, width), F32),
            jax.ShapeDtypeStruct((part, width), F32),
            jax.ShapeDtypeStruct((part, entries), F32),
        ),
        in_specs=vmem(len(terms) + len(terms_o)),
        out_specs=tuple(vmem(3)),
        compiler_params=big,
        name="totals",
    )(*terms, *terms_o)
    return (feature_grad, src_grad, dst_grad, out_grad)


def solution(mesh):
    placed = (
        P(("groups", "space"), None),
        P(),
        P(),
        P(),
        P("space", "groups", None, None),
        P(("groups", "space")),
        P(("groups", "space")),
        P(("groups", "space")),
    )
    return jax.shard_map(
        on_device,
        mesh=mesh,
        in_specs=placed,
        out_specs=(
            P(("groups", "space"), None),
            P(("groups", "space"), None),
            P(("groups", "space"), None),
            P(("groups", "space"), None),
        ),
        check_vma=False,
    )
```

```python
import functools

import jax
import jax.numpy as jnp
from jax import lax
from jax.experimental import pallas as pl
from jax.experimental.pallas import tpu as pltpu
from jax.sharding import PartitionSpec as P

F32 = jnp.float32
BF16 = jnp.bfloat16
LANES = 128
PACK = 16
NN = (((1,), (0,)), ((), ()))
NT = (((1,), (1,)), ((), ()))


def mm(left, right, dims=NN):
    return lax.dot_general(left, right, dims, preferred_element_type=F32)


def halves(x):
    high = x.astype(BF16)
    return high, (x - high.astype(F32)).astype(BF16)


def round_up(x, to):
    return -(-x // to) * to


def vmem(count):
    return [pl.BlockSpec(memory_space=pltpu.VMEM)] * count


def pack_kernel(rows, half, linked, me_ref, feats_ref, g_ref, even_ref, odd_ref, low_ref, top_ref, here_ref, sems, rim_sems):
    entries, slabs, cap = g_ref.shape
    mols = feats_ref.shape[0]
    reach = low_ref.shape[0]
    groups = LANES // half
    blocks = rows // PACK
    count = sems.shape[0]
    stages = []
    for stage in range(count):
        begin, end = stage * blocks // count, (stage + 1) * blocks // count
        copies = []
        for group in range(groups):
            first = min(entries, group * rows + begin * PACK)
            last = min(entries, group * rows + end * PACK)
            if first < last:
                copies.append(
                    pltpu.make_async_copy(g_ref.at[first:last], here_ref.at[first:last], sems.at[stage, group])
                )
        stages.append((begin, end, copies))
        for copy in copies:
            copy.start()
    rims = [
        pltpu.make_async_copy(feats_ref.at[:reach], low_ref, rim_sems.at[0]),
        pltpu.make_async_copy(feats_ref.at[mols - reach :], top_ref, rim_sems.at[1]),
    ]
    for copy in rims:
        copy.start()
    size = PACK * slabs
    to = lax.broadcasted_iota(jnp.int32, (size, size), 0)
    source = lax.broadcasted_iota(jnp.int32, (size, size), 1)
    slab = to // PACK
    if linked:
        slab = slab ^ me_ref[0]
    perm = jnp.where((to % PACK) * slabs + slab == source, 1.0, 0.0).astype(BF16)

    def lanes_of(block):
        early = []
        for group in range(groups):
            first = group * rows + block * PACK
            valid = max(0, min(PACK, entries - first))
            tiles = []
            if valid:
                tiles.append(here_ref[first : first + valid])
            if valid < PACK:
                tiles.append(jnp.zeros((PACK - valid, slabs, cap), BF16))
            tile = tiles[0] if len(tiles) == 1 else jnp.concatenate(tiles, axis=0)
            early.append(tile.reshape(size, cap)[:, :half])
        return early

    for begin, end, copies in stages:
        for copy in copies:
            copy.wait()
        for block in range(begin, end, 2):
            together = range(block, min(block + 2, end))
            lanes = [piece for one in together for piece in lanes_of(one)]
            moved = mm(perm, jnp.concatenate(lanes, axis=1)).astype(BF16)
            for index, one in enumerate(together):
                chunk = moved[:, index * LANES : (index + 1) * LANES].reshape(slabs // 2, 2, PACK, LANES)
                here = pl.ds(one * PACK, PACK)
                even_ref[:, here, :] = chunk[:, 0]
                odd_ref[:, here, :] = chunk[:, 1]
    for copy in rims:
        copy.wait()


def by_core(pair, me):
    return pair[0] + (me % 2) * (pair[1] - pair[0])


def join_kernel(turns, me_ref, even_ref, other_ref, *message_refs):
    for pair, message_ref in zip(turns, message_refs):
        k = by_core(pair, me_ref[0])
        message_ref[0] = even_ref[k]
        message_ref[1] = other_ref[k]


def unpack(half, refs, g_ref):
    groups = LANES // half
    rows = g_ref.shape[0] // groups
    chunks = [(ref, index) for ref in refs for index in range(ref.shape[0])]
    tiles = len(chunks) // groups
    for tile in range(tiles):
        here = [ref[index] for ref, index in chunks[tile * groups : (tile + 1) * groups]]
        for group in range(groups):
            lanes = slice(group * half, (group + 1) * half)
            g_ref[group * rows : (group + 1) * rows, tile * LANES : (tile + 1) * LANES] = jnp.concatenate(
                [chunk[:, lanes] for chunk in here], axis=1
            )
    return tiles * LANES


def slot_rows(ref, me, half, linked, near, far):
    per = LANES // half

    def rows_of(ids):
        rows = []
        for tile in range(len(ids) // per):
            here = ids[tile * per : (tile + 1) * per]
            pieces = [ref[pl.ds(me ^ by_core(i, me) if linked else i, 1), :] for i in here]
            rows.append(jnp.concatenate([piece[:, :half] for piece in pieces], axis=1))
        return rows

    own = ref[pl.ds(me, 1), :][:, half:]
    own = jnp.concatenate([own, jnp.full((1, LANES - half), -1, jnp.int32)], axis=1)
    return rows_of(near) + [own] + rows_of(far)


def edge_kernel(
    half, linked, near, far, me_ref, feats_hbm, w_src_hbm, w_dst_hbm, w_out_hbm, below_ref, above_ref, src_ref, dst_ref,
    live_ref, onehot_hbm, slope_hbm, ext_hbm, near_hidden_ref, far_hidden_ref, w_wide_ref,
    onehot_ref, slope_ref, ext_ref, w_rows_ref, feats_ref, w_src_ref, w_dst_ref, w_out_ref, sems, in_sems,
):
    inputs = [
        pltpu.make_async_copy(hbm, ref, in_sems.at[index])
        for index, (hbm, ref) in enumerate(
            ((feats_hbm, feats_ref), (w_src_hbm, w_src_ref), (w_dst_hbm, w_dst_ref), (w_out_hbm, w_out_ref))
        )
    ]
    for copy in inputs:
        copy.start()
    me = me_ref[0]
    mols = feats_ref.shape[0]
    reach = below_ref.shape[0]
    wide = mols + 2 * reach
    slots = slope_ref.shape[1]
    entries = w_out_ref.shape[0]
    near_slots = near_hidden_ref.shape[1]
    copies = []

    def send(source, target):
        copy = pltpu.make_async_copy(source, target, sems.at[len(copies)])
        copy.start()
        copies.append(copy)

    mol_src = lax.broadcasted_iota(jnp.int32, (mols, LANES), 0)
    mol_dst = lax.broadcasted_iota(jnp.int32, (wide, LANES), 0)
    lists = [slot_rows(ref, me, half, linked, near, far) for ref in (src_ref, dst_ref, live_ref)]
    for tile, (src, dst, live) in enumerate(zip(*lists)):
        src = jnp.where(live > 0, src, -1)
        moved = jnp.where(dst < reach, dst + mols, jnp.where(dst < reach + mols, dst - reach, dst))
        dst = jnp.where(live > 0, moved, -1)
        one_src = jnp.where(mol_src == src, 1.0, 0.0).astype(BF16)
        one_dst = jnp.where(mol_dst == dst, 1.0, 0.0).astype(BF16)
        here = pl.ds(tile * LANES, LANES)
        onehot_ref[:, here] = jnp.concatenate([one_src, one_dst], axis=0)
    for copy in inputs[:3]:
        copy.wait()
    feats = feats_ref[...]
    ext = jnp.concatenate([feats, below_ref[...], above_ref[...]], axis=0)
    ext_ref[...] = ext.T
    send(ext_ref, ext_hbm)
    proj_src = mm(feats, w_src_ref[...])
    proj_dst = mm(ext, w_dst_ref[...])
    proj = jnp.concatenate([proj_src, proj_dst], axis=0).T
    high, low = halves(proj)
    for first, last in slot_tiles(near_slots) + [(near_slots + f, near_slots + l) for f, l in slot_tiles(slots - near_slots)]:
        here = pl.ds(first, last - first)
        send(onehot_ref.at[:, here], onehot_hbm.at[:, here])
        onehot = onehot_ref[:, here]
        pre = mm(high, onehot) + mm(low, onehot)
        sigma = 1.0 / (1.0 + jnp.exp(-pre))
        hidden = (pre * sigma).astype(BF16)
        if first < near_slots:
            near_hidden_ref[:, here] = hidden
        else:
            far_hidden_ref[:, pl.ds(first - near_slots, last - first)] = hidden
        slope_ref[:, here] = sigma * (1.0 + pre * (1.0 - sigma))
        send(slope_ref.at[:, here], slope_hbm.at[:, here])
    inputs[3].wait()
    whole = entries // LANES * LANES
    w_rows_ref[whole:] = jnp.zeros((w_rows_ref.shape[0] - whole, w_rows_ref.shape[1]), BF16)
    w_rows_ref[:whole] = w_out_ref[:whole]
    w_rows_ref[whole:entries] = w_out_ref[whole:]
    w_wide_ref[...] = w_rows_ref[...].T
    for copy in copies:
        copy.wait()


def halve(terms, odd, place, keep_ref, send_ref, first):
    count, rows, _ = keep_ref.shape
    width = terms.shape[-1]
    lanes = slice(first, first + width)
    inner = 1 << place
    pairs = terms.reshape(count // inner, 2, inner, rows, width)
    even_part = pairs[:, 0].reshape(count, rows, width)
    odd_part = pairs[:, 1].reshape(count, rows, width)
    keep_ref[:, :, lanes] = jnp.where(odd > 0, odd_part, even_part)
    send_ref[:, :, lanes] = jnp.where(odd > 0, even_part, odd_part).astype(BF16)


def fold_kernel(bit, place, me_ref, keep_ref, came_ref, next_ref, send_ref):
    odd = (me_ref[0] >> bit) % 2
    halve(keep_ref[...] + came_ref[...].astype(F32), odd, place, next_ref, send_ref, 0)


def close_kernel(keep_ref, came_ref, send_ref):
    send_ref[...] = (keep_ref[...] + came_ref[...].astype(F32)).astype(BF16)


def slot_tiles(slots):
    step = 2 * LANES
    return [(first, min(first + step, slots)) for first in range(0, slots, step)]


def start_tiles(slots, offset, slope_hbm, onehot_hbm, slope_ref, onehot_ref, sems):
    tiles = []
    for tile, (first, last) in enumerate(slot_tiles(slots)):
        there, here = pl.ds(offset + first, last - first), pl.ds(first, last - first)
        copies = [
            pltpu.make_async_copy(slope_hbm.at[:, there], slope_ref.at[:, here], sems.at[tile, 0]),
            pltpu.make_async_copy(onehot_hbm.at[:, there], onehot_ref.at[:, here], sems.at[tile, 1]),
        ]
        for copy in copies:
            copy.start()
        tiles.append((slice(first, last), copies))
    return tiles


def sum_edges(tiles, w_out_ref, g_ref, slope_ref, onehot_ref):
    sums = None
    for lanes, copies in tiles:
        dh = mm(w_out_ref[...], g_ref[:, lanes])
        for copy in copies:
            copy.wait()
        dpre = (dh * slope_ref[:, lanes]).astype(BF16)
        term = mm(onehot_ref[:, lanes], dpre, NT)
        sums = term if sums is None else sums + term
    return sums


def near_kernel(half, own_ref, w_out_ref, hidden_ref, slope_hbm, onehot_hbm, *rest):
    *came_refs, sums_hbm, outer_hbm, g_ref, slope_ref, onehot_ref, sums_ref, outer_ref, sems, out_sems = rest
    slots = g_ref.shape[1]
    tiles = start_tiles(slots, 0, slope_hbm, onehot_hbm, slope_ref, onehot_ref, sems)
    filled = unpack(half, came_refs, g_ref)
    g_ref[:, filled:] = own_ref[...]
    outer_ref[...] = mm(hidden_ref[...], g_ref[...], NT)
    outer_copy = pltpu.make_async_copy(outer_ref, outer_hbm, out_sems.at[0])
    outer_copy.start()
    sums_ref[...] = sum_edges(tiles, w_out_ref, g_ref, slope_ref, onehot_ref)
    sums_copy = pltpu.make_async_copy(sums_ref, sums_hbm, out_sems.at[1])
    sums_copy.start()
    outer_copy.wait()
    sums_copy.wait()


def grad_kernel(half, factor, me_ref, w_out_ref, slope_hbm, onehot_hbm, ext_hbm, near_hbm, *rest):
    (
        *came_refs, keep_ref, send_ref, sums_ref, lower_ref, upper_ref, g_ref,
        slope_ref, onehot_ref, ext_ref, near_ref, tile_sems, sems,
    ) = rest
    odd = me_ref[0] % 2
    width = w_out_ref.shape[0]
    slots = g_ref.shape[1]
    inside = sums_ref.shape[0]
    mols = inside // 2
    reach = lower_ref.shape[0]
    tiles = start_tiles(slots, slope_hbm.shape[1] - slots, slope_hbm, onehot_hbm, slope_ref, onehot_ref, tile_sems)
    whole = [
        pltpu.make_async_copy(near_hbm, near_ref, sems.at[0]),
        pltpu.make_async_copy(ext_hbm, ext_ref, sems.at[1]),
    ]
    for copy in whole:
        copy.start()
    unpack(half, came_refs, g_ref)
    sums = sum_edges(tiles, w_out_ref, g_ref, slope_ref, onehot_ref)
    for copy in whole:
        copy.wait()
    sums = sums + near_ref[...]
    lower_ref[...] = sums[inside : inside + reach].astype(BF16)
    upper_ref[...] = sums[inside + reach :].astype(BF16)
    sums_ref[...] = sums[:inside]
    high, low = halves(sums)
    feats = ext_ref[:, :mols]
    rim = ext_ref[:, mols:]
    halve(factor * (mm(feats, high[:mols]) + mm(feats, low[:mols])), odd, 0, keep_ref, send_ref, 0)
    rim_term = mm(jnp.concatenate([rim, rim], axis=1), jnp.concatenate([high[inside:], low[inside:]], axis=0))
    dst_term = mm(feats, high[mols:inside]) + mm(feats, low[mols:inside]) + rim_term
    halve(factor * dst_term, odd, 0, keep_ref, send_ref, width)


def outer_kernel(factor, me_ref, hidden_ref, g_ref, near_hbm, keep_ref, send_ref, near_ref, sem):
    copy = pltpu.make_async_copy(near_hbm, near_ref, sem)
    copy.start()
    term = mm(hidden_ref[...], g_ref[...], NT)
    copy.wait()
    term = factor * (term + near_ref[...])
    padding = keep_ref.shape[2] - term.shape[1]
    if padding > 0:
        term = jnp.concatenate([term, jnp.zeros((term.shape[0], padding), F32)], axis=1)
    halve(term, me_ref[0] % 2, 0, keep_ref, send_ref, 0)


def rim_kernel(sums_ref, from_below_ref, from_above_ref, w_src_ref, w_dst_ref, out_ref):
    mols = out_ref.shape[0]
    reach = from_below_ref.shape[0]
    src = sums_ref[:mols]
    dst = sums_ref[mols:]
    dst = jnp.concatenate(
        [
            dst[:reach] + from_below_ref[...].astype(F32),
            dst[reach : mols - reach],
            dst[mols - reach :] + from_above_ref[...].astype(F32),
        ],
        axis=0,
    )
    w_src = w_src_ref[...]
    w_dst = w_dst_ref[...]
    src_high, src_low = halves(src)
    dst_high, dst_low = halves(dst)
    out_ref[...] = mm(src_high, w_src, NT) + mm(src_low, w_src, NT) + mm(dst_high, w_dst, NT) + mm(dst_low, w_dst, NT)


def total_kernel(*refs):
    *refs, src_ref, dst_ref, out_ref = refs
    count = len(refs) // 2
    width = src_ref.shape[1]
    totals = []
    for piece in (refs[:count], refs[count:]):
        terms = [ref[slab].astype(F32) for ref in piece for slab in range(ref.shape[0])]
        totals.append(functools.reduce(jnp.add, terms))
    sides, outer = totals
    src_ref[...] = sides[:, :width]
    dst_ref[...] = sides[:, width:]
    out_ref[...] = outer[:, : out_ref.shape[1]]


def in_hbm(x):
    return pltpu.with_memory_space_constraint(x, pltpu.HBM)


def swap(block, bit, slabs):
    return lax.ppermute(block, "space", [(i, i ^ (1 << bit)) for i in range(slabs)])


def on_device(mol_feats, w_src, w_dst, w_out, grad_blocks, edge_src, edge_dst, edge_live):
    slabs = lax.axis_size("space")
    mols, width = mol_feats.shape
    entries = w_out.shape[1]
    cap = grad_blocks.shape[2]
    half = cap // 2
    reach = mols // 4
    groups = LANES // half
    slots = (slabs // groups + 1) * LANES
    bits = slabs.bit_length() - 1
    if 3 <= bits <= 4:
        late_bits = tuple((bit, 0) for bit in range(3, bits))
        paths = (((0, 0), (1, 0), (2, 0)) + late_bits, ((0, 0), (2, 1), (1, 0)) + late_bits)
    else:
        paths = (tuple((bit, 0) for bit in range(min(bits, 2))),) * 2
    rest = slabs >> len(paths[0])
    part = width // slabs
    factor = float(edge_src.shape[0] * slabs) ** (-0.5)
    me = lax.axis_index("space").astype(jnp.int32).reshape(1)
    smem = pl.BlockSpec(memory_space=pltpu.SMEM)
    hbm = pl.BlockSpec(memory_space=pltpu.HBM)
    big = pltpu.CompilerParams(vmem_limit_bytes=24 * 1024 * 1024)
    up = [(i, (i + 1) % slabs) for i in range(slabs)]
    down = [((i + 1) % slabs, i) for i in range(slabs)]

    rows = round_up(pl.cdiv(entries, groups), PACK)
    stages = 4
    linked = slabs <= 16
    even, odd, low, top = pl.pallas_call(
        functools.partial(pack_kernel, rows, half, linked),
        out_shape=(
            jax.ShapeDtypeStruct((slabs // 2, rows, LANES), BF16),
            jax.ShapeDtypeStruct((slabs // 2, rows, LANES), BF16),
            jax.ShapeDtypeStruct((reach, width), BF16),
            jax.ShapeDtypeStruct((reach, width), BF16),
        ),
        in_specs=[smem, hbm, hbm],
        out_specs=tuple(vmem(4)),
        scratch_shapes=[
            pltpu.VMEM((entries, slabs, cap), BF16),
            pltpu.SemaphoreType.DMA((stages, groups)),
            pltpu.SemaphoreType.DMA((2,)),
        ],
        compiler_params=big,
        name="pack",
    )(me, in_hbm(mol_feats), in_hbm(jnp.transpose(grad_blocks[0], (2, 0, 1))))
    below = lax.ppermute(top, "space", up)
    above = lax.ppermute(low, "space", down)
    late = lax.dynamic_index_in_dim(grad_blocks[0], me[0], 0, keepdims=False)[half:]
    own = jnp.pad(late.T, ((0, groups * rows - entries), (0, LANES - half)))
    if linked:
        other = swap(odd, 0, slabs)
        other, below, above, own = lax.optimization_barrier((other, below, above, own))
        quarter = slabs // 4
        mixed = [pair for k in range(1, quarter) for pair in ((quarter + k - 1, k), (k, quarter + k - 1))]
        turns = [(0, 0), *mixed, (2 * quarter - 1, 2 * quarter - 1)]
        messages = pl.pallas_call(
            functools.partial(join_kernel, turns),
            out_shape=(jax.ShapeDtypeStruct((2, rows, LANES), BF16),) * (slabs // 2),
            in_specs=[smem] + vmem(2),
            out_specs=tuple(vmem(slabs // 2)),
            compiler_params=big,
            name="join",
        )(me, even, other)
        came = [messages[0]]
        for turn in range(1, 2 * quarter):
            route = [(i, i ^ (2 * turns[turn][i % 2])) for i in range(slabs)]
            came.append(lax.ppermute(messages[turn], "space", route))
        ids = [(2 * first + j, 2 * second + j) for first, second in turns for j in range(2)]
        near, far = tuple(ids[: 2 * quarter]), tuple(ids[2 * quarter :])
        came_near, came_far = came[:quarter], came[quarter:]
    else:
        packed = jnp.stack([even, odd], axis=1).reshape(slabs, rows, LANES)
        near, far = (), tuple(range(slabs))
        came_near = []
        came_far = [lax.all_to_all(packed, "space", split_axis=0, concat_axis=0, tiled=True)]
    far_slots = len(far) * half
    near_slots = slots - far_slots

    wide = mols + 2 * reach
    entries_wide = groups * rows
    pieces = len(slot_tiles(near_slots)) + len(slot_tiles(far_slots))
    onehot, slope, ext, near_hidden, far_hidden, w_out_wide = pl.pallas_call(
        functools.partial(edge_kernel, half, linked, near, far),
        out_shape=(
            pltpu.HBM((mols + wide, slots), BF16),
            pltpu.HBM((width, slots), F32),
            pltpu.HBM((width, wide), BF16),
            jax.ShapeDtypeStruct((width, near_slots), BF16),
            jax.ShapeDtypeStruct((width, far_slots), BF16),
            jax.ShapeDtypeStruct((width, entries_wide), BF16),
        ),
        in_specs=[smem] + [hbm] * 4 + vmem(5),
        out_specs=(hbm,) * 3 + tuple(vmem(3)),
        scratch_shapes=[
            pltpu.VMEM((mols + wide, slots), BF16),
            pltpu.VMEM((width, slots), F32),
            pltpu.VMEM((width, wide), BF16),
            pltpu.VMEM((entries_wide, width), BF16),
            pltpu.VMEM((mols, width), BF16),
            pltpu.VMEM((width, width), BF16),
            pltpu.VMEM((width, width), BF16),
            pltpu.VMEM((entries, width), BF16),
            pltpu.SemaphoreType.DMA((2 * pieces + 1,)),
            pltpu.SemaphoreType.DMA((4,)),
        ],
        compiler_params=big,
        name="edges",
        cost_estimate=pl.CostEstimate(
            flops=40 * width * slots * 2 * (2 * mols + 2 * reach), bytes_accessed=8 * 1024 * 1024,
            transcendentals=width * slots,
        ),
    )(
        me, in_hbm(mol_feats), in_hbm(w_src), in_hbm(w_dst), in_hbm(w_out.T), below, above,
        edge_src.reshape(slabs, cap), edge_dst.reshape(slabs, cap), edge_live.reshape(slabs, cap),
    )
    onehot, slope, ext = in_hbm(onehot), in_hbm(slope), in_hbm(ext)

    def chunks(count, lanes, dtype):
        return jax.ShapeDtypeStruct((count, part, lanes), dtype)

    near_sums, near_outer = pl.pallas_call(
        functools.partial(near_kernel, half),
        out_shape=(
            pltpu.HBM((mols + wide, width), F32),
            pltpu.HBM((width, entries_wide), F32),
        ),
        in_specs=vmem(3) + [hbm] * 2 + vmem(len(came_near)),
        out_specs=(hbm, hbm),
        scratch_shapes=[
            pltpu.VMEM((entries_wide, near_slots), BF16),
            pltpu.VMEM((width, near_slots), F32),
            pltpu.VMEM((mols + wide, near_slots), BF16),
            pltpu.VMEM((mols + wide, width), F32),
            pltpu.VMEM((width, entries_wide), F32),
            pltpu.SemaphoreType.DMA((len(slot_tiles(near_slots)), 2)),
            pltpu.SemaphoreType.DMA((2,)),
        ],
        compiler_params=big,
        name="near",
        cost_estimate=pl.CostEstimate(
            flops=40 * width * near_slots * entries_wide, bytes_accessed=6 * 1024 * 1024, transcendentals=0
        ),
    )(own, w_out_wide, near_hidden, slope, onehot, *came_near)
    near_sums, near_outer = in_hbm(near_sums), in_hbm(near_outer)
    keep, send, sums, lower, upper, g = pl.pallas_call(
        functools.partial(grad_kernel, half, factor),
        out_shape=(
            chunks(slabs // 2, 2 * width, F32),
            chunks(slabs // 2, 2 * width, BF16),
            jax.ShapeDtypeStruct((2 * mols, width), F32),
            jax.ShapeDtypeStruct((reach, width), BF16),
            jax.ShapeDtypeStruct((reach, width), BF16),
            jax.ShapeDtypeStruct((entries_wide, far_slots), BF16),
        ),
        in_specs=[smem] + vmem(1) + [hbm] * 4 + vmem(len(came_far)),
        out_specs=tuple(vmem(6)),
        scratch_shapes=[
            pltpu.VMEM((width, far_slots), F32),
            pltpu.VMEM((mols + wide, far_slots), BF16),
            pltpu.VMEM((width, wide), BF16),
            pltpu.VMEM((mols + wide, width), F32),
            pltpu.SemaphoreType.DMA((len(slot_tiles(far_slots)), 2)),
            pltpu.SemaphoreType.DMA((2,)),
        ],
        compiler_params=big,
        name="grads",
    )(me, w_out_wide, slope, onehot, ext, near_sums, *came_far)
    lanes = round_up(entries_wide, LANES)
    keep_o, send_o = pl.pallas_call(
        functools.partial(outer_kernel, factor),
        out_shape=(chunks(slabs // 2, lanes, F32), chunks(slabs // 2, lanes, BF16)),
        in_specs=[smem] + vmem(2) + [hbm],
        out_specs=tuple(vmem(2)),
        scratch_shapes=[pltpu.VMEM((width, entries_wide), F32), pltpu.SemaphoreType.DMA(())],
        compiler_params=big,
        name="outer",
        cost_estimate=pl.CostEstimate(
            flops=40 * width * slots * entries_wide, bytes_accessed=4 * 1024 * 1024, transcendentals=0
        ),
    )(me, far_hidden, g, near_outer)

    def fold(bit, place, keep, crossed):
        shape = (keep.shape[0] // 2, keep.shape[2])
        return pl.pallas_call(
            functools.partial(fold_kernel, bit, place),
            out_shape=(chunks(*shape, F32), chunks(*shape, BF16)),
            in_specs=[smem] + vmem(2),
            out_specs=tuple(vmem(2)),
            compiler_params=big,
            name="fold",
        )(me, keep, crossed)

    def close(keep, crossed):
        if rest == 1:
            return [keep, crossed]
        sends = pl.pallas_call(
            close_kernel,
            out_shape=chunks(rest, keep.shape[2], BF16),
            in_specs=vmem(2),
            out_specs=vmem(1)[0],
            compiler_params=big,
            name="close",
        )(keep, crossed)
        same = [[low + rank * (slabs // rest) for rank in range(rest)] for low in range(slabs // rest)]
        return [
            lax.all_to_all(sends, "space", split_axis=0, concat_axis=0, tiled=True, axis_index_groups=same)
        ]

    from_above = lax.ppermute(lower, "space", down)
    from_below = lax.ppermute(upper, "space", up)
    crossed = swap(send, 0, slabs)
    crossed_o = swap(send_o, 0, slabs)
    for (bit, place), (bit_o, place_o) in zip(paths[0][1:], paths[1][1:]):
        if bit == 2:
            keep, crossed, from_above, from_below = lax.optimization_barrier((keep, crossed, from_above, from_below))
        keep, send = fold(bit, place, keep, crossed)
        crossed = swap(send, bit, slabs)
        keep_o, crossed_o, _ = lax.optimization_barrier((keep_o, crossed_o, send))
        keep_o, send_o = fold(bit_o, place_o, keep_o, crossed_o)
        crossed_o = swap(send_o, bit_o, slabs)
    terms = close(keep, crossed)
    terms_o = close(keep_o, crossed_o)
    feature_grad = pl.pallas_call(
        rim_kernel,
        out_shape=jax.ShapeDtypeStruct((mols, width), F32),
        in_specs=vmem(5),
        out_specs=vmem(1)[0],
        compiler_params=big,
        name="rims",
        cost_estimate=pl.CostEstimate(flops=2 * width * slots * width * 40, bytes_accessed=4 * 1024 * 1024, transcendentals=0),
    )(sums, from_below, from_above, w_src, w_dst)
    src_grad, dst_grad, out_grad = pl.pallas_call(
        total_kernel,
        out_shape=(
            jax.ShapeDtypeStruct((part, width), F32),
            jax.ShapeDtypeStruct((part, width), F32),
            jax.ShapeDtypeStruct((part, entries), F32),
        ),
        in_specs=vmem(len(terms) + len(terms_o)),
        out_specs=tuple(vmem(3)),
        compiler_params=big,
        name="totals",
    )(*terms, *terms_o)
    return (feature_grad, src_grad, dst_grad, out_grad)


def solution(mesh):
    placed = (
        P(("groups", "space"), None),
        P(),
        P(),
        P(),
        P("space", "groups", None, None),
        P(("groups", "space")),
        P(("groups", "space")),
        P(("groups", "space")),
    )
    return jax.shard_map(
        on_device,
        mesh=mesh,
        in_specs=placed,
        out_specs=(
            P(("groups", "space"), None),
            P(("groups", "space"), None),
            P(("groups", "space"), None),
            P(("groups", "space"), None),
        ),
        check_vma=False,
    )
```

```python
import functools

import jax
import jax.numpy as jnp
from jax import lax
from jax.experimental import pallas as pl
from jax.experimental.pallas import tpu as pltpu
from jax.sharding import PartitionSpec as P

F32 = jnp.float32
BF16 = jnp.bfloat16
LANES = 128
PACK = 16
NN = (((1,), (0,)), ((), ()))
NT = (((1,), (1,)), ((), ()))


def mm(left, right, dims=NN):
    return lax.dot_general(left, right, dims, preferred_element_type=F32)


def halves(x):
    high = x.astype(BF16)
    return high, (x - high.astype(F32)).astype(BF16)


def round_up(x, to):
    return -(-x // to) * to


def vmem(count):
    return [pl.BlockSpec(memory_space=pltpu.VMEM)] * count


def pack_kernel(rows, half, linked, me_ref, feats_ref, g_ref, even_ref, odd_ref, low_ref, top_ref, here_ref, sems, rim_sems):
    entries, slabs, cap = g_ref.shape
    mols = feats_ref.shape[0]
    reach = low_ref.shape[0]
    groups = LANES // half
    blocks = rows // PACK
    count = sems.shape[0]
    stages = []
    for stage in range(count):
        begin, end = stage * blocks // count, (stage + 1) * blocks // count
        copies = []
        for group in range(groups):
            first = min(entries, group * rows + begin * PACK)
            last = min(entries, group * rows + end * PACK)
            if first < last:
                copies.append(
                    pltpu.make_async_copy(g_ref.at[first:last], here_ref.at[first:last], sems.at[stage, group])
                )
        stages.append((begin, end, copies))
        for copy in copies:
            copy.start()
    rims = [
        pltpu.make_async_copy(feats_ref.at[:reach], low_ref, rim_sems.at[0]),
        pltpu.make_async_copy(feats_ref.at[mols - reach :], top_ref, rim_sems.at[1]),
    ]
    for copy in rims:
        copy.start()
    size = PACK * slabs
    to = lax.broadcasted_iota(jnp.int32, (size, size), 0)
    source = lax.broadcasted_iota(jnp.int32, (size, size), 1)
    slab = to // PACK
    if linked:
        slab = slab ^ me_ref[0]
    perm = jnp.where((to % PACK) * slabs + slab == source, 1.0, 0.0).astype(BF16)

    def lanes_of(block):
        early = []
        for group in range(groups):
            first = group * rows + block * PACK
            valid = max(0, min(PACK, entries - first))
            tiles = []
            if valid:
                tiles.append(here_ref[first : first + valid])
            if valid < PACK:
                tiles.append(jnp.zeros((PACK - valid, slabs, cap), BF16))
            tile = tiles[0] if len(tiles) == 1 else jnp.concatenate(tiles, axis=0)
            early.append(tile.reshape(size, cap)[:, :half])
        return early

    for begin, end, copies in stages:
        for copy in copies:
            copy.wait()
        for block in range(begin, end, 2):
            together = range(block, min(block + 2, end))
            lanes = [piece for one in together for piece in lanes_of(one)]
            moved = mm(perm, jnp.concatenate(lanes, axis=1)).astype(BF16)
            for index, one in enumerate(together):
                chunk = moved[:, index * LANES : (index + 1) * LANES].reshape(slabs // 2, 2, PACK, LANES)
                here = pl.ds(one * PACK, PACK)
                even_ref[:, here, :] = chunk[:, 0]
                odd_ref[:, here, :] = chunk[:, 1]
    for copy in rims:
        copy.wait()


def by_core(pair, me):
    return pair[0] + (me % 2) * (pair[1] - pair[0])


def join_kernel(turns, me_ref, even_ref, other_ref, *message_refs):
    for pair, message_ref in zip(turns, message_refs):
        k = by_core(pair, me_ref[0])
        message_ref[0] = even_ref[k]
        message_ref[1] = other_ref[k]


def unpack(half, refs, g_ref):
    groups = LANES // half
    rows = g_ref.shape[0] // groups
    chunks = [(ref, index) for ref in refs for index in range(ref.shape[0])]
    tiles = len(chunks) // groups
    for tile in range(tiles):
        here = [ref[index] for ref, index in chunks[tile * groups : (tile + 1) * groups]]
        for group in range(groups):
            lanes = slice(group * half, (group + 1) * half)
            g_ref[group * rows : (group + 1) * rows, tile * LANES : (tile + 1) * LANES] = jnp.concatenate(
                [chunk[:, lanes] for chunk in here], axis=1
            )
    return tiles * LANES


def slot_rows(ref, me, half, linked, near, far):
    per = LANES // half

    def rows_of(ids):
        rows = []
        for tile in range(len(ids) // per):
            here = ids[tile * per : (tile + 1) * per]
            pieces = [ref[pl.ds(me ^ by_core(i, me) if linked else i, 1), :] for i in here]
            rows.append(jnp.concatenate([piece[:, :half] for piece in pieces], axis=1))
        return rows

    own = ref[pl.ds(me, 1), :][:, half:]
    own = jnp.concatenate([own, jnp.full((1, LANES - half), -1, jnp.int32)], axis=1)
    return rows_of(near) + [own] + rows_of(far)


def edge_kernel(
    half, linked, near, far, me_ref, feats_hbm, w_src_hbm, w_dst_hbm, w_out_hbm, below_ref, above_ref, src_ref, dst_ref,
    live_ref, onehot_hbm, slope_hbm, ext_hbm, near_hidden_ref, far_hidden_ref, w_wide_ref,
    onehot_ref, slope_ref, ext_ref, w_rows_ref, feats_ref, w_src_ref, w_dst_ref, w_out_ref, sems, in_sems,
):
    inputs = [
        pltpu.make_async_copy(hbm, ref, in_sems.at[index])
        for index, (hbm, ref) in enumerate(
            ((feats_hbm, feats_ref), (w_src_hbm, w_src_ref), (w_dst_hbm, w_dst_ref), (w_out_hbm, w_out_ref))
        )
    ]
    for copy in inputs:
        copy.start()
    me = me_ref[0]
    mols = feats_ref.shape[0]
    reach = below_ref.shape[0]
    wide = mols + 2 * reach
    slots = slope_ref.shape[1]
    entries = w_out_ref.shape[0]
    near_slots = near_hidden_ref.shape[1]
    copies = []

    def send(source, target):
        copy = pltpu.make_async_copy(source, target, sems.at[len(copies)])
        copy.start()
        copies.append(copy)

    mol_src = lax.broadcasted_iota(jnp.int32, (mols, LANES), 0)
    mol_dst = lax.broadcasted_iota(jnp.int32, (wide, LANES), 0)
    lists = [slot_rows(ref, me, half, linked, near, far) for ref in (src_ref, dst_ref, live_ref)]
    for tile, (src, dst, live) in enumerate(zip(*lists)):
        src = jnp.where(live > 0, src, -1)
        moved = jnp.where(dst < reach, dst + mols, jnp.where(dst < reach + mols, dst - reach, dst))
        dst = jnp.where(live > 0, moved, -1)
        one_src = jnp.where(mol_src == src, 1.0, 0.0).astype(BF16)
        one_dst = jnp.where(mol_dst == dst, 1.0, 0.0).astype(BF16)
        here = pl.ds(tile * LANES, LANES)
        onehot_ref[:, here] = jnp.concatenate([one_src, one_dst], axis=0)
    for copy in inputs[:3]:
        copy.wait()
    feats = feats_ref[...]
    ext = jnp.concatenate([feats, below_ref[...], above_ref[...]], axis=0)
    ext_ref[...] = ext.T
    send(ext_ref, ext_hbm)
    proj_src = mm(feats, w_src_ref[...])
    proj_dst = mm(ext, w_dst_ref[...])
    proj = jnp.concatenate([proj_src, proj_dst], axis=0).T
    high, low = halves(proj)
    for first, last in slot_tiles(near_slots) + [(near_slots + f, near_slots + l) for f, l in slot_tiles(slots - near_slots)]:
        here = pl.ds(first, last - first)
        send(onehot_ref.at[:, here], onehot_hbm.at[:, here])
        onehot = onehot_ref[:, here]
        pre = mm(high, onehot) + mm(low, onehot)
        sigma = 1.0 / (1.0 + jnp.exp(-pre))
        hidden = (pre * sigma).astype(BF16)
        if first < near_slots:
            near_hidden_ref[:, here] = hidden
        else:
            far_hidden_ref[:, pl.ds(first - near_slots, last - first)] = hidden
        slope_ref[:, here] = sigma * (1.0 + pre * (1.0 - sigma))
        send(slope_ref.at[:, here], slope_hbm.at[:, here])
    inputs[3].wait()
    whole = entries // LANES * LANES
    w_rows_ref[whole:] = jnp.zeros((w_rows_ref.shape[0] - whole, w_rows_ref.shape[1]), BF16)
    w_rows_ref[:whole] = w_out_ref[:whole]
    w_rows_ref[whole:entries] = w_out_ref[whole:]
    w_wide_ref[...] = w_rows_ref[...].T
    for copy in copies:
        copy.wait()


def halve(terms, odd, place, keep_ref, send_ref, first):
    count, rows, _ = keep_ref.shape
    width = terms.shape[-1]
    lanes = slice(first, first + width)
    inner = 1 << place
    pairs = terms.reshape(count // inner, 2, inner, rows, width)
    even_part = pairs[:, 0].reshape(count, rows, width)
    odd_part = pairs[:, 1].reshape(count, rows, width)
    keep_ref[:, :, lanes] = jnp.where(odd > 0, odd_part, even_part)
    send_ref[:, :, lanes] = jnp.where(odd > 0, even_part, odd_part).astype(BF16)


def fold_kernel(bit, place, me_ref, keep_ref, came_ref, next_ref, send_ref):
    odd = (me_ref[0] >> bit) % 2
    halve(keep_ref[...] + came_ref[...].astype(F32), odd, place, next_ref, send_ref, 0)


def close_kernel(keep_ref, came_ref, send_ref):
    send_ref[...] = (keep_ref[...] + came_ref[...].astype(F32)).astype(BF16)


def slot_tiles(slots):
    step = 2 * LANES
    return [(first, min(first + step, slots)) for first in range(0, slots, step)]


def start_tiles(slots, offset, slope_hbm, onehot_hbm, slope_ref, onehot_ref, sems):
    tiles = []
    for tile, (first, last) in enumerate(slot_tiles(slots)):
        there, here = pl.ds(offset + first, last - first), pl.ds(first, last - first)
        copies = [
            pltpu.make_async_copy(slope_hbm.at[:, there], slope_ref.at[:, here], sems.at[tile, 0]),
            pltpu.make_async_copy(onehot_hbm.at[:, there], onehot_ref.at[:, here], sems.at[tile, 1]),
        ]
        for copy in copies:
            copy.start()
        tiles.append((slice(first, last), copies))
    return tiles


def sum_edges(tiles, w_out_ref, g_ref, slope_ref, onehot_ref):
    sums = None
    for lanes, copies in tiles:
        dh = mm(w_out_ref[...], g_ref[:, lanes])
        for copy in copies:
            copy.wait()
        dpre = (dh * slope_ref[:, lanes]).astype(BF16)
        term = mm(onehot_ref[:, lanes], dpre, NT)
        sums = term if sums is None else sums + term
    return sums


def near_kernel(half, own_ref, w_out_ref, hidden_ref, slope_hbm, onehot_hbm, *rest):
    *came_refs, sums_hbm, outer_hbm, g_ref, slope_ref, onehot_ref, sums_ref, outer_ref, sems, out_sems = rest
    slots = g_ref.shape[1]
    tiles = start_tiles(slots, 0, slope_hbm, onehot_hbm, slope_ref, onehot_ref, sems)
    filled = unpack(half, came_refs, g_ref)
    g_ref[:, filled:] = own_ref[...]
    outer_ref[...] = mm(hidden_ref[...], g_ref[...], NT)
    outer_copy = pltpu.make_async_copy(outer_ref, outer_hbm, out_sems.at[0])
    outer_copy.start()
    sums_ref[...] = sum_edges(tiles, w_out_ref, g_ref, slope_ref, onehot_ref)
    sums_copy = pltpu.make_async_copy(sums_ref, sums_hbm, out_sems.at[1])
    sums_copy.start()
    outer_copy.wait()
    sums_copy.wait()


def grad_kernel(half, factor, me_ref, w_out_ref, slope_hbm, onehot_hbm, ext_hbm, near_hbm, *rest):
    (
        *came_refs, keep_ref, send_ref, sums_ref, lower_ref, upper_ref, g_ref,
        slope_ref, onehot_ref, ext_ref, near_ref, tile_sems, sems,
    ) = rest
    odd = me_ref[0] % 2
    width = w_out_ref.shape[0]
    slots = g_ref.shape[1]
    inside = sums_ref.shape[0]
    mols = inside // 2
    reach = lower_ref.shape[0]
    tiles = start_tiles(slots, slope_hbm.shape[1] - slots, slope_hbm, onehot_hbm, slope_ref, onehot_ref, tile_sems)
    whole = [
        pltpu.make_async_copy(near_hbm, near_ref, sems.at[0]),
        pltpu.make_async_copy(ext_hbm, ext_ref, sems.at[1]),
    ]
    for copy in whole:
        copy.start()
    unpack(half, came_refs, g_ref)
    sums = sum_edges(tiles, w_out_ref, g_ref, slope_ref, onehot_ref)
    for copy in whole:
        copy.wait()
    sums = sums + near_ref[...]
    lower_ref[...] = sums[inside : inside + reach].astype(BF16)
    upper_ref[...] = sums[inside + reach :].astype(BF16)
    sums_ref[...] = sums[:inside]
    high, low = halves(sums)
    feats = ext_ref[:, :mols]
    rim = ext_ref[:, mols:]
    halve(factor * (mm(feats, high[:mols]) + mm(feats, low[:mols])), odd, 0, keep_ref, send_ref, 0)
    rim_term = mm(jnp.concatenate([rim, rim], axis=1), jnp.concatenate([high[inside:], low[inside:]], axis=0))
    dst_term = mm(feats, high[mols:inside]) + mm(feats, low[mols:inside]) + rim_term
    halve(factor * dst_term, odd, 0, keep_ref, send_ref, width)


def outer_kernel(factor, me_ref, hidden_ref, g_ref, near_hbm, keep_ref, send_ref, near_ref, sem):
    copy = pltpu.make_async_copy(near_hbm, near_ref, sem)
    copy.start()
    term = mm(hidden_ref[...], g_ref[...], NT)
    copy.wait()
    term = factor * (term + near_ref[...])
    padding = keep_ref.shape[2] - term.shape[1]
    if padding > 0:
        term = jnp.concatenate([term, jnp.zeros((term.shape[0], padding), F32)], axis=1)
    halve(term, me_ref[0] % 2, 0, keep_ref, send_ref, 0)


def rim_kernel(sums_ref, from_below_ref, from_above_ref, w_src_ref, w_dst_ref, out_ref):
    mols = out_ref.shape[0]
    reach = from_below_ref.shape[0]
    src = sums_ref[:mols]
    dst = sums_ref[mols:]
    dst = jnp.concatenate(
        [
            dst[:reach] + from_below_ref[...].astype(F32),
            dst[reach : mols - reach],
            dst[mols - reach :] + from_above_ref[...].astype(F32),
        ],
        axis=0,
    )
    w_src = w_src_ref[...]
    w_dst = w_dst_ref[...]
    src_high, src_low = halves(src)
    dst_high, dst_low = halves(dst)
    out_ref[...] = mm(src_high, w_src, NT) + mm(src_low, w_src, NT) + mm(dst_high, w_dst, NT) + mm(dst_low, w_dst, NT)


def total_kernel(*refs):
    *refs, src_ref, dst_ref, out_ref = refs
    count = len(refs) // 2
    width = src_ref.shape[1]
    totals = []
    for piece in (refs[:count], refs[count:]):
        terms = [ref[slab].astype(F32) for ref in piece for slab in range(ref.shape[0])]
        totals.append(functools.reduce(jnp.add, terms))
    sides, outer = totals
    src_ref[...] = sides[:, :width]
    dst_ref[...] = sides[:, width:]
    out_ref[...] = outer[:, : out_ref.shape[1]]


def in_hbm(x):
    return pltpu.with_memory_space_constraint(x, pltpu.HBM)


def swap(block, bit, slabs):
    return lax.ppermute(block, "space", [(i, i ^ (1 << bit)) for i in range(slabs)])


def on_device(mol_feats, w_src, w_dst, w_out, grad_blocks, edge_src, edge_dst, edge_live):
    slabs = lax.axis_size("space")
    mols, width = mol_feats.shape
    entries = w_out.shape[1]
    cap = grad_blocks.shape[2]
    half = cap // 2
    reach = mols // 4
    groups = LANES // half
    slots = (slabs // groups + 1) * LANES
    bits = slabs.bit_length() - 1
    if 3 <= bits <= 4:
        late_bits = tuple((bit, 0) for bit in range(3, bits))
        paths = (((0, 0), (1, 0), (2, 0)) + late_bits, ((0, 0), (2, 1), (1, 0)) + late_bits)
    else:
        paths = (tuple((bit, 0) for bit in range(min(bits, 2))),) * 2
    rest = slabs >> len(paths[0])
    part = width // slabs
    factor = float(edge_src.shape[0] * slabs) ** (-0.5)
    me = lax.axis_index("space").astype(jnp.int32).reshape(1)
    smem = pl.BlockSpec(memory_space=pltpu.SMEM)
    hbm = pl.BlockSpec(memory_space=pltpu.HBM)
    big = pltpu.CompilerParams(vmem_limit_bytes=24 * 1024 * 1024)
    up = [(i, (i + 1) % slabs) for i in range(slabs)]
    down = [((i + 1) % slabs, i) for i in range(slabs)]

    rows = round_up(pl.cdiv(entries, groups), PACK)
    stages = 4
    linked = slabs <= 16
    even, odd, low, top = pl.pallas_call(
        functools.partial(pack_kernel, rows, half, linked),
        out_shape=(
            jax.ShapeDtypeStruct((slabs // 2, rows, LANES), BF16),
            jax.ShapeDtypeStruct((slabs // 2, rows, LANES), BF16),
            jax.ShapeDtypeStruct((reach, width), BF16),
            jax.ShapeDtypeStruct((reach, width), BF16),
        ),
        in_specs=[smem, hbm, hbm],
        out_specs=tuple(vmem(4)),
        scratch_shapes=[
            pltpu.VMEM((entries, slabs, cap), BF16),
            pltpu.SemaphoreType.DMA((stages, groups)),
            pltpu.SemaphoreType.DMA((2,)),
        ],
        compiler_params=big,
        name="pack",
    )(me, in_hbm(mol_feats), in_hbm(jnp.transpose(grad_blocks[0], (2, 0, 1))))
    below = lax.ppermute(top, "space", up)
    above = lax.ppermute(low, "space", down)
    late = lax.dynamic_index_in_dim(grad_blocks[0], me[0], 0, keepdims=False)[half:]
    own = jnp.pad(late.T, ((0, groups * rows - entries), (0, LANES - half)))
    if linked:
        other = swap(odd, 0, slabs)
        other, below, above, own = lax.optimization_barrier((other, below, above, own))
        quarter = slabs // 4
        mixed = [pair for k in range(1, quarter) for pair in ((quarter + k - 1, k), (k, quarter + k - 1))]
        turns = [(0, 0), *mixed, (2 * quarter - 1, 2 * quarter - 1)]
        messages = pl.pallas_call(
            functools.partial(join_kernel, turns),
            out_shape=(jax.ShapeDtypeStruct((2, rows, LANES), BF16),) * (slabs // 2),
            in_specs=[smem] + vmem(2),
            out_specs=tuple(vmem(slabs // 2)),
            compiler_params=big,
            name="join",
        )(me, even, other)
        came = [messages[0]]
        for turn in range(1, 2 * quarter):
            route = [(i, i ^ (2 * turns[turn][i % 2])) for i in range(slabs)]
            came.append(lax.ppermute(messages[turn], "space", route))
        ids = [(2 * first + j, 2 * second + j) for first, second in turns for j in range(2)]
        near, far = tuple(ids[: 2 * quarter]), tuple(ids[2 * quarter :])
        came_near, came_far = came[:quarter], came[quarter:]
    else:
        packed = jnp.stack([even, odd], axis=1).reshape(slabs, rows, LANES)
        near, far = (), tuple(range(slabs))
        came_near = []
        came_far = [lax.all_to_all(packed, "space", split_axis=0, concat_axis=0, tiled=True)]
    far_slots = len(far) * half
    near_slots = slots - far_slots

    wide = mols + 2 * reach
    entries_wide = groups * rows
    pieces = len(slot_tiles(near_slots)) + len(slot_tiles(far_slots))
    onehot, slope, ext, near_hidden, far_hidden, w_out_wide = pl.pallas_call(
        functools.partial(edge_kernel, half, linked, near, far),
        out_shape=(
            pltpu.HBM((mols + wide, slots), BF16),
            pltpu.HBM((width, slots), F32),
            pltpu.HBM((width, wide), BF16),
            jax.ShapeDtypeStruct((width, near_slots), BF16),
            jax.ShapeDtypeStruct((width, far_slots), BF16),
            jax.ShapeDtypeStruct((width, entries_wide), BF16),
        ),
        in_specs=[smem] + [hbm] * 4 + vmem(5),
        out_specs=(hbm,) * 3 + tuple(vmem(3)),
        scratch_shapes=[
            pltpu.VMEM((mols + wide, slots), BF16),
            pltpu.VMEM((width, slots), F32),
            pltpu.VMEM((width, wide), BF16),
            pltpu.VMEM((entries_wide, width), BF16),
            pltpu.VMEM((mols, width), BF16),
            pltpu.VMEM((width, width), BF16),
            pltpu.VMEM((width, width), BF16),
            pltpu.VMEM((entries, width), BF16),
            pltpu.SemaphoreType.DMA((2 * pieces + 1,)),
            pltpu.SemaphoreType.DMA((4,)),
        ],
        compiler_params=big,
        name="edges",
        cost_estimate=pl.CostEstimate(
            flops=40 * width * slots * 2 * (2 * mols + 2 * reach), bytes_accessed=8 * 1024 * 1024,
            transcendentals=width * slots,
        ),
    )(
        me, in_hbm(mol_feats), in_hbm(w_src), in_hbm(w_dst), in_hbm(w_out.T), below, above,
        edge_src.reshape(slabs, cap), edge_dst.reshape(slabs, cap), edge_live.reshape(slabs, cap),
    )
    onehot, slope, ext = in_hbm(onehot), in_hbm(slope), in_hbm(ext)

    def chunks(count, lanes, dtype):
        return jax.ShapeDtypeStruct((count, part, lanes), dtype)

    near_sums, near_outer = pl.pallas_call(
        functools.partial(near_kernel, half),
        out_shape=(
            pltpu.HBM((mols + wide, width), F32),
            pltpu.HBM((width, entries_wide), F32),
        ),
        in_specs=vmem(3) + [hbm] * 2 + vmem(len(came_near)),
        out_specs=(hbm, hbm),
        scratch_shapes=[
            pltpu.VMEM((entries_wide, near_slots), BF16),
            pltpu.VMEM((width, near_slots), F32),
            pltpu.VMEM((mols + wide, near_slots), BF16),
            pltpu.VMEM((mols + wide, width), F32),
            pltpu.VMEM((width, entries_wide), F32),
            pltpu.SemaphoreType.DMA((len(slot_tiles(near_slots)), 2)),
            pltpu.SemaphoreType.DMA((2,)),
        ],
        compiler_params=big,
        name="near",
        cost_estimate=pl.CostEstimate(
            flops=40 * width * near_slots * entries_wide, bytes_accessed=6 * 1024 * 1024, transcendentals=0
        ),
    )(own, w_out_wide, near_hidden, slope, onehot, *came_near)
    near_sums, near_outer = in_hbm(near_sums), in_hbm(near_outer)
    keep, send, sums, lower, upper, g = pl.pallas_call(
        functools.partial(grad_kernel, half, factor),
        out_shape=(
            chunks(slabs // 2, 2 * width, F32),
            chunks(slabs // 2, 2 * width, BF16),
            jax.ShapeDtypeStruct((2 * mols, width), F32),
            jax.ShapeDtypeStruct((reach, width), BF16),
            jax.ShapeDtypeStruct((reach, width), BF16),
            jax.ShapeDtypeStruct((entries_wide, far_slots), BF16),
        ),
        in_specs=[smem] + vmem(1) + [hbm] * 4 + vmem(len(came_far)),
        out_specs=tuple(vmem(6)),
        scratch_shapes=[
            pltpu.VMEM((width, far_slots), F32),
            pltpu.VMEM((mols + wide, far_slots), BF16),
            pltpu.VMEM((width, wide), BF16),
            pltpu.VMEM((mols + wide, width), F32),
            pltpu.SemaphoreType.DMA((len(slot_tiles(far_slots)), 2)),
            pltpu.SemaphoreType.DMA((2,)),
        ],
        compiler_params=big,
        name="grads",
    )(me, w_out_wide, slope, onehot, ext, near_sums, *came_far)
    lanes = round_up(entries_wide, LANES)
    keep_o, send_o = pl.pallas_call(
        functools.partial(outer_kernel, factor),
        out_shape=(chunks(slabs // 2, lanes, F32), chunks(slabs // 2, lanes, BF16)),
        in_specs=[smem] + vmem(2) + [hbm],
        out_specs=tuple(vmem(2)),
        scratch_shapes=[pltpu.VMEM((width, entries_wide), F32), pltpu.SemaphoreType.DMA(())],
        compiler_params=big,
        name="outer",
        cost_estimate=pl.CostEstimate(
            flops=40 * width * slots * entries_wide, bytes_accessed=4 * 1024 * 1024, transcendentals=0
        ),
    )(me, far_hidden, g, near_outer)

    def fold(bit, place, keep, crossed):
        shape = (keep.shape[0] // 2, keep.shape[2])
        return pl.pallas_call(
            functools.partial(fold_kernel, bit, place),
            out_shape=(chunks(*shape, F32), chunks(*shape, BF16)),
            in_specs=[smem] + vmem(2),
            out_specs=tuple(vmem(2)),
            compiler_params=big,
            name="fold",
        )(me, keep, crossed)

    def close(keep, crossed):
        if rest == 1:
            return [keep, crossed]
        sends = pl.pallas_call(
            close_kernel,
            out_shape=chunks(rest, keep.shape[2], BF16),
            in_specs=vmem(2),
            out_specs=vmem(1)[0],
            compiler_params=big,
            name="close",
        )(keep, crossed)
        same = [[low + rank * (slabs // rest) for rank in range(rest)] for low in range(slabs // rest)]
        return [
            lax.all_to_all(sends, "space", split_axis=0, concat_axis=0, tiled=True, axis_index_groups=same)
        ]

    from_above = lax.ppermute(lower, "space", down)
    from_below = lax.ppermute(upper, "space", up)
    crossed = swap(send, 0, slabs)
    crossed_o = swap(send_o, 0, slabs)
    for (bit, place), (bit_o, place_o) in zip(paths[0][1:], paths[1][1:]):
        if bit == 3:
            keep, crossed, from_above, from_below = lax.optimization_barrier((keep, crossed, from_above, from_below))
        keep, send = fold(bit, place, keep, crossed)
        crossed = swap(send, bit, slabs)
        keep_o, crossed_o, _ = lax.optimization_barrier((keep_o, crossed_o, send))
        keep_o, send_o = fold(bit_o, place_o, keep_o, crossed_o)
        crossed_o = swap(send_o, bit_o, slabs)
    terms = close(keep, crossed)
    terms_o = close(keep_o, crossed_o)
    feature_grad = pl.pallas_call(
        rim_kernel,
        out_shape=jax.ShapeDtypeStruct((mols, width), F32),
        in_specs=vmem(5),
        out_specs=vmem(1)[0],
        compiler_params=big,
        name="rims",
        cost_estimate=pl.CostEstimate(flops=2 * width * slots * width * 40, bytes_accessed=4 * 1024 * 1024, transcendentals=0),
    )(sums, from_below, from_above, w_src, w_dst)
    src_grad, dst_grad, out_grad = pl.pallas_call(
        total_kernel,
        out_shape=(
            jax.ShapeDtypeStruct((part, width), F32),
            jax.ShapeDtypeStruct((part, width), F32),
            jax.ShapeDtypeStruct((part, entries), F32),
        ),
        in_specs=vmem(len(terms) + len(terms_o)),
        out_specs=tuple(vmem(3)),
        compiler_params=big,
        name="totals",
    )(*terms, *terms_o)
    return (feature_grad, src_grad, dst_grad, out_grad)


def solution(mesh):
    placed = (
        P(("groups", "space"), None),
        P(),
        P(),
        P(),
        P("space", "groups", None, None),
        P(("groups", "space")),
        P(("groups", "space")),
        P(("groups", "space")),
    )
    return jax.shard_map(
        on_device,
        mesh=mesh,
        in_specs=placed,
        out_specs=(
            P(("groups", "space"), None),
            P(("groups", "space"), None),
            P(("groups", "space"), None),
            P(("groups", "space"), None),
        ),
        check_vma=False,
    )
```

```python
import functools

import jax
import jax.numpy as jnp
from jax import lax
from jax.experimental import pallas as pl
from jax.experimental.pallas import tpu as pltpu
from jax.sharding import PartitionSpec as P

F32 = jnp.float32
BF16 = jnp.bfloat16
LANES = 128
PACK = 16
NN = (((1,), (0,)), ((), ()))
NT = (((1,), (1,)), ((), ()))


def mm(left, right, dims=NN):
    return lax.dot_general(left, right, dims, preferred_element_type=F32)


def halves(x):
    high = x.astype(BF16)
    return high, (x - high.astype(F32)).astype(BF16)


def round_up(x, to):
    return -(-x // to) * to


def vmem(count):
    return [pl.BlockSpec(memory_space=pltpu.VMEM)] * count


def pack_kernel(rows, half, linked, me_ref, feats_ref, g_ref, even_ref, odd_ref, low_ref, top_ref, here_ref, sems, rim_sems):
    entries, slabs, cap = g_ref.shape
    mols = feats_ref.shape[0]
    reach = low_ref.shape[0]
    groups = LANES // half
    blocks = rows // PACK
    count = sems.shape[0]
    stages = []
    for stage in range(count):
        begin, end = stage * blocks // count, (stage + 1) * blocks // count
        copies = []
        for group in range(groups):
            first = min(entries, group * rows + begin * PACK)
            last = min(entries, group * rows + end * PACK)
            if first < last:
                copies.append(
                    pltpu.make_async_copy(g_ref.at[first:last], here_ref.at[first:last], sems.at[stage, group])
                )
        stages.append((begin, end, copies))
        for copy in copies:
            copy.start()
    rims = [
        pltpu.make_async_copy(feats_ref.at[:reach], low_ref, rim_sems.at[0]),
        pltpu.make_async_copy(feats_ref.at[mols - reach :], top_ref, rim_sems.at[1]),
    ]
    for copy in rims:
        copy.start()
    size = PACK * slabs
    to = lax.broadcasted_iota(jnp.int32, (size, size), 0)
    source = lax.broadcasted_iota(jnp.int32, (size, size), 1)
    slab = to // PACK
    if linked:
        slab = slab ^ me_ref[0]
    perm = jnp.where((to % PACK) * slabs + slab == source, 1.0, 0.0).astype(BF16)

    def lanes_of(block):
        early = []
        for group in range(groups):
            first = group * rows + block * PACK
            valid = max(0, min(PACK, entries - first))
            tiles = []
            if valid:
                tiles.append(here_ref[first : first + valid])
            if valid < PACK:
                tiles.append(jnp.zeros((PACK - valid, slabs, cap), BF16))
            tile = tiles[0] if len(tiles) == 1 else jnp.concatenate(tiles, axis=0)
            early.append(tile.reshape(size, cap)[:, :half])
        return early

    for begin, end, copies in stages:
        for copy in copies:
            copy.wait()
        for block in range(begin, end, 2):
            together = range(block, min(block + 2, end))
            lanes = [piece for one in together for piece in lanes_of(one)]
            moved = mm(perm, jnp.concatenate(lanes, axis=1)).astype(BF16)
            for index, one in enumerate(together):
                chunk = moved[:, index * LANES : (index + 1) * LANES].reshape(slabs // 2, 2, PACK, LANES)
                here = pl.ds(one * PACK, PACK)
                even_ref[:, here, :] = chunk[:, 0]
                odd_ref[:, here, :] = chunk[:, 1]
    for copy in rims:
        copy.wait()


def by_core(pair, me):
    return pair[0] + (me % 2) * (pair[1] - pair[0])


def join_kernel(turns, me_ref, even_ref, other_ref, *message_refs):
    for pair, message_ref in zip(turns, message_refs):
        k = by_core(pair, me_ref[0])
        message_ref[0] = even_ref[k]
        message_ref[1] = other_ref[k]


def unpack(half, refs, g_ref):
    groups = LANES // half
    rows = g_ref.shape[0] // groups
    chunks = [(ref, index) for ref in refs for index in range(ref.shape[0])]
    tiles = len(chunks) // groups
    for tile in range(tiles):
        here = [ref[index] for ref, index in chunks[tile * groups : (tile + 1) * groups]]
        for group in range(groups):
            lanes = slice(group * half, (group + 1) * half)
            g_ref[group * rows : (group + 1) * rows, tile * LANES : (tile + 1) * LANES] = jnp.concatenate(
                [chunk[:, lanes] for chunk in here], axis=1
            )
    return tiles * LANES


def slot_rows(ref, me, half, linked, near, far):
    per = LANES // half

    def rows_of(ids):
        rows = []
        for tile in range(len(ids) // per):
            here = ids[tile * per : (tile + 1) * per]
            pieces = [ref[pl.ds(me ^ by_core(i, me) if linked else i, 1), :] for i in here]
            rows.append(jnp.concatenate([piece[:, :half] for piece in pieces], axis=1))
        return rows

    own = ref[pl.ds(me, 1), :][:, half:]
    own = jnp.concatenate([own, jnp.full((1, LANES - half), -1, jnp.int32)], axis=1)
    return rows_of(near) + [own] + rows_of(far)


def edge_kernel(
    half, linked, near, far, me_ref, feats_hbm, w_src_hbm, w_dst_hbm, w_out_hbm, below_ref, above_ref, src_ref, dst_ref,
    live_ref, onehot_hbm, slope_hbm, ext_hbm, near_hidden_ref, far_hidden_ref, w_wide_ref,
    onehot_ref, slope_ref, ext_ref, w_rows_ref, feats_ref, w_src_ref, w_dst_ref, w_out_ref, sems, in_sems,
):
    inputs = [
        pltpu.make_async_copy(hbm, ref, in_sems.at[index])
        for index, (hbm, ref) in enumerate(
            ((feats_hbm, feats_ref), (w_src_hbm, w_src_ref), (w_dst_hbm, w_dst_ref), (w_out_hbm, w_out_ref))
        )
    ]
    for copy in inputs:
        copy.start()
    me = me_ref[0]
    mols = feats_ref.shape[0]
    reach = below_ref.shape[0]
    wide = mols + 2 * reach
    slots = slope_ref.shape[1]
    entries = w_out_ref.shape[0]
    near_slots = near_hidden_ref.shape[1]
    copies = []

    def send(source, target):
        copy = pltpu.make_async_copy(source, target, sems.at[len(copies)])
        copy.start()
        copies.append(copy)

    mol_src = lax.broadcasted_iota(jnp.int32, (mols, LANES), 0)
    mol_dst = lax.broadcasted_iota(jnp.int32, (wide, LANES), 0)
    lists = [slot_rows(ref, me, half, linked, near, far) for ref in (src_ref, dst_ref, live_ref)]
    for tile, (src, dst, live) in enumerate(zip(*lists)):
        src = jnp.where(live > 0, src, -1)
        moved = jnp.where(dst < reach, dst + mols, jnp.where(dst < reach + mols, dst - reach, dst))
        dst = jnp.where(live > 0, moved, -1)
        one_src = jnp.where(mol_src == src, 1.0, 0.0).astype(BF16)
        one_dst = jnp.where(mol_dst == dst, 1.0, 0.0).astype(BF16)
        here = pl.ds(tile * LANES, LANES)
        onehot_ref[:, here] = jnp.concatenate([one_src, one_dst], axis=0)
    for copy in inputs[:3]:
        copy.wait()
    feats = feats_ref[...]
    ext = jnp.concatenate([feats, below_ref[...], above_ref[...]], axis=0)
    ext_ref[...] = ext.T
    send(ext_ref, ext_hbm)
    proj_src = mm(feats, w_src_ref[...])
    proj_dst = mm(ext, w_dst_ref[...])
    proj = jnp.concatenate([proj_src, proj_dst], axis=0).T
    high, low = halves(proj)
    for first, last in slot_tiles(near_slots) + [(near_slots + f, near_slots + l) for f, l in slot_tiles(slots - near_slots)]:
        here = pl.ds(first, last - first)
        send(onehot_ref.at[:, here], onehot_hbm.at[:, here])
        onehot = onehot_ref[:, here]
        pre = mm(high, onehot) + mm(low, onehot)
        sigma = 1.0 / (1.0 + jnp.exp(-pre))
        hidden = (pre * sigma).astype(BF16)
        if first < near_slots:
            near_hidden_ref[:, here] = hidden
        else:
            far_hidden_ref[:, pl.ds(first - near_slots, last - first)] = hidden
        slope_ref[:, here] = sigma * (1.0 + pre * (1.0 - sigma))
        send(slope_ref.at[:, here], slope_hbm.at[:, here])
    inputs[3].wait()
    whole = entries // LANES * LANES
    w_rows_ref[whole:] = jnp.zeros((w_rows_ref.shape[0] - whole, w_rows_ref.shape[1]), BF16)
    w_rows_ref[:whole] = w_out_ref[:whole]
    w_rows_ref[whole:entries] = w_out_ref[whole:]
    w_wide_ref[...] = w_rows_ref[...].T
    for copy in copies:
        copy.wait()


def halve(terms, odd, place, keep_ref, send_ref, first):
    count, rows, _ = keep_ref.shape
    width = terms.shape[-1]
    lanes = slice(first, first + width)
    inner = 1 << place
    pairs = terms.reshape(count // inner, 2, inner, rows, width)
    even_part = pairs[:, 0].reshape(count, rows, width)
    odd_part = pairs[:, 1].reshape(count, rows, width)
    keep_ref[:, :, lanes] = jnp.where(odd > 0, odd_part, even_part)
    send_ref[:, :, lanes] = jnp.where(odd > 0, even_part, odd_part).astype(BF16)


def fold_kernel(bit, place, me_ref, keep_ref, came_ref, next_ref, send_ref):
    odd = (me_ref[0] >> bit) % 2
    halve(keep_ref[...] + came_ref[...].astype(F32), odd, place, next_ref, send_ref, 0)


def close_kernel(keep_ref, came_ref, send_ref):
    send_ref[...] = (keep_ref[...] + came_ref[...].astype(F32)).astype(BF16)


def slot_tiles(slots):
    step = 2 * LANES
    return [(first, min(first + step, slots)) for first in range(0, slots, step)]


def start_tiles(slots, offset, slope_hbm, onehot_hbm, slope_ref, onehot_ref, sems):
    tiles = []
    for tile, (first, last) in enumerate(slot_tiles(slots)):
        there, here = pl.ds(offset + first, last - first), pl.ds(first, last - first)
        copies = [
            pltpu.make_async_copy(slope_hbm.at[:, there], slope_ref.at[:, here], sems.at[tile, 0]),
            pltpu.make_async_copy(onehot_hbm.at[:, there], onehot_ref.at[:, here], sems.at[tile, 1]),
        ]
        for copy in copies:
            copy.start()
        tiles.append((slice(first, last), copies))
    return tiles


def sum_edges(tiles, w_out_ref, g_ref, slope_ref, onehot_ref):
    sums = None
    for lanes, copies in tiles:
        dh = mm(w_out_ref[...], g_ref[:, lanes])
        for copy in copies:
            copy.wait()
        dpre = (dh * slope_ref[:, lanes]).astype(BF16)
        term = mm(onehot_ref[:, lanes], dpre, NT)
        sums = term if sums is None else sums + term
    return sums


def near_kernel(half, own_ref, w_out_ref, hidden_ref, slope_hbm, onehot_hbm, *rest):
    *came_refs, sums_hbm, outer_hbm, g_ref, slope_ref, onehot_ref, sums_ref, outer_ref, sems, out_sems = rest
    slots = g_ref.shape[1]
    tiles = start_tiles(slots, 0, slope_hbm, onehot_hbm, slope_ref, onehot_ref, sems)
    filled = unpack(half, came_refs, g_ref)
    g_ref[:, filled:] = own_ref[...]
    outer_ref[...] = mm(hidden_ref[...], g_ref[...], NT)
    outer_copy = pltpu.make_async_copy(outer_ref, outer_hbm, out_sems.at[0])
    outer_copy.start()
    sums_ref[...] = sum_edges(tiles, w_out_ref, g_ref, slope_ref, onehot_ref)
    sums_copy = pltpu.make_async_copy(sums_ref, sums_hbm, out_sems.at[1])
    sums_copy.start()
    outer_copy.wait()
    sums_copy.wait()


def grad_kernel(half, factor, me_ref, w_out_ref, slope_hbm, onehot_hbm, ext_hbm, near_hbm, *rest):
    (
        *came_refs, keep_ref, send_ref, sums_ref, lower_ref, upper_ref, g_ref,
        slope_ref, onehot_ref, ext_ref, near_ref, tile_sems, sems,
    ) = rest
    odd = me_ref[0] % 2
    width = w_out_ref.shape[0]
    slots = g_ref.shape[1]
    inside = sums_ref.shape[0]
    mols = inside // 2
    reach = lower_ref.shape[0]
    tiles = start_tiles(slots, slope_hbm.shape[1] - slots, slope_hbm, onehot_hbm, slope_ref, onehot_ref, tile_sems)
    whole = [
        pltpu.make_async_copy(near_hbm, near_ref, sems.at[0]),
        pltpu.make_async_copy(ext_hbm, ext_ref, sems.at[1]),
    ]
    for copy in whole:
        copy.start()
    unpack(half, came_refs, g_ref)
    sums = sum_edges(tiles, w_out_ref, g_ref, slope_ref, onehot_ref)
    for copy in whole:
        copy.wait()
    sums = sums + near_ref[...]
    lower_ref[...] = sums[inside : inside + reach].astype(BF16)
    upper_ref[...] = sums[inside + reach :].astype(BF16)
    sums_ref[...] = sums[:inside]
    high, low = halves(sums)
    feats = ext_ref[:, :mols]
    rim = ext_ref[:, mols:]
    halve(factor * (mm(feats, high[:mols]) + mm(feats, low[:mols])), odd, 0, keep_ref, send_ref, 0)
    rim_term = mm(jnp.concatenate([rim, rim], axis=1), jnp.concatenate([high[inside:], low[inside:]], axis=0))
    dst_term = mm(feats, high[mols:inside]) + mm(feats, low[mols:inside]) + rim_term
    halve(factor * dst_term, odd, 0, keep_ref, send_ref, width)


def outer_kernel(factor, me_ref, hidden_ref, g_ref, near_hbm, keep_ref, send_ref, near_ref, sem):
    copy = pltpu.make_async_copy(near_hbm, near_ref, sem)
    copy.start()
    term = mm(hidden_ref[...], g_ref[...], NT)
    copy.wait()
    term = factor * (term + near_ref[...])
    padding = keep_ref.shape[2] - term.shape[1]
    if padding > 0:
        term = jnp.concatenate([term, jnp.zeros((term.shape[0], padding), F32)], axis=1)
    halve(term, me_ref[0] % 2, 0, keep_ref, send_ref, 0)


def rim_kernel(sums_ref, from_below_ref, from_above_ref, w_src_ref, w_dst_ref, out_ref):
    mols = out_ref.shape[0]
    reach = from_below_ref.shape[0]
    src = sums_ref[:mols]
    dst = sums_ref[mols:]
    dst = jnp.concatenate(
        [
            dst[:reach] + from_below_ref[...].astype(F32),
            dst[reach : mols - reach],
            dst[mols - reach :] + from_above_ref[...].astype(F32),
        ],
        axis=0,
    )
    w_src = w_src_ref[...]
    w_dst = w_dst_ref[...]
    src_high, src_low = halves(src)
    dst_high, dst_low = halves(dst)
    out_ref[...] = mm(src_high, w_src, NT) + mm(src_low, w_src, NT) + mm(dst_high, w_dst, NT) + mm(dst_low, w_dst, NT)


def total_kernel(*refs):
    *refs, src_ref, dst_ref, out_ref = refs
    count = len(refs) // 2
    width = src_ref.shape[1]
    totals = []
    for piece in (refs[:count], refs[count:]):
        terms = [ref[slab].astype(F32) for ref in piece for slab in range(ref.shape[0])]
        totals.append(functools.reduce(jnp.add, terms))
    sides, outer = totals
    src_ref[...] = sides[:, :width]
    dst_ref[...] = sides[:, width:]
    out_ref[...] = outer[:, : out_ref.shape[1]]


def in_hbm(x):
    return pltpu.with_memory_space_constraint(x, pltpu.HBM)


def swap(block, bit, slabs):
    return lax.ppermute(block, "space", [(i, i ^ (1 << bit)) for i in range(slabs)])


def on_device(mol_feats, w_src, w_dst, w_out, grad_blocks, edge_src, edge_dst, edge_live):
    slabs = lax.axis_size("space")
    mols, width = mol_feats.shape
    entries = w_out.shape[1]
    cap = grad_blocks.shape[2]
    half = cap // 2
    reach = mols // 4
    groups = LANES // half
    slots = (slabs // groups + 1) * LANES
    bits = slabs.bit_length() - 1
    if 3 <= bits <= 4:
        late_bits = tuple((bit, 0) for bit in range(3, bits))
        paths = (((0, 0), (1, 0), (2, 0)) + late_bits, ((0, 0), (2, 1), (1, 0)) + late_bits)
    else:
        paths = (tuple((bit, 0) for bit in range(min(bits, 2))),) * 2
    rest = slabs >> len(paths[0])
    part = width // slabs
    factor = float(edge_src.shape[0] * slabs) ** (-0.5)
    me = lax.axis_index("space").astype(jnp.int32).reshape(1)
    smem = pl.BlockSpec(memory_space=pltpu.SMEM)
    hbm = pl.BlockSpec(memory_space=pltpu.HBM)
    big = pltpu.CompilerParams(vmem_limit_bytes=24 * 1024 * 1024)
    up = [(i, (i + 1) % slabs) for i in range(slabs)]
    down = [((i + 1) % slabs, i) for i in range(slabs)]

    rows = round_up(pl.cdiv(entries, groups), PACK)
    stages = 4
    linked = slabs <= 16
    even, odd, low, top = pl.pallas_call(
        functools.partial(pack_kernel, rows, half, linked),
        out_shape=(
            jax.ShapeDtypeStruct((slabs // 2, rows, LANES), BF16),
            jax.ShapeDtypeStruct((slabs // 2, rows, LANES), BF16),
            jax.ShapeDtypeStruct((reach, width), BF16),
            jax.ShapeDtypeStruct((reach, width), BF16),
        ),
        in_specs=[smem, hbm, hbm],
        out_specs=tuple(vmem(4)),
        scratch_shapes=[
            pltpu.VMEM((entries, slabs, cap), BF16),
            pltpu.SemaphoreType.DMA((stages, groups)),
            pltpu.SemaphoreType.DMA((2,)),
        ],
        compiler_params=big,
        name="pack",
    )(me, in_hbm(mol_feats), in_hbm(jnp.transpose(grad_blocks[0], (2, 0, 1))))
    below = lax.ppermute(top, "space", up)
    above = lax.ppermute(low, "space", down)
    late = lax.dynamic_index_in_dim(grad_blocks[0], me[0], 0, keepdims=False)[half:]
    own = jnp.pad(late.T, ((0, groups * rows - entries), (0, LANES - half)))
    if linked:
        other = swap(odd, 0, slabs)
        other, below, above, own = lax.optimization_barrier((other, below, above, own))
        quarter = slabs // 4
        mixed = [pair for k in range(1, quarter) for pair in ((quarter + k - 1, k), (k, quarter + k - 1))]
        turns = [(0, 0), *mixed, (2 * quarter - 1, 2 * quarter - 1)]
        messages = pl.pallas_call(
            functools.partial(join_kernel, turns),
            out_shape=(jax.ShapeDtypeStruct((2, rows, LANES), BF16),) * (slabs // 2),
            in_specs=[smem] + vmem(2),
            out_specs=tuple(vmem(slabs // 2)),
            compiler_params=big,
            name="join",
        )(me, even, other)
        came = [messages[0]]
        for turn in range(1, 2 * quarter):
            route = [(i, i ^ (2 * turns[turn][i % 2])) for i in range(slabs)]
            came.append(lax.ppermute(messages[turn], "space", route))
        ids = [(2 * first + j, 2 * second + j) for first, second in turns for j in range(2)]
        near, far = tuple(ids[: 2 * quarter + 2]), tuple(ids[2 * quarter + 2 :])
        came_near, came_far = came[: quarter + 1], came[quarter + 1 :]
    else:
        packed = jnp.stack([even, odd], axis=1).reshape(slabs, rows, LANES)
        near, far = (), tuple(range(slabs))
        came_near = []
        came_far = [lax.all_to_all(packed, "space", split_axis=0, concat_axis=0, tiled=True)]
    far_slots = len(far) * half
    near_slots = slots - far_slots

    wide = mols + 2 * reach
    entries_wide = groups * rows
    pieces = len(slot_tiles(near_slots)) + len(slot_tiles(far_slots))
    onehot, slope, ext, near_hidden, far_hidden, w_out_wide = pl.pallas_call(
        functools.partial(edge_kernel, half, linked, near, far),
        out_shape=(
            pltpu.HBM((mols + wide, slots), BF16),
            pltpu.HBM((width, slots), F32),
            pltpu.HBM((width, wide), BF16),
            jax.ShapeDtypeStruct((width, near_slots), BF16),
            jax.ShapeDtypeStruct((width, far_slots), BF16),
            jax.ShapeDtypeStruct((width, entries_wide), BF16),
        ),
        in_specs=[smem] + [hbm] * 4 + vmem(5),
        out_specs=(hbm,) * 3 + tuple(vmem(3)),
        scratch_shapes=[
            pltpu.VMEM((mols + wide, slots), BF16),
            pltpu.VMEM((width, slots), F32),
            pltpu.VMEM((width, wide), BF16),
            pltpu.VMEM((entries_wide, width), BF16),
            pltpu.VMEM((mols, width), BF16),
            pltpu.VMEM((width, width), BF16),
            pltpu.VMEM((width, width), BF16),
            pltpu.VMEM((entries, width), BF16),
            pltpu.SemaphoreType.DMA((2 * pieces + 1,)),
            pltpu.SemaphoreType.DMA((4,)),
        ],
        compiler_params=big,
        name="edges",
        cost_estimate=pl.CostEstimate(
            flops=40 * width * slots * 2 * (2 * mols + 2 * reach), bytes_accessed=8 * 1024 * 1024,
            transcendentals=width * slots,
        ),
    )(
        me, in_hbm(mol_feats), in_hbm(w_src), in_hbm(w_dst), in_hbm(w_out.T), below, above,
        edge_src.reshape(slabs, cap), edge_dst.reshape(slabs, cap), edge_live.reshape(slabs, cap),
    )
    onehot, slope, ext = in_hbm(onehot), in_hbm(slope), in_hbm(ext)

    def chunks(count, lanes, dtype):
        return jax.ShapeDtypeStruct((count, part, lanes), dtype)

    near_sums, near_outer = pl.pallas_call(
        functools.partial(near_kernel, half),
        out_shape=(
            pltpu.HBM((mols + wide, width), F32),
            pltpu.HBM((width, entries_wide), F32),
        ),
        in_specs=vmem(3) + [hbm] * 2 + vmem(len(came_near)),
        out_specs=(hbm, hbm),
        scratch_shapes=[
            pltpu.VMEM((entries_wide, near_slots), BF16),
            pltpu.VMEM((width, near_slots), F32),
            pltpu.VMEM((mols + wide, near_slots), BF16),
            pltpu.VMEM((mols + wide, width), F32),
            pltpu.VMEM((width, entries_wide), F32),
            pltpu.SemaphoreType.DMA((len(slot_tiles(near_slots)), 2)),
            pltpu.SemaphoreType.DMA((2,)),
        ],
        compiler_params=big,
        name="near",
        cost_estimate=pl.CostEstimate(
            flops=40 * width * near_slots * entries_wide, bytes_accessed=6 * 1024 * 1024, transcendentals=0
        ),
    )(own, w_out_wide, near_hidden, slope, onehot, *came_near)
    near_sums, near_outer = in_hbm(near_sums), in_hbm(near_outer)
    keep, send, sums, lower, upper, g = pl.pallas_call(
        functools.partial(grad_kernel, half, factor),
        out_shape=(
            chunks(slabs // 2, 2 * width, F32),
            chunks(slabs // 2, 2 * width, BF16),
            jax.ShapeDtypeStruct((2 * mols, width), F32),
            jax.ShapeDtypeStruct((reach, width), BF16),
            jax.ShapeDtypeStruct((reach, width), BF16),
            jax.ShapeDtypeStruct((entries_wide, far_slots), BF16),
        ),
        in_specs=[smem] + vmem(1) + [hbm] * 4 + vmem(len(came_far)),
        out_specs=tuple(vmem(6)),
        scratch_shapes=[
            pltpu.VMEM((width, far_slots), F32),
            pltpu.VMEM((mols + wide, far_slots), BF16),
            pltpu.VMEM((width, wide), BF16),
            pltpu.VMEM((mols + wide, width), F32),
            pltpu.SemaphoreType.DMA((len(slot_tiles(far_slots)), 2)),
            pltpu.SemaphoreType.DMA((2,)),
        ],
        compiler_params=big,
        name="grads",
    )(me, w_out_wide, slope, onehot, ext, near_sums, *came_far)
    lanes = round_up(entries_wide, LANES)
    keep_o, send_o = pl.pallas_call(
        functools.partial(outer_kernel, factor),
        out_shape=(chunks(slabs // 2, lanes, F32), chunks(slabs // 2, lanes, BF16)),
        in_specs=[smem] + vmem(2) + [hbm],
        out_specs=tuple(vmem(2)),
        scratch_shapes=[pltpu.VMEM((width, entries_wide), F32), pltpu.SemaphoreType.DMA(())],
        compiler_params=big,
        name="outer",
        cost_estimate=pl.CostEstimate(
            flops=40 * width * slots * entries_wide, bytes_accessed=4 * 1024 * 1024, transcendentals=0
        ),
    )(me, far_hidden, g, near_outer)

    def fold(bit, place, keep, crossed):
        shape = (keep.shape[0] // 2, keep.shape[2])
        return pl.pallas_call(
            functools.partial(fold_kernel, bit, place),
            out_shape=(chunks(*shape, F32), chunks(*shape, BF16)),
            in_specs=[smem] + vmem(2),
            out_specs=tuple(vmem(2)),
            compiler_params=big,
            name="fold",
        )(me, keep, crossed)

    def close(keep, crossed):
        if rest == 1:
            return [keep, crossed]
        sends = pl.pallas_call(
            close_kernel,
            out_shape=chunks(rest, keep.shape[2], BF16),
            in_specs=vmem(2),
            out_specs=vmem(1)[0],
            compiler_params=big,
            name="close",
        )(keep, crossed)
        same = [[low + rank * (slabs // rest) for rank in range(rest)] for low in range(slabs // rest)]
        return [
            lax.all_to_all(sends, "space", split_axis=0, concat_axis=0, tiled=True, axis_index_groups=same)
        ]

    from_above = lax.ppermute(lower, "space", down)
    from_below = lax.ppermute(upper, "space", up)
    crossed = swap(send, 0, slabs)
    crossed_o = swap(send_o, 0, slabs)
    for (bit, place), (bit_o, place_o) in zip(paths[0][1:], paths[1][1:]):
        if bit == 2:
            keep, crossed, from_above, from_below = lax.optimization_barrier((keep, crossed, from_above, from_below))
        keep, send = fold(bit, place, keep, crossed)
        crossed = swap(send, bit, slabs)
        keep_o, crossed_o, _ = lax.optimization_barrier((keep_o, crossed_o, send))
        keep_o, send_o = fold(bit_o, place_o, keep_o, crossed_o)
        crossed_o = swap(send_o, bit_o, slabs)
    terms = close(keep, crossed)
    terms_o = close(keep_o, crossed_o)
    feature_grad = pl.pallas_call(
        rim_kernel,
        out_shape=jax.ShapeDtypeStruct((mols, width), F32),
        in_specs=vmem(5),
        out_specs=vmem(1)[0],
        compiler_params=big,
        name="rims",
        cost_estimate=pl.CostEstimate(flops=2 * width * slots * width * 40, bytes_accessed=4 * 1024 * 1024, transcendentals=0),
    )(sums, from_below, from_above, w_src, w_dst)
    src_grad, dst_grad, out_grad = pl.pallas_call(
        total_kernel,
        out_shape=(
            jax.ShapeDtypeStruct((part, width), F32),
            jax.ShapeDtypeStruct((part, width), F32),
            jax.ShapeDtypeStruct((part, entries), F32),
        ),
        in_specs=vmem(len(terms) + len(terms_o)),
        out_specs=tuple(vmem(3)),
        compiler_params=big,
        name="totals",
    )(*terms, *terms_o)
    return (feature_grad, src_grad, dst_grad, out_grad)


def solution(mesh):
    placed = (
        P(("groups", "space"), None),
        P(),
        P(),
        P(),
        P("space", "groups", None, None),
        P(("groups", "space")),
        P(("groups", "space")),
        P(("groups", "space")),
    )
    return jax.shard_map(
        on_device,
        mesh=mesh,
        in_specs=placed,
        out_specs=(
            P(("groups", "space"), None),
            P(("groups", "space"), None),
            P(("groups", "space"), None),
            P(("groups", "space"), None),
        ),
        check_vma=False,
    )
```

```python
import functools

import jax
import jax.numpy as jnp
from jax import lax
from jax.experimental import pallas as pl
from jax.experimental.pallas import tpu as pltpu
from jax.sharding import PartitionSpec as P

F32 = jnp.float32
BF16 = jnp.bfloat16
LANES = 128
PACK = 16
NN = (((1,), (0,)), ((), ()))
NT = (((1,), (1,)), ((), ()))


def mm(left, right, dims=NN):
    return lax.dot_general(left, right, dims, preferred_element_type=F32)


def halves(x):
    high = x.astype(BF16)
    return high, (x - high.astype(F32)).astype(BF16)


def round_up(x, to):
    return -(-x // to) * to


def vmem(count):
    return [pl.BlockSpec(memory_space=pltpu.VMEM)] * count


def pack_kernel(rows, half, linked, me_ref, feats_ref, g_ref, even_ref, odd_ref, low_ref, top_ref, here_ref, sems, rim_sems):
    entries, slabs, cap = g_ref.shape
    mols = feats_ref.shape[0]
    reach = low_ref.shape[0]
    groups = LANES // half
    blocks = rows // PACK
    count = sems.shape[0]
    stages = []
    for stage in range(count):
        begin, end = stage * blocks // count, (stage + 1) * blocks // count
        copies = []
        for group in range(groups):
            first = min(entries, group * rows + begin * PACK)
            last = min(entries, group * rows + end * PACK)
            if first < last:
                copies.append(
                    pltpu.make_async_copy(g_ref.at[first:last], here_ref.at[first:last], sems.at[stage, group])
                )
        stages.append((begin, end, copies))
        for copy in copies:
            copy.start()
    rims = [
        pltpu.make_async_copy(feats_ref.at[:reach], low_ref, rim_sems.at[0]),
        pltpu.make_async_copy(feats_ref.at[mols - reach :], top_ref, rim_sems.at[1]),
    ]
    for copy in rims:
        copy.start()
    size = PACK * slabs
    to = lax.broadcasted_iota(jnp.int32, (size, size), 0)
    source = lax.broadcasted_iota(jnp.int32, (size, size), 1)
    slab = to // PACK
    if linked:
        slab = slab ^ me_ref[0]
    perm = jnp.where((to % PACK) * slabs + slab == source, 1.0, 0.0).astype(BF16)

    def lanes_of(block):
        early = []
        for group in range(groups):
            first = group * rows + block * PACK
            valid = max(0, min(PACK, entries - first))
            tiles = []
            if valid:
                tiles.append(here_ref[first : first + valid])
            if valid < PACK:
                tiles.append(jnp.zeros((PACK - valid, slabs, cap), BF16))
            tile = tiles[0] if len(tiles) == 1 else jnp.concatenate(tiles, axis=0)
            early.append(tile.reshape(size, cap)[:, :half])
        return early

    for begin, end, copies in stages:
        for copy in copies:
            copy.wait()
        for block in range(begin, end, 2):
            together = range(block, min(block + 2, end))
            lanes = [piece for one in together for piece in lanes_of(one)]
            moved = mm(perm, jnp.concatenate(lanes, axis=1)).astype(BF16)
            for index, one in enumerate(together):
                chunk = moved[:, index * LANES : (index + 1) * LANES].reshape(slabs // 2, 2, PACK, LANES)
                here = pl.ds(one * PACK, PACK)
                even_ref[:, here, :] = chunk[:, 0]
                odd_ref[:, here, :] = chunk[:, 1]
    for copy in rims:
        copy.wait()


def inner(slab, slabs):
    bits = slabs.bit_length() - 1
    return ((slab >> (bits - 1)) ^ (slab >> (bits - 2))) & 1


def by_place(pair, me, slabs):
    return pair[0] + inner(me, slabs) * (pair[1] - pair[0])


def join_kernel(turns, me_ref, even_ref, other_ref, *message_refs):
    for pair, message_ref in zip(turns, message_refs):
        k = by_place(pair, me_ref[0], 2 * even_ref.shape[0])
        message_ref[0] = even_ref[k]
        message_ref[1] = other_ref[k]


def unpack(half, refs, g_ref):
    groups = LANES // half
    rows = g_ref.shape[0] // groups
    chunks = [(ref, index) for ref in refs for index in range(ref.shape[0])]
    tiles = len(chunks) // groups
    for tile in range(tiles):
        here = [ref[index] for ref, index in chunks[tile * groups : (tile + 1) * groups]]
        for group in range(groups):
            lanes = slice(group * half, (group + 1) * half)
            g_ref[group * rows : (group + 1) * rows, tile * LANES : (tile + 1) * LANES] = jnp.concatenate(
                [chunk[:, lanes] for chunk in here], axis=1
            )
    return tiles * LANES


def slot_rows(ref, me, half, linked, near, far):
    per = LANES // half

    def rows_of(ids):
        rows = []
        for tile in range(len(ids) // per):
            here = ids[tile * per : (tile + 1) * per]
            pieces = [ref[pl.ds(me ^ by_place(i, me, ref.shape[0]) if linked else i, 1), :] for i in here]
            rows.append(jnp.concatenate([piece[:, :half] for piece in pieces], axis=1))
        return rows

    own = ref[pl.ds(me, 1), :][:, half:]
    own = jnp.concatenate([own, jnp.full((1, LANES - half), -1, jnp.int32)], axis=1)
    return rows_of(near) + [own] + rows_of(far)


def edge_kernel(
    half, linked, near, far, me_ref, feats_hbm, w_src_hbm, w_dst_hbm, w_out_hbm, below_ref, above_ref, src_ref, dst_ref,
    live_ref, onehot_hbm, slope_hbm, ext_hbm, near_hidden_ref, far_hidden_ref, w_wide_ref,
    onehot_ref, slope_ref, ext_ref, w_rows_ref, feats_ref, w_src_ref, w_dst_ref, w_out_ref, sems, in_sems,
):
    inputs = [
        pltpu.make_async_copy(hbm, ref, in_sems.at[index])
        for index, (hbm, ref) in enumerate(
            ((feats_hbm, feats_ref), (w_src_hbm, w_src_ref), (w_dst_hbm, w_dst_ref), (w_out_hbm, w_out_ref))
        )
    ]
    for copy in inputs:
        copy.start()
    me = me_ref[0]
    mols = feats_ref.shape[0]
    reach = below_ref.shape[0]
    wide = mols + 2 * reach
    slots = slope_ref.shape[1]
    entries = w_out_ref.shape[0]
    near_slots = near_hidden_ref.shape[1]
    copies = []

    def send(source, target):
        copy = pltpu.make_async_copy(source, target, sems.at[len(copies)])
        copy.start()
        copies.append(copy)

    mol_src = lax.broadcasted_iota(jnp.int32, (mols, LANES), 0)
    mol_dst = lax.broadcasted_iota(jnp.int32, (wide, LANES), 0)
    lists = [slot_rows(ref, me, half, linked, near, far) for ref in (src_ref, dst_ref, live_ref)]
    for tile, (src, dst, live) in enumerate(zip(*lists)):
        src = jnp.where(live > 0, src, -1)
        moved = jnp.where(dst < reach, dst + mols, jnp.where(dst < reach + mols, dst - reach, dst))
        dst = jnp.where(live > 0, moved, -1)
        one_src = jnp.where(mol_src == src, 1.0, 0.0).astype(BF16)
        one_dst = jnp.where(mol_dst == dst, 1.0, 0.0).astype(BF16)
        here = pl.ds(tile * LANES, LANES)
        onehot_ref[:, here] = jnp.concatenate([one_src, one_dst], axis=0)
    for copy in inputs[:3]:
        copy.wait()
    feats = feats_ref[...]
    ext = jnp.concatenate([feats, below_ref[...], above_ref[...]], axis=0)
    ext_ref[...] = ext.T
    send(ext_ref, ext_hbm)
    proj_src = mm(feats, w_src_ref[...])
    proj_dst = mm(ext, w_dst_ref[...])
    proj = jnp.concatenate([proj_src, proj_dst], axis=0).T
    high, low = halves(proj)
    for first, last in slot_tiles(near_slots) + [(near_slots + f, near_slots + l) for f, l in slot_tiles(slots - near_slots)]:
        here = pl.ds(first, last - first)
        send(onehot_ref.at[:, here], onehot_hbm.at[:, here])
        onehot = onehot_ref[:, here]
        pre = mm(high, onehot) + mm(low, onehot)
        sigma = 1.0 / (1.0 + jnp.exp(-pre))
        hidden = (pre * sigma).astype(BF16)
        if first < near_slots:
            near_hidden_ref[:, here] = hidden
        else:
            far_hidden_ref[:, pl.ds(first - near_slots, last - first)] = hidden
        slope_ref[:, here] = sigma * (1.0 + pre * (1.0 - sigma))
        send(slope_ref.at[:, here], slope_hbm.at[:, here])
    inputs[3].wait()
    whole = entries // LANES * LANES
    w_rows_ref[whole:] = jnp.zeros((w_rows_ref.shape[0] - whole, w_rows_ref.shape[1]), BF16)
    w_rows_ref[:whole] = w_out_ref[:whole]
    w_rows_ref[whole:entries] = w_out_ref[whole:]
    w_wide_ref[...] = w_rows_ref[...].T
    for copy in copies:
        copy.wait()


def halve(terms, odd, place, keep_ref, send_ref, first):
    count, rows, _ = keep_ref.shape
    width = terms.shape[-1]
    lanes = slice(first, first + width)
    inner = 1 << place
    pairs = terms.reshape(count // inner, 2, inner, rows, width)
    even_part = pairs[:, 0].reshape(count, rows, width)
    odd_part = pairs[:, 1].reshape(count, rows, width)
    keep_ref[:, :, lanes] = jnp.where(odd > 0, odd_part, even_part)
    send_ref[:, :, lanes] = jnp.where(odd > 0, even_part, odd_part).astype(BF16)


def fold_kernel(bit, place, me_ref, keep_ref, came_ref, next_ref, send_ref):
    odd = (me_ref[0] >> bit) % 2
    halve(keep_ref[...] + came_ref[...].astype(F32), odd, place, next_ref, send_ref, 0)


def close_kernel(keep_ref, came_ref, send_ref):
    send_ref[...] = (keep_ref[...] + came_ref[...].astype(F32)).astype(BF16)


def slot_tiles(slots):
    step = 2 * LANES
    return [(first, min(first + step, slots)) for first in range(0, slots, step)]


def start_tiles(slots, offset, slope_hbm, onehot_hbm, slope_ref, onehot_ref, sems):
    tiles = []
    for tile, (first, last) in enumerate(slot_tiles(slots)):
        there, here = pl.ds(offset + first, last - first), pl.ds(first, last - first)
        copies = [
            pltpu.make_async_copy(slope_hbm.at[:, there], slope_ref.at[:, here], sems.at[tile, 0]),
            pltpu.make_async_copy(onehot_hbm.at[:, there], onehot_ref.at[:, here], sems.at[tile, 1]),
        ]
        for copy in copies:
            copy.start()
        tiles.append((slice(first, last), copies))
    return tiles


def sum_edges(tiles, w_out_ref, g_ref, slope_ref, onehot_ref):
    sums = None
    for lanes, copies in tiles:
        dh = mm(w_out_ref[...], g_ref[:, lanes])
        for copy in copies:
            copy.wait()
        dpre = (dh * slope_ref[:, lanes]).astype(BF16)
        term = mm(onehot_ref[:, lanes], dpre, NT)
        sums = term if sums is None else sums + term
    return sums


def near_kernel(half, own_ref, w_out_ref, hidden_ref, slope_hbm, onehot_hbm, *rest):
    *came_refs, sums_hbm, outer_hbm, g_ref, slope_ref, onehot_ref, sums_ref, outer_ref, sems, out_sems = rest
    slots = g_ref.shape[1]
    tiles = start_tiles(slots, 0, slope_hbm, onehot_hbm, slope_ref, onehot_ref, sems)
    filled = unpack(half, came_refs, g_ref)
    g_ref[:, filled:] = own_ref[...]
    outer_ref[...] = mm(hidden_ref[...], g_ref[...], NT)
    outer_copy = pltpu.make_async_copy(outer_ref, outer_hbm, out_sems.at[0])
    outer_copy.start()
    sums_ref[...] = sum_edges(tiles, w_out_ref, g_ref, slope_ref, onehot_ref)
    sums_copy = pltpu.make_async_copy(sums_ref, sums_hbm, out_sems.at[1])
    sums_copy.start()
    outer_copy.wait()
    sums_copy.wait()


def grad_kernel(half, factor, me_ref, w_out_ref, slope_hbm, onehot_hbm, ext_hbm, near_hbm, *rest):
    (
        *came_refs, keep_ref, send_ref, sums_ref, lower_ref, upper_ref, g_ref,
        slope_ref, onehot_ref, ext_ref, near_ref, tile_sems, sems,
    ) = rest
    odd = me_ref[0] % 2
    width = w_out_ref.shape[0]
    slots = g_ref.shape[1]
    inside = sums_ref.shape[0]
    mols = inside // 2
    reach = lower_ref.shape[0]
    tiles = start_tiles(slots, slope_hbm.shape[1] - slots, slope_hbm, onehot_hbm, slope_ref, onehot_ref, tile_sems)
    whole = [
        pltpu.make_async_copy(near_hbm, near_ref, sems.at[0]),
        pltpu.make_async_copy(ext_hbm, ext_ref, sems.at[1]),
    ]
    for copy in whole:
        copy.start()
    unpack(half, came_refs, g_ref)
    sums = sum_edges(tiles, w_out_ref, g_ref, slope_ref, onehot_ref)
    for copy in whole:
        copy.wait()
    sums = sums + near_ref[...]
    lower_ref[...] = sums[inside : inside + reach].astype(BF16)
    upper_ref[...] = sums[inside + reach :].astype(BF16)
    sums_ref[...] = sums[:inside]
    high, low = halves(sums)
    feats = ext_ref[:, :mols]
    rim = ext_ref[:, mols:]
    halve(factor * (mm(feats, high[:mols]) + mm(feats, low[:mols])), odd, 0, keep_ref, send_ref, 0)
    rim_term = mm(jnp.concatenate([rim, rim], axis=1), jnp.concatenate([high[inside:], low[inside:]], axis=0))
    dst_term = mm(feats, high[mols:inside]) + mm(feats, low[mols:inside]) + rim_term
    halve(factor * dst_term, odd, 0, keep_ref, send_ref, width)


def outer_kernel(factor, me_ref, hidden_ref, g_ref, near_hbm, keep_ref, send_ref, near_ref, sem):
    copy = pltpu.make_async_copy(near_hbm, near_ref, sem)
    copy.start()
    term = mm(hidden_ref[...], g_ref[...], NT)
    copy.wait()
    term = factor * (term + near_ref[...])
    padding = keep_ref.shape[2] - term.shape[1]
    if padding > 0:
        term = jnp.concatenate([term, jnp.zeros((term.shape[0], padding), F32)], axis=1)
    halve(term, me_ref[0] % 2, 0, keep_ref, send_ref, 0)


def rim_kernel(sums_ref, from_below_ref, from_above_ref, w_src_ref, w_dst_ref, out_ref):
    mols = out_ref.shape[0]
    reach = from_below_ref.shape[0]
    src = sums_ref[:mols]
    dst = sums_ref[mols:]
    dst = jnp.concatenate(
        [
            dst[:reach] + from_below_ref[...].astype(F32),
            dst[reach : mols - reach],
            dst[mols - reach :] + from_above_ref[...].astype(F32),
        ],
        axis=0,
    )
    w_src = w_src_ref[...]
    w_dst = w_dst_ref[...]
    src_high, src_low = halves(src)
    dst_high, dst_low = halves(dst)
    out_ref[...] = mm(src_high, w_src, NT) + mm(src_low, w_src, NT) + mm(dst_high, w_dst, NT) + mm(dst_low, w_dst, NT)


def total_kernel(*refs):
    *refs, src_ref, dst_ref, out_ref = refs
    count = len(refs) // 2
    width = src_ref.shape[1]
    totals = []
    for piece in (refs[:count], refs[count:]):
        terms = [ref[slab].astype(F32) for ref in piece for slab in range(ref.shape[0])]
        totals.append(functools.reduce(jnp.add, terms))
    sides, outer = totals
    src_ref[...] = sides[:, :width]
    dst_ref[...] = sides[:, width:]
    out_ref[...] = outer[:, : out_ref.shape[1]]


def in_hbm(x):
    return pltpu.with_memory_space_constraint(x, pltpu.HBM)


def swap(block, bit, slabs):
    return lax.ppermute(block, "space", [(i, i ^ (1 << bit)) for i in range(slabs)])


def on_device(mol_feats, w_src, w_dst, w_out, grad_blocks, edge_src, edge_dst, edge_live):
    slabs = lax.axis_size("space")
    mols, width = mol_feats.shape
    entries = w_out.shape[1]
    cap = grad_blocks.shape[2]
    half = cap // 2
    reach = mols // 4
    groups = LANES // half
    slots = (slabs // groups + 1) * LANES
    bits = slabs.bit_length() - 1
    if 3 <= bits <= 4:
        late_bits = tuple((bit, 0) for bit in range(3, bits))
        paths = (((0, 0), (1, 0), (2, 0)) + late_bits, ((0, 0), (2, 1), (1, 0)) + late_bits)
    else:
        paths = (tuple((bit, 0) for bit in range(min(bits, 2))),) * 2
    rest = slabs >> len(paths[0])
    part = width // slabs
    factor = float(edge_src.shape[0] * slabs) ** (-0.5)
    me = lax.axis_index("space").astype(jnp.int32).reshape(1)
    smem = pl.BlockSpec(memory_space=pltpu.SMEM)
    hbm = pl.BlockSpec(memory_space=pltpu.HBM)
    big = pltpu.CompilerParams(vmem_limit_bytes=24 * 1024 * 1024)
    up = [(i, (i + 1) % slabs) for i in range(slabs)]
    down = [((i + 1) % slabs, i) for i in range(slabs)]

    rows = round_up(pl.cdiv(entries, groups), PACK)
    stages = 4
    linked = slabs == 16
    even, odd, low, top = pl.pallas_call(
        functools.partial(pack_kernel, rows, half, linked),
        out_shape=(
            jax.ShapeDtypeStruct((slabs // 2, rows, LANES), BF16),
            jax.ShapeDtypeStruct((slabs // 2, rows, LANES), BF16),
            jax.ShapeDtypeStruct((reach, width), BF16),
            jax.ShapeDtypeStruct((reach, width), BF16),
        ),
        in_specs=[smem, hbm, hbm],
        out_specs=tuple(vmem(4)),
        scratch_shapes=[
            pltpu.VMEM((entries, slabs, cap), BF16),
            pltpu.SemaphoreType.DMA((stages, groups)),
            pltpu.SemaphoreType.DMA((2,)),
        ],
        compiler_params=big,
        name="pack",
    )(me, in_hbm(mol_feats), in_hbm(jnp.transpose(grad_blocks[0], (2, 0, 1))))
    below = lax.ppermute(top, "space", up)
    above = lax.ppermute(low, "space", down)
    late = lax.dynamic_index_in_dim(grad_blocks[0], me[0], 0, keepdims=False)[half:]
    own = jnp.pad(late.T, ((0, groups * rows - entries), (0, LANES - half)))
    if linked:
        other = swap(odd, 0, slabs)
        other, below, above, own = lax.optimization_barrier((other, below, above, own))
        quarter = slabs // 4
        turns = [(0, 0), (1, 6), (2, 4), (3, 5), (6, 7), (7, 1), (4, 2), (5, 3)]
        kept = (0, 1, 6, 7)
        messages = pl.pallas_call(
            functools.partial(join_kernel, turns),
            out_shape=(jax.ShapeDtypeStruct((2, rows, LANES), BF16),) * (slabs // 2),
            in_specs=[smem] + vmem(2),
            out_specs=tuple(vmem(slabs // 2)),
            compiler_params=big,
            name="join",
        )(me, even, other)
        came = [messages[0]]
        for turn in range(1, 2 * quarter):
            route = [(i, i ^ (2 * turns[turn][inner(i, slabs)])) for i in range(slabs)]
            came.append(lax.ppermute(messages[turn], "space", route))
        sources = [pair if pair[0] in kept else pair[::-1] for pair in turns]
        ids = [(2 * first + j, 2 * second + j) for first, second in sources for j in range(2)]
        near, far = tuple(ids[: 2 * quarter + 2]), tuple(ids[2 * quarter + 2 :])
        came_near, came_far = came[: quarter + 1], came[quarter + 1 :]
    else:
        packed = jnp.stack([even, odd], axis=1).reshape(slabs, rows, LANES)
        near, far = (), tuple(range(slabs))
        came_near = []
        came_far = [lax.all_to_all(packed, "space", split_axis=0, concat_axis=0, tiled=True)]
    far_slots = len(far) * half
    near_slots = slots - far_slots

    wide = mols + 2 * reach
    entries_wide = groups * rows
    pieces = len(slot_tiles(near_slots)) + len(slot_tiles(far_slots))
    onehot, slope, ext, near_hidden, far_hidden, w_out_wide = pl.pallas_call(
        functools.partial(edge_kernel, half, linked, near, far),
        out_shape=(
            pltpu.HBM((mols + wide, slots), BF16),
            pltpu.HBM((width, slots), F32),
            pltpu.HBM((width, wide), BF16),
            jax.ShapeDtypeStruct((width, near_slots), BF16),
            jax.ShapeDtypeStruct((width, far_slots), BF16),
            jax.ShapeDtypeStruct((width, entries_wide), BF16),
        ),
        in_specs=[smem] + [hbm] * 4 + vmem(5),
        out_specs=(hbm,) * 3 + tuple(vmem(3)),
        scratch_shapes=[
            pltpu.VMEM((mols + wide, slots), BF16),
            pltpu.VMEM((width, slots), F32),
            pltpu.VMEM((width, wide), BF16),
            pltpu.VMEM((entries_wide, width), BF16),
            pltpu.VMEM((mols, width), BF16),
            pltpu.VMEM((width, width), BF16),
            pltpu.VMEM((width, width), BF16),
            pltpu.VMEM((entries, width), BF16),
            pltpu.SemaphoreType.DMA((2 * pieces + 1,)),
            pltpu.SemaphoreType.DMA((4,)),
        ],
        compiler_params=big,
        name="edges",
        cost_estimate=pl.CostEstimate(
            flops=40 * width * slots * 2 * (2 * mols + 2 * reach), bytes_accessed=8 * 1024 * 1024,
            transcendentals=width * slots,
        ),
    )(
        me, in_hbm(mol_feats), in_hbm(w_src), in_hbm(w_dst), in_hbm(w_out.T), below, above,
        edge_src.reshape(slabs, cap), edge_dst.reshape(slabs, cap), edge_live.reshape(slabs, cap),
    )
    onehot, slope, ext = in_hbm(onehot), in_hbm(slope), in_hbm(ext)

    def chunks(count, lanes, dtype):
        return jax.ShapeDtypeStruct((count, part, lanes), dtype)

    near_sums, near_outer = pl.pallas_call(
        functools.partial(near_kernel, half),
        out_shape=(
            pltpu.HBM((mols + wide, width), F32),
            pltpu.HBM((width, entries_wide), F32),
        ),
        in_specs=vmem(3) + [hbm] * 2 + vmem(len(came_near)),
        out_specs=(hbm, hbm),
        scratch_shapes=[
            pltpu.VMEM((entries_wide, near_slots), BF16),
            pltpu.VMEM((width, near_slots), F32),
            pltpu.VMEM((mols + wide, near_slots), BF16),
            pltpu.VMEM((mols + wide, width), F32),
            pltpu.VMEM((width, entries_wide), F32),
            pltpu.SemaphoreType.DMA((len(slot_tiles(near_slots)), 2)),
            pltpu.SemaphoreType.DMA((2,)),
        ],
        compiler_params=big,
        name="near",
        cost_estimate=pl.CostEstimate(
            flops=40 * width * near_slots * entries_wide, bytes_accessed=6 * 1024 * 1024, transcendentals=0
        ),
    )(own, w_out_wide, near_hidden, slope, onehot, *came_near)
    near_sums, near_outer = in_hbm(near_sums), in_hbm(near_outer)
    keep, send, sums, lower, upper, g = pl.pallas_call(
        functools.partial(grad_kernel, half, factor),
        out_shape=(
            chunks(slabs // 2, 2 * width, F32),
            chunks(slabs // 2, 2 * width, BF16),
            jax.ShapeDtypeStruct((2 * mols, width), F32),
            jax.ShapeDtypeStruct((reach, width), BF16),
            jax.ShapeDtypeStruct((reach, width), BF16),
            jax.ShapeDtypeStruct((entries_wide, far_slots), BF16),
        ),
        in_specs=[smem] + vmem(1) + [hbm] * 4 + vmem(len(came_far)),
        out_specs=tuple(vmem(6)),
        scratch_shapes=[
            pltpu.VMEM((width, far_slots), F32),
            pltpu.VMEM((mols + wide, far_slots), BF16),
            pltpu.VMEM((width, wide), BF16),
            pltpu.VMEM((mols + wide, width), F32),
            pltpu.SemaphoreType.DMA((len(slot_tiles(far_slots)), 2)),
            pltpu.SemaphoreType.DMA((2,)),
        ],
        compiler_params=big,
        name="grads",
    )(me, w_out_wide, slope, onehot, ext, near_sums, *came_far)
    lanes = round_up(entries_wide, LANES)
    keep_o, send_o = pl.pallas_call(
        functools.partial(outer_kernel, factor),
        out_shape=(chunks(slabs // 2, lanes, F32), chunks(slabs // 2, lanes, BF16)),
        in_specs=[smem] + vmem(2) + [hbm],
        out_specs=tuple(vmem(2)),
        scratch_shapes=[pltpu.VMEM((width, entries_wide), F32), pltpu.SemaphoreType.DMA(())],
        compiler_params=big,
        name="outer",
        cost_estimate=pl.CostEstimate(
            flops=40 * width * slots * entries_wide, bytes_accessed=4 * 1024 * 1024, transcendentals=0
        ),
    )(me, far_hidden, g, near_outer)

    def fold(bit, place, keep, crossed):
        shape = (keep.shape[0] // 2, keep.shape[2])
        return pl.pallas_call(
            functools.partial(fold_kernel, bit, place),
            out_shape=(chunks(*shape, F32), chunks(*shape, BF16)),
            in_specs=[smem] + vmem(2),
            out_specs=tuple(vmem(2)),
            compiler_params=big,
            name="fold",
        )(me, keep, crossed)

    def close(keep, crossed):
        if rest == 1:
            return [keep, crossed]
        sends = pl.pallas_call(
            close_kernel,
            out_shape=chunks(rest, keep.shape[2], BF16),
            in_specs=vmem(2),
            out_specs=vmem(1)[0],
            compiler_params=big,
            name="close",
        )(keep, crossed)
        same = [[low + rank * (slabs // rest) for rank in range(rest)] for low in range(slabs // rest)]
        return [
            lax.all_to_all(sends, "space", split_axis=0, concat_axis=0, tiled=True, axis_index_groups=same)
        ]

    from_above = lax.ppermute(lower, "space", down)
    from_below = lax.ppermute(upper, "space", up)
    crossed = swap(send, 0, slabs)
    crossed_o = swap(send_o, 0, slabs)
    for (bit, place), (bit_o, place_o) in zip(paths[0][1:], paths[1][1:]):
        if bit == 2:
            keep, crossed, from_above, from_below = lax.optimization_barrier((keep, crossed, from_above, from_below))
        keep, send = fold(bit, place, keep, crossed)
        crossed = swap(send, bit, slabs)
        keep_o, crossed_o, _ = lax.optimization_barrier((keep_o, crossed_o, send))
        keep_o, send_o = fold(bit_o, place_o, keep_o, crossed_o)
        crossed_o = swap(send_o, bit_o, slabs)
    terms = close(keep, crossed)
    terms_o = close(keep_o, crossed_o)
    feature_grad = pl.pallas_call(
        rim_kernel,
        out_shape=jax.ShapeDtypeStruct((mols, width), F32),
        in_specs=vmem(5),
        out_specs=vmem(1)[0],
        compiler_params=big,
        name="rims",
        cost_estimate=pl.CostEstimate(flops=2 * width * slots * width * 40, bytes_accessed=4 * 1024 * 1024, transcendentals=0),
    )(sums, from_below, from_above, w_src, w_dst)
    src_grad, dst_grad, out_grad = pl.pallas_call(
        total_kernel,
        out_shape=(
            jax.ShapeDtypeStruct((part, width), F32),
            jax.ShapeDtypeStruct((part, width), F32),
            jax.ShapeDtypeStruct((part, entries), F32),
        ),
        in_specs=vmem(len(terms) + len(terms_o)),
        out_specs=tuple(vmem(3)),
        compiler_params=big,
        name="totals",
    )(*terms, *terms_o)
    return (feature_grad, src_grad, dst_grad, out_grad)


def solution(mesh):
    placed = (
        P(("groups", "space"), None),
        P(),
        P(),
        P(),
        P("space", "groups", None, None),
        P(("groups", "space")),
        P(("groups", "space")),
        P(("groups", "space")),
    )
    return jax.shard_map(
        on_device,
        mesh=mesh,
        in_specs=placed,
        out_specs=(
            P(("groups", "space"), None),
            P(("groups", "space"), None),
            P(("groups", "space"), None),
            P(("groups", "space"), None),
        ),
        check_vma=False,
    )
```
